32 devices in a mesh: dp: 2 (over x), row: 4 (over y, core), col: 4 (over z).
Axes of the slice: x: 2, y: 2, z: 4, core: 2. Of those that a mesh axis runs over, the one named last changes fastest.
Arguments:
- layer_input: bfloat16 [8192, 2560], P('dp', ('row', 'col')), may hold values from -6 to 6
- attn_gain: float32 [2560], P(('row', 'col')), may hold values from 0.5 to 1.5
- mlp_gain: float32 [2560], P(('row', 'col')), may hold values from 0.5 to 1.5
- query_weight: bfloat16 [2560, 2560], P('row', 'col'), may hold values from -0.125 to 0.125
- key_weight: bfloat16 [2560, 640], P('row', 'col'), may hold values from -0.125 to 0.125
- value_weight: bfloat16 [2560, 640], P('row', 'col'), may hold values from -0.125 to 0.125
- mix_weight: bfloat16 [2560, 2560], P('col', 'row'), may hold values from -1.5 to 1.5
- gate_weight: bfloat16 [2560, 6912], P('row', 'col'), may hold values from -0.125 to 0.125
- up_weight: bfloat16 [2560, 6912], P('row', 'col'), may hold values from -0.125 to 0.125
- down_weight: bfloat16 [6912, 2560], P('col', 'row'), may hold values from -0.078125 to 0.078125
- output_grad: bfloat16 [8192, 2560], P('dp', ('row', 'col')), may hold values from -6 to 6
- segment_ids: int32 [8192], P(('dp', 'row')), may hold values from 0 to 8, as said below
- position_ids: int32 [8192], P(('dp', 'row')), may hold values from 0 to 4095, as said below
Outputs:
- layer_output: bfloat16 [8192, 2560], P('dp', ('row', 'col'))
- input_grad: float32 [8192, 2560], P('dp', ('row', 'col'))
- attn_gain_grad: float32 [2560], P(('row', 'col'))
- mlp_gain_grad: float32 [2560], P(('row', 'col'))
- query_grad: float32 [2560, 2560], P('row', 'col')
- key_grad: float32 [2560, 640], P('row', 'col')
- value_grad: float32 [2560, 640], P('row', 'col')
- mix_grad: float32 [2560, 2560], P('col', 'row')
- gate_grad: float32 [2560, 6912], P('row', 'col')
- up_grad: float32 [2560, 6912], P('row', 'col')
- down_grad: float32 [6912, 2560], P('col', 'row')
The draws below stay inside these ranges and needn't reach their ends.
Inputs may be any that keep to these rules, and one draw needn't show every extreme that they name: `segment_ids`: tokens come in groups of 2048: the first 1024 have id 0, the rest are 8 runs of consecutive tokens with ids 1 to 8 in order, each run one token or more. `position_ids`: each group has an offset: its prompt's positions are the offset plus 0 to 1023, a continuation's the offset plus 1024 plus the token's place within that continuation; some group has offset 0 and some group's largest position is 4095.
All inputs are finite; a program needn't handle non-finite values.
Results may differ from the reference program's by a relative error of at most 0.017.
Values may be sent and summed in bfloat16 or wider, within the bound.
No kernel may reach another device: no remote copies, remote signals or barrier semaphores. Data moves between devices by JAX's collectives and lax.ppermute only.
A program may use at most 320 MiB of HBM per device.

```python
import jax
import jax.numpy as jnp
from jax import lax

D = 2560
HEADS = 32
KV_HEADS = 8
HEAD = 80
FF = 6912
PROMPT = 1024
CONTS = 8
TOKENS = 8192


def group_layout(key):
    groups = TOKENS // (2 * PROMPT)
    keys = jax.random.split(jax.random.fold_in(key, 71), groups)

    def one(group_key):
        picks = jax.random.permutation(group_key, PROMPT - 1)[:CONTS - 1] + 1
        cuts = jnp.sort(picks).astype(jnp.int32)
        place = jnp.arange(PROMPT, dtype=jnp.int32)
        after = place[:, None] >= cuts[None, :]
        labels = 1 + jnp.sum(after.astype(jnp.int32), axis=1)
        begins = jnp.max(jnp.where(after, cuts[None, :], 0), axis=1)
        segment = jnp.concatenate([jnp.zeros((PROMPT,), jnp.int32), labels.astype(jnp.int32)])
        position = jnp.concatenate([place, PROMPT + place - begins])
        return (segment.astype(jnp.int32), position.astype(jnp.int32))
    segment, local = jax.vmap(one)(keys)
    tops = jnp.max(local, axis=1).astype(jnp.int32)
    room = (4096 - tops).astype(jnp.int32)
    noise = jax.random.randint(jax.random.fold_in(key, 72), (groups,), 0, 1 << 20).astype(jnp.int32)
    offsets = (noise % room).astype(jnp.int32)
    group_index = jnp.arange(groups, dtype=jnp.int32)
    offsets = jnp.where(group_index == 0, 4095 - tops, offsets)
    offsets = jnp.where(group_index == 1, 0, offsets).astype(jnp.int32)
    position = (local + offsets[:, None]).astype(jnp.int32)
    return (segment.reshape(-1), position.reshape(-1))


def draw_segment_ids(key, part):
    return group_layout(key)[0]


def draw_position_ids(key, part):
    return group_layout(key)[1]


def levels(key, extent, cuts, low, top_value):
    factor_of = 1.0
    for dim, blocks in cuts:
        draws = jax.random.uniform(jax.random.fold_in(jax.random.fold_in(key, 6), dim), (blocks,), jnp.float32, low / len(cuts), top_value / len(cuts))
        factor_of = factor_of * jnp.repeat(jnp.exp(draws), extent[dim] // blocks).reshape((-1,) + (1,) * (len(extent) - 1 - dim))
    return factor_of


def gaussian(key, shape, deviation, bound, cuts=(), held_as=jnp.bfloat16):
    level = levels(key, shape, cuts, -0.22, 0.18) if cuts else 1.0
    drawn = jax.random.normal(key, shape, jnp.float32) * deviation * level
    return jnp.minimum(jnp.maximum(drawn, -bound), bound).astype(held_as)


def setup_inputs(seed: int = 0) -> dict:
    seeds = jax.random.split(jax.random.key(seed), 14)
    return {
        "layer_input": gaussian(seeds[0], (TOKENS, D), 1.0, 6.0, ((0, 2), (1, 16))),
        "attn_gain": jnp.clip(1.0 + 0.1 * jax.random.normal(seeds[1], (D,), jnp.float32), 0.5, 1.5),
        "mlp_gain": jnp.clip(1.0 + 0.1 * jax.random.normal(seeds[2], (D,), jnp.float32), 0.5, 1.5),
        "query_weight": gaussian(seeds[3], (D, HEADS * HEAD), D ** -0.5, 0.125, ((0, 4), (1, 4))),
        "key_weight": gaussian(seeds[4], (D, KV_HEADS * HEAD), D ** -0.5, 0.125, ((0, 4), (1, 4))),
        "value_weight": gaussian(seeds[5], (D, KV_HEADS * HEAD), D ** -0.5, 0.125, ((0, 4), (1, 4))),
        "mix_weight": gaussian(seeds[6], (HEADS * HEAD, D), 16 ** -0.5, 1.5, ((0, 4), (1, 4))),
        "gate_weight": gaussian(seeds[7], (D, FF), D ** -0.5, 0.125, ((0, 4), (1, 4))),
        "up_weight": gaussian(seeds[8], (D, FF), D ** -0.5, 0.125, ((0, 4), (1, 4))),
        "down_weight": gaussian(seeds[9], (FF, D), FF ** -0.5, 0.078125, ((0, 4), (1, 4))),
        "output_grad": gaussian(seeds[10], (TOKENS, D), 1.0, 6.0, ((0, 2), (1, 16))),
        "segment_ids": draw_segment_ids(jax.random.fold_in(seeds[13], 71), 0),
        "position_ids": draw_position_ids(jax.random.fold_in(seeds[13], 71), 0),
    }


@jax.custom_vjp
def low(v):
    return lax.optimization_barrier(v.astype(jnp.bfloat16)).astype(jnp.float32)

@jax.custom_vjp
def low_back(v):
    return v

def low_keep(v):
    return (low(v), None)

def low_pass(kept, grad):
    return (grad,)

def back_keep(v):
    return (v, None)

def back_low(kept, grad):
    return (low(grad),)
low.defvjp(low_keep, low_pass)
low_back.defvjp(back_keep, back_low)
EPS = 1e-05
THETA = 10000.0
NEG = -1e+30
HIGH = lax.Precision.HIGHEST

def matmul(left, right):
    return jnp.dot(left, right, precision=HIGH, preferred_element_type=jnp.float32)

def rms_norm(value, gain):
    return value * lax.rsqrt(lax.optimization_barrier(jnp.mean(value * value, axis=1, keepdims=True)) + EPS) * gain[None, :]

def rope_parts(positions):
    half = HEAD // 2
    freq = THETA ** (-jnp.arange(half, dtype=jnp.float32) * 2.0 / HEAD)
    angle = positions.astype(jnp.float32)[:, None] * freq[None, :]
    return (jnp.cos(angle), jnp.sin(angle))

def rotate(value, cos_part, sin_part):
    half = HEAD // 2
    first = value[..., :half]
    second = value[..., half:]
    cosine = cos_part[:, None, :]
    sine = sin_part[:, None, :]
    return jnp.concatenate([first * cosine - second * sine, second * cosine + first * sine], axis=-1)

def attention(queries, keys, values, segments):
    span = 2 * PROMPT
    groups = queries.shape[0] // span
    block = min(512, PROMPT)
    repeat = HEADS // KV_HEADS
    scale = HEAD ** (-0.5)
    q_groups = queries.reshape(groups, span // block, block, KV_HEADS, repeat, HEAD)
    k_groups = keys.reshape(groups, span, KV_HEADS, HEAD)
    v_groups = values.reshape(groups, span, KV_HEADS, HEAD)
    s_groups = segments.reshape(groups, span)
    key_index = jnp.arange(span, dtype=jnp.int32)

    def group_fn(inputs):
        q_all, k_all, v_all, seg_all = inputs

        def block_fn(binputs):
            q_block, index = binputs
            start = (index * block).astype(jnp.int32)
            rows_index = start + jnp.arange(block, dtype=jnp.int32)
            seg_rows = lax.dynamic_slice_in_dim(seg_all, start, block, 0)
            scores = jnp.einsum('bgrd,kgd->grbk', q_block, k_all, precision=HIGH) * scale
            scores = low_back(scores)
            visible = (key_index[None, :] <= rows_index[:, None]) & ((seg_all[None, :] == 0) | (seg_all[None, :] == seg_rows[:, None]))
            scores = jnp.where(visible[None, None], scores, NEG)
            peak = lax.optimization_barrier(jnp.max(scores, axis=-1, keepdims=True))
            weights = jnp.exp(scores - peak)
            weights = weights / lax.optimization_barrier(jnp.sum(weights, axis=-1, keepdims=True))
            weights = low(weights)
            return jnp.einsum('grbk,kgd->bgrd', weights, v_all, precision=HIGH)
        outs = lax.map(jax.checkpoint(block_fn), (q_all, jnp.arange(span // block, dtype=jnp.int32)))
        return outs.reshape(span, HEADS * HEAD)
    result = lax.map(jax.checkpoint(group_fn), (q_groups, k_groups, v_groups, s_groups))
    return result.reshape(-1, HEADS * HEAD)

def reference(layer_input, attn_gain, mlp_gain, query_weight, key_weight, value_weight, mix_weight, gate_weight, up_weight, down_weight, output_grad, segment_ids, position_ids):
    cos_part, sin_part = rope_parts(position_ids)
    count = layer_input.shape[0]

    def forward(source, gain_one, gain_two, w_query, w_key, w_value, w_mix, w_gate, w_up, w_down):
        norm_one = low(rms_norm(source, gain_one))
        q_raw = low_back(matmul(norm_one, w_query)).reshape(count, HEADS, HEAD)
        k_raw = low_back(matmul(norm_one, w_key)).reshape(count, KV_HEADS, HEAD)
        v_all = low(low_back(matmul(norm_one, w_value))).reshape(count, KV_HEADS, HEAD)
        q_all = low(rotate(q_raw, cos_part, sin_part))
        k_all = low(rotate(k_raw, cos_part, sin_part))
        attn = low(low_back(attention(q_all, k_all, v_all, segment_ids)))
        residual = source + low_back(matmul(attn, w_mix))
        norm_two = low(rms_norm(residual, gain_two))
        gate = low_back(matmul(norm_two, w_gate))
        up = low_back(matmul(norm_two, w_up))
        act = low(jax.nn.silu(gate) * up)
        return residual + low_back(matmul(act, w_down))
    floats = (layer_input.astype(jnp.float32), attn_gain.astype(jnp.float32), mlp_gain.astype(jnp.float32), query_weight.astype(jnp.float32), key_weight.astype(jnp.float32), value_weight.astype(jnp.float32), mix_weight.astype(jnp.float32), gate_weight.astype(jnp.float32), up_weight.astype(jnp.float32), down_weight.astype(jnp.float32))
    result, pull = jax.vjp(forward, *floats)
    grads = pull(output_grad.astype(jnp.float32))
    return (result.astype(jnp.bfloat16), grads[0], grads[1], grads[2], grads[3], grads[4], grads[5], grads[6], grads[7], grads[8], grads[9])
```

```python
import functools

import jax
import jax.numpy as jnp
from jax import lax
from jax.experimental import pallas as pl
from jax.experimental.pallas import tpu as pltpu
from jax.sharding import PartitionSpec as P

D = 2560
HEAD = 80
EPS = 1e-05
THETA = 10000.0
NEG = -1e30
LOG2E = 1.4426950408889634
LN2 = 0.6931471805599453
BF = jnp.bfloat16
F32 = jnp.float32
TN = (((0,), (0,)), ((), ()))
NT = (((1,), (1,)), ((), ()))


def dot(left, right, dims=(((1,), (0,)), ((), ()))):
    return lax.dot_general(left, right, dims, preferred_element_type=F32)


def swapped(value, axis, mask):
    size = lax.axis_size(axis)
    return lax.ppermute(value, axis, [(i, i ^ mask) for i in range(size)])


def bit_order(size):
    bits = [1 << i for i in range(size.bit_length() - 1)]
    return bits[1:] + bits[:1]


def gather_blocks(own, axis):
    size = lax.axis_size(axis)
    blocks = {0: own}
    for bit in bit_order(size):
        for k in list(blocks):
            blocks[k | bit] = swapped(blocks[k], axis, bit)
    return [blocks[k] for k in range(size)]


def reduce_blocks(blocks, axis, low=True):
    size = lax.axis_size(axis)
    held = {k: blocks[k] for k in range(size)}
    for bit in reversed(bit_order(size)):
        for k in [k for k in held if k & bit]:
            other = swapped(held.pop(k), axis, bit)
            total = held[k ^ bit].astype(F32) + other.astype(F32)
            held[k ^ bit] = total.astype(BF) if low else total
    return held[0]


def exchange_blocks(blocks, axis):
    return [blocks[0]] + [swapped(blocks[k], axis, k) for k in range(1, len(blocks))]


def by_xor(value, index, axis):
    parts = [
        lax.dynamic_index_in_dim(value, index ^ k, axis, keepdims=True)
        for k in range(value.shape[axis])
    ]
    return jnp.concatenate(parts, axis=axis)


def grant(mib):
    return pltpu.CompilerParams(vmem_limit_bytes=mib * 1024 * 1024)


def project_kernel(count, *refs):
    weights, x_ref, out_ref = refs[:count], refs[count], refs[count + 1]
    total = None
    for k in range(count):
        part = dot(weights[k][...], x_ref[k], TN)
        total = part if total is None else total + part
    out_ref[...] = total.astype(out_ref.dtype)


def project(weights, x, tile, dtype):
    count, depth, tokens = x.shape
    width = weights[0].shape[1]
    return pl.pallas_call(
        functools.partial(project_kernel, count),
        out_shape=jax.ShapeDtypeStruct((width, tokens), dtype),
        grid=(pl.cdiv(width, tile),),
        in_specs=[pl.BlockSpec((depth, tile), lambda n: (0, n))] * count
        + [pl.BlockSpec((count, depth, tokens), lambda n: (0, 0, 0))],
        out_specs=pl.BlockSpec((tile, tokens), lambda n: (n, 0)),
        compiler_params=grant(56),
        name="project",
    )(*weights, x)


def fan_kernel(count, cols, *refs):
    weights, x_ref, out_ref = refs[:count], refs[count], refs[count + 1]
    piece = out_ref.shape[2]
    for k in range(count):
        part = dot(weights[k][...], x_ref[...], TN)
        for c in range(cols):
            out_ref[c, k] = part[c * piece : (c + 1) * piece].astype(out_ref.dtype)


def fan_out(weights, x, cols):
    count = len(weights)
    piece = weights[0].shape[1] // cols
    return pl.pallas_call(
        functools.partial(fan_kernel, count, cols),
        out_shape=jax.ShapeDtypeStruct((cols, count, piece, x.shape[1]), BF),
        compiler_params=grant(56),
        name="fan_out",
    )(*weights, x)


def pull_kernel(count, *refs):
    weights, x_ref, out_ref = refs[:count], refs[count], refs[count + 1]
    total = None
    for k in range(count):
        part = dot(weights[k][...], x_ref[k])
        total = part if total is None else total + part
    out_ref[...] = total.astype(out_ref.dtype)


def pull(weights, x, tile, dtype):
    count, depth, tokens = x.shape
    width = weights[0].shape[0]
    return pl.pallas_call(
        functools.partial(pull_kernel, count),
        out_shape=jax.ShapeDtypeStruct((width, tokens), dtype),
        grid=(width // tile,),
        in_specs=[pl.BlockSpec((tile, depth), lambda n: (n, 0))] * count
        + [pl.BlockSpec((count, depth, tokens), lambda n: (0, 0, 0))],
        out_specs=pl.BlockSpec((tile, tokens), lambda n: (n, 0)),
        compiler_params=grant(56),
        name="pull",
    )(*weights, x)


def tile_masks(seg_q, seg_k, start_q, start_k, size_q, size_k):
    rows = lax.broadcasted_iota(jnp.int32, (size_k, size_q), 0) + start_k
    cols = lax.broadcasted_iota(jnp.int32, (size_k, size_q), 1) + start_q
    seen = rows <= cols
    if seg_q is not None:
        seen = seen & (seg_k == seg_q)
    return seen


def attend_kernel(tile, q_ref, k_ref, v_ref, seg_row, seg_col, out_ref, lse_ref):
    tokens = q_ref.shape[-1]
    for half in range(2):
        for i in range(tokens // tile):
            at = i * tile
            span = slice(at, at + tile)
            query = q_ref[half, 0, :, span]
            ends = at + tile
            pieces = []
            if half == 1:
                pieces.append((0, 0, tokens, None))
                pieces.append((1, 0, ends, (seg_row[:, span], seg_col[:ends])))
            else:
                if at:
                    pieces.append((0, 0, at, None))
                pieces.append((0, at, ends, (None, None)))
            scores = []
            for which, begin, end, segs in pieces:
                part = dot(k_ref[which, begin:end, :], query)
                if segs is not None:
                    seen = tile_masks(segs[0], segs[1], at, begin, tile, end - begin)
                    part = jnp.where(seen, part, NEG)
                scores.append(part)
            peak = functools.reduce(
                jnp.maximum, [jnp.max(s, axis=0, keepdims=True) for s in scores]
            )
            total = None
            out = None
            for (which, begin, end, _), part in zip(pieces, scores):
                weights = jnp.exp2(part - peak)
                mass = jnp.sum(weights, axis=0, keepdims=True)
                value = dot(v_ref[which, :, begin:end], weights.astype(BF))
                total = mass if total is None else total + mass
                out = value if out is None else out + value
            out_ref[half, 0, :, span] = (out / total).astype(BF)
            lse_ref[half, 0, :, span] = peak + jnp.log2(total)


def attend(q, k, v, seg):
    _, heads, width, tokens = q.shape
    tile = min(256, tokens)
    head_block = pl.BlockSpec((2, 1, width, tokens), lambda h: (0, h, 0, 0))
    whole = lambda a: pl.BlockSpec(a.shape, lambda h: (0,) * a.ndim)
    seg_row, seg_col = seg[None, :], seg[:, None]
    return pl.pallas_call(
        functools.partial(attend_kernel, tile),
        out_shape=(
            jax.ShapeDtypeStruct(q.shape, BF),
            jax.ShapeDtypeStruct((2, heads, 1, tokens), F32),
        ),
        grid=(heads,),
        in_specs=[head_block, whole(k), whole(v), whole(seg_row), whole(seg_col)],
        out_specs=(head_block, pl.BlockSpec((2, 1, 1, tokens), lambda h: (0, h, 0, 0))),
        compiler_params=grant(56),
        name="attend",
    )(q, k, v, seg_row, seg_col)


def attend_back_kernel(
    tile,
    q_ref,
    g_ref,
    qn_ref,
    gn_ref,
    o_ref,
    k_ref,
    kt_ref,
    v_ref,
    lse_ref,
    seg_row,
    seg_col,
    dq_ref,
    dk_ref,
    dv_ref,
):
    tokens = q_ref.shape[-1]

    @pl.when(pl.program_id(0) == 0)
    def _():
        dk_ref[...] = jnp.zeros_like(dk_ref)
        dv_ref[...] = jnp.zeros_like(dv_ref)

    for half in range(2):
        for i in range(tokens // tile):
            at = i * tile
            span = slice(at, at + tile)
            ends = at + tile
            query = q_ref[half, 0, :, span]
            grad = g_ref[half, 0, :, span]
            lse = lse_ref[half, 0, :, span]
            delta = jnp.sum(
                grad.astype(F32) * o_ref[half, 0, :, span].astype(F32), axis=0, keepdims=True
            )
            query_rows = qn_ref[half, 0, span, :]
            grad_rows = gn_ref[half, 0, span, :]
            pieces = []
            if half == 1:
                pieces.append((0, 0, tokens, None))
                pieces.append((1, 0, ends, (seg_row[:, span], seg_col[:ends])))
            else:
                if at:
                    pieces.append((0, 0, at, None))
                pieces.append((0, at, ends, (None, None)))
            dq = None
            for which, begin, end, segs in pieces:
                part = dot(k_ref[which, begin:end, :], query)
                if segs is not None:
                    seen = tile_masks(segs[0], segs[1], at, begin, tile, end - begin)
                    part = jnp.where(seen, part, NEG)
                weights = jnp.exp2(part - lse)
                dprod = dot(v_ref[which, begin:end, :], grad)
                dscore = (weights * (dprod - delta)).astype(BF)
                dv_ref[which, begin:end, :] += dot(weights.astype(BF), grad_rows)
                dk_ref[which, begin:end, :] += dot(dscore, query_rows)
                more = dot(kt_ref[which, :, begin:end], dscore)
                dq = more if dq is None else dq + more
            dq_ref[half, 0, :, span] = dq


def attend_back(q, g, out, k, v, lse, seg):
    _, heads, width, tokens = q.shape
    tile = min(256, tokens)
    head_block = pl.BlockSpec((2, 1, width, tokens), lambda h: (0, h, 0, 0))
    row_block = pl.BlockSpec((2, 1, tokens, width), lambda h: (0, h, 0, 0))
    whole = lambda a: pl.BlockSpec(a.shape, lambda h: (0,) * a.ndim)
    seg_row, seg_col = seg[None, :], seg[:, None]
    k_rows, v_rows = k.swapaxes(1, 2), v.swapaxes(1, 2)
    fixed = pl.BlockSpec((2, tokens, width), lambda h: (0, 0, 0))
    return pl.pallas_call(
        functools.partial(attend_back_kernel, tile),
        out_shape=(
            jax.ShapeDtypeStruct(q.shape, F32),
            jax.ShapeDtypeStruct((2, tokens, width), F32),
            jax.ShapeDtypeStruct((2, tokens, width), F32),
        ),
        grid=(heads,),
        in_specs=[
            head_block,
            head_block,
            row_block,
            row_block,
            head_block,
            whole(k_rows),
            whole(k),
            whole(v_rows),
            pl.BlockSpec((2, 1, 1, tokens), lambda h: (0, h, 0, 0)),
            whole(seg_row),
            whole(seg_col),
        ],
        out_specs=(head_block, fixed, fixed),
        compiler_params=grant(56),
        name="attend_back",
    )(q, g, q.swapaxes(2, 3), g.swapaxes(2, 3), out, k_rows, k, v_rows, lse, seg_row, seg_col)


def rope_parts(positions, width):
    half = width // 2
    freq = THETA ** (-jnp.arange(half, dtype=F32) * 2.0 / width)
    angle = freq[:, None] * positions.astype(F32)[None, :]
    return (jnp.cos(angle), jnp.sin(angle))


def rotate(value, cosine, sine):
    half = value.shape[-2] // 2
    first, second = value[..., :half, :], value[..., half:, :]
    return jnp.concatenate(
        [first * cosine - second * sine, second * cosine + first * sine], axis=-2
    )


def normed(gathered, gain):
    cols, count, piece, tokens = gathered.shape
    value = gathered.astype(F32)
    scale = lax.rsqrt(jnp.sum(value * value, axis=(0, 1, 2)) / D + EPS)
    low = (value * scale * gain[..., None]).astype(BF)
    return by_row(low), scale


def by_row(value):
    cols, count, piece, tokens = value.shape
    return value.swapaxes(0, 1).reshape(count, cols * piece, tokens)


def norm_back(partials, gathered, gain, scale, inner):
    cols, count, piece, tokens = gathered.shape
    grads = jnp.stack(partials).reshape(count, cols, piece, tokens).swapaxes(0, 1)
    value = gathered.astype(F32)
    gain_share = jnp.sum(grads * (value * scale), axis=3)
    share = scale * (gain[..., None] * grads) - value * (scale * scale * inner / D)
    return share.astype(BF), gain_share


def spread_cols(value):
    return lax.all_gather(value, "col", axis=0, tiled=False)


def sum_cols(value):
    return lax.psum_scatter(value, "col", scatter_dimension=0, tiled=False)


def over_dp(value):
    low = value.astype(BF)
    total = low.astype(F32)
    size = lax.axis_size("dp")
    for step in range(1, size):
        other = lax.ppermute(low, "dp", [(i, (i + step) % size) for i in range(size)])
        total = total + other.astype(F32)
    return total


def gain_total(share):
    cols, count, piece = share.shape
    mine = lax.psum_scatter(share, "col", scatter_dimension=0, tiled=False)
    mine = reduce_blocks([mine[k] for k in range(count)], "row", low=False)
    return over_dp(mine)


def weight_total(blocks):
    return over_dp(reduce_blocks(blocks, "row"))


def body(
    layer_input,
    attn_gain,
    mlp_gain,
    query_weight,
    key_weight,
    value_weight,
    mix_weight,
    gate_weight,
    up_weight,
    down_weight,
    output_grad,
    segment_ids,
    position_ids,
):
    rows = segment_ids.shape[0]
    count = lax.axis_size("row")
    cols = lax.axis_size("col")
    piece = layer_input.shape[1]
    row = lax.axis_index("row")
    first_core = row % 2 == 0
    q_width = query_weight.shape[1]
    kv_width = key_weight.shape[1]
    kv_local = kv_width // HEAD
    q_half = q_width // 2
    own_kv = kv_local % 2 == 0
    kv_half = kv_width // 2 if own_kv else kv_width
    assert kv_half == HEAD
    heads = q_half // HEAD
    ff_width = gate_weight.shape[1]

    halves = []
    for h in range(2):
        halves.append(query_weight[:, h * q_half : (h + 1) * q_half])
        at = h * kv_half if own_kv else 0
        if own_kv or h == 0:
            halves.append(key_weight[:, at : at + kv_half])
            halves.append(value_weight[:, at : at + kv_half])
    qkv_width = q_width + 2 * kv_width
    padded = -(-qkv_width // 256) * 256
    halves.append(jnp.zeros((query_weight.shape[0], padded - qkv_width), BF))
    qkv_weight = jnp.concatenate(halves, axis=1)
    gate_up_weight = jnp.concatenate([gate_weight, up_weight], axis=1)

    both = jnp.concatenate([layer_input.T, output_grad.T], axis=0)
    both = both.reshape(2 * piece, count, rows)
    outgoing = [
        lax.dynamic_index_in_dim(both, row ^ k, axis=1, keepdims=False) for k in range(count)
    ]
    incoming = exchange_blocks(outgoing, "row")
    source_own = jnp.stack([b[:piece] for b in incoming])
    grad_own = jnp.stack([b[piece:] for b in incoming])

    qkv_blocks = gather_blocks(qkv_weight, "row")
    mix_blocks = gather_blocks(mix_weight, "row")
    gate_up_blocks = gather_blocks(gate_up_weight, "row")
    down_blocks = gather_blocks(down_weight, "row")

    gains = lax.all_gather(jnp.stack([attn_gain, mlp_gain]), ("row", "col"), axis=1, tiled=True)
    gains = gains.reshape(2, count, cols, piece)
    gains = by_xor(gains, row, 1).swapaxes(1, 2)
    gain_one, gain_two = gains[0], gains[1]

    cosine, sine = rope_parts(position_ids, HEAD)
    other_seg = swapped(segment_ids, "row", 1)
    seg = jnp.where(first_core, other_seg, segment_ids)

    source = spread_cols(source_own)
    norm_one, scale_one = normed(source, gain_one)
    qkv = project(qkv_blocks, norm_one, 256, F32)
    scale = HEAD ** (-0.5) * LOG2E

    def half_of(values, at, factor):
        queries = values[at : at + q_half].reshape(heads, HEAD, rows)
        return (rotate(queries, cosine, sine) * factor).astype(BF).reshape(q_half, rows)

    def kv_of(values, at):
        key = rotate(values[at : at + HEAD], cosine, sine).astype(BF)
        return key, values[at + HEAD : at + 2 * HEAD].astype(BF)

    step = q_half + 2 * kv_half
    low_q = [half_of(qkv, 0, scale), half_of(qkv, step, scale)]
    low_k0, low_v0 = kv_of(qkv, q_half)
    low_k1, low_v1 = kv_of(qkv, step + q_half) if own_kv else (low_k0, low_v0)
    sets = [
        jnp.concatenate([low_q[0], low_k0, low_v0]),
        jnp.concatenate([low_q[1], low_k1, low_v1]),
    ]

    def trade(pair):
        mine = jnp.where(first_core, pair[0], pair[1])
        other = swapped(jnp.where(first_core, pair[1], pair[0]), "row", 1)
        return jnp.stack([jnp.where(first_core, mine, other), jnp.where(first_core, other, mine)])

    def trade_back(pair):
        mine = jnp.where(first_core, pair[0], pair[1])
        other = swapped(jnp.where(first_core, pair[1], pair[0]), "row", 1)
        return jnp.where(first_core, mine, other), jnp.where(first_core, other, mine)

    traded = trade(sets)
    queries = traded[:, :q_half].reshape(2, heads, HEAD, rows)
    keys = traded[:, q_half : q_half + HEAD]
    values = traded[:, q_half + HEAD : q_half + 2 * HEAD]
    attn_half, lse = attend(queries, keys.swapaxes(1, 2), values, seg)
    attn_low = jnp.concatenate(trade_back(attn_half.reshape(2, q_half, rows)))
    attn_sum = sum_cols(fan_out(mix_blocks, attn_low, cols))
    residual_own = source_own.astype(F32) + attn_sum.astype(F32)

    residual = spread_cols(residual_own.astype(BF))
    norm_two, scale_two = normed(residual, gain_two)
    gate_up = project(gate_up_blocks, norm_two, 384 if 2 * ff_width % 384 == 0 else 128, BF)
    gate = gate_up[:ff_width].astype(F32)
    up = gate_up[ff_width:].astype(F32)
    sigma = jax.nn.sigmoid(gate)
    act_low = (gate * sigma * up).astype(BF)
    ff_sum = sum_cols(fan_out(down_blocks, act_low, cols))
    output_own = (residual_own + ff_sum.astype(F32)).astype(BF)

    out_grad = by_row(spread_cols(grad_own))
    act_grad = pull(down_blocks, out_grad, 432 if ff_width % 432 == 0 else ff_width, F32)
    gate_part = act_grad * up * sigma * (1.0 + gate * (1.0 - sigma))
    up_part = act_grad * gate * sigma
    inner = jnp.sum(gate_part * gate + up_part * up, axis=0)
    gate_up_grad = jnp.concatenate([gate_part, up_part]).astype(BF)
    share, gain_share = norm_back(
        [dot(w, gate_up_grad) for w in gate_up_blocks], residual, gain_two, scale_two, inner
    )
    residual_grad_own = grad_own.astype(F32) + sum_cols(share).astype(F32)
    mlp_gain_grad = gain_total(gain_share)
    down_grad = weight_total([dot(act_low, out_grad[k], NT).astype(BF) for k in range(count)])
    gate_up_wgrad = weight_total(
        [dot(norm_two[k], gate_up_grad, NT).astype(BF) for k in range(count)]
    )

    mix_cols = by_row(spread_cols(residual_grad_own.astype(BF)))
    attn_grad = pull(mix_blocks, mix_cols, q_width, BF)
    mix_grad = weight_total([dot(attn_low, mix_cols[k], NT).astype(BF) for k in range(count)])
    grad_half = trade([attn_grad[:q_half], attn_grad[q_half:]]).reshape(2, heads, HEAD, rows)
    dq, dk, dv = attend_back(queries, grad_half, attn_half, keys, values, lse, seg)
    dq = (dq * HEAD ** (-0.5)).astype(BF).reshape(2, q_half, rows)
    dk = (dk * LN2).astype(BF).swapaxes(1, 2)
    dv = dv.astype(BF).swapaxes(1, 2)
    back0, back1 = trade_back(jnp.concatenate([dq, dk, dv], axis=1))

    def unturned(values, heads_in):
        turned = rotate(values.astype(F32).reshape(heads_in, HEAD, rows), cosine, -sine)
        return turned.reshape(heads_in * HEAD, rows).astype(BF)

    back = [unturned(back0[:q_half], heads)]
    kv0, kv1 = back0[q_half:], back1[q_half:]
    if own_kv:
        back += [unturned(kv0[:HEAD], 1), kv0[HEAD:]]
        back += [unturned(back1[:q_half], heads), unturned(kv1[:HEAD], 1), kv1[HEAD:]]
    else:
        kv = kv0.astype(F32) + kv1.astype(F32)
        back += [unturned(kv[:HEAD], 1), kv[HEAD:].astype(BF), unturned(back1[:q_half], heads)]
    back.append(jnp.zeros((padded - qkv_width, rows), BF))
    qkv_grad = jnp.concatenate(back)
    raw_low = qkv
    inner = jnp.sum(qkv_grad.astype(F32) * raw_low, axis=0)
    share, gain_share = norm_back(
        [dot(w, qkv_grad) for w in qkv_blocks], source, gain_one, scale_one, inner
    )
    input_grad_own = residual_grad_own + sum_cols(share).astype(F32)
    attn_gain_grad = gain_total(gain_share)
    qkv_wgrad = weight_total([dot(norm_one[k], qkv_grad, NT).astype(BF) for k in range(count)])

    def all_tokens(value):
        got = exchange_blocks([value[k] for k in range(count)], "row")
        placed = by_xor(jnp.stack(got), row, 0)
        return placed.transpose(0, 2, 1).reshape(count * rows, piece)

    layer_output = all_tokens(output_own)
    input_grad = all_tokens(input_grad_own)

    q_grad = [qkv_wgrad[:, :q_half], qkv_wgrad[:, step : step + q_half]]
    if own_kv:
        at = step + q_half
        k_grad = [qkv_wgrad[:, q_half : q_half + HEAD], qkv_wgrad[:, at : at + HEAD]]
        v_grad = [
            qkv_wgrad[:, q_half + HEAD : q_half + 2 * HEAD],
            qkv_wgrad[:, at + HEAD : at + 2 * HEAD],
        ]
    else:
        k_grad = [qkv_wgrad[:, q_half : q_half + HEAD]]
        v_grad = [qkv_wgrad[:, q_half + HEAD : q_half + 2 * HEAD]]
    return (
        layer_output,
        input_grad,
        attn_gain_grad,
        mlp_gain_grad,
        jnp.concatenate(q_grad, axis=1),
        jnp.concatenate(k_grad, axis=1),
        jnp.concatenate(v_grad, axis=1),
        mix_grad,
        gate_up_wgrad[:, :ff_width],
        gate_up_wgrad[:, ff_width:],
        down_grad,
    )


def solution(mesh):
    return jax.shard_map(
        body,
        mesh=mesh,
        in_specs=(
            P("dp", ("row", "col")),
            P(("row", "col")),
            P(("row", "col")),
            P("row", "col"),
            P("row", "col"),
            P("row", "col"),
            P("col", "row"),
            P("row", "col"),
            P("row", "col"),
            P("col", "row"),
            P("dp", ("row", "col")),
            P(("dp", "row")),
            P(("dp", "row")),
        ),
        out_specs=(
            P("dp", ("row", "col")),
            P("dp", ("row", "col")),
            P(("row", "col")),
            P(("row", "col")),
            P("row", "col"),
            P("row", "col"),
            P("row", "col"),
            P("col", "row"),
            P("row", "col"),
            P("row", "col"),
            P("col", "row"),
        ),
        check_vma=False,
    )
```

```python
import functools

import jax
import jax.numpy as jnp
from jax import lax
from jax.experimental import pallas as pl
from jax.experimental.pallas import tpu as pltpu
from jax.sharding import PartitionSpec as P

D = 2560
HEAD = 80
EPS = 1e-05
THETA = 10000.0
NEG = -1e30
LOG2E = 1.4426950408889634
LN2 = 0.6931471805599453
ROOT = HEAD ** (-0.5)
BF = jnp.bfloat16
F32 = jnp.float32
NN = (((1,), (0,)), ((), ()))
TN = (((0,), (0,)), ((), ()))
NT = (((1,), (1,)), ((), ()))


def dot(left, right, dims=NN):
    return lax.dot_general(left, right, dims, preferred_element_type=F32)


def together(*values):
    return lax.optimization_barrier(values)


def swapped(value, axis, mask):
    size = lax.axis_size(axis)
    return lax.ppermute(value, axis, [(i, i ^ mask) for i in range(size)])


def spread(blocks, axis, bits):
    blocks = dict(blocks)
    for bit in bits:
        for k in list(blocks):
            blocks[k | bit] = swapped(blocks[k], axis, bit)
    return blocks


def fold(blocks, axis, bits, low=True):
    held = dict(blocks)
    for bit in bits:
        for k in [k for k in held if k & bit]:
            other = swapped(held.pop(k), axis, bit)
            total = held[k ^ bit].astype(F32) + other.astype(F32)
            held[k ^ bit] = total.astype(BF) if low else total
    return held


def far_bits(size):
    return [1 << i for i in range(1, size.bit_length() - 1)]


def near_bits(size):
    return [1] if size > 1 else []


def exchange_blocks(blocks, axis):
    return [blocks[0]] + [swapped(blocks[k], axis, k) for k in range(1, len(blocks))]


def by_xor(value, index, axis):
    parts = [
        lax.dynamic_index_in_dim(value, index ^ k, axis, keepdims=True)
        for k in range(value.shape[axis])
    ]
    return jnp.concatenate(parts, axis=axis)


def params(mib=58):
    return pltpu.CompilerParams(vmem_limit_bytes=mib * 1024 * 1024)


def shape(dims, dtype):
    return jax.ShapeDtypeStruct(dims, dtype)


SMALL = pl.BlockSpec(memory_space=pltpu.SMEM)
RAW = pl.BlockSpec(memory_space=pl.ANY)


def resident(dims, buffers=None):
    zeros = (0,) * len(dims)
    mode = {} if buffers is None else {"pipeline_mode": pl.Buffered(buffers)}
    return pl.BlockSpec(dims, lambda *_: zeros, **mode)


def normalise(x_ref, gain_ref, out_ref, scale_ref):
    cols, count, piece, _ = x_ref.shape
    total = None
    for c in range(cols):
        for k in range(count):
            value = x_ref[c, k].astype(F32)
            part = jnp.sum(value * value, axis=0, keepdims=True)
            total = part if total is None else total + part
    scale = lax.rsqrt(total / D + EPS)
    scale_ref[...] = scale
    for c in range(cols):
        for k in range(count):
            value = x_ref[c, k].astype(F32) * scale * gain_ref[c, k]
            out_ref[k, c * piece : (c + 1) * piece, :] = value.astype(BF)


def turn(value, cosine, sine):
    half = value.shape[0] // 2
    first, second = value[:half], value[half:]
    return jnp.concatenate([first * cosine - second * sine, second * cosine + first * sine])


def qkv_kernel(count, shared, x_ref, gain_ref, cos_ref, sin_ref, *refs):
    q_w, kv_w = refs[:count], refs[count : 2 * count]
    norm_ref, scale_ref, sets_ref = refs[2 * count :]
    normalise(x_ref, gain_ref, norm_ref, scale_ref)
    query = keyval = None
    for k in range(count):
        normed = norm_ref[k]
        part = dot(q_w[k][...], normed, TN)
        query = part if query is None else query + part
        part = dot(kv_w[k][...], normed)
        keyval = part if keyval is None else keyval + part
    cosine, sine = cos_ref[...], sin_ref[...]
    half = query.shape[0] // 2
    kv_half = keyval.shape[0] // 2
    for h in range(2):
        for at in range(0, half, HEAD):
            value = turn(query[h * half + at : h * half + at + HEAD], cosine, sine)
            sets_ref[h, at : at + HEAD, :] = (value * (ROOT * LOG2E)).astype(BF)
        at = 0 if shared else h * HEAD
        key = turn(keyval[at : at + HEAD], cosine, sine)
        sets_ref[h, half : half + HEAD, :] = key.astype(BF)
        sets_ref[h, half + HEAD : half + 2 * HEAD, :] = keyval[
            kv_half + at : kv_half + at + HEAD
        ].astype(BF)


def qkv_project(x, gain, cosine, sine, q_w, kv_w):
    cols, count, piece, tokens = x.shape
    half = q_w[0].shape[1] // 2
    shared = kv_w[0].shape[0] == 2 * HEAD
    return pl.pallas_call(
        functools.partial(qkv_kernel, count, shared),
        out_shape=(
            shape((count, cols * piece, tokens), BF),
            shape((1, tokens), F32),
            shape((2, half + 2 * HEAD, tokens), BF),
        ),
        compiler_params=params(),
        name="qkv_project",
    )(x, gain, cosine, sine, *q_w, *kv_w)


def pieces_of(half, at, tile, tokens):
    if half == 1:
        return [(0, 0, tokens, False), (1, 0, at + tile, True)]
    head = [(0, 0, at, False)] if at else []
    return head + [(0, at, at + tile, True)]


def seen_of(half, at, begin, end, tile, seg_row, seg_col):
    rows = lax.broadcasted_iota(jnp.int32, (end - begin, tile), 0) + begin
    cols = lax.broadcasted_iota(jnp.int32, (end - begin, tile), 1) + at
    seen = rows <= cols
    if half == 1:
        seen = seen & (seg_col[begin:end] == seg_row[:, at : at + tile])
    return seen


def place(parity, own_ref, other_ref, sets):
    sets[parity] = own_ref[...]
    sets[1 - parity] = other_ref[...]


def attend_kernel(
    tile, parity_ref, own_ref, other_ref, seg_row, seg_col, mine_ref, send_ref, lse_ref, sets, rows
):
    tokens = own_ref.shape[-1]
    heads = pl.num_programs(0)
    head = pl.program_id(0)
    parity = parity_ref[0]
    half_rows = own_ref.shape[0] - 2 * HEAD

    @pl.when(head == 0)
    def _():
        place(parity, own_ref, other_ref, sets)
        for half in range(2):
            keys = sets[half, half_rows : half_rows + HEAD, :]
            rows[half] = keys.astype(F32).T.astype(BF)

    at_head = pl.ds(pl.multiple_of(head * HEAD, 16), HEAD)
    for half in range(2):
        for at in range(0, tokens, tile):
            span = slice(at, at + tile)
            query = sets[half, at_head, span]
            pieces = pieces_of(half, at, tile, tokens)
            scores = []
            for which, begin, end, masked in pieces:
                part = dot(rows[which, begin:end, :], query)
                if masked:
                    part = jnp.where(
                        seen_of(half, at, begin, end, tile, seg_row, seg_col), part, NEG
                    )
                scores.append(part)
            peak = functools.reduce(
                jnp.maximum, [jnp.max(s, axis=0, keepdims=True) for s in scores]
            )
            total = out = None
            for (which, begin, end, _), part in zip(pieces, scores):
                weights = jnp.exp2(part - peak)
                mass = jnp.sum(weights, axis=0, keepdims=True)
                value = dot(sets[which, half_rows + HEAD :, begin:end], weights.astype(BF))
                total = mass if total is None else total + mass
                out = value if out is None else out + value
            out = (out / total).astype(BF)
            lse_ref[half, 0, :, span] = peak + jnp.log2(total)

            @pl.when(parity == half)
            def _():
                mine_ref[at_head, span] = out

            @pl.when(parity != half)
            def _():
                send_ref[at_head, span] = out


def attend(parity, own, other, seg):
    depth, tokens = own.shape
    half_rows = depth - 2 * HEAD
    heads = half_rows // HEAD
    tile = min(256, tokens)
    out = resident((half_rows, tokens))
    return pl.pallas_call(
        functools.partial(attend_kernel, tile),
        out_shape=(
            shape((half_rows, tokens), BF),
            shape((half_rows, tokens), BF),
            shape((2, heads, 1, tokens), F32),
        ),
        grid=(heads,),
        in_specs=[
            SMALL,
            resident((depth, tokens)),
            resident((depth, tokens)),
            resident((1, tokens)),
            resident((tokens, 1)),
        ],
        out_specs=(out, out, pl.BlockSpec((2, 1, 1, tokens), lambda h: (0, h, 0, 0))),
        scratch_shapes=[
            pltpu.VMEM((2, depth, tokens), BF),
            pltpu.VMEM((2, tokens, HEAD), BF),
        ],
        compiler_params=params(),
        name="attend",
    )(parity, own, other, seg[None, :], seg[:, None])


def attend_back_kernel(
    tile,
    parity_ref,
    own_ref,
    other_ref,
    own_out,
    other_out,
    own_grad,
    other_grad,
    lse_ref,
    seg_row,
    seg_col,
    mine_ref,
    send_ref,
    sets,
    outs,
    grads,
    rows,
    key_acc,
    value_acc,
):
    tokens = own_ref.shape[-1]
    heads = pl.num_programs(0)
    head = pl.program_id(0)
    parity = parity_ref[0]
    half_rows = own_ref.shape[0] - 2 * HEAD

    @pl.when(head == 0)
    def _():
        place(parity, own_ref, other_ref, sets)
        place(parity, own_out, other_out, outs)
        place(parity, own_grad, other_grad, grads)
        for half in range(2):
            for i in range(2):
                at = half_rows + i * HEAD
                rows[i, half] = sets[half, at : at + HEAD, :].astype(F32).T.astype(BF)
        key_acc[...] = jnp.zeros_like(key_acc)
        value_acc[...] = jnp.zeros_like(value_acc)

    at_head = pl.ds(pl.multiple_of(head * HEAD, 16), HEAD)
    for half in range(2):
        for at in range(0, tokens, tile):
            span = slice(at, at + tile)
            query = sets[half, at_head, span]
            grad = grads[half, at_head, span]
            lse = lse_ref[half, 0, :, span]
            delta = jnp.sum(
                grad.astype(F32) * outs[half, at_head, span].astype(F32), axis=0, keepdims=True
            )
            total = None
            for which, begin, end, masked in pieces_of(half, at, tile, tokens):
                part = dot(rows[0, which, begin:end, :], query)
                if masked:
                    part = jnp.where(
                        seen_of(half, at, begin, end, tile, seg_row, seg_col), part, NEG
                    )
                weights = jnp.exp2(part - lse)
                dprod = dot(rows[1, which, begin:end, :], grad)
                dscore = (weights * (dprod - delta)).astype(BF)
                value_acc[which, :, begin:end] += dot(grad, weights.astype(BF), NT)
                key_acc[which, :, begin:end] += dot(query, dscore, NT)
                more = dot(sets[which, half_rows : half_rows + HEAD, begin:end], dscore)
                total = more if total is None else total + more
            total = (total * ROOT).astype(BF)

            @pl.when(parity == half)
            def _():
                mine_ref[at_head, span] = total

            @pl.when(parity != half)
            def _():
                send_ref[at_head, span] = total

    @pl.when(head == heads - 1)
    def _():
        for ref, which in ((mine_ref, parity), (send_ref, 1 - parity)):
            ref[half_rows : half_rows + HEAD, :] = (key_acc[which] * LN2).astype(BF)
            ref[half_rows + HEAD :, :] = value_acc[which].astype(BF)


def attend_back(parity, own, other, own_out, other_out, own_grad, other_grad, lse, seg):
    depth, tokens = own.shape
    half_rows = depth - 2 * HEAD
    heads = half_rows // HEAD
    tile = min(256, tokens)
    full, part = resident((depth, tokens)), resident((half_rows, tokens))
    return pl.pallas_call(
        functools.partial(attend_back_kernel, tile),
        out_shape=(shape((depth, tokens), BF), shape((depth, tokens), BF)),
        grid=(heads,),
        in_specs=[
            SMALL,
            full,
            full,
            part,
            part,
            part,
            part,
            pl.BlockSpec((2, 1, 1, tokens), lambda h: (0, h, 0, 0)),
            resident((1, tokens)),
            resident((tokens, 1)),
        ],
        out_specs=(full, full),
        scratch_shapes=[
            pltpu.VMEM((2, depth, tokens), BF),
            pltpu.VMEM((2, half_rows, tokens), BF),
            pltpu.VMEM((2, half_rows, tokens), BF),
            pltpu.VMEM((2, 2, tokens, HEAD), BF),
            pltpu.VMEM((2, HEAD, tokens), F32),
            pltpu.VMEM((2, HEAD, tokens), F32),
        ],
        compiler_params=params(),
        name="attend_back",
    )(
        parity,
        own,
        other,
        own_out,
        other_out,
        own_grad,
        other_grad,
        lse,
        seg[None, :],
        seg[:, None],
    )


def halves_at(parity, half_rows):
    mine = pl.ds(pl.multiple_of(parity * half_rows, 16), half_rows)
    other = pl.ds(pl.multiple_of((1 - parity) * half_rows, 16), half_rows)
    return mine, other


def mix_out_kernel(count, parity_ref, own_ref, other_ref, *refs):
    weights, out_ref = refs[:count], refs[count]
    cols, _, piece, _ = out_ref.shape
    mine, other = halves_at(parity_ref[0], own_ref.shape[0])
    for k in range(count):
        part = dot(weights[k][mine, :], own_ref[...], TN)
        part = part + dot(weights[k][other, :], other_ref[...], TN)
        for c in range(cols):
            out_ref[c, k] = part[c * piece : (c + 1) * piece].astype(BF)


def mix_out(parity, own, other, weights, cols):
    count = len(weights)
    piece = weights[0].shape[1] // cols
    vmem = pl.BlockSpec(memory_space=pltpu.VMEM)
    return pl.pallas_call(
        functools.partial(mix_out_kernel, count),
        out_shape=shape((cols, count, piece, own.shape[1]), BF),
        in_specs=[SMALL] + [vmem] * (2 + count),
        compiler_params=params(),
        name="mix_out",
    )(parity, own, other, *weights)


def mix_back_kernel(count, parity_ref, x_ref, *refs):
    weights = refs[:count]
    rows_ref, own_ref, other_ref = refs[count:]
    cols, _, piece, _ = x_ref.shape
    for c in range(cols):
        for k in range(count):
            rows_ref[k, c * piece : (c + 1) * piece, :] = x_ref[c, k]
    mine, other = halves_at(parity_ref[0], own_ref.shape[0])
    for at, out_ref in ((other, other_ref), (mine, own_ref)):
        total = None
        for k in range(count):
            part = dot(weights[k][at, :], rows_ref[k])
            total = part if total is None else total + part
        out_ref[...] = total.astype(BF)


def mix_back(parity, x, weights):
    cols, count, piece, tokens = x.shape
    half_rows = weights[0].shape[0] // 2
    vmem = pl.BlockSpec(memory_space=pltpu.VMEM)
    return pl.pallas_call(
        functools.partial(mix_back_kernel, count),
        out_shape=(
            shape((count, cols * piece, tokens), BF),
            shape((half_rows, tokens), BF),
            shape((half_rows, tokens), BF),
        ),
        in_specs=[SMALL] + [vmem] * (1 + count),
        compiler_params=params(),
        name="mix_back",
    )(parity, x, *weights)


def fan_kernel(count, x_ref, *refs):
    weights, out_ref = refs[:count], refs[count]
    cols, _, piece, _ = out_ref.shape
    for k in range(count):
        part = dot(weights[k][...], x_ref[...], TN)
        for c in range(cols):
            out_ref[c, k] = part[c * piece : (c + 1) * piece].astype(BF)


def fan_out(weights, x, cols):
    count = len(weights)
    piece = weights[0].shape[1] // cols
    return pl.pallas_call(
        functools.partial(fan_kernel, count),
        out_shape=shape((cols, count, piece, x.shape[1]), BF),
        compiler_params=params(),
        name="fan_out",
    )(x, *weights)


def ff_kernel(count, x_ref, g_ref, gain_ref, *refs):
    gate_w, up_w, down_w = refs[:count], refs[count : 2 * count], refs[2 * count : 3 * count]
    norm_ref, scale_ref, rows_ref, inner_ref, act_ref, dgate_ref, dup_ref = refs[3 * count :]
    cols, _, piece, _ = x_ref.shape

    @pl.when(pl.program_id(0) == 0)
    def _():
        normalise(x_ref, gain_ref, norm_ref, scale_ref)
        for c in range(cols):
            for k in range(count):
                rows_ref[k, c * piece : (c + 1) * piece, :] = g_ref[c, k]
        inner_ref[...] = jnp.zeros_like(inner_ref)

    def summed(weights, ref):
        total = None
        for k in range(count):
            part = dot(weights[k][...], ref[k])
            total = part if total is None else total + part
        return total

    gate = summed(gate_w, norm_ref)
    up = summed(up_w, norm_ref)
    sigma = jax.nn.sigmoid(gate)
    silu = gate * sigma
    act_ref[...] = (silu * up).astype(BF)
    grad = summed(down_w, rows_ref)
    dup = grad * silu
    dgate = grad * up * (sigma + silu * (1.0 - sigma))
    inner_ref[...] += jnp.sum(dgate * gate + dup * up, axis=0, keepdims=True)
    dgate_ref[...] = dgate.astype(BF)
    dup_ref[...] = dup.astype(BF)


def feed_forward(x, g, gain, gate_w, up_w, down_w):
    cols, count, piece, tokens = x.shape
    width, depth = gate_w[0].shape
    tile = 432 if width % 432 == 0 else width
    whole = resident(x.shape, 1)
    rows = (count, cols * piece, tokens)
    w_spec = pl.BlockSpec((tile, depth), lambda n: (n, 0))
    h_spec = pl.BlockSpec((tile, tokens), lambda n: (n, 0))
    hidden = shape((width, tokens), BF)
    return pl.pallas_call(
        functools.partial(ff_kernel, count),
        out_shape=(
            shape(rows, BF),
            shape((1, tokens), F32),
            shape(rows, BF),
            shape((1, tokens), F32),
            hidden,
            hidden,
            hidden,
        ),
        grid=(width // tile,),
        in_specs=[whole, whole, resident(gain.shape, 1)] + [w_spec] * (3 * count),
        out_specs=(
            resident(rows, 1),
            resident((1, tokens)),
            resident(rows, 1),
            resident((1, tokens)),
            h_spec,
            h_spec,
            h_spec,
        ),
        compiler_params=params(60),
        name="feed_forward",
    )(x, g, gain, *gate_w, *up_w, *down_w)


def norm_back(grads, k, x_ref, gain_ref, scale, coef, share_ref, gain_share_ref):
    cols, _, piece, _ = x_ref.shape
    for c in range(cols):
        grad = grads[c * piece : (c + 1) * piece]
        value = x_ref[c, k].astype(F32)
        gain_share_ref[c, k] = jnp.sum(grad * (value * scale), axis=1, keepdims=True)
        share_ref[c, k] = ((grad * gain_ref[c, k]) * scale - value * coef).astype(BF)


def ff_back_kernel(count, x_ref, gain_ref, scale_ref, inner_ref, dgate, dup, *refs):
    gate_w, up_w = refs[:count], refs[count : 2 * count]
    share_ref, gain_share_ref, dgate_buf, dup_buf, gate_buf, up_buf, sems = refs[2 * count :]
    copies = [
        pltpu.make_async_copy(dgate, dgate_buf, sems.at[0]),
        pltpu.make_async_copy(dup, dup_buf, sems.at[1]),
    ]
    for k in range(count):
        copies.append(pltpu.make_async_copy(gate_w[k], gate_buf.at[k], sems.at[2 + 2 * k]))
        copies.append(pltpu.make_async_copy(up_w[k], up_buf.at[k], sems.at[3 + 2 * k]))
    for copy in copies:
        copy.start()
    scale = scale_ref[...]
    coef = scale * scale * inner_ref[...] / D
    copies[0].wait()
    copies[1].wait()
    for k in range(count):
        copies[2 + 2 * k].wait()
        copies[3 + 2 * k].wait()
        grads = dot(gate_buf[k], dgate_buf[...], TN) + dot(up_buf[k], dup_buf[...], TN)
        norm_back(grads, k, x_ref, gain_ref, scale, coef, share_ref, gain_share_ref)


def ff_back(x, gain, scale, inner, dgate, dup, gate_w, up_w):
    count = len(gate_w)
    vmem = pl.BlockSpec(memory_space=pltpu.VMEM)
    width, depth = gate_w[0].shape
    return pl.pallas_call(
        functools.partial(ff_back_kernel, count),
        out_shape=(shape(x.shape, BF), shape(gain.shape, F32)),
        in_specs=[vmem] * 4 + [RAW] * (2 + 2 * count),
        scratch_shapes=[
            pltpu.VMEM(dgate.shape, BF),
            pltpu.VMEM(dup.shape, BF),
            pltpu.VMEM((count, width, depth), BF),
            pltpu.VMEM((count, width, depth), BF),
            pltpu.SemaphoreType.DMA((2 + 2 * count,)),
        ],
        compiler_params=params(60),
        name="ff_back",
    )(x, gain, scale, inner, dgate, dup, *gate_w, *up_w)


def qkv_back_kernel(
    count,
    shared,
    parity_ref,
    x_ref,
    gain_ref,
    scale_ref,
    cos_ref,
    sin_ref,
    sets_ref,
    own_ref,
    other_ref,
    *refs,
):
    q_w, kv_w = refs[:count], refs[count : 2 * count]
    dq_ref, dkv_ref, share_ref, gain_share_ref = refs[2 * count :]
    parity = parity_ref[0]
    half_rows = own_ref.shape[0] - 2 * HEAD
    kv_half = dkv_ref.shape[0] // 2
    cosine, sine = cos_ref[...], -sin_ref[...]
    inner = None
    folded = None
    for grads, which in ((own_ref, parity), (other_ref, 1 - parity)):
        for at in range(0, half_rows + 2 * HEAD, HEAD):
            value = grads[at : at + HEAD, :].astype(F32)
            part = value * sets_ref[which, at : at + HEAD, :].astype(F32)
            part = jnp.sum(part, axis=0, keepdims=True)
            if at < half_rows:
                part = part * (1.0 / (ROOT * LOG2E))
                start = pl.multiple_of(which * half_rows + at, 16)
                dq_ref[pl.ds(start, HEAD), :] = turn(value, cosine, sine).astype(BF)
            else:
                is_key = at == half_rows
                raw = turn(value, cosine, sine) if is_key else value
                base = 0 if is_key else kv_half
                if not shared:
                    start = pl.multiple_of(base + which * HEAD, 16)
                    dkv_ref[pl.ds(start, HEAD), :] = raw.astype(BF)
                elif folded is None or at not in folded:
                    folded = {**(folded or {}), at: raw}
                else:
                    dkv_ref[base : base + HEAD, :] = (folded[at] + raw).astype(BF)
            inner = part if inner is None else inner + part
    scale = scale_ref[...]
    coef = scale * scale * inner / D
    for k in range(count):
        grads = dot(q_w[k][...], dq_ref[...]) + dot(kv_w[k][...], dkv_ref[...], TN)
        norm_back(grads, k, x_ref, gain_ref, scale, coef, share_ref, gain_share_ref)


def qkv_back(parity, x, gain, scale, cosine, sine, sets, own, other, q_w, kv_w):
    cols, count, piece, tokens = x.shape
    shared = kv_w[0].shape[0] == 2 * HEAD
    vmem = pl.BlockSpec(memory_space=pltpu.VMEM)
    return pl.pallas_call(
        functools.partial(qkv_back_kernel, count, shared),
        out_shape=(
            shape((q_w[0].shape[1], tokens), BF),
            shape((kv_w[0].shape[0], tokens), BF),
            shape(x.shape, BF),
            shape(gain.shape, F32),
        ),
        in_specs=[SMALL] + [vmem] * (8 + 2 * count),
        compiler_params=params(),
        name="qkv_back",
    )(parity, x, gain, scale, cosine, sine, sets, own, other, *q_w, *kv_w)


def rope_parts(positions):
    half = HEAD // 2
    freq = THETA ** (-jnp.arange(half, dtype=F32) * 2.0 / HEAD)
    angle = freq[:, None] * positions.astype(F32)[None, :]
    return (jnp.cos(angle), jnp.sin(angle))


def spread_cols(value):
    return lax.all_gather(value, "col", axis=0, tiled=False)


def sum_cols(value):
    return lax.psum_scatter(value, "col", scatter_dimension=0, tiled=False)


def over_dp(value):
    low = value.astype(BF)
    total = low.astype(F32)
    size = lax.axis_size("dp")
    for step in range(1, size):
        other = lax.ppermute(low, "dp", [(i, (i + step) % size) for i in range(size)])
        total = total + other.astype(F32)
    return total


def body(
    layer_input,
    attn_gain,
    mlp_gain,
    query_weight,
    key_weight,
    value_weight,
    mix_weight,
    gate_weight,
    up_weight,
    down_weight,
    output_grad,
    segment_ids,
    position_ids,
):
    rows = segment_ids.shape[0]
    count = lax.axis_size("row")
    cols = lax.axis_size("col")
    piece = layer_input.shape[1]
    row = lax.axis_index("row")
    parity = (row % 2).astype(jnp.int32)
    own_core = parity.reshape(1)
    q_half = query_weight.shape[1] // 2
    near, far = near_bits(count), far_bits(count)

    def row_tokens(value):
        turned = value.T
        outgoing = [
            lax.dynamic_slice(turned, (0, (row ^ k) * rows), (piece, rows)) for k in range(count)
        ]
        return jnp.stack(exchange_blocks(outgoing, "row"))

    def all_tokens(blocks):
        got = exchange_blocks([blocks[k] for k in range(count)], "row")
        result = jnp.zeros((piece, count * rows), blocks.dtype)
        for k in range(count):
            result = lax.dynamic_update_slice(result, got[k], (0, (row ^ k) * rows))
        return result.T

    def listed(blocks):
        return [blocks[k] for k in range(count)]

    source_own = row_tokens(layer_input)
    kv_weight = jnp.concatenate([key_weight.T, value_weight.T])
    q_first = spread({0: query_weight}, "row", far)
    kv_first = spread({0: kv_weight}, "row", far)
    mix_first = spread({0: mix_weight}, "row", far)
    gate_first = spread({0: gate_weight.T}, "row", far)
    up_first = spread({0: up_weight.T}, "row", far)
    down_first = spread({0: down_weight}, "row", far)
    q_blocks = spread(q_first, "row", near)
    kv_blocks = spread(kv_first, "row", near)

    gains = lax.all_gather(jnp.stack([attn_gain, mlp_gain]), ("row", "col"), axis=1, tiled=True)
    gains = gains.reshape(2, count, cols, piece)
    gains = by_xor(gains, row, 1).swapaxes(1, 2)[..., None]
    gain_one, gain_two = gains[0], gains[1]

    cosine, sine = rope_parts(position_ids)
    other_seg = swapped(segment_ids, "row", 1)
    seg = jnp.where(parity == 0, other_seg, segment_ids)

    source = spread_cols(source_own)
    source, q_blocks, kv_blocks, mix_first, gate_first, gain_one, cosine, sine, seg = together(
        source, q_blocks, kv_blocks, mix_first, gate_first, gain_one, cosine, sine, seg
    )
    grad_own = row_tokens(output_grad)
    grad_own, source = together(grad_own, source)
    grad_all = spread_cols(grad_own)
    norm_one, scale_one, sets = qkv_project(
        source, gain_one, cosine, sine, listed(q_blocks), listed(kv_blocks)
    )
    own_set = lax.dynamic_index_in_dim(sets, parity, 0, keepdims=False)
    other_set = swapped(lax.dynamic_index_in_dim(sets, 1 - parity, 0, keepdims=False), "row", 1)
    attn_mine, attn_send, lse = attend(own_core, own_set, other_set, seg)
    attn_other = swapped(attn_send, "row", 1)
    mix_blocks = spread(mix_first, "row", near)
    attn_mine, attn_other, mix_blocks, up_first = together(
        attn_mine, attn_other, mix_blocks, up_first
    )
    attn_part = mix_out(own_core, attn_mine, attn_other, listed(mix_blocks), cols)
    attn_part, grad_all = together(attn_part, grad_all)
    attn_sum = sum_cols(attn_part)
    gate_blocks = spread(gate_first, "row", near)
    up_blocks = spread(up_first, "row", near)
    down_blocks = spread(down_first, "row", near)
    attn_sum, gate_blocks, up_blocks, down_blocks = together(
        attn_sum, gate_blocks, up_blocks, down_blocks
    )
    residual_own = source_own.astype(F32) + attn_sum.astype(F32)

    residual = spread_cols(residual_own.astype(BF))
    norm_two, scale_two, grad_rows, inner, act, dgate, dup = feed_forward(
        residual,
        grad_all,
        gain_two,
        listed(gate_blocks),
        listed(up_blocks),
        listed(down_blocks),
    )
    share, gain_share_two = ff_back(
        residual, gain_two, scale_two, inner, dgate, dup, listed(gate_blocks), listed(up_blocks)
    )
    share_sum = sum_cols(share)
    share, dgate, dup, act, grad_rows, norm_two = together(
        share, dgate, dup, act, grad_rows, norm_two
    )
    down_grads = {k: dot(act, grad_rows[k], NT).astype(BF) for k in range(count)}
    gate_grads = {k: dot(dgate, norm_two[k], NT).astype(BF) for k in range(count)}
    up_grads = {k: dot(dup, norm_two[k], NT).astype(BF) for k in range(count)}
    down_grads = fold(down_grads, "row", near)
    gate_grads = fold(gate_grads, "row", near)
    up_grads = fold(up_grads, "row", near)
    share_sum, down_grads, gate_grads, up_grads = together(
        share_sum, down_grads, gate_grads, up_grads
    )
    residual_grad_own = grad_own.astype(F32) + share_sum.astype(F32)
    down_total = fold(down_grads, "row", far)[0]
    gate_total = fold(gate_grads, "row", far)[0]
    up_total = fold(up_grads, "row", far)[0]

    mix_cols = spread_cols(residual_grad_own.astype(BF))
    ff_part = fan_out(listed(down_blocks), act, cols)
    mix_cols, ff_part = together(mix_cols, ff_part)
    mix_rows, grad_mine, grad_send = mix_back(own_core, mix_cols, listed(mix_blocks))
    ff_sum = sum_cols(ff_part)
    grad_other = swapped(grad_send, "row", 1)
    back_mine, back_send = attend_back(
        own_core, own_set, other_set, attn_mine, attn_send, grad_mine, grad_other, lse, seg
    )
    back_other = swapped(back_send, "row", 1)
    dq, dkv, share, gain_share_one = qkv_back(
        own_core,
        source,
        gain_one,
        scale_one,
        cosine,
        sine,
        sets,
        back_mine,
        back_other,
        listed(q_blocks),
        listed(kv_blocks),
    )
    share, ff_sum = together(share, ff_sum)
    input_sum = sum_cols(share)
    output_own = (residual_own + ff_sum.astype(F32)).astype(BF)
    layer_output = all_tokens(output_own)

    share, dq, dkv, gain_share_one, gain_share_two = together(
        share, dq, dkv, gain_share_one, gain_share_two
    )
    q_grads = {k: dot(norm_one[k], dq, NT).astype(BF) for k in range(count)}
    kv_grads = {k: dot(dkv, norm_one[k], NT).astype(BF) for k in range(count)}
    attn_low = jnp.concatenate(
        [
            jnp.where(parity == 0, attn_mine, attn_other),
            jnp.where(parity == 0, attn_other, attn_mine),
        ]
    )
    mix_grads = {k: dot(attn_low, mix_rows[k], NT).astype(BF) for k in range(count)}
    bits = near + far[::-1]
    q_total = over_dp(fold(q_grads, "row", bits)[0])
    kv_total = over_dp(fold(kv_grads, "row", bits)[0])
    mix_total = over_dp(fold(mix_grads, "row", bits)[0])
    down_total = over_dp(down_total)
    gate_total = over_dp(gate_total)
    up_total = over_dp(up_total)

    shares = jnp.stack([gain_share_one[..., 0], gain_share_two[..., 0]], axis=2)
    shares = by_xor(shares, lax.axis_index("col"), 0)
    shares = {c: shares[c] for c in range(cols)}
    shares = fold(shares, "col", near_bits(cols) + far_bits(cols), low=False)[0]
    shares = fold({k: shares[k] for k in range(count)}, "row", bits, low=False)[0]
    gain_totals = over_dp(shares)

    input_grad = all_tokens((residual_grad_own + input_sum.astype(F32)).astype(BF)).astype(F32)
    kv_rows = kv_total.shape[0] // 2
    return (
        layer_output,
        input_grad,
        gain_totals[0],
        gain_totals[1],
        q_total,
        kv_total[:kv_rows].T,
        kv_total[kv_rows:].T,
        mix_total,
        gate_total.T,
        up_total.T,
        down_total,
    )


def solution(mesh):
    return jax.shard_map(
        body,
        mesh=mesh,
        in_specs=(
            P("dp", ("row", "col")),
            P(("row", "col")),
            P(("row", "col")),
            P("row", "col"),
            P("row", "col"),
            P("row", "col"),
            P("col", "row"),
            P("row", "col"),
            P("row", "col"),
            P("col", "row"),
            P("dp", ("row", "col")),
            P(("dp", "row")),
            P(("dp", "row")),
        ),
        out_specs=(
            P("dp", ("row", "col")),
            P("dp", ("row", "col")),
            P(("row", "col")),
            P(("row", "col")),
            P("row", "col"),
            P("row", "col"),
            P("row", "col"),
            P("col", "row"),
            P("row", "col"),
            P("row", "col"),
            P("col", "row"),
        ),
        check_vma=False,
    )
```

```python
import functools

import jax
import jax.numpy as jnp
from jax import lax
from jax.experimental import pallas as pl
from jax.experimental.pallas import tpu as pltpu
from jax.sharding import PartitionSpec as P

D = 2560
HEAD = 80
EPS = 1e-05
THETA = 10000.0
NEG = -1e30
LOG2E = 1.4426950408889634
LN2 = 0.6931471805599453
ROOT = HEAD ** (-0.5)
BF = jnp.bfloat16
F32 = jnp.float32
NN = (((1,), (0,)), ((), ()))
TN = (((0,), (0,)), ((), ()))
NT = (((1,), (1,)), ((), ()))


def dot(left, right, dims=NN):
    return lax.dot_general(left, right, dims, preferred_element_type=F32)


def together(*values):
    return lax.optimization_barrier(values)


def swapped(value, axis, mask):
    size = lax.axis_size(axis)
    return lax.ppermute(value, axis, [(i, i ^ mask) for i in range(size)])


def spread(blocks, axis, bits):
    blocks = dict(blocks)
    for bit in bits:
        for k in list(blocks):
            blocks[k | bit] = swapped(blocks[k], axis, bit)
    return blocks


def fold(blocks, axis, bits, low=True):
    held = dict(blocks)
    for bit in bits:
        for k in [k for k in held if k & bit]:
            other = swapped(held.pop(k), axis, bit)
            total = held[k ^ bit].astype(F32) + other.astype(F32)
            held[k ^ bit] = total.astype(BF) if low else total
    return held


def far_bits(size):
    return [1 << i for i in range(1, size.bit_length() - 1)]


def near_bits(size):
    return [1] if size > 1 else []


def exchange_blocks(blocks, axis):
    return [blocks[0]] + [swapped(blocks[k], axis, k) for k in range(1, len(blocks))]


def by_xor(value, index, axis):
    parts = [
        lax.dynamic_index_in_dim(value, index ^ k, axis, keepdims=True)
        for k in range(value.shape[axis])
    ]
    return jnp.concatenate(parts, axis=axis)


def params(mib=58):
    return pltpu.CompilerParams(vmem_limit_bytes=mib * 1024 * 1024)


def shape(dims, dtype):
    return jax.ShapeDtypeStruct(dims, dtype)


SMALL = pl.BlockSpec(memory_space=pltpu.SMEM)
RAW = pl.BlockSpec(memory_space=pl.ANY)


def resident(dims, buffers=None):
    zeros = (0,) * len(dims)
    mode = {} if buffers is None else {"pipeline_mode": pl.Buffered(buffers)}
    return pl.BlockSpec(dims, lambda *_: zeros, **mode)


def normalise(x_ref, gain_ref, out_ref, scale_ref):
    cols, count, piece, _ = x_ref.shape
    total = None
    for c in range(cols):
        for k in range(count):
            value = x_ref[c, k].astype(F32)
            part = jnp.sum(value * value, axis=0, keepdims=True)
            total = part if total is None else total + part
    scale = lax.rsqrt(total / D + EPS)
    scale_ref[...] = scale
    for c in range(cols):
        for k in range(count):
            value = x_ref[c, k].astype(F32) * scale * gain_ref[c, k]
            out_ref[k, c * piece : (c + 1) * piece, :] = value.astype(BF)


def turn(value, cosine, sine):
    half = value.shape[0] // 2
    first, second = value[:half], value[half:]
    return jnp.concatenate([first * cosine - second * sine, second * cosine + first * sine])


def qkv_kernel(count, shared, x_ref, gain_ref, cos_ref, sin_ref, *refs):
    q_w, kv_w = refs[:count], refs[count : 2 * count]
    norm_ref, scale_ref, sets_ref = refs[2 * count :]
    normalise(x_ref, gain_ref, norm_ref, scale_ref)
    query = keyval = None
    for k in range(count):
        normed = norm_ref[k]
        part = dot(q_w[k][...], normed, TN)
        query = part if query is None else query + part
        part = dot(kv_w[k][...], normed)
        keyval = part if keyval is None else keyval + part
    cosine, sine = cos_ref[...], sin_ref[...]
    half = query.shape[0] // 2
    kv_half = keyval.shape[0] // 2
    for h in range(2):
        for at in range(0, half, HEAD):
            value = turn(query[h * half + at : h * half + at + HEAD], cosine, sine)
            sets_ref[h, at : at + HEAD, :] = (value * (ROOT * LOG2E)).astype(BF)
        at = 0 if shared else h * HEAD
        key = turn(keyval[at : at + HEAD], cosine, sine)
        sets_ref[h, half : half + HEAD, :] = key.astype(BF)
        sets_ref[h, half + HEAD : half + 2 * HEAD, :] = keyval[
            kv_half + at : kv_half + at + HEAD
        ].astype(BF)


def qkv_project(x, gain, cosine, sine, q_w, kv_w):
    cols, count, piece, tokens = x.shape
    half = q_w[0].shape[1] // 2
    shared = kv_w[0].shape[0] == 2 * HEAD
    return pl.pallas_call(
        functools.partial(qkv_kernel, count, shared),
        out_shape=(
            shape((count, cols * piece, tokens), BF),
            shape((1, tokens), F32),
            shape((2, half + 2 * HEAD, tokens), BF),
        ),
        compiler_params=params(),
        name="qkv_project",
    )(x, gain, cosine, sine, *q_w, *kv_w)


def pieces_of(half, at, tile, tokens):
    if half == 1:
        return [(0, 0, tokens, False), (1, 0, at + tile, True)]
    head = [(0, 0, at, False)] if at else []
    return head + [(0, at, at + tile, True)]


def seen_of(half, at, begin, end, tile, seg_row, seg_col):
    rows = lax.broadcasted_iota(jnp.int32, (end - begin, tile), 0) + begin
    cols = lax.broadcasted_iota(jnp.int32, (end - begin, tile), 1) + at
    seen = rows <= cols
    if half == 1:
        seen = seen & (seg_col[begin:end] == seg_row[:, at : at + tile])
    return seen


def place(parity, own_ref, other_ref, sets):
    sets[parity] = own_ref[...]
    sets[1 - parity] = other_ref[...]


def attend_kernel(
    tile, parity_ref, own_ref, other_ref, seg_row, seg_col, mine_ref, send_ref, lse_ref, sets, rows
):
    tokens = own_ref.shape[-1]
    heads = pl.num_programs(0)
    head = pl.program_id(0)
    parity = parity_ref[0]
    half_rows = own_ref.shape[0] - 2 * HEAD

    @pl.when(head == 0)
    def _():
        place(parity, own_ref, other_ref, sets)
        for half in range(2):
            keys = sets[half, half_rows : half_rows + HEAD, :]
            rows[half] = keys.astype(F32).T.astype(BF)

    at_head = pl.ds(pl.multiple_of(head * HEAD, 16), HEAD)
    for half in range(2):
        for at in range(0, tokens, tile):
            span = slice(at, at + tile)
            query = sets[half, at_head, span]
            pieces = pieces_of(half, at, tile, tokens)
            scores = []
            for which, begin, end, masked in pieces:
                part = dot(rows[which, begin:end, :], query)
                if masked:
                    part = jnp.where(
                        seen_of(half, at, begin, end, tile, seg_row, seg_col), part, NEG
                    )
                scores.append(part)
            peak = functools.reduce(
                jnp.maximum, [jnp.max(s, axis=0, keepdims=True) for s in scores]
            )
            total = out = None
            for (which, begin, end, _), part in zip(pieces, scores):
                weights = jnp.exp2(part - peak)
                mass = jnp.sum(weights, axis=0, keepdims=True)
                value = dot(sets[which, half_rows + HEAD :, begin:end], weights.astype(BF))
                total = mass if total is None else total + mass
                out = value if out is None else out + value
            out = (out / total).astype(BF)
            lse_ref[half, 0, :, span] = peak + jnp.log2(total)

            @pl.when(parity == half)
            def _():
                mine_ref[at_head, span] = out

            @pl.when(parity != half)
            def _():
                send_ref[at_head, span] = out


def attend(parity, own, other, seg):
    depth, tokens = own.shape
    half_rows = depth - 2 * HEAD
    heads = half_rows // HEAD
    tile = min(256, tokens)
    out = resident((half_rows, tokens))
    return pl.pallas_call(
        functools.partial(attend_kernel, tile),
        out_shape=(
            shape((half_rows, tokens), BF),
            shape((half_rows, tokens), BF),
            shape((2, heads, 1, tokens), F32),
        ),
        grid=(heads,),
        in_specs=[
            SMALL,
            resident((depth, tokens)),
            resident((depth, tokens)),
            resident((1, tokens)),
            resident((tokens, 1)),
        ],
        out_specs=(out, out, pl.BlockSpec((2, 1, 1, tokens), lambda h: (0, h, 0, 0))),
        scratch_shapes=[
            pltpu.VMEM((2, depth, tokens), BF),
            pltpu.VMEM((2, tokens, HEAD), BF),
        ],
        compiler_params=params(),
        name="attend",
    )(parity, own, other, seg[None, :], seg[:, None])


def attend_back_kernel(
    tile,
    parity_ref,
    own_ref,
    other_ref,
    own_out,
    other_out,
    own_grad,
    other_grad,
    lse_ref,
    seg_row,
    seg_col,
    mine_ref,
    send_ref,
    sets,
    outs,
    grads,
    rows,
    key_acc,
    value_acc,
):
    tokens = own_ref.shape[-1]
    heads = pl.num_programs(0)
    head = pl.program_id(0)
    parity = parity_ref[0]
    half_rows = own_ref.shape[0] - 2 * HEAD

    @pl.when(head == 0)
    def _():
        place(parity, own_ref, other_ref, sets)
        place(parity, own_out, other_out, outs)
        place(parity, own_grad, other_grad, grads)
        for half in range(2):
            for i in range(2):
                at = half_rows + i * HEAD
                rows[i, half] = sets[half, at : at + HEAD, :].astype(F32).T.astype(BF)
        key_acc[...] = jnp.zeros_like(key_acc)
        value_acc[...] = jnp.zeros_like(value_acc)

    at_head = pl.ds(pl.multiple_of(head * HEAD, 16), HEAD)
    for half in range(2):
        for at in range(0, tokens, tile):
            span = slice(at, at + tile)
            query = sets[half, at_head, span]
            grad = grads[half, at_head, span]
            lse = lse_ref[half, 0, :, span]
            delta = jnp.sum(
                grad.astype(F32) * outs[half, at_head, span].astype(F32), axis=0, keepdims=True
            )
            total = None
            for which, begin, end, masked in pieces_of(half, at, tile, tokens):
                part = dot(rows[0, which, begin:end, :], query)
                if masked:
                    part = jnp.where(
                        seen_of(half, at, begin, end, tile, seg_row, seg_col), part, NEG
                    )
                weights = jnp.exp2(part - lse)
                dprod = dot(rows[1, which, begin:end, :], grad)
                dscore = (weights * (dprod - delta)).astype(BF)
                value_acc[which, :, begin:end] += dot(grad, weights.astype(BF), NT)
                key_acc[which, :, begin:end] += dot(query, dscore, NT)
                more = dot(sets[which, half_rows : half_rows + HEAD, begin:end], dscore)
                total = more if total is None else total + more
            total = (total * ROOT).astype(BF)

            @pl.when(parity == half)
            def _():
                mine_ref[at_head, span] = total

            @pl.when(parity != half)
            def _():
                send_ref[at_head, span] = total

    @pl.when(head == heads - 1)
    def _():
        for ref, which in ((mine_ref, parity), (send_ref, 1 - parity)):
            ref[half_rows : half_rows + HEAD, :] = (key_acc[which] * LN2).astype(BF)
            ref[half_rows + HEAD :, :] = value_acc[which].astype(BF)


def attend_back(parity, own, other, own_out, other_out, own_grad, other_grad, lse, seg):
    depth, tokens = own.shape
    half_rows = depth - 2 * HEAD
    heads = half_rows // HEAD
    tile = min(256, tokens)
    full, part = resident((depth, tokens)), resident((half_rows, tokens))
    return pl.pallas_call(
        functools.partial(attend_back_kernel, tile),
        out_shape=(shape((depth, tokens), BF), shape((depth, tokens), BF)),
        grid=(heads,),
        in_specs=[
            SMALL,
            full,
            full,
            part,
            part,
            part,
            part,
            pl.BlockSpec((2, 1, 1, tokens), lambda h: (0, h, 0, 0)),
            resident((1, tokens)),
            resident((tokens, 1)),
        ],
        out_specs=(full, full),
        scratch_shapes=[
            pltpu.VMEM((2, depth, tokens), BF),
            pltpu.VMEM((2, half_rows, tokens), BF),
            pltpu.VMEM((2, half_rows, tokens), BF),
            pltpu.VMEM((2, 2, tokens, HEAD), BF),
            pltpu.VMEM((2, HEAD, tokens), F32),
            pltpu.VMEM((2, HEAD, tokens), F32),
        ],
        compiler_params=params(),
        name="attend_back",
    )(
        parity,
        own,
        other,
        own_out,
        other_out,
        own_grad,
        other_grad,
        lse,
        seg[None, :],
        seg[:, None],
    )


def halves_at(parity, half_rows):
    mine = pl.ds(pl.multiple_of(parity * half_rows, 16), half_rows)
    other = pl.ds(pl.multiple_of((1 - parity) * half_rows, 16), half_rows)
    return mine, other


def mix_out_kernel(count, parity_ref, own_ref, other_ref, *refs):
    weights, out_ref = refs[:count], refs[count]
    cols, _, piece, _ = out_ref.shape
    mine, other = halves_at(parity_ref[0], own_ref.shape[0])
    for k in range(count):
        part = dot(weights[k][mine, :], own_ref[...], TN)
        part = part + dot(weights[k][other, :], other_ref[...], TN)
        for c in range(cols):
            out_ref[c, k] = part[c * piece : (c + 1) * piece].astype(BF)


def mix_out(parity, own, other, weights, cols):
    count = len(weights)
    piece = weights[0].shape[1] // cols
    vmem = pl.BlockSpec(memory_space=pltpu.VMEM)
    return pl.pallas_call(
        functools.partial(mix_out_kernel, count),
        out_shape=shape((cols, count, piece, own.shape[1]), BF),
        in_specs=[SMALL] + [vmem] * (2 + count),
        compiler_params=params(),
        name="mix_out",
    )(parity, own, other, *weights)


def mix_back_kernel(count, parts, parity_ref, *refs):
    x_refs, weights = refs[:parts], refs[parts : parts + count]
    rows_ref, own_ref, other_ref = refs[parts + count :]
    for i, x_ref in enumerate(x_refs):
        cols, _, piece, tokens = x_ref.shape
        for c in range(cols):
            for k in range(count):
                rows_ref[k, c * piece : (c + 1) * piece, i * tokens : (i + 1) * tokens] = x_ref[
                    c, k
                ]
    mine, other = halves_at(parity_ref[0], own_ref.shape[0])
    for at, out_ref in ((other, other_ref), (mine, own_ref)):
        total = None
        for k in range(count):
            part = dot(weights[k][at, :], rows_ref[k])
            total = part if total is None else total + part
        out_ref[...] = total.astype(BF)


def mix_back(parity, x_parts, weights):
    parts = len(x_parts)
    cols, count, piece, tokens = x_parts[0].shape
    tokens = tokens * parts
    half_rows = weights[0].shape[0] // 2
    vmem = pl.BlockSpec(memory_space=pltpu.VMEM)
    return pl.pallas_call(
        functools.partial(mix_back_kernel, count, parts),
        out_shape=(
            shape((count, cols * piece, tokens), BF),
            shape((half_rows, tokens), BF),
            shape((half_rows, tokens), BF),
        ),
        in_specs=[SMALL] + [vmem] * (parts + count),
        compiler_params=params(),
        name="mix_back",
    )(parity, *x_parts, *weights)


def fan_kernel(count, x_ref, *refs):
    weights, out_ref = refs[:count], refs[count]
    cols, _, piece, _ = out_ref.shape
    for k in range(count):
        part = dot(weights[k][...], x_ref[...], TN)
        for c in range(cols):
            out_ref[c, k] = part[c * piece : (c + 1) * piece].astype(BF)


def fan_out(weights, x, cols):
    count = len(weights)
    piece = weights[0].shape[1] // cols
    return pl.pallas_call(
        functools.partial(fan_kernel, count),
        out_shape=shape((cols, count, piece, x.shape[1]), BF),
        compiler_params=params(),
        name="fan_out",
    )(x, *weights)


def norm_back(grads, k, x_ref, gain_ref, scale, coef, share_ref, gain_share_ref):
    cols, _, piece, _ = x_ref.shape
    for c in range(cols):
        grad = grads[c * piece : (c + 1) * piece]
        value = x_ref[c, k].astype(F32)
        gain_share_ref[c, k] = jnp.sum(grad * (value * scale), axis=1, keepdims=True)
        share_ref[c, k] = ((grad * gain_ref[c, k]) * scale - value * coef).astype(BF)


def ff_kernel(count, chained, x_ref, g_ref, gain_ref, *refs):
    gate_w, up_w, down_w = refs[:count], refs[count : 2 * count], refs[2 * count : 3 * count]
    refs = refs[3 * count + (5 if chained else 0) :]
    norm_ref, rows_ref, act_ref, dgate_ref, dup_ref, share_ref, gain_share_ref = refs[:7]
    scale_ref, inner_ref, back_ref = refs[7:]
    cols, _, piece, _ = x_ref.shape
    step = pl.program_id(0)

    @pl.when(step == 0)
    def _():
        normalise(x_ref, gain_ref, norm_ref, scale_ref)
        for c in range(cols):
            for k in range(count):
                rows_ref[k, c * piece : (c + 1) * piece, :] = g_ref[c, k]
        inner_ref[...] = jnp.zeros_like(inner_ref)
        back_ref[...] = jnp.zeros_like(back_ref)

    def summed(weights, ref):
        total = None
        for k in range(count):
            part = dot(weights[k][...], ref[k])
            total = part if total is None else total + part
        return total

    gate = summed(gate_w, norm_ref)
    up = summed(up_w, norm_ref)
    sigma = jax.nn.sigmoid(gate)
    silu = gate * sigma
    act_ref[...] = (silu * up).astype(BF)
    grad = summed(down_w, rows_ref)
    dup = grad * silu
    dgate = grad * up * (sigma + silu * (1.0 - sigma))
    inner_ref[...] += jnp.sum(dgate * gate + dup * up, axis=0, keepdims=True)
    dgate_ref[...] = dgate.astype(BF)
    dup_ref[...] = dup.astype(BF)
    for k in range(count):
        back_ref[k] += dot(gate_w[k][...], dgate_ref[...], TN) + dot(
            up_w[k][...], dup_ref[...], TN
        )

    @pl.when(step == pl.num_programs(0) - 1)
    def _():
        scale = scale_ref[...]
        coef = scale * scale * inner_ref[...] / D
        for k in range(count):
            norm_back(back_ref[k], k, x_ref, gain_ref, scale, coef, share_ref, gain_share_ref)


def feed_forward(x, g, part, parts, gain, gate_w, up_w, down_w, before):
    cols, count, piece, tokens = x.shape
    width, depth = gate_w[0].shape
    tile = 432 if width % 432 == 0 else width
    g_spec = pl.BlockSpec(x.shape, lambda n: (0, 0, 0, part), pipeline_mode=pl.Buffered(1))
    rows = (count, cols * piece, tokens)
    rows_spec = pl.BlockSpec(rows, lambda n: (0, 0, part), pipeline_mode=pl.Buffered(1))
    w_spec = pl.BlockSpec((tile, depth), lambda n: (n, 0))
    h_spec = pl.BlockSpec((tile, tokens), lambda n: (n, part))
    rows_all = shape((count, cols * piece, tokens * parts), BF)
    hidden = shape((width, tokens * parts), BF)
    first = 3 + 3 * count
    return pl.pallas_call(
        functools.partial(ff_kernel, count, bool(before)),
        out_shape=(
            rows_all,
            rows_all,
            hidden,
            hidden,
            hidden,
            shape(x.shape, BF),
            shape(gain.shape, F32),
        ),
        grid=(width // tile,),
        in_specs=[resident(x.shape, 1), g_spec, resident(gain.shape, 1)]
        + [w_spec] * (3 * count)
        + [RAW] * len(before),
        out_specs=(
            rows_spec,
            rows_spec,
            h_spec,
            h_spec,
            h_spec,
            resident(x.shape, 1),
            resident(gain.shape, 1),
        ),
        scratch_shapes=[
            pltpu.VMEM((1, tokens), F32),
            pltpu.VMEM((1, tokens), F32),
            pltpu.VMEM(rows, F32),
        ],
        input_output_aliases={first + i: i for i in range(len(before))},
        compiler_params=params(60),
        name="feed_forward",
    )(x, g, gain, *gate_w, *up_w, *down_w, *before)


def qkv_back_kernel(
    count,
    shared,
    parity_ref,
    x_ref,
    gain_ref,
    scale_ref,
    cos_ref,
    sin_ref,
    sets_ref,
    own_ref,
    other_ref,
    *refs,
):
    q_w, kv_w = refs[:count], refs[count : 2 * count]
    dq_ref, dkv_ref, share_ref, gain_share_ref = refs[2 * count :]
    parity = parity_ref[0]
    half_rows = own_ref.shape[0] - 2 * HEAD
    kv_half = dkv_ref.shape[0] // 2
    cosine, sine = cos_ref[...], -sin_ref[...]
    inner = None
    folded = None
    for grads, which in ((own_ref, parity), (other_ref, 1 - parity)):
        for at in range(0, half_rows + 2 * HEAD, HEAD):
            value = grads[at : at + HEAD, :].astype(F32)
            part = value * sets_ref[which, at : at + HEAD, :].astype(F32)
            part = jnp.sum(part, axis=0, keepdims=True)
            if at < half_rows:
                part = part * (1.0 / (ROOT * LOG2E))
                start = pl.multiple_of(which * half_rows + at, 16)
                dq_ref[pl.ds(start, HEAD), :] = turn(value, cosine, sine).astype(BF)
            else:
                is_key = at == half_rows
                raw = turn(value, cosine, sine) if is_key else value
                base = 0 if is_key else kv_half
                if not shared:
                    start = pl.multiple_of(base + which * HEAD, 16)
                    dkv_ref[pl.ds(start, HEAD), :] = raw.astype(BF)
                elif folded is None or at not in folded:
                    folded = {**(folded or {}), at: raw}
                else:
                    dkv_ref[base : base + HEAD, :] = (folded[at] + raw).astype(BF)
            inner = part if inner is None else inner + part
    scale = scale_ref[...]
    coef = scale * scale * inner / D
    for k in range(count):
        grads = dot(q_w[k][...], dq_ref[...]) + dot(kv_w[k][...], dkv_ref[...], TN)
        norm_back(grads, k, x_ref, gain_ref, scale, coef, share_ref, gain_share_ref)


def qkv_back(parity, x, gain, scale, cosine, sine, sets, own, other, q_w, kv_w):
    cols, count, piece, tokens = x.shape
    shared = kv_w[0].shape[0] == 2 * HEAD
    vmem = pl.BlockSpec(memory_space=pltpu.VMEM)
    return pl.pallas_call(
        functools.partial(qkv_back_kernel, count, shared),
        out_shape=(
            shape((q_w[0].shape[1], tokens), BF),
            shape((kv_w[0].shape[0], tokens), BF),
            shape(x.shape, BF),
            shape(gain.shape, F32),
        ),
        in_specs=[SMALL] + [vmem] * (8 + 2 * count),
        compiler_params=params(),
        name="qkv_back",
    )(parity, x, gain, scale, cosine, sine, sets, own, other, *q_w, *kv_w)


def rope_parts(positions):
    half = HEAD // 2
    freq = THETA ** (-jnp.arange(half, dtype=F32) * 2.0 / HEAD)
    angle = freq[:, None] * positions.astype(F32)[None, :]
    return (jnp.cos(angle), jnp.sin(angle))


def spread_cols(value):
    return lax.all_gather(value, "col", axis=0, tiled=False)


def sum_cols(value):
    return lax.psum_scatter(value, "col", scatter_dimension=0, tiled=False)


def over_dp(value):
    low = value.astype(BF)
    total = low.astype(F32)
    size = lax.axis_size("dp")
    for step in range(1, size):
        other = lax.ppermute(low, "dp", [(i, (i + step) % size) for i in range(size)])
        total = total + other.astype(F32)
    return total


def body(
    layer_input,
    attn_gain,
    mlp_gain,
    query_weight,
    key_weight,
    value_weight,
    mix_weight,
    gate_weight,
    up_weight,
    down_weight,
    output_grad,
    segment_ids,
    position_ids,
):
    rows = segment_ids.shape[0]
    count = lax.axis_size("row")
    cols = lax.axis_size("col")
    piece = layer_input.shape[1]
    row = lax.axis_index("row")
    parity = (row % 2).astype(jnp.int32)
    own_core = parity.reshape(1)
    q_half = query_weight.shape[1] // 2
    near, far = near_bits(count), far_bits(count)

    def row_tokens(value):
        turned = value.T
        outgoing = [
            lax.dynamic_slice(turned, (0, (row ^ k) * rows), (piece, rows)) for k in range(count)
        ]
        return jnp.stack(exchange_blocks(outgoing, "row"))

    def all_tokens(blocks):
        got = exchange_blocks([blocks[k] for k in range(count)], "row")
        result = jnp.zeros((piece, count * rows), blocks.dtype)
        for k in range(count):
            result = lax.dynamic_update_slice(result, got[k], (0, (row ^ k) * rows))
        return result.T

    def listed(blocks):
        return [blocks[k] for k in range(count)]

    source_own = row_tokens(layer_input)
    kv_weight = jnp.concatenate([key_weight.T, value_weight.T])
    q_first = spread({0: query_weight}, "row", far)
    kv_first = spread({0: kv_weight}, "row", far)
    mix_first = spread({0: mix_weight}, "row", far)
    gate_first = spread({0: gate_weight.T}, "row", far)
    up_first = spread({0: up_weight.T}, "row", far)
    down_first = spread({0: down_weight}, "row", far)
    q_blocks = spread(q_first, "row", near)
    kv_blocks = spread(kv_first, "row", near)

    gains = lax.all_gather(jnp.stack([attn_gain, mlp_gain]), ("row", "col"), axis=1, tiled=True)
    gains = gains.reshape(2, count, cols, piece)
    gains = by_xor(gains, row, 1).swapaxes(1, 2)[..., None]
    gain_one, gain_two = gains[0], gains[1]

    cosine, sine = rope_parts(position_ids)
    other_seg = swapped(segment_ids, "row", 1)
    seg = jnp.where(parity == 0, other_seg, segment_ids)

    source = spread_cols(source_own)
    source, q_blocks, kv_blocks, mix_first, gate_first, gain_one, cosine, sine, seg = together(
        source, q_blocks, kv_blocks, mix_first, gate_first, gain_one, cosine, sine, seg
    )
    grad_own = row_tokens(output_grad)
    grad_own, source = together(grad_own, source)
    grad_all = spread_cols(grad_own)
    norm_one, scale_one, sets = qkv_project(
        source, gain_one, cosine, sine, listed(q_blocks), listed(kv_blocks)
    )
    own_set = lax.dynamic_index_in_dim(sets, parity, 0, keepdims=False)
    other_set = swapped(lax.dynamic_index_in_dim(sets, 1 - parity, 0, keepdims=False), "row", 1)
    attn_mine, attn_send, lse = attend(own_core, own_set, other_set, seg)
    attn_other = swapped(attn_send, "row", 1)
    mix_blocks = spread(mix_first, "row", near)
    attn_mine, attn_other, mix_blocks, up_first = together(
        attn_mine, attn_other, mix_blocks, up_first
    )
    attn_part = mix_out(own_core, attn_mine, attn_other, listed(mix_blocks), cols)
    attn_part, grad_all = together(attn_part, grad_all)
    attn_sum = sum_cols(attn_part)
    gate_blocks = spread(gate_first, "row", near)
    up_blocks = spread(up_first, "row", near)
    down_blocks = spread(down_first, "row", near)
    attn_sum, gate_blocks, up_blocks, down_blocks = together(
        attn_sum, gate_blocks, up_blocks, down_blocks
    )
    residual_own = source_own.astype(F32) + attn_sum.astype(F32)

    parts = 2 if rows % 256 == 0 else 1
    size = rows // parts
    spans = [slice(i * size, (i + 1) * size) for i in range(parts)]
    residual_low = residual_own.astype(BF)
    residual = [spread_cols(residual_low[..., span]) for span in spans]
    before, shares = (), []
    gain_share_two = 0.0
    for i in range(parts):
        out = feed_forward(
            residual[i],
            grad_all,
            i,
            parts,
            gain_two,
            listed(gate_blocks),
            listed(up_blocks),
            listed(down_blocks),
            before,
        )
        before = out[:5]
        shares.append(out[5])
        gain_share_two = gain_share_two + out[6]
    norm_two, grad_rows, act, dgate, dup = before
    share_sums = [sum_cols(share) for share in shares]
    down_grads = {k: dot(act, grad_rows[k], NT).astype(BF) for k in range(count)}
    gate_grads = {k: dot(dgate, norm_two[k], NT).astype(BF) for k in range(count)}
    up_grads = {k: dot(dup, norm_two[k], NT).astype(BF) for k in range(count)}
    down_grads = fold(down_grads, "row", near)
    gate_grads = fold(gate_grads, "row", near)
    up_grads = fold(up_grads, "row", near)
    *share_sums, down_grads, gate_grads, up_grads = together(
        *share_sums, down_grads, gate_grads, up_grads
    )
    residual_grad_own = [
        grad_own[..., span].astype(F32) + total.astype(F32)
        for span, total in zip(spans, share_sums)
    ]
    down_total = fold(down_grads, "row", far)[0]
    gate_total = fold(gate_grads, "row", far)[0]

    mix_cols = [spread_cols(value.astype(BF)) for value in residual_grad_own]
    ff_part = fan_out(listed(down_blocks), act, cols)
    *mix_cols, ff_part, down_total, gate_total, up_grads = together(
        *mix_cols, ff_part, down_total, gate_total, up_grads
    )
    up_total = fold(up_grads, "row", far)[0]
    down_total = over_dp(down_total)
    mix_rows, grad_mine, grad_send = mix_back(own_core, mix_cols, listed(mix_blocks))
    ff_sum = sum_cols(ff_part)
    grad_other = swapped(grad_send, "row", 1)
    back_mine, back_send = attend_back(
        own_core, own_set, other_set, attn_mine, attn_send, grad_mine, grad_other, lse, seg
    )
    back_other = swapped(back_send, "row", 1)
    back_other, up_total, down_total, gate_total = together(
        back_other, up_total, down_total, gate_total
    )
    gate_total = over_dp(gate_total)
    dq, dkv, share, gain_share_one = qkv_back(
        own_core,
        source,
        gain_one,
        scale_one,
        cosine,
        sine,
        sets,
        back_mine,
        back_other,
        listed(q_blocks),
        listed(kv_blocks),
    )
    attn_low = jnp.concatenate(
        [
            jnp.where(parity == 0, attn_mine, attn_other),
            jnp.where(parity == 0, attn_other, attn_mine),
        ]
    )
    mix_grads = {k: dot(attn_low, mix_rows[k], NT).astype(BF) for k in range(count)}
    mix_grads = fold(mix_grads, "row", near)
    share, ff_sum, mix_grads, gate_total, up_total = together(
        share, ff_sum, mix_grads, gate_total, up_total
    )
    input_sum = sum_cols(share)
    up_total = over_dp(up_total)
    mix_total = over_dp(fold(mix_grads, "row", far)[0])
    output_own = (residual_own + ff_sum.astype(F32)).astype(BF)
    layer_output = all_tokens(output_own)
    q_grads = {k: dot(norm_one[k], dq, NT).astype(BF) for k in range(count)}
    kv_grads = {k: dot(dkv, norm_one[k], NT).astype(BF) for k in range(count)}
    bits = near + far[::-1]
    q_total = fold(q_grads, "row", bits)[0]
    kv_total = fold(kv_grads, "row", bits)[0]

    gain_shares = jnp.stack([gain_share_one[..., 0], gain_share_two[..., 0]], axis=2)
    gain_shares = by_xor(gain_shares, lax.axis_index("col"), 0)
    gain_shares = {c: gain_shares[c] for c in range(cols)}
    gain_shares = fold(gain_shares, "col", near_bits(cols) + far_bits(cols), low=False)[0]
    gain_shares = fold({k: gain_shares[k] for k in range(count)}, "row", bits, low=False)[0]
    gain_totals = over_dp(gain_shares)
    input_sum, q_total, kv_total, mix_total, up_total, gain_totals, layer_output = together(
        input_sum, q_total, kv_total, mix_total, up_total, gain_totals, layer_output
    )
    q_total = over_dp(q_total)
    kv_total = over_dp(kv_total)
    residual_grad_own = jnp.concatenate(residual_grad_own, axis=2)

    input_grad = all_tokens((residual_grad_own + input_sum.astype(F32)).astype(BF)).astype(F32)
    kv_rows = kv_total.shape[0] // 2
    return (
        layer_output,
        input_grad,
        gain_totals[0],
        gain_totals[1],
        q_total,
        kv_total[:kv_rows].T,
        kv_total[kv_rows:].T,
        mix_total,
        gate_total.T,
        up_total.T,
        down_total,
    )


def solution(mesh):
    return jax.shard_map(
        body,
        mesh=mesh,
        in_specs=(
            P("dp", ("row", "col")),
            P(("row", "col")),
            P(("row", "col")),
            P("row", "col"),
            P("row", "col"),
            P("row", "col"),
            P("col", "row"),
            P("row", "col"),
            P("row", "col"),
            P("col", "row"),
            P("dp", ("row", "col")),
            P(("dp", "row")),
            P(("dp", "row")),
        ),
        out_specs=(
            P("dp", ("row", "col")),
            P("dp", ("row", "col")),
            P(("row", "col")),
            P(("row", "col")),
            P("row", "col"),
            P("row", "col"),
            P("row", "col"),
            P("col", "row"),
            P("row", "col"),
            P("row", "col"),
            P("col", "row"),
        ),
        check_vma=False,
    )
```

```python
import functools

import jax
import jax.numpy as jnp
from jax import lax
from jax.experimental import pallas as pl
from jax.experimental.pallas import tpu as pltpu
from jax.sharding import PartitionSpec as P

D = 2560
HEAD = 80
EPS = 1e-05
THETA = 10000.0
NEG = -1e30
LOG2E = 1.4426950408889634
LN2 = 0.6931471805599453
ROOT = HEAD ** (-0.5)
BF = jnp.bfloat16
F32 = jnp.float32
NN = (((1,), (0,)), ((), ()))
TN = (((0,), (0,)), ((), ()))
NT = (((1,), (1,)), ((), ()))


def dot(left, right, dims=NN):
    return lax.dot_general(left, right, dims, preferred_element_type=F32)


def together(*values):
    return lax.optimization_barrier(values)


def swapped(value, axis, mask):
    size = lax.axis_size(axis)
    return lax.ppermute(value, axis, [(i, i ^ mask) for i in range(size)])


def spread(blocks, axis, bits):
    blocks = dict(blocks)
    for bit in bits:
        for k in list(blocks):
            blocks[k | bit] = swapped(blocks[k], axis, bit)
    return blocks


def fold(blocks, axis, bits, low=True):
    held = dict(blocks)
    for bit in bits:
        for k in [k for k in held if k & bit]:
            other = swapped(held.pop(k), axis, bit)
            total = held[k ^ bit].astype(F32) + other.astype(F32)
            held[k ^ bit] = total.astype(BF) if low else total
    return held


def far_bits(size):
    return [1 << i for i in range(1, size.bit_length() - 1)]


def near_bits(size):
    return [1] if size > 1 else []


def exchange_blocks(blocks, axis):
    return [blocks[0]] + [swapped(blocks[k], axis, k) for k in range(1, len(blocks))]


def by_xor(value, index, axis):
    parts = [
        lax.dynamic_index_in_dim(value, index ^ k, axis, keepdims=True)
        for k in range(value.shape[axis])
    ]
    return jnp.concatenate(parts, axis=axis)


def params(mib=58):
    return pltpu.CompilerParams(vmem_limit_bytes=mib * 1024 * 1024)


def shape(dims, dtype):
    return jax.ShapeDtypeStruct(dims, dtype)


SMALL = pl.BlockSpec(memory_space=pltpu.SMEM)
RAW = pl.BlockSpec(memory_space=pl.ANY)


def resident(dims, buffers=None):
    zeros = (0,) * len(dims)
    mode = {} if buffers is None else {"pipeline_mode": pl.Buffered(buffers)}
    return pl.BlockSpec(dims, lambda *_: zeros, **mode)


def normalise(x_ref, gain_ref, out_ref, scale_ref):
    cols, count, piece, _ = x_ref.shape
    total = None
    for c in range(cols):
        for k in range(count):
            value = x_ref[c, k].astype(F32)
            part = jnp.sum(value * value, axis=0, keepdims=True)
            total = part if total is None else total + part
    scale = lax.rsqrt(total / D + EPS)
    scale_ref[...] = scale
    for c in range(cols):
        for k in range(count):
            value = x_ref[c, k].astype(F32) * scale * gain_ref[c, k]
            out_ref[k, c * piece : (c + 1) * piece, :] = value.astype(BF)


def turn(value, cosine, sine):
    half = value.shape[0] // 2
    first, second = value[:half], value[half:]
    return jnp.concatenate([first * cosine - second * sine, second * cosine + first * sine])


def qkv_kernel(count, shared, x_ref, gain_ref, cos_ref, sin_ref, *refs):
    q_w, kv_w = refs[:count], refs[count : 2 * count]
    norm_ref, scale_ref, sets_ref = refs[2 * count :]
    normalise(x_ref, gain_ref, norm_ref, scale_ref)
    query = keyval = None
    for k in range(count):
        normed = norm_ref[k]
        part = dot(q_w[k][...], normed, TN)
        query = part if query is None else query + part
        part = dot(kv_w[k][...], normed)
        keyval = part if keyval is None else keyval + part
    cosine, sine = cos_ref[...], sin_ref[...]
    half = query.shape[0] // 2
    kv_half = keyval.shape[0] // 2
    for h in range(2):
        for at in range(0, half, HEAD):
            value = turn(query[h * half + at : h * half + at + HEAD], cosine, sine)
            sets_ref[h, at : at + HEAD, :] = (value * (ROOT * LOG2E)).astype(BF)
        at = 0 if shared else h * HEAD
        key = turn(keyval[at : at + HEAD], cosine, sine)
        sets_ref[h, half : half + HEAD, :] = key.astype(BF)
        sets_ref[h, half + HEAD : half + 2 * HEAD, :] = keyval[
            kv_half + at : kv_half + at + HEAD
        ].astype(BF)


def qkv_project(x, gain, cosine, sine, q_w, kv_w):
    cols, count, piece, tokens = x.shape
    half = q_w[0].shape[1] // 2
    shared = kv_w[0].shape[0] == 2 * HEAD
    return pl.pallas_call(
        functools.partial(qkv_kernel, count, shared),
        out_shape=(
            shape((count, cols * piece, tokens), BF),
            shape((1, tokens), F32),
            shape((2, half + 2 * HEAD, tokens), BF),
        ),
        compiler_params=params(),
        name="qkv_project",
    )(x, gain, cosine, sine, *q_w, *kv_w)


def pieces_of(half, at, tile, tokens):
    if half == 1:
        return [(0, 0, tokens, False), (1, 0, at + tile, True)]
    head = [(0, 0, at, False)] if at else []
    return head + [(0, at, at + tile, True)]


def seen_of(half, at, begin, end, tile, seg_row, seg_col):
    rows = lax.broadcasted_iota(jnp.int32, (end - begin, tile), 0) + begin
    cols = lax.broadcasted_iota(jnp.int32, (end - begin, tile), 1) + at
    seen = rows <= cols
    if half == 1:
        seen = seen & (seg_col[begin:end] == seg_row[:, at : at + tile])
    return seen


def place(parity, own_ref, other_ref, sets):
    sets[parity] = own_ref[...]
    sets[1 - parity] = other_ref[...]


def attend_kernel(
    tile, parity_ref, own_ref, other_ref, seg_row, seg_col, mine_ref, send_ref, lse_ref, sets, rows
):
    tokens = own_ref.shape[-1]
    heads = pl.num_programs(0)
    head = pl.program_id(0)
    parity = parity_ref[0]
    half_rows = own_ref.shape[0] - 2 * HEAD

    @pl.when(head == 0)
    def _():
        place(parity, own_ref, other_ref, sets)
        for half in range(2):
            keys = sets[half, half_rows : half_rows + HEAD, :]
            rows[half] = keys.astype(F32).T.astype(BF)

    at_head = pl.ds(pl.multiple_of(head * HEAD, 16), HEAD)
    for half in range(2):
        for at in range(0, tokens, tile):
            span = slice(at, at + tile)
            query = sets[half, at_head, span]
            pieces = pieces_of(half, at, tile, tokens)
            scores = []
            for which, begin, end, masked in pieces:
                part = dot(rows[which, begin:end, :], query)
                if masked:
                    part = jnp.where(
                        seen_of(half, at, begin, end, tile, seg_row, seg_col), part, NEG
                    )
                scores.append(part)
            peak = functools.reduce(
                jnp.maximum, [jnp.max(s, axis=0, keepdims=True) for s in scores]
            )
            total = out = None
            for (which, begin, end, _), part in zip(pieces, scores):
                weights = jnp.exp2(part - peak)
                mass = jnp.sum(weights, axis=0, keepdims=True)
                value = dot(sets[which, half_rows + HEAD :, begin:end], weights.astype(BF))
                total = mass if total is None else total + mass
                out = value if out is None else out + value
            out = (out / total).astype(BF)
            lse_ref[half, 0, :, span] = peak + jnp.log2(total)

            @pl.when(parity == half)
            def _():
                mine_ref[at_head, span] = out

            @pl.when(parity != half)
            def _():
                send_ref[at_head, span] = out


def attend(parity, own, other, seg):
    depth, tokens = own.shape
    half_rows = depth - 2 * HEAD
    heads = half_rows // HEAD
    tile = min(256, tokens)
    out = resident((half_rows, tokens))
    return pl.pallas_call(
        functools.partial(attend_kernel, tile),
        out_shape=(
            shape((half_rows, tokens), BF),
            shape((half_rows, tokens), BF),
            shape((2, heads, 1, tokens), F32),
        ),
        grid=(heads,),
        in_specs=[
            SMALL,
            resident((depth, tokens)),
            resident((depth, tokens)),
            resident((1, tokens)),
            resident((tokens, 1)),
        ],
        out_specs=(out, out, pl.BlockSpec((2, 1, 1, tokens), lambda h: (0, h, 0, 0))),
        scratch_shapes=[
            pltpu.VMEM((2, depth, tokens), BF),
            pltpu.VMEM((2, tokens, HEAD), BF),
        ],
        compiler_params=params(),
        name="attend",
    )(parity, own, other, seg[None, :], seg[:, None])


def attend_back_kernel(
    tile,
    parity_ref,
    own_ref,
    other_ref,
    own_out,
    other_out,
    own_grad,
    other_grad,
    lse_ref,
    seg_row,
    seg_col,
    mine_ref,
    send_ref,
    sets,
    outs,
    grads,
    rows,
    key_acc,
    value_acc,
):
    tokens = own_ref.shape[-1]
    heads = pl.num_programs(0)
    head = pl.program_id(0)
    parity = parity_ref[0]
    half_rows = own_ref.shape[0] - 2 * HEAD

    @pl.when(head == 0)
    def _():
        place(parity, own_ref, other_ref, sets)
        place(parity, own_out, other_out, outs)
        place(parity, own_grad, other_grad, grads)
        for half in range(2):
            for i in range(2):
                at = half_rows + i * HEAD
                rows[i, half] = sets[half, at : at + HEAD, :].astype(F32).T.astype(BF)
        key_acc[...] = jnp.zeros_like(key_acc)
        value_acc[...] = jnp.zeros_like(value_acc)

    at_head = pl.ds(pl.multiple_of(head * HEAD, 16), HEAD)
    for half in range(2):
        for at in range(0, tokens, tile):
            span = slice(at, at + tile)
            query = sets[half, at_head, span]
            grad = grads[half, at_head, span]
            lse = lse_ref[half, 0, :, span]
            delta = jnp.sum(
                grad.astype(F32) * outs[half, at_head, span].astype(F32), axis=0, keepdims=True
            )
            total = None
            for which, begin, end, masked in pieces_of(half, at, tile, tokens):
                part = dot(rows[0, which, begin:end, :], query)
                if masked:
                    part = jnp.where(
                        seen_of(half, at, begin, end, tile, seg_row, seg_col), part, NEG
                    )
                weights = jnp.exp2(part - lse)
                dprod = dot(rows[1, which, begin:end, :], grad)
                dscore = (weights * (dprod - delta)).astype(BF)
                value_acc[which, :, begin:end] += dot(grad, weights.astype(BF), NT)
                key_acc[which, :, begin:end] += dot(query, dscore, NT)
                more = dot(sets[which, half_rows : half_rows + HEAD, begin:end], dscore)
                total = more if total is None else total + more
            total = (total * ROOT).astype(BF)

            @pl.when(parity == half)
            def _():
                mine_ref[at_head, span] = total

            @pl.when(parity != half)
            def _():
                send_ref[at_head, span] = total

    @pl.when(head == heads - 1)
    def _():
        for ref, which in ((mine_ref, parity), (send_ref, 1 - parity)):
            ref[half_rows : half_rows + HEAD, :] = (key_acc[which] * LN2).astype(BF)
            ref[half_rows + HEAD :, :] = value_acc[which].astype(BF)


def attend_back(parity, own, other, own_out, other_out, own_grad, other_grad, lse, seg):
    depth, tokens = own.shape
    half_rows = depth - 2 * HEAD
    heads = half_rows // HEAD
    tile = min(256, tokens)
    full, part = resident((depth, tokens)), resident((half_rows, tokens))
    return pl.pallas_call(
        functools.partial(attend_back_kernel, tile),
        out_shape=(shape((depth, tokens), BF), shape((depth, tokens), BF)),
        grid=(heads,),
        in_specs=[
            SMALL,
            full,
            full,
            part,
            part,
            part,
            part,
            pl.BlockSpec((2, 1, 1, tokens), lambda h: (0, h, 0, 0)),
            resident((1, tokens)),
            resident((tokens, 1)),
        ],
        out_specs=(full, full),
        scratch_shapes=[
            pltpu.VMEM((2, depth, tokens), BF),
            pltpu.VMEM((2, half_rows, tokens), BF),
            pltpu.VMEM((2, half_rows, tokens), BF),
            pltpu.VMEM((2, 2, tokens, HEAD), BF),
            pltpu.VMEM((2, HEAD, tokens), F32),
            pltpu.VMEM((2, HEAD, tokens), F32),
        ],
        compiler_params=params(),
        name="attend_back",
    )(
        parity,
        own,
        other,
        own_out,
        other_out,
        own_grad,
        other_grad,
        lse,
        seg[None, :],
        seg[:, None],
    )


def halves_at(parity, half_rows):
    mine = pl.ds(pl.multiple_of(parity * half_rows, 16), half_rows)
    other = pl.ds(pl.multiple_of((1 - parity) * half_rows, 16), half_rows)
    return mine, other


def mix_out_kernel(count, parity_ref, own_ref, other_ref, *refs):
    weights, out_ref = refs[:count], refs[count]
    cols, _, piece, _ = out_ref.shape
    mine, other = halves_at(parity_ref[0], own_ref.shape[0])
    for k in range(count):
        part = dot(weights[k][mine, :], own_ref[...], TN)
        part = part + dot(weights[k][other, :], other_ref[...], TN)
        for c in range(cols):
            out_ref[c, k] = part[c * piece : (c + 1) * piece].astype(BF)


def mix_out(parity, own, other, weights, cols):
    count = len(weights)
    piece = weights[0].shape[1] // cols
    vmem = pl.BlockSpec(memory_space=pltpu.VMEM)
    return pl.pallas_call(
        functools.partial(mix_out_kernel, count),
        out_shape=shape((cols, count, piece, own.shape[1]), BF),
        in_specs=[SMALL] + [vmem] * (2 + count),
        compiler_params=params(),
        name="mix_out",
    )(parity, own, other, *weights)


def mix_back_kernel(count, parts, parity_ref, *refs):
    x_refs, weights = refs[:parts], refs[parts : parts + count]
    rows_ref, own_ref, other_ref = refs[parts + count :]
    for i, x_ref in enumerate(x_refs):
        cols, _, piece, tokens = x_ref.shape
        for c in range(cols):
            for k in range(count):
                rows_ref[k, c * piece : (c + 1) * piece, i * tokens : (i + 1) * tokens] = x_ref[
                    c, k
                ]
    mine, other = halves_at(parity_ref[0], own_ref.shape[0])
    for at, out_ref in ((other, other_ref), (mine, own_ref)):
        total = None
        for k in range(count):
            part = dot(weights[k][at, :], rows_ref[k])
            total = part if total is None else total + part
        out_ref[...] = total.astype(BF)


def mix_back(parity, x_parts, weights):
    parts = len(x_parts)
    cols, count, piece, tokens = x_parts[0].shape
    tokens = tokens * parts
    half_rows = weights[0].shape[0] // 2
    vmem = pl.BlockSpec(memory_space=pltpu.VMEM)
    return pl.pallas_call(
        functools.partial(mix_back_kernel, count, parts),
        out_shape=(
            shape((count, cols * piece, tokens), BF),
            shape((half_rows, tokens), BF),
            shape((half_rows, tokens), BF),
        ),
        in_specs=[SMALL] + [vmem] * (parts + count),
        compiler_params=params(),
        name="mix_back",
    )(parity, *x_parts, *weights)


def fan_kernel(count, x_ref, *refs):
    weights, out_ref = refs[:count], refs[count]
    cols, _, piece, _ = out_ref.shape
    for k in range(count):
        part = dot(weights[k][...], x_ref[...], TN)
        for c in range(cols):
            out_ref[c, k] = part[c * piece : (c + 1) * piece].astype(BF)


def fan_out(weights, x, cols):
    count = len(weights)
    piece = weights[0].shape[1] // cols
    return pl.pallas_call(
        functools.partial(fan_kernel, count),
        out_shape=shape((cols, count, piece, x.shape[1]), BF),
        compiler_params=params(),
        name="fan_out",
    )(x, *weights)


def norm_back(grads, k, x_ref, gain_ref, scale, coef, share_ref, gain_share_ref):
    cols, _, piece, _ = x_ref.shape
    for c in range(cols):
        grad = grads[c * piece : (c + 1) * piece]
        value = x_ref[c, k].astype(F32)
        gain_share_ref[c, k] = jnp.sum(grad * (value * scale), axis=1, keepdims=True)
        share_ref[c, k] = ((grad * gain_ref[c, k]) * scale - value * coef).astype(BF)


def ff_kernel(count, chained, x_ref, g_ref, gain_ref, *refs):
    gate_w, up_w, down_w = refs[:count], refs[count : 2 * count], refs[2 * count : 3 * count]
    refs = refs[3 * count + (5 if chained else 0) :]
    norm_ref, rows_ref, act_ref, dgate_ref, dup_ref, share_ref, gain_share_ref = refs[:7]
    scale_ref, inner_ref, back_ref = refs[7:]
    cols, _, piece, _ = x_ref.shape
    step = pl.program_id(0)

    @pl.when(step == 0)
    def _():
        normalise(x_ref, gain_ref, norm_ref, scale_ref)
        for c in range(cols):
            for k in range(count):
                rows_ref[k, c * piece : (c + 1) * piece, :] = g_ref[c, k]
        inner_ref[...] = jnp.zeros_like(inner_ref)
        back_ref[...] = jnp.zeros_like(back_ref)

    def summed(weights, ref):
        total = None
        for k in range(count):
            part = dot(weights[k][...], ref[k])
            total = part if total is None else total + part
        return total

    gate = summed(gate_w, norm_ref)
    up = summed(up_w, norm_ref)
    sigma = jax.nn.sigmoid(gate)
    silu = gate * sigma
    act_ref[...] = (silu * up).astype(BF)
    grad = summed(down_w, rows_ref)
    dup = grad * silu
    dgate = grad * up * (sigma + silu * (1.0 - sigma))
    inner_ref[...] += jnp.sum(dgate * gate + dup * up, axis=0, keepdims=True)
    dgate_ref[...] = dgate.astype(BF)
    dup_ref[...] = dup.astype(BF)
    for k in range(count):
        back_ref[k] += dot(gate_w[k][...], dgate_ref[...], TN) + dot(
            up_w[k][...], dup_ref[...], TN
        )

    @pl.when(step == pl.num_programs(0) - 1)
    def _():
        scale = scale_ref[...]
        coef = scale * scale * inner_ref[...] / D
        for k in range(count):
            norm_back(back_ref[k], k, x_ref, gain_ref, scale, coef, share_ref, gain_share_ref)


def feed_forward(x, g, part, parts, gain, gate_w, up_w, down_w, before):
    cols, count, piece, tokens = x.shape
    width, depth = gate_w[0].shape
    tile = 432 if width % 432 == 0 else width
    g_spec = pl.BlockSpec(x.shape, lambda n: (0, 0, 0, part), pipeline_mode=pl.Buffered(1))
    rows = (count, cols * piece, tokens)
    rows_spec = pl.BlockSpec(rows, lambda n: (0, 0, part), pipeline_mode=pl.Buffered(1))
    w_spec = pl.BlockSpec((tile, depth), lambda n: (n, 0))
    h_spec = pl.BlockSpec((tile, tokens), lambda n: (n, part))
    rows_all = shape((count, cols * piece, tokens * parts), BF)
    hidden = shape((width, tokens * parts), BF)
    first = 3 + 3 * count
    return pl.pallas_call(
        functools.partial(ff_kernel, count, bool(before)),
        out_shape=(
            rows_all,
            rows_all,
            hidden,
            hidden,
            hidden,
            shape(x.shape, BF),
            shape(gain.shape, F32),
        ),
        grid=(width // tile,),
        in_specs=[resident(x.shape, 1), g_spec, resident(gain.shape, 1)]
        + [w_spec] * (3 * count)
        + [RAW] * len(before),
        out_specs=(
            rows_spec,
            rows_spec,
            h_spec,
            h_spec,
            h_spec,
            resident(x.shape, 1),
            resident(gain.shape, 1),
        ),
        scratch_shapes=[
            pltpu.VMEM((1, tokens), F32),
            pltpu.VMEM((1, tokens), F32),
            pltpu.VMEM(rows, F32),
        ],
        input_output_aliases={first + i: i for i in range(len(before))},
        compiler_params=params(60),
        name="feed_forward",
    )(x, g, gain, *gate_w, *up_w, *down_w, *before)


def qkv_back_kernel(
    count,
    shared,
    parity_ref,
    x_ref,
    gain_ref,
    scale_ref,
    cos_ref,
    sin_ref,
    sets_ref,
    own_ref,
    other_ref,
    *refs,
):
    q_w, kv_w = refs[:count], refs[count : 2 * count]
    dq_ref, dkv_ref, share_ref, gain_share_ref = refs[2 * count :]
    parity = parity_ref[0]
    half_rows = own_ref.shape[0] - 2 * HEAD
    kv_half = dkv_ref.shape[0] // 2
    cosine, sine = cos_ref[...], -sin_ref[...]
    inner = None
    folded = None
    for grads, which in ((own_ref, parity), (other_ref, 1 - parity)):
        for at in range(0, half_rows + 2 * HEAD, HEAD):
            value = grads[at : at + HEAD, :].astype(F32)
            part = value * sets_ref[which, at : at + HEAD, :].astype(F32)
            part = jnp.sum(part, axis=0, keepdims=True)
            if at < half_rows:
                part = part * (1.0 / (ROOT * LOG2E))
                start = pl.multiple_of(which * half_rows + at, 16)
                dq_ref[pl.ds(start, HEAD), :] = turn(value, cosine, sine).astype(BF)
            else:
                is_key = at == half_rows
                raw = turn(value, cosine, sine) if is_key else value
                base = 0 if is_key else kv_half
                if not shared:
                    start = pl.multiple_of(base + which * HEAD, 16)
                    dkv_ref[pl.ds(start, HEAD), :] = raw.astype(BF)
                elif folded is None or at not in folded:
                    folded = {**(folded or {}), at: raw}
                else:
                    dkv_ref[base : base + HEAD, :] = (folded[at] + raw).astype(BF)
            inner = part if inner is None else inner + part
    scale = scale_ref[...]
    coef = scale * scale * inner / D
    for k in range(count):
        grads = dot(q_w[k][...], dq_ref[...]) + dot(kv_w[k][...], dkv_ref[...], TN)
        norm_back(grads, k, x_ref, gain_ref, scale, coef, share_ref, gain_share_ref)


def qkv_back(parity, x, gain, scale, cosine, sine, sets, own, other, q_w, kv_w):
    cols, count, piece, tokens = x.shape
    shared = kv_w[0].shape[0] == 2 * HEAD
    vmem = pl.BlockSpec(memory_space=pltpu.VMEM)
    return pl.pallas_call(
        functools.partial(qkv_back_kernel, count, shared),
        out_shape=(
            shape((q_w[0].shape[1], tokens), BF),
            shape((kv_w[0].shape[0], tokens), BF),
            shape(x.shape, BF),
            shape(gain.shape, F32),
        ),
        in_specs=[SMALL] + [vmem] * (8 + 2 * count),
        compiler_params=params(),
        name="qkv_back",
    )(parity, x, gain, scale, cosine, sine, sets, own, other, *q_w, *kv_w)


def rope_parts(positions):
    half = HEAD // 2
    freq = THETA ** (-jnp.arange(half, dtype=F32) * 2.0 / HEAD)
    angle = freq[:, None] * positions.astype(F32)[None, :]
    return (jnp.cos(angle), jnp.sin(angle))


def spread_cols(value):
    return lax.all_gather(value, "col", axis=0, tiled=False)


def sum_cols(value):
    return lax.psum_scatter(value, "col", scatter_dimension=0, tiled=False)


def over_dp(value):
    low = value.astype(BF)
    total = low.astype(F32)
    size = lax.axis_size("dp")
    for step in range(1, size):
        other = lax.ppermute(low, "dp", [(i, (i + step) % size) for i in range(size)])
        total = total + other.astype(F32)
    return total


def body(
    layer_input,
    attn_gain,
    mlp_gain,
    query_weight,
    key_weight,
    value_weight,
    mix_weight,
    gate_weight,
    up_weight,
    down_weight,
    output_grad,
    segment_ids,
    position_ids,
):
    rows = segment_ids.shape[0]
    count = lax.axis_size("row")
    cols = lax.axis_size("col")
    piece = layer_input.shape[1]
    row = lax.axis_index("row")
    parity = (row % 2).astype(jnp.int32)
    own_core = parity.reshape(1)
    q_half = query_weight.shape[1] // 2
    near, far = near_bits(count), far_bits(count)

    def row_tokens(value):
        turned = value.T
        outgoing = [
            lax.dynamic_slice(turned, (0, (row ^ k) * rows), (piece, rows)) for k in range(count)
        ]
        return jnp.stack(exchange_blocks(outgoing, "row"))

    def all_tokens(blocks):
        got = exchange_blocks([blocks[k] for k in range(count)], "row")
        result = jnp.zeros((piece, count * rows), blocks.dtype)
        for k in range(count):
            result = lax.dynamic_update_slice(result, got[k], (0, (row ^ k) * rows))
        return result.T

    def listed(blocks):
        return [blocks[k] for k in range(count)]

    source_own = row_tokens(layer_input)
    kv_weight = jnp.concatenate([key_weight.T, value_weight.T])
    q_first = spread({0: query_weight}, "row", far)
    kv_first = spread({0: kv_weight}, "row", far)
    mix_first = spread({0: mix_weight}, "row", far)
    gate_first = spread({0: gate_weight.T}, "row", far)
    up_first = spread({0: up_weight.T}, "row", far)
    down_first = spread({0: down_weight}, "row", far)
    q_blocks = spread(q_first, "row", near)
    kv_blocks = spread(kv_first, "row", near)

    gains = lax.all_gather(jnp.stack([attn_gain, mlp_gain]), ("row", "col"), axis=1, tiled=True)
    gains = gains.reshape(2, count, cols, piece)
    gains = by_xor(gains, row, 1).swapaxes(1, 2)[..., None]
    gain_one, gain_two = gains[0], gains[1]

    cosine, sine = rope_parts(position_ids)
    other_seg = swapped(segment_ids, "row", 1)
    seg = jnp.where(parity == 0, other_seg, segment_ids)

    source = spread_cols(source_own)
    source, q_blocks, kv_blocks, mix_first, gate_first, gain_one, cosine, sine, seg = together(
        source, q_blocks, kv_blocks, mix_first, gate_first, gain_one, cosine, sine, seg
    )
    grad_own = row_tokens(output_grad)
    grad_own, source = together(grad_own, source)
    grad_all = spread_cols(grad_own)
    norm_one, scale_one, sets = qkv_project(
        source, gain_one, cosine, sine, listed(q_blocks), listed(kv_blocks)
    )
    own_set = lax.dynamic_index_in_dim(sets, parity, 0, keepdims=False)
    other_set = swapped(lax.dynamic_index_in_dim(sets, 1 - parity, 0, keepdims=False), "row", 1)
    attn_mine, attn_send, lse = attend(own_core, own_set, other_set, seg)
    attn_other = swapped(attn_send, "row", 1)
    mix_blocks = spread(mix_first, "row", near)
    attn_mine, attn_other, mix_blocks, up_first = together(
        attn_mine, attn_other, mix_blocks, up_first
    )
    attn_part = mix_out(own_core, attn_mine, attn_other, listed(mix_blocks), cols)
    attn_part, grad_all = together(attn_part, grad_all)
    attn_sum = sum_cols(attn_part)
    gate_blocks = spread(gate_first, "row", near)
    up_blocks = spread(up_first, "row", near)
    down_blocks = spread(down_first, "row", near)
    attn_sum, gate_blocks, up_blocks, down_blocks = together(
        attn_sum, gate_blocks, up_blocks, down_blocks
    )
    residual_own = source_own.astype(F32) + attn_sum.astype(F32)

    parts = 2 if rows % 256 == 0 else 1
    size = rows // parts
    spans = [slice(i * size, (i + 1) * size) for i in range(parts)]
    residual_low = residual_own.astype(BF)
    residual = [spread_cols(residual_low[..., span]) for span in spans]
    before, shares = (), []
    gain_share_two = 0.0
    for i in range(parts):
        out = feed_forward(
            residual[i],
            grad_all,
            i,
            parts,
            gain_two,
            listed(gate_blocks),
            listed(up_blocks),
            listed(down_blocks),
            before,
        )
        before = out[:5]
        shares.append(out[5])
        gain_share_two = gain_share_two + out[6]
    norm_two, grad_rows, act, dgate, dup = before
    share_sums = [sum_cols(share) for share in shares]
    down_grads = {k: dot(act, grad_rows[k], NT).astype(BF) for k in range(count)}
    gate_grads = {k: dot(dgate, norm_two[k], NT).astype(BF) for k in range(count)}
    up_grads = {k: dot(dup, norm_two[k], NT).astype(BF) for k in range(count)}
    down_grads = fold(down_grads, "row", near)
    gate_grads = fold(gate_grads, "row", near)
    up_grads = fold(up_grads, "row", near)
    *share_sums, down_grads, gate_grads, up_grads = together(
        *share_sums, down_grads, gate_grads, up_grads
    )
    residual_grad_own = grad_own.astype(F32) + jnp.concatenate(share_sums, axis=2).astype(F32)
    down_total = fold(down_grads, "row", far)[0]
    gate_total = fold(gate_grads, "row", far)[0]
    down_total_all = over_dp(down_total)

    mix_cols = spread_cols(residual_grad_own.astype(BF))
    ff_part = fan_out(listed(down_blocks), act, cols)
    mix_cols, ff_part, down_total, gate_total, up_grads = together(
        mix_cols, ff_part, down_total_all, gate_total, up_grads
    )
    up_total = fold(up_grads, "row", far)[0]
    gate_total = over_dp(gate_total)
    mix_rows, grad_mine, grad_send = mix_back(own_core, [mix_cols], listed(mix_blocks))
    ff_sum = sum_cols(ff_part)
    grad_other = swapped(grad_send, "row", 1)
    back_mine, back_send = attend_back(
        own_core, own_set, other_set, attn_mine, attn_send, grad_mine, grad_other, lse, seg
    )
    back_other = swapped(back_send, "row", 1)
    back_other, up_total, gate_total = together(back_other, up_total, gate_total)
    up_total = over_dp(up_total)
    dq, dkv, share, gain_share_one = qkv_back(
        own_core,
        source,
        gain_one,
        scale_one,
        cosine,
        sine,
        sets,
        back_mine,
        back_other,
        listed(q_blocks),
        listed(kv_blocks),
    )
    share, ff_sum = together(share, ff_sum)
    input_sum = sum_cols(share)
    output_own = (residual_own + ff_sum.astype(F32)).astype(BF)
    layer_output = all_tokens(output_own)

    share, dq, dkv, mix_rows = together(share, dq, dkv, mix_rows)
    bits = near + far[::-1]
    q_grads = {k: dot(norm_one[k], dq, NT).astype(BF) for k in range(count)}
    kv_grads = {k: dot(dkv, norm_one[k], NT).astype(BF) for k in range(count)}
    attn_low = jnp.concatenate(
        [
            jnp.where(parity == 0, attn_mine, attn_other),
            jnp.where(parity == 0, attn_other, attn_mine),
        ]
    )
    mix_grads = {k: dot(attn_low, mix_rows[k], NT).astype(BF) for k in range(count)}
    q_total = over_dp(fold(q_grads, "row", bits)[0])
    kv_total = over_dp(fold(kv_grads, "row", bits)[0])
    mix_total = over_dp(fold(mix_grads, "row", bits)[0])

    gain_shares = jnp.stack([gain_share_one[..., 0], gain_share_two[..., 0]], axis=2)
    gain_shares = by_xor(gain_shares, lax.axis_index("col"), 0)
    gain_shares = {c: gain_shares[c] for c in range(cols)}
    gain_shares = fold(gain_shares, "col", near_bits(cols) + far_bits(cols), low=False)[0]
    gain_shares = fold({k: gain_shares[k] for k in range(count)}, "row", bits, low=False)[0]
    gain_totals = over_dp(gain_shares)
    input_sum, q_total, kv_total, mix_total, up_total, gain_totals, layer_output = together(
        input_sum, q_total, kv_total, mix_total, up_total, gain_totals, layer_output
    )

    input_grad = all_tokens((residual_grad_own + input_sum.astype(F32)).astype(BF)).astype(F32)
    kv_rows = kv_total.shape[0] // 2
    return (
        layer_output,
        input_grad,
        gain_totals[0],
        gain_totals[1],
        q_total,
        kv_total[:kv_rows].T,
        kv_total[kv_rows:].T,
        mix_total,
        gate_total.T,
        up_total.T,
        down_total,
    )


def solution(mesh):
    return jax.shard_map(
        body,
        mesh=mesh,
        in_specs=(
            P("dp", ("row", "col")),
            P(("row", "col")),
            P(("row", "col")),
            P("row", "col"),
            P("row", "col"),
            P("row", "col"),
            P("col", "row"),
            P("row", "col"),
            P("row", "col"),
            P("col", "row"),
            P("dp", ("row", "col")),
            P(("dp", "row")),
            P(("dp", "row")),
        ),
        out_specs=(
            P("dp", ("row", "col")),
            P("dp", ("row", "col")),
            P(("row", "col")),
            P(("row", "col")),
            P("row", "col"),
            P("row", "col"),
            P("row", "col"),
            P("col", "row"),
            P("row", "col"),
            P("row", "col"),
            P("col", "row"),
        ),
        check_vma=False,
    )
```

```python
import functools

import jax
import jax.numpy as jnp
from jax import lax
from jax.experimental import pallas as pl
from jax.experimental.pallas import tpu as pltpu
from jax.sharding import PartitionSpec as P

D = 2560
HEAD = 80
EPS = 1e-05
THETA = 10000.0
NEG = -1e30
LOG2E = 1.4426950408889634
LN2 = 0.6931471805599453
ROOT = HEAD ** (-0.5)
BF = jnp.bfloat16
F32 = jnp.float32
NN = (((1,), (0,)), ((), ()))
TN = (((0,), (0,)), ((), ()))
NT = (((1,), (1,)), ((), ()))


def dot(left, right, dims=NN):
    return lax.dot_general(left, right, dims, preferred_element_type=F32)


def together(*values):
    return lax.optimization_barrier(values)


def swapped(value, axis, mask):
    size = lax.axis_size(axis)
    return lax.ppermute(value, axis, [(i, i ^ mask) for i in range(size)])


def spread(blocks, axis, bits):
    blocks = dict(blocks)
    for bit in bits:
        for k in list(blocks):
            blocks[k | bit] = swapped(blocks[k], axis, bit)
    return blocks


def fold(blocks, axis, bits, low=True):
    held = dict(blocks)
    for bit in bits:
        for k in [k for k in held if k & bit]:
            other = swapped(held.pop(k), axis, bit)
            total = held[k ^ bit].astype(F32) + other.astype(F32)
            held[k ^ bit] = total.astype(BF) if low else total
    return held


def far_bits(size):
    return [1 << i for i in range(1, size.bit_length() - 1)]


def near_bits(size):
    return [1] if size > 1 else []


def exchange_blocks(blocks, axis):
    return [blocks[0]] + [swapped(blocks[k], axis, k) for k in range(1, len(blocks))]


def by_xor(value, index, axis):
    parts = [
        lax.dynamic_index_in_dim(value, index ^ k, axis, keepdims=True)
        for k in range(value.shape[axis])
    ]
    return jnp.concatenate(parts, axis=axis)


def params(mib=58):
    return pltpu.CompilerParams(vmem_limit_bytes=mib * 1024 * 1024)


def shape(dims, dtype):
    return jax.ShapeDtypeStruct(dims, dtype)


SMALL = pl.BlockSpec(memory_space=pltpu.SMEM)
RAW = pl.BlockSpec(memory_space=pl.ANY)


def resident(dims, buffers=None):
    zeros = (0,) * len(dims)
    mode = {} if buffers is None else {"pipeline_mode": pl.Buffered(buffers)}
    return pl.BlockSpec(dims, lambda *_: zeros, **mode)


def normalise(x_ref, gain_ref, out_ref, scale_ref):
    cols, count, piece, _ = x_ref.shape
    total = None
    for c in range(cols):
        for k in range(count):
            value = x_ref[c, k].astype(F32)
            part = jnp.sum(value * value, axis=0, keepdims=True)
            total = part if total is None else total + part
    scale = lax.rsqrt(total / D + EPS)
    scale_ref[...] = scale
    for c in range(cols):
        for k in range(count):
            value = x_ref[c, k].astype(F32) * scale * gain_ref[c, k]
            out_ref[k, c * piece : (c + 1) * piece, :] = value.astype(BF)


def turn(value, cosine, sine):
    half = value.shape[0] // 2
    first, second = value[:half], value[half:]
    return jnp.concatenate([first * cosine - second * sine, second * cosine + first * sine])


def qkv_kernel(count, shared, x_ref, gain_ref, cos_ref, sin_ref, *refs):
    q_w, kv_w = refs[:count], refs[count : 2 * count]
    norm_ref, scale_ref, sets_ref = refs[2 * count :]
    normalise(x_ref, gain_ref, norm_ref, scale_ref)
    query = keyval = None
    for k in range(count):
        normed = norm_ref[k]
        part = dot(q_w[k][...], normed, TN)
        query = part if query is None else query + part
        part = dot(kv_w[k][...], normed)
        keyval = part if keyval is None else keyval + part
    cosine, sine = cos_ref[...], sin_ref[...]
    half = query.shape[0] // 2
    kv_half = keyval.shape[0] // 2
    for h in range(2):
        for at in range(0, half, HEAD):
            value = turn(query[h * half + at : h * half + at + HEAD], cosine, sine)
            sets_ref[h, at : at + HEAD, :] = (value * (ROOT * LOG2E)).astype(BF)
        at = 0 if shared else h * HEAD
        key = turn(keyval[at : at + HEAD], cosine, sine)
        sets_ref[h, half : half + HEAD, :] = key.astype(BF)
        sets_ref[h, half + HEAD : half + 2 * HEAD, :] = keyval[
            kv_half + at : kv_half + at + HEAD
        ].astype(BF)


def qkv_project(x, gain, cosine, sine, q_w, kv_w):
    cols, count, piece, tokens = x.shape
    half = q_w[0].shape[1] // 2
    shared = kv_w[0].shape[0] == 2 * HEAD
    return pl.pallas_call(
        functools.partial(qkv_kernel, count, shared),
        out_shape=(
            shape((count, cols * piece, tokens), BF),
            shape((1, tokens), F32),
            shape((2, half + 2 * HEAD, tokens), BF),
        ),
        compiler_params=params(),
        name="qkv_project",
    )(x, gain, cosine, sine, *q_w, *kv_w)


def pieces_of(half, at, tile, tokens):
    if half == 1:
        return [(0, 0, tokens, False), (1, 0, at + tile, True)]
    head = [(0, 0, at, False)] if at else []
    return head + [(0, at, at + tile, True)]


def seen_of(half, at, begin, end, tile, seg_row, seg_col):
    rows = lax.broadcasted_iota(jnp.int32, (end - begin, tile), 0) + begin
    cols = lax.broadcasted_iota(jnp.int32, (end - begin, tile), 1) + at
    seen = rows <= cols
    if half == 1:
        seen = seen & (seg_col[begin:end] == seg_row[:, at : at + tile])
    return seen


def place(parity, own_ref, other_ref, sets):
    sets[parity] = own_ref[...]
    sets[1 - parity] = other_ref[...]


def attend_kernel(
    tile, parity_ref, own_ref, other_ref, seg_row, seg_col, mine_ref, send_ref, lse_ref, sets, rows
):
    tokens = own_ref.shape[-1]
    heads = pl.num_programs(0)
    head = pl.program_id(0)
    parity = parity_ref[0]
    half_rows = own_ref.shape[0] - 2 * HEAD

    @pl.when(head == 0)
    def _():
        place(parity, own_ref, other_ref, sets)
        for half in range(2):
            keys = sets[half, half_rows : half_rows + HEAD, :]
            rows[half] = keys.astype(F32).T.astype(BF)

    at_head = pl.ds(pl.multiple_of(head * HEAD, 16), HEAD)
    for half in range(2):
        for at in range(0, tokens, tile):
            span = slice(at, at + tile)
            query = sets[half, at_head, span]
            pieces = pieces_of(half, at, tile, tokens)
            scores = []
            for which, begin, end, masked in pieces:
                part = dot(rows[which, begin:end, :], query)
                if masked:
                    part = jnp.where(
                        seen_of(half, at, begin, end, tile, seg_row, seg_col), part, NEG
                    )
                scores.append(part)
            peak = functools.reduce(
                jnp.maximum, [jnp.max(s, axis=0, keepdims=True) for s in scores]
            )
            total = out = None
            for (which, begin, end, _), part in zip(pieces, scores):
                weights = jnp.exp2(part - peak)
                mass = jnp.sum(weights, axis=0, keepdims=True)
                value = dot(sets[which, half_rows + HEAD :, begin:end], weights.astype(BF))
                total = mass if total is None else total + mass
                out = value if out is None else out + value
            out = (out / total).astype(BF)
            lse_ref[half, 0, :, span] = peak + jnp.log2(total)

            @pl.when(parity == half)
            def _():
                mine_ref[at_head, span] = out

            @pl.when(parity != half)
            def _():
                send_ref[at_head, span] = out


def attend(parity, own, other, seg):
    depth, tokens = own.shape
    half_rows = depth - 2 * HEAD
    heads = half_rows // HEAD
    tile = min(256, tokens)
    out = resident((half_rows, tokens))
    return pl.pallas_call(
        functools.partial(attend_kernel, tile),
        out_shape=(
            shape((half_rows, tokens), BF),
            shape((half_rows, tokens), BF),
            shape((2, heads, 1, tokens), F32),
        ),
        grid=(heads,),
        in_specs=[
            SMALL,
            resident((depth, tokens)),
            resident((depth, tokens)),
            resident((1, tokens)),
            resident((tokens, 1)),
        ],
        out_specs=(out, out, pl.BlockSpec((2, 1, 1, tokens), lambda h: (0, h, 0, 0))),
        scratch_shapes=[
            pltpu.VMEM((2, depth, tokens), BF),
            pltpu.VMEM((2, tokens, HEAD), BF),
        ],
        compiler_params=params(),
        name="attend",
    )(parity, own, other, seg[None, :], seg[:, None])


def attend_back_kernel(
    tile,
    parity_ref,
    own_ref,
    other_ref,
    own_out,
    other_out,
    own_grad,
    other_grad,
    lse_ref,
    seg_row,
    seg_col,
    mine_ref,
    send_ref,
    sets,
    outs,
    grads,
    rows,
    key_acc,
    value_acc,
):
    tokens = own_ref.shape[-1]
    heads = pl.num_programs(0)
    head = pl.program_id(0)
    parity = parity_ref[0]
    half_rows = own_ref.shape[0] - 2 * HEAD

    @pl.when(head == 0)
    def _():
        place(parity, own_ref, other_ref, sets)
        place(parity, own_out, other_out, outs)
        place(parity, own_grad, other_grad, grads)
        for half in range(2):
            for i in range(2):
                at = half_rows + i * HEAD
                rows[i, half] = sets[half, at : at + HEAD, :].astype(F32).T.astype(BF)
        key_acc[...] = jnp.zeros_like(key_acc)
        value_acc[...] = jnp.zeros_like(value_acc)

    at_head = pl.ds(pl.multiple_of(head * HEAD, 16), HEAD)
    for half in range(2):
        for at in range(0, tokens, tile):
            span = slice(at, at + tile)
            query = sets[half, at_head, span]
            grad = grads[half, at_head, span]
            lse = lse_ref[half, 0, :, span]
            delta = jnp.sum(
                grad.astype(F32) * outs[half, at_head, span].astype(F32), axis=0, keepdims=True
            )
            total = None
            for which, begin, end, masked in pieces_of(half, at, tile, tokens):
                part = dot(rows[0, which, begin:end, :], query)
                if masked:
                    part = jnp.where(
                        seen_of(half, at, begin, end, tile, seg_row, seg_col), part, NEG
                    )
                weights = jnp.exp2(part - lse)
                dprod = dot(rows[1, which, begin:end, :], grad)
                dscore = (weights * (dprod - delta)).astype(BF)
                value_acc[which, :, begin:end] += dot(grad, weights.astype(BF), NT)
                key_acc[which, :, begin:end] += dot(query, dscore, NT)
                more = dot(sets[which, half_rows : half_rows + HEAD, begin:end], dscore)
                total = more if total is None else total + more
            total = (total * ROOT).astype(BF)

            @pl.when(parity == half)
            def _():
                mine_ref[at_head, span] = total

            @pl.when(parity != half)
            def _():
                send_ref[at_head, span] = total

    @pl.when(head == heads - 1)
    def _():
        for ref, which in ((mine_ref, parity), (send_ref, 1 - parity)):
            ref[half_rows : half_rows + HEAD, :] = (key_acc[which] * LN2).astype(BF)
            ref[half_rows + HEAD :, :] = value_acc[which].astype(BF)


def attend_back(parity, own, other, own_out, other_out, own_grad, other_grad, lse, seg):
    depth, tokens = own.shape
    half_rows = depth - 2 * HEAD
    heads = half_rows // HEAD
    tile = min(256, tokens)
    full, part = resident((depth, tokens)), resident((half_rows, tokens))
    return pl.pallas_call(
        functools.partial(attend_back_kernel, tile),
        out_shape=(shape((depth, tokens), BF), shape((depth, tokens), BF)),
        grid=(heads,),
        in_specs=[
            SMALL,
            full,
            full,
            part,
            part,
            part,
            part,
            pl.BlockSpec((2, 1, 1, tokens), lambda h: (0, h, 0, 0)),
            resident((1, tokens)),
            resident((tokens, 1)),
        ],
        out_specs=(full, full),
        scratch_shapes=[
            pltpu.VMEM((2, depth, tokens), BF),
            pltpu.VMEM((2, half_rows, tokens), BF),
            pltpu.VMEM((2, half_rows, tokens), BF),
            pltpu.VMEM((2, 2, tokens, HEAD), BF),
            pltpu.VMEM((2, HEAD, tokens), F32),
            pltpu.VMEM((2, HEAD, tokens), F32),
        ],
        compiler_params=params(),
        name="attend_back",
    )(
        parity,
        own,
        other,
        own_out,
        other_out,
        own_grad,
        other_grad,
        lse,
        seg[None, :],
        seg[:, None],
    )


def halves_at(parity, half_rows):
    mine = pl.ds(pl.multiple_of(parity * half_rows, 16), half_rows)
    other = pl.ds(pl.multiple_of((1 - parity) * half_rows, 16), half_rows)
    return mine, other


def mix_out_kernel(count, parity_ref, own_ref, other_ref, *refs):
    weights, out_ref = refs[:count], refs[count]
    cols, _, piece, _ = out_ref.shape
    mine, other = halves_at(parity_ref[0], own_ref.shape[0])
    for k in range(count):
        part = dot(weights[k][mine, :], own_ref[...], TN)
        part = part + dot(weights[k][other, :], other_ref[...], TN)
        for c in range(cols):
            out_ref[c, k] = part[c * piece : (c + 1) * piece].astype(BF)


def mix_out(parity, own, other, weights, cols):
    count = len(weights)
    piece = weights[0].shape[1] // cols
    vmem = pl.BlockSpec(memory_space=pltpu.VMEM)
    return pl.pallas_call(
        functools.partial(mix_out_kernel, count),
        out_shape=shape((cols, count, piece, own.shape[1]), BF),
        in_specs=[SMALL] + [vmem] * (2 + count),
        compiler_params=params(),
        name="mix_out",
    )(parity, own, other, *weights)


def mix_back_kernel(count, parts, parity_ref, *refs):
    x_refs, weights = refs[:parts], refs[parts : parts + count]
    rows_ref, own_ref, other_ref = refs[parts + count :]
    for i, x_ref in enumerate(x_refs):
        cols, _, piece, tokens = x_ref.shape
        for c in range(cols):
            for k in range(count):
                rows_ref[k, c * piece : (c + 1) * piece, i * tokens : (i + 1) * tokens] = x_ref[
                    c, k
                ]
    mine, other = halves_at(parity_ref[0], own_ref.shape[0])
    for at, out_ref in ((other, other_ref), (mine, own_ref)):
        total = None
        for k in range(count):
            part = dot(weights[k][at, :], rows_ref[k])
            total = part if total is None else total + part
        out_ref[...] = total.astype(BF)


def mix_back(parity, x_parts, weights):
    parts = len(x_parts)
    cols, count, piece, tokens = x_parts[0].shape
    tokens = tokens * parts
    half_rows = weights[0].shape[0] // 2
    vmem = pl.BlockSpec(memory_space=pltpu.VMEM)
    return pl.pallas_call(
        functools.partial(mix_back_kernel, count, parts),
        out_shape=(
            shape((count, cols * piece, tokens), BF),
            shape((half_rows, tokens), BF),
            shape((half_rows, tokens), BF),
        ),
        in_specs=[SMALL] + [vmem] * (parts + count),
        compiler_params=params(),
        name="mix_back",
    )(parity, *x_parts, *weights)


def fan_kernel(count, x_ref, *refs):
    weights, out_ref = refs[:count], refs[count]
    cols, _, piece, _ = out_ref.shape
    for k in range(count):
        part = dot(weights[k][...], x_ref[...], TN)
        for c in range(cols):
            out_ref[c, k] = part[c * piece : (c + 1) * piece].astype(BF)


def fan_out(weights, x, cols):
    count = len(weights)
    piece = weights[0].shape[1] // cols
    return pl.pallas_call(
        functools.partial(fan_kernel, count),
        out_shape=shape((cols, count, piece, x.shape[1]), BF),
        compiler_params=params(),
        name="fan_out",
    )(x, *weights)


def norm_back(grads, k, x_ref, gain_ref, scale, coef, share_ref, gain_share_ref):
    cols, _, piece, _ = x_ref.shape
    for c in range(cols):
        grad = grads[c * piece : (c + 1) * piece]
        value = x_ref[c, k].astype(F32)
        gain_share_ref[c, k] = jnp.sum(grad * (value * scale), axis=1, keepdims=True)
        share_ref[c, k] = ((grad * gain_ref[c, k]) * scale - value * coef).astype(BF)


def ff_kernel(count, chained, x_ref, g_ref, gain_ref, *refs):
    gate_w, up_w, down_w = refs[:count], refs[count : 2 * count], refs[2 * count : 3 * count]
    refs = refs[3 * count + (5 if chained else 0) :]
    norm_ref, rows_ref, act_ref, dgate_ref, dup_ref, share_ref, gain_share_ref = refs[:7]
    scale_ref, inner_ref, back_ref = refs[7:]
    cols, _, piece, _ = x_ref.shape
    step = pl.program_id(0)

    @pl.when(step == 0)
    def _():
        normalise(x_ref, gain_ref, norm_ref, scale_ref)
        for c in range(cols):
            for k in range(count):
                rows_ref[k, c * piece : (c + 1) * piece, :] = g_ref[c, k]
        inner_ref[...] = jnp.zeros_like(inner_ref)
        back_ref[...] = jnp.zeros_like(back_ref)

    def summed(weights, ref):
        total = None
        for k in range(count):
            part = dot(weights[k][...], ref[k])
            total = part if total is None else total + part
        return total

    gate = summed(gate_w, norm_ref)
    up = summed(up_w, norm_ref)
    sigma = jax.nn.sigmoid(gate)
    silu = gate * sigma
    act_ref[...] = (silu * up).astype(BF)
    grad = summed(down_w, rows_ref)
    dup = grad * silu
    dgate = grad * up * (sigma + silu * (1.0 - sigma))
    inner_ref[...] += jnp.sum(dgate * gate + dup * up, axis=0, keepdims=True)
    dgate_ref[...] = dgate.astype(BF)
    dup_ref[...] = dup.astype(BF)
    for k in range(count):
        back_ref[k] += dot(gate_w[k][...], dgate_ref[...], TN) + dot(
            up_w[k][...], dup_ref[...], TN
        )

    @pl.when(step == pl.num_programs(0) - 1)
    def _():
        scale = scale_ref[...]
        coef = scale * scale * inner_ref[...] / D
        for k in range(count):
            norm_back(back_ref[k], k, x_ref, gain_ref, scale, coef, share_ref, gain_share_ref)


def feed_forward(x, g, part, parts, gain, gate_w, up_w, down_w, before):
    cols, count, piece, tokens = x.shape
    width, depth = gate_w[0].shape
    tile = 432 if width % 432 == 0 else width
    g_spec = pl.BlockSpec(x.shape, lambda n: (0, 0, 0, part), pipeline_mode=pl.Buffered(1))
    rows = (count, cols * piece, tokens)
    rows_spec = pl.BlockSpec(rows, lambda n: (0, 0, part), pipeline_mode=pl.Buffered(1))
    w_spec = pl.BlockSpec((tile, depth), lambda n: (n, 0))
    h_spec = pl.BlockSpec((tile, tokens), lambda n: (n, part))
    rows_all = shape((count, cols * piece, tokens * parts), BF)
    hidden = shape((width, tokens * parts), BF)
    first = 3 + 3 * count
    return pl.pallas_call(
        functools.partial(ff_kernel, count, bool(before)),
        out_shape=(
            rows_all,
            rows_all,
            hidden,
            hidden,
            hidden,
            shape(x.shape, BF),
            shape(gain.shape, F32),
        ),
        grid=(width // tile,),
        in_specs=[resident(x.shape, 1), g_spec, resident(gain.shape, 1)]
        + [w_spec] * (3 * count)
        + [RAW] * len(before),
        out_specs=(
            rows_spec,
            rows_spec,
            h_spec,
            h_spec,
            h_spec,
            resident(x.shape, 1),
            resident(gain.shape, 1),
        ),
        scratch_shapes=[
            pltpu.VMEM((1, tokens), F32),
            pltpu.VMEM((1, tokens), F32),
            pltpu.VMEM(rows, F32),
        ],
        input_output_aliases={first + i: i for i in range(len(before))},
        compiler_params=params(60),
        name="feed_forward",
    )(x, g, gain, *gate_w, *up_w, *down_w, *before)


def qkv_back_kernel(
    count,
    shared,
    parity_ref,
    x_ref,
    gain_ref,
    scale_ref,
    cos_ref,
    sin_ref,
    sets_ref,
    own_ref,
    other_ref,
    *refs,
):
    q_w, kv_w = refs[:count], refs[count : 2 * count]
    dq_ref, dkv_ref, share_ref, gain_share_ref = refs[2 * count :]
    parity = parity_ref[0]
    half_rows = own_ref.shape[0] - 2 * HEAD
    kv_half = dkv_ref.shape[0] // 2
    cosine, sine = cos_ref[...], -sin_ref[...]
    inner = None
    folded = None
    for grads, which in ((own_ref, parity), (other_ref, 1 - parity)):
        for at in range(0, half_rows + 2 * HEAD, HEAD):
            value = grads[at : at + HEAD, :].astype(F32)
            part = value * sets_ref[which, at : at + HEAD, :].astype(F32)
            part = jnp.sum(part, axis=0, keepdims=True)
            if at < half_rows:
                part = part * (1.0 / (ROOT * LOG2E))
                start = pl.multiple_of(which * half_rows + at, 16)
                dq_ref[pl.ds(start, HEAD), :] = turn(value, cosine, sine).astype(BF)
            else:
                is_key = at == half_rows
                raw = turn(value, cosine, sine) if is_key else value
                base = 0 if is_key else kv_half
                if not shared:
                    start = pl.multiple_of(base + which * HEAD, 16)
                    dkv_ref[pl.ds(start, HEAD), :] = raw.astype(BF)
                elif folded is None or at not in folded:
                    folded = {**(folded or {}), at: raw}
                else:
                    dkv_ref[base : base + HEAD, :] = (folded[at] + raw).astype(BF)
            inner = part if inner is None else inner + part
    scale = scale_ref[...]
    coef = scale * scale * inner / D
    for k in range(count):
        grads = dot(q_w[k][...], dq_ref[...]) + dot(kv_w[k][...], dkv_ref[...], TN)
        norm_back(grads, k, x_ref, gain_ref, scale, coef, share_ref, gain_share_ref)


def qkv_back(parity, x, gain, scale, cosine, sine, sets, own, other, q_w, kv_w):
    cols, count, piece, tokens = x.shape
    shared = kv_w[0].shape[0] == 2 * HEAD
    vmem = pl.BlockSpec(memory_space=pltpu.VMEM)
    return pl.pallas_call(
        functools.partial(qkv_back_kernel, count, shared),
        out_shape=(
            shape((q_w[0].shape[1], tokens), BF),
            shape((kv_w[0].shape[0], tokens), BF),
            shape(x.shape, BF),
            shape(gain.shape, F32),
        ),
        in_specs=[SMALL] + [vmem] * (8 + 2 * count),
        compiler_params=params(),
        name="qkv_back",
    )(parity, x, gain, scale, cosine, sine, sets, own, other, *q_w, *kv_w)


def rope_parts(positions):
    half = HEAD // 2
    freq = THETA ** (-jnp.arange(half, dtype=F32) * 2.0 / HEAD)
    angle = freq[:, None] * positions.astype(F32)[None, :]
    return (jnp.cos(angle), jnp.sin(angle))


def spread_cols(value):
    return lax.all_gather(value, "col", axis=0, tiled=False)


def sum_cols(value):
    return lax.psum_scatter(value, "col", scatter_dimension=0, tiled=False)


def over_dp(value):
    low = value.astype(BF)
    total = low.astype(F32)
    size = lax.axis_size("dp")
    for step in range(1, size):
        other = lax.ppermute(low, "dp", [(i, (i + step) % size) for i in range(size)])
        total = total + other.astype(F32)
    return total


def body(
    layer_input,
    attn_gain,
    mlp_gain,
    query_weight,
    key_weight,
    value_weight,
    mix_weight,
    gate_weight,
    up_weight,
    down_weight,
    output_grad,
    segment_ids,
    position_ids,
):
    rows = segment_ids.shape[0]
    count = lax.axis_size("row")
    cols = lax.axis_size("col")
    piece = layer_input.shape[1]
    row = lax.axis_index("row")
    parity = (row % 2).astype(jnp.int32)
    own_core = parity.reshape(1)
    q_half = query_weight.shape[1] // 2
    near, far = near_bits(count), far_bits(count)

    def row_tokens(value):
        turned = value.T
        outgoing = [
            lax.dynamic_slice(turned, (0, (row ^ k) * rows), (piece, rows)) for k in range(count)
        ]
        return jnp.stack(exchange_blocks(outgoing, "row"))

    def all_tokens(blocks):
        got = exchange_blocks([blocks[k] for k in range(count)], "row")
        result = jnp.zeros((piece, count * rows), blocks.dtype)
        for k in range(count):
            result = lax.dynamic_update_slice(result, got[k], (0, (row ^ k) * rows))
        return result.T

    def listed(blocks):
        return [blocks[k] for k in range(count)]

    source_own = row_tokens(layer_input)
    kv_weight = jnp.concatenate([key_weight.T, value_weight.T])
    q_first = spread({0: query_weight}, "row", far)
    kv_first = spread({0: kv_weight}, "row", far)
    mix_first = spread({0: mix_weight}, "row", far)
    gate_first = spread({0: gate_weight.T}, "row", far)
    up_first = spread({0: up_weight.T}, "row", far)
    down_first = spread({0: down_weight}, "row", far)
    q_blocks = spread(q_first, "row", near)
    kv_blocks = spread(kv_first, "row", near)

    gains = lax.all_gather(jnp.stack([attn_gain, mlp_gain]), ("row", "col"), axis=1, tiled=True)
    gains = gains.reshape(2, count, cols, piece)
    gains = by_xor(gains, row, 1).swapaxes(1, 2)[..., None]
    gain_one, gain_two = gains[0], gains[1]

    cosine, sine = rope_parts(position_ids)
    other_seg = swapped(segment_ids, "row", 1)
    seg = jnp.where(parity == 0, other_seg, segment_ids)

    source = spread_cols(source_own)
    source, q_blocks, kv_blocks, mix_first, gate_first, gain_one, cosine, sine, seg = together(
        source, q_blocks, kv_blocks, mix_first, gate_first, gain_one, cosine, sine, seg
    )
    grad_own = row_tokens(output_grad)
    grad_own, source = together(grad_own, source)
    grad_all = spread_cols(grad_own)
    norm_one, scale_one, sets = qkv_project(
        source, gain_one, cosine, sine, listed(q_blocks), listed(kv_blocks)
    )
    own_set = lax.dynamic_index_in_dim(sets, parity, 0, keepdims=False)
    other_set = swapped(lax.dynamic_index_in_dim(sets, 1 - parity, 0, keepdims=False), "row", 1)
    attn_mine, attn_send, lse = attend(own_core, own_set, other_set, seg)
    attn_other = swapped(attn_send, "row", 1)
    mix_blocks = spread(mix_first, "row", near)
    attn_mine, attn_other, mix_blocks, up_first = together(
        attn_mine, attn_other, mix_blocks, up_first
    )
    attn_part = mix_out(own_core, attn_mine, attn_other, listed(mix_blocks), cols)
    attn_part, grad_all = together(attn_part, grad_all)
    attn_sum = sum_cols(attn_part)
    gate_blocks = spread(gate_first, "row", near)
    up_blocks = spread(up_first, "row", near)
    down_blocks = spread(down_first, "row", near)
    attn_sum, gate_blocks, up_blocks, down_blocks = together(
        attn_sum, gate_blocks, up_blocks, down_blocks
    )
    residual_own = source_own.astype(F32) + attn_sum.astype(F32)

    parts = 2 if rows % 256 == 0 else 1
    size = rows // parts
    spans = [slice(i * size, (i + 1) * size) for i in range(parts)]
    residual_low = residual_own.astype(BF)
    residual = [spread_cols(residual_low[..., span]) for span in spans]
    before, shares = (), []
    gain_share_two = 0.0
    for i in range(parts):
        out = feed_forward(
            residual[i],
            grad_all,
            i,
            parts,
            gain_two,
            listed(gate_blocks),
            listed(up_blocks),
            listed(down_blocks),
            before,
        )
        before = out[:5]
        shares.append(out[5])
        gain_share_two = gain_share_two + out[6]
    norm_two, grad_rows, act, dgate, dup = before
    share_sums = [sum_cols(share) for share in shares]
    down_near = fold({k: dot(act, grad_rows[k], NT).astype(BF) for k in range(count)}, "row", near)
    dgate, dup, norm_two, down_near = together(dgate, dup, norm_two, down_near)
    down_far = fold(down_near, "row", far)[0]
    gate_near = {k: dot(dgate, norm_two[k], NT).astype(BF) for k in range(count)}
    gate_near = fold(gate_near, "row", near)
    up_near = {k: dot(dup, norm_two[k], NT).astype(BF) for k in range(count)}
    up_near = fold(up_near, "row", near)
    *share_sums, gate_near, up_near, down_far = together(
        *share_sums, gate_near, up_near, down_far
    )
    gate_far = fold(gate_near, "row", far)[0]
    up_near, gate_far = together(up_near, gate_far)
    up_far = fold(up_near, "row", far)[0]
    down_total = over_dp(down_far)
    gate_total = over_dp(gate_far)
    residual_grad_own = grad_own.astype(F32) + jnp.concatenate(share_sums, axis=2).astype(F32)

    mix_cols = spread_cols(residual_grad_own.astype(BF))
    ff_part = fan_out(listed(down_blocks), act, cols)
    mix_cols, ff_part, down_total = together(mix_cols, ff_part, down_total)
    mix_rows, grad_mine, grad_send = mix_back(own_core, [mix_cols], listed(mix_blocks))
    ff_sum = sum_cols(ff_part)
    grad_other = swapped(grad_send, "row", 1)
    back_mine, back_send = attend_back(
        own_core, own_set, other_set, attn_mine, attn_send, grad_mine, grad_other, lse, seg
    )
    back_other = swapped(back_send, "row", 1)
    back_other, gate_total = together(back_other, gate_total)
    up_total = over_dp(up_far)
    dq, dkv, share, gain_share_one = qkv_back(
        own_core,
        source,
        gain_one,
        scale_one,
        cosine,
        sine,
        sets,
        back_mine,
        back_other,
        listed(q_blocks),
        listed(kv_blocks),
    )
    share, attn_mine, mix_rows = together(share, attn_mine, mix_rows)
    attn_low = jnp.concatenate(
        [
            jnp.where(parity == 0, attn_mine, attn_other),
            jnp.where(parity == 0, attn_other, attn_mine),
        ]
    )
    mix_near = {k: dot(attn_low, mix_rows[k], NT).astype(BF) for k in range(count)}
    mix_near = fold(mix_near, "row", near)
    share, ff_sum, mix_near, up_total = together(share, ff_sum, mix_near, up_total)
    input_sum = sum_cols(share)

    share, dq, dkv = together(share, dq, dkv)
    mix_total = over_dp(fold(mix_near, "row", far)[0])
    q_near = fold({k: dot(norm_one[k], dq, NT).astype(BF) for k in range(count)}, "row", near)
    kv_near = fold({k: dot(dkv, norm_one[k], NT).astype(BF) for k in range(count)}, "row", near)
    ff_sum, gain_share_one, q_near, kv_near = together(ff_sum, gain_share_one, q_near, kv_near)
    q_total = over_dp(fold(q_near, "row", far)[0])
    kv_total = over_dp(fold(kv_near, "row", far)[0])
    output_own = (residual_own + ff_sum.astype(F32)).astype(BF)
    layer_output = all_tokens(output_own)

    bits = near + far[::-1]
    gain_shares = jnp.stack([gain_share_one[..., 0], gain_share_two[..., 0]], axis=2)
    gain_shares = by_xor(gain_shares, lax.axis_index("col"), 0)
    gain_shares = {c: gain_shares[c] for c in range(cols)}
    gain_shares = fold(gain_shares, "col", near_bits(cols) + far_bits(cols), low=False)[0]
    gain_shares = fold({k: gain_shares[k] for k in range(count)}, "row", bits, low=False)[0]
    gain_totals = over_dp(gain_shares)
    input_sum, q_total, kv_total, mix_total, gain_totals, layer_output = together(
        input_sum, q_total, kv_total, mix_total, gain_totals, layer_output
    )

    input_grad = all_tokens((residual_grad_own + input_sum.astype(F32)).astype(BF)).astype(F32)
    kv_rows = kv_total.shape[0] // 2
    return (
        layer_output,
        input_grad,
        gain_totals[0],
        gain_totals[1],
        q_total,
        kv_total[:kv_rows].T,
        kv_total[kv_rows:].T,
        mix_total,
        gate_total.T,
        up_total.T,
        down_total,
    )


def solution(mesh):
    return jax.shard_map(
        body,
        mesh=mesh,
        in_specs=(
            P("dp", ("row", "col")),
            P(("row", "col")),
            P(("row", "col")),
            P("row", "col"),
            P("row", "col"),
            P("row", "col"),
            P("col", "row"),
            P("row", "col"),
            P("row", "col"),
            P("col", "row"),
            P("dp", ("row", "col")),
            P(("dp", "row")),
            P(("dp", "row")),
        ),
        out_specs=(
            P("dp", ("row", "col")),
            P("dp", ("row", "col")),
            P(("row", "col")),
            P(("row", "col")),
            P("row", "col"),
            P("row", "col"),
            P("row", "col"),
            P("col", "row"),
            P("row", "col"),
            P("row", "col"),
            P("col", "row"),
        ),
        check_vma=False,
    )
```

```python
import functools

import jax
import jax.numpy as jnp
from jax import lax
from jax.experimental import pallas as pl
from jax.experimental.pallas import tpu as pltpu
from jax.sharding import PartitionSpec as P

D = 2560
HEAD = 80
EPS = 1e-05
THETA = 10000.0
NEG = -1e30
LOG2E = 1.4426950408889634
LN2 = 0.6931471805599453
ROOT = HEAD ** (-0.5)
BF = jnp.bfloat16
F32 = jnp.float32
NN = (((1,), (0,)), ((), ()))
TN = (((0,), (0,)), ((), ()))
NT = (((1,), (1,)), ((), ()))


def dot(left, right, dims=NN):
    return lax.dot_general(left, right, dims, preferred_element_type=F32)


def together(*values):
    return lax.optimization_barrier(values)


def swapped(value, axis, mask):
    size = lax.axis_size(axis)
    return lax.ppermute(value, axis, [(i, i ^ mask) for i in range(size)])


def spread(blocks, axis, bits):
    blocks = dict(blocks)
    for bit in bits:
        for k in list(blocks):
            blocks[k | bit] = swapped(blocks[k], axis, bit)
    return blocks


def fold(blocks, axis, bits, low=True):
    held = dict(blocks)
    for bit in bits:
        for k in [k for k in held if k & bit]:
            other = swapped(held.pop(k), axis, bit)
            total = held[k ^ bit].astype(F32) + other.astype(F32)
            held[k ^ bit] = total.astype(BF) if low else total
    return held


def fold_landed(held, moved, bit):
    return {
        k ^ bit: (held[k ^ bit].astype(F32) + other.astype(F32)).astype(BF)
        for k, other in moved.items()
    }


def far_bits(size):
    return [1 << i for i in range(1, size.bit_length() - 1)]


def near_bits(size):
    return [1] if size > 1 else []


def exchange_blocks(blocks, axis):
    return [blocks[0]] + [swapped(blocks[k], axis, k) for k in range(1, len(blocks))]


def by_xor(value, index, axis):
    parts = [
        lax.dynamic_index_in_dim(value, index ^ k, axis, keepdims=True)
        for k in range(value.shape[axis])
    ]
    return jnp.concatenate(parts, axis=axis)


def params(mib=58):
    return pltpu.CompilerParams(vmem_limit_bytes=mib * 1024 * 1024)


def takes(micros):
    return pl.CostEstimate(flops=int(micros * 1.0e9), transcendentals=0, bytes_accessed=0)


def shape(dims, dtype):
    return jax.ShapeDtypeStruct(dims, dtype)


SMALL = pl.BlockSpec(memory_space=pltpu.SMEM)
RAW = pl.BlockSpec(memory_space=pl.ANY)


def resident(dims, buffers=None):
    zeros = (0,) * len(dims)
    mode = {} if buffers is None else {"pipeline_mode": pl.Buffered(buffers)}
    return pl.BlockSpec(dims, lambda *_: zeros, **mode)


def normalise(x_ref, gain_ref, out_ref, scale_ref):
    cols, count, piece, _ = x_ref.shape
    total = None
    for c in range(cols):
        for k in range(count):
            value = x_ref[c, k].astype(F32)
            part = jnp.sum(value * value, axis=0, keepdims=True)
            total = part if total is None else total + part
    scale = lax.rsqrt(total / D + EPS)
    scale_ref[...] = scale
    for c in range(cols):
        for k in range(count):
            value = x_ref[c, k].astype(F32) * scale * gain_ref[c, k]
            out_ref[k, c * piece : (c + 1) * piece, :] = value.astype(BF)


def turn(value, cosine, sine):
    half = value.shape[0] // 2
    first, second = value[:half], value[half:]
    return jnp.concatenate([first * cosine - second * sine, second * cosine + first * sine])


def qkv_kernel(count, shared, x_ref, gain_ref, cos_ref, sin_ref, *refs):
    q_w, kv_w = refs[:count], refs[count : 2 * count]
    norm_ref, scale_ref, sets_ref = refs[2 * count :]
    normalise(x_ref, gain_ref, norm_ref, scale_ref)
    query = keyval = None
    for k in range(count):
        normed = norm_ref[k]
        part = dot(q_w[k][...], normed, TN)
        query = part if query is None else query + part
        part = dot(kv_w[k][...], normed)
        keyval = part if keyval is None else keyval + part
    cosine, sine = cos_ref[...], sin_ref[...]
    half = query.shape[0] // 2
    kv_half = keyval.shape[0] // 2
    for h in range(2):
        for at in range(0, half, HEAD):
            value = turn(query[h * half + at : h * half + at + HEAD], cosine, sine)
            sets_ref[h, at : at + HEAD, :] = (value * (ROOT * LOG2E)).astype(BF)
        at = 0 if shared else h * HEAD
        key = turn(keyval[at : at + HEAD], cosine, sine)
        sets_ref[h, half : half + HEAD, :] = key.astype(BF)
        sets_ref[h, half + HEAD : half + 2 * HEAD, :] = keyval[
            kv_half + at : kv_half + at + HEAD
        ].astype(BF)


def qkv_project(x, gain, cosine, sine, q_w, kv_w):
    cols, count, piece, tokens = x.shape
    half = q_w[0].shape[1] // 2
    shared = kv_w[0].shape[0] == 2 * HEAD
    return pl.pallas_call(
        functools.partial(qkv_kernel, count, shared),
        out_shape=(
            shape((count, cols * piece, tokens), BF),
            shape((1, tokens), F32),
            shape((2, half + 2 * HEAD, tokens), BF),
        ),
        compiler_params=params(),
        name="qkv_project",
        cost_estimate=takes(12),
    )(x, gain, cosine, sine, *q_w, *kv_w)


def pieces_of(half, at, tile, tokens):
    if half == 1:
        return [(0, 0, tokens, False), (1, 0, at + tile, True)]
    head = [(0, 0, at, False)] if at else []
    return head + [(0, at, at + tile, True)]


def seen_of(half, at, begin, end, tile, seg_row, seg_col):
    rows = lax.broadcasted_iota(jnp.int32, (end - begin, tile), 0) + begin
    cols = lax.broadcasted_iota(jnp.int32, (end - begin, tile), 1) + at
    seen = rows <= cols
    if half == 1:
        seen = seen & (seg_col[begin:end] == seg_row[:, at : at + tile])
    return seen


def place(parity, own_ref, other_ref, sets):
    sets[parity] = own_ref[...]
    sets[1 - parity] = other_ref[...]


def attend_kernel(
    tile, parity_ref, own_ref, other_ref, seg_row, seg_col, mine_ref, send_ref, lse_ref, sets, rows
):
    tokens = own_ref.shape[-1]
    heads = pl.num_programs(0)
    head = pl.program_id(0)
    parity = parity_ref[0]
    half_rows = own_ref.shape[0] - 2 * HEAD

    @pl.when(head == 0)
    def _():
        place(parity, own_ref, other_ref, sets)
        for half in range(2):
            keys = sets[half, half_rows : half_rows + HEAD, :]
            rows[half] = keys.astype(F32).T.astype(BF)

    at_head = pl.ds(pl.multiple_of(head * HEAD, 16), HEAD)
    for half in range(2):
        for at in range(0, tokens, tile):
            span = slice(at, at + tile)
            query = sets[half, at_head, span]
            pieces = pieces_of(half, at, tile, tokens)
            scores = []
            for which, begin, end, masked in pieces:
                part = dot(rows[which, begin:end, :], query)
                if masked:
                    part = jnp.where(
                        seen_of(half, at, begin, end, tile, seg_row, seg_col), part, NEG
                    )
                scores.append(part)
            peak = functools.reduce(
                jnp.maximum, [jnp.max(s, axis=0, keepdims=True) for s in scores]
            )
            total = out = None
            for (which, begin, end, _), part in zip(pieces, scores):
                weights = jnp.exp2(part - peak)
                mass = jnp.sum(weights, axis=0, keepdims=True)
                value = dot(sets[which, half_rows + HEAD :, begin:end], weights.astype(BF))
                total = mass if total is None else total + mass
                out = value if out is None else out + value
            out = (out / total).astype(BF)
            lse_ref[half, 0, :, span] = peak + jnp.log2(total)

            @pl.when(parity == half)
            def _():
                mine_ref[at_head, span] = out

            @pl.when(parity != half)
            def _():
                send_ref[at_head, span] = out


def attend(parity, own, other, seg):
    depth, tokens = own.shape
    half_rows = depth - 2 * HEAD
    heads = half_rows // HEAD
    tile = min(256, tokens)
    out = resident((half_rows, tokens))
    return pl.pallas_call(
        functools.partial(attend_kernel, tile),
        out_shape=(
            shape((half_rows, tokens), BF),
            shape((half_rows, tokens), BF),
            shape((2, heads, 1, tokens), F32),
        ),
        grid=(heads,),
        in_specs=[
            SMALL,
            resident((depth, tokens)),
            resident((depth, tokens)),
            resident((1, tokens)),
            resident((tokens, 1)),
        ],
        out_specs=(out, out, pl.BlockSpec((2, 1, 1, tokens), lambda h: (0, h, 0, 0))),
        scratch_shapes=[
            pltpu.VMEM((2, depth, tokens), BF),
            pltpu.VMEM((2, tokens, HEAD), BF),
        ],
        compiler_params=params(),
        name="attend",
        cost_estimate=takes(27),
    )(parity, own, other, seg[None, :], seg[:, None])


def attend_back_kernel(
    tile,
    parity_ref,
    own_ref,
    other_ref,
    own_out,
    other_out,
    own_grad,
    other_grad,
    lse_ref,
    seg_row,
    seg_col,
    mine_ref,
    send_ref,
    sets,
    outs,
    grads,
    rows,
    key_acc,
    value_acc,
):
    tokens = own_ref.shape[-1]
    heads = pl.num_programs(0)
    head = pl.program_id(0)
    parity = parity_ref[0]
    half_rows = own_ref.shape[0] - 2 * HEAD

    @pl.when(head == 0)
    def _():
        place(parity, own_ref, other_ref, sets)
        place(parity, own_out, other_out, outs)
        place(parity, own_grad, other_grad, grads)
        for half in range(2):
            for i in range(2):
                at = half_rows + i * HEAD
                rows[i, half] = sets[half, at : at + HEAD, :].astype(F32).T.astype(BF)
        key_acc[...] = jnp.zeros_like(key_acc)
        value_acc[...] = jnp.zeros_like(value_acc)

    at_head = pl.ds(pl.multiple_of(head * HEAD, 16), HEAD)
    for half in range(2):
        for at in range(0, tokens, tile):
            span = slice(at, at + tile)
            query = sets[half, at_head, span]
            grad = grads[half, at_head, span]
            lse = lse_ref[half, 0, :, span]
            delta = jnp.sum(
                grad.astype(F32) * outs[half, at_head, span].astype(F32), axis=0, keepdims=True
            )
            total = None
            for which, begin, end, masked in pieces_of(half, at, tile, tokens):
                part = dot(rows[0, which, begin:end, :], query)
                if masked:
                    part = jnp.where(
                        seen_of(half, at, begin, end, tile, seg_row, seg_col), part, NEG
                    )
                weights = jnp.exp2(part - lse)
                dprod = dot(rows[1, which, begin:end, :], grad)
                dscore = (weights * (dprod - delta)).astype(BF)
                value_acc[which, :, begin:end] += dot(grad, weights.astype(BF), NT)
                key_acc[which, :, begin:end] += dot(query, dscore, NT)
                more = dot(sets[which, half_rows : half_rows + HEAD, begin:end], dscore)
                total = more if total is None else total + more
            total = (total * ROOT).astype(BF)

            @pl.when(parity == half)
            def _():
                mine_ref[at_head, span] = total

            @pl.when(parity != half)
            def _():
                send_ref[at_head, span] = total

    @pl.when(head == heads - 1)
    def _():
        for ref, which in ((mine_ref, parity), (send_ref, 1 - parity)):
            ref[half_rows : half_rows + HEAD, :] = (key_acc[which] * LN2).astype(BF)
            ref[half_rows + HEAD :, :] = value_acc[which].astype(BF)


def attend_back(parity, own, other, own_out, other_out, own_grad, other_grad, lse, seg):
    depth, tokens = own.shape
    half_rows = depth - 2 * HEAD
    heads = half_rows // HEAD
    tile = min(256, tokens)
    full, part = resident((depth, tokens)), resident((half_rows, tokens))
    return pl.pallas_call(
        functools.partial(attend_back_kernel, tile),
        out_shape=(shape((depth, tokens), BF), shape((depth, tokens), BF)),
        grid=(heads,),
        in_specs=[
            SMALL,
            full,
            full,
            part,
            part,
            part,
            part,
            pl.BlockSpec((2, 1, 1, tokens), lambda h: (0, h, 0, 0)),
            resident((1, tokens)),
            resident((tokens, 1)),
        ],
        out_specs=(full, full),
        scratch_shapes=[
            pltpu.VMEM((2, depth, tokens), BF),
            pltpu.VMEM((2, half_rows, tokens), BF),
            pltpu.VMEM((2, half_rows, tokens), BF),
            pltpu.VMEM((2, 2, tokens, HEAD), BF),
            pltpu.VMEM((2, HEAD, tokens), F32),
            pltpu.VMEM((2, HEAD, tokens), F32),
        ],
        compiler_params=params(),
        name="attend_back",
        cost_estimate=takes(37),
    )(
        parity,
        own,
        other,
        own_out,
        other_out,
        own_grad,
        other_grad,
        lse,
        seg[None, :],
        seg[:, None],
    )


def halves_at(parity, half_rows):
    mine = pl.ds(pl.multiple_of(parity * half_rows, 16), half_rows)
    other = pl.ds(pl.multiple_of((1 - parity) * half_rows, 16), half_rows)
    return mine, other


def mix_out_kernel(count, parity_ref, own_ref, other_ref, *refs):
    weights, out_ref = refs[:count], refs[count]
    cols, _, piece, _ = out_ref.shape
    mine, other = halves_at(parity_ref[0], own_ref.shape[0])
    for k in range(count):
        part = dot(weights[k][mine, :], own_ref[...], TN)
        part = part + dot(weights[k][other, :], other_ref[...], TN)
        for c in range(cols):
            out_ref[c, k] = part[c * piece : (c + 1) * piece].astype(BF)


def mix_out(parity, own, other, weights, cols):
    count = len(weights)
    piece = weights[0].shape[1] // cols
    vmem = pl.BlockSpec(memory_space=pltpu.VMEM)
    return pl.pallas_call(
        functools.partial(mix_out_kernel, count),
        out_shape=shape((cols, count, piece, own.shape[1]), BF),
        in_specs=[SMALL] + [vmem] * (2 + count),
        compiler_params=params(),
        name="mix_out",
        cost_estimate=takes(10),
    )(parity, own, other, *weights)


def mix_back_kernel(count, parts, parity_ref, *refs):
    x_refs, weights = refs[:parts], refs[parts : parts + count]
    rows_ref, own_ref, other_ref = refs[parts + count :]
    for i, x_ref in enumerate(x_refs):
        cols, _, piece, tokens = x_ref.shape
        for c in range(cols):
            for k in range(count):
                rows_ref[k, c * piece : (c + 1) * piece, i * tokens : (i + 1) * tokens] = x_ref[
                    c, k
                ]
    mine, other = halves_at(parity_ref[0], own_ref.shape[0])
    for at, out_ref in ((other, other_ref), (mine, own_ref)):
        total = None
        for k in range(count):
            part = dot(weights[k][at, :], rows_ref[k])
            total = part if total is None else total + part
        out_ref[...] = total.astype(BF)


def mix_back(parity, x_parts, weights):
    parts = len(x_parts)
    cols, count, piece, tokens = x_parts[0].shape
    tokens = tokens * parts
    half_rows = weights[0].shape[0] // 2
    vmem = pl.BlockSpec(memory_space=pltpu.VMEM)
    return pl.pallas_call(
        functools.partial(mix_back_kernel, count, parts),
        out_shape=(
            shape((count, cols * piece, tokens), BF),
            shape((half_rows, tokens), BF),
            shape((half_rows, tokens), BF),
        ),
        in_specs=[SMALL] + [vmem] * (parts + count),
        compiler_params=params(),
        name="mix_back",
        cost_estimate=takes(9),
    )(parity, *x_parts, *weights)


def fan_kernel(count, x_ref, *refs):
    weights, out_ref = refs[:count], refs[count]
    cols, _, piece, _ = out_ref.shape
    for k in range(count):
        part = dot(weights[k][...], x_ref[...], TN)
        for c in range(cols):
            out_ref[c, k] = part[c * piece : (c + 1) * piece].astype(BF)


def fan_out(weights, x, cols):
    count = len(weights)
    piece = weights[0].shape[1] // cols
    return pl.pallas_call(
        functools.partial(fan_kernel, count),
        out_shape=shape((cols, count, piece, x.shape[1]), BF),
        compiler_params=params(),
        name="fan_out",
        cost_estimate=takes(17),
    )(x, *weights)


def norm_back(grads, k, x_ref, gain_ref, scale, coef, share_ref, gain_share_ref):
    cols, _, piece, _ = x_ref.shape
    for c in range(cols):
        grad = grads[c * piece : (c + 1) * piece]
        value = x_ref[c, k].astype(F32)
        gain_share_ref[c, k] = jnp.sum(grad * (value * scale), axis=1, keepdims=True)
        share_ref[c, k] = ((grad * gain_ref[c, k]) * scale - value * coef).astype(BF)


def ff_kernel(count, chained, x_ref, g_ref, gain_ref, *refs):
    gate_w, up_w, down_w = refs[:count], refs[count : 2 * count], refs[2 * count : 3 * count]
    refs = refs[3 * count + (5 if chained else 0) :]
    norm_ref, rows_ref, act_ref, dgate_ref, dup_ref, share_ref, gain_share_ref = refs[:7]
    scale_ref, inner_ref, back_ref = refs[7:]
    cols, _, piece, _ = x_ref.shape
    step = pl.program_id(0)

    @pl.when(step == 0)
    def _():
        normalise(x_ref, gain_ref, norm_ref, scale_ref)
        for c in range(cols):
            for k in range(count):
                rows_ref[k, c * piece : (c + 1) * piece, :] = g_ref[c, k]
        inner_ref[...] = jnp.zeros_like(inner_ref)
        back_ref[...] = jnp.zeros_like(back_ref)

    def summed(weights, ref):
        total = None
        for k in range(count):
            part = dot(weights[k][...], ref[k])
            total = part if total is None else total + part
        return total

    gate = summed(gate_w, norm_ref)
    up = summed(up_w, norm_ref)
    sigma = jax.nn.sigmoid(gate)
    silu = gate * sigma
    act_ref[...] = (silu * up).astype(BF)
    grad = summed(down_w, rows_ref)
    dup = grad * silu
    dgate = grad * up * (sigma + silu * (1.0 - sigma))
    inner_ref[...] += jnp.sum(dgate * gate + dup * up, axis=0, keepdims=True)
    dgate_ref[...] = dgate.astype(BF)
    dup_ref[...] = dup.astype(BF)
    for k in range(count):
        back_ref[k] += dot(gate_w[k][...], dgate_ref[...], TN) + dot(
            up_w[k][...], dup_ref[...], TN
        )

    @pl.when(step == pl.num_programs(0) - 1)
    def _():
        scale = scale_ref[...]
        coef = scale * scale * inner_ref[...] / D
        for k in range(count):
            norm_back(back_ref[k], k, x_ref, gain_ref, scale, coef, share_ref, gain_share_ref)


def feed_forward(x, g, part, parts, gain, gate_w, up_w, down_w, before):
    cols, count, piece, tokens = x.shape
    width, depth = gate_w[0].shape
    tile = 432 if width % 432 == 0 else width
    g_spec = pl.BlockSpec(x.shape, lambda n: (0, 0, 0, part), pipeline_mode=pl.Buffered(1))
    rows = (count, cols * piece, tokens)
    rows_spec = pl.BlockSpec(rows, lambda n: (0, 0, part), pipeline_mode=pl.Buffered(1))
    w_spec = pl.BlockSpec((tile, depth), lambda n: (n, 0))
    h_spec = pl.BlockSpec((tile, tokens), lambda n: (n, part))
    rows_all = shape((count, cols * piece, tokens * parts), BF)
    hidden = shape((width, tokens * parts), BF)
    first = 3 + 3 * count
    return pl.pallas_call(
        functools.partial(ff_kernel, count, bool(before)),
        out_shape=(
            rows_all,
            rows_all,
            hidden,
            hidden,
            hidden,
            shape(x.shape, BF),
            shape(gain.shape, F32),
        ),
        grid=(width // tile,),
        in_specs=[resident(x.shape, 1), g_spec, resident(gain.shape, 1)]
        + [w_spec] * (3 * count)
        + [RAW] * len(before),
        out_specs=(
            rows_spec,
            rows_spec,
            h_spec,
            h_spec,
            h_spec,
            resident(x.shape, 1),
            resident(gain.shape, 1),
        ),
        scratch_shapes=[
            pltpu.VMEM((1, tokens), F32),
            pltpu.VMEM((1, tokens), F32),
            pltpu.VMEM(rows, F32),
        ],
        input_output_aliases={first + i: i for i in range(len(before))},
        compiler_params=params(60),
        name="feed_forward",
        cost_estimate=takes(42),
    )(x, g, gain, *gate_w, *up_w, *down_w, *before)


def qkv_back_kernel(
    count,
    shared,
    parity_ref,
    x_ref,
    gain_ref,
    scale_ref,
    cos_ref,
    sin_ref,
    sets_ref,
    own_ref,
    other_ref,
    *refs,
):
    q_w, kv_w = refs[:count], refs[count : 2 * count]
    dq_ref, dkv_ref, share_ref, gain_share_ref = refs[2 * count :]
    parity = parity_ref[0]
    half_rows = own_ref.shape[0] - 2 * HEAD
    kv_half = dkv_ref.shape[0] // 2
    cosine, sine = cos_ref[...], -sin_ref[...]
    inner = None
    folded = None
    for grads, which in ((own_ref, parity), (other_ref, 1 - parity)):
        for at in range(0, half_rows + 2 * HEAD, HEAD):
            value = grads[at : at + HEAD, :].astype(F32)
            part = value * sets_ref[which, at : at + HEAD, :].astype(F32)
            part = jnp.sum(part, axis=0, keepdims=True)
            if at < half_rows:
                part = part * (1.0 / (ROOT * LOG2E))
                start = pl.multiple_of(which * half_rows + at, 16)
                dq_ref[pl.ds(start, HEAD), :] = turn(value, cosine, sine).astype(BF)
            else:
                is_key = at == half_rows
                raw = turn(value, cosine, sine) if is_key else value
                base = 0 if is_key else kv_half
                if not shared:
                    start = pl.multiple_of(base + which * HEAD, 16)
                    dkv_ref[pl.ds(start, HEAD), :] = raw.astype(BF)
                elif folded is None or at not in folded:
                    folded = {**(folded or {}), at: raw}
                else:
                    dkv_ref[base : base + HEAD, :] = (folded[at] + raw).astype(BF)
            inner = part if inner is None else inner + part
    scale = scale_ref[...]
    coef = scale * scale * inner / D
    for k in range(count):
        grads = dot(q_w[k][...], dq_ref[...]) + dot(kv_w[k][...], dkv_ref[...], TN)
        norm_back(grads, k, x_ref, gain_ref, scale, coef, share_ref, gain_share_ref)


def qkv_back(parity, x, gain, scale, cosine, sine, sets, own, other, q_w, kv_w):
    cols, count, piece, tokens = x.shape
    shared = kv_w[0].shape[0] == 2 * HEAD
    vmem = pl.BlockSpec(memory_space=pltpu.VMEM)
    return pl.pallas_call(
        functools.partial(qkv_back_kernel, count, shared),
        out_shape=(
            shape((q_w[0].shape[1], tokens), BF),
            shape((kv_w[0].shape[0], tokens), BF),
            shape(x.shape, BF),
            shape(gain.shape, F32),
        ),
        in_specs=[SMALL] + [vmem] * (8 + 2 * count),
        compiler_params=params(),
        name="qkv_back",
        cost_estimate=takes(17),
    )(parity, x, gain, scale, cosine, sine, sets, own, other, *q_w, *kv_w)


def rope_parts(positions):
    half = HEAD // 2
    freq = THETA ** (-jnp.arange(half, dtype=F32) * 2.0 / HEAD)
    angle = freq[:, None] * positions.astype(F32)[None, :]
    return (jnp.cos(angle), jnp.sin(angle))


def spread_cols(value):
    return lax.all_gather(value, "col", axis=0, tiled=False)


def sum_cols(value):
    return lax.psum_scatter(value, "col", scatter_dimension=0, tiled=False)


def over_dp(value):
    low = value.astype(BF)
    total = low.astype(F32)
    size = lax.axis_size("dp")
    for step in range(1, size):
        other = lax.ppermute(low, "dp", [(i, (i + step) % size) for i in range(size)])
        total = total + other.astype(F32)
    return total


def body(
    layer_input,
    attn_gain,
    mlp_gain,
    query_weight,
    key_weight,
    value_weight,
    mix_weight,
    gate_weight,
    up_weight,
    down_weight,
    output_grad,
    segment_ids,
    position_ids,
):
    rows = segment_ids.shape[0]
    count = lax.axis_size("row")
    cols = lax.axis_size("col")
    piece = layer_input.shape[1]
    row = lax.axis_index("row")
    parity = (row % 2).astype(jnp.int32)
    own_core = parity.reshape(1)
    q_half = query_weight.shape[1] // 2
    near, far = near_bits(count), far_bits(count)
    far_mask = far[-1]

    def row_tokens(value):
        turned = value.T
        outgoing = [
            lax.dynamic_slice(turned, (0, (row ^ k) * rows), (piece, rows)) for k in range(count)
        ]
        return jnp.stack(exchange_blocks(outgoing, "row"))

    def all_tokens(blocks):
        got = exchange_blocks([blocks[k] for k in range(count)], "row")
        result = jnp.zeros((piece, count * rows), blocks.dtype)
        for k in range(count):
            result = lax.dynamic_update_slice(result, got[k], (0, (row ^ k) * rows))
        return result.T

    def listed(blocks):
        return [blocks[k] for k in range(count)]

    source_own = row_tokens(layer_input)
    kv_weight = jnp.concatenate([key_weight.T, value_weight.T])
    q_first = spread({0: query_weight}, "row", far)
    kv_first = spread({0: kv_weight}, "row", far)
    mix_first = spread({0: mix_weight}, "row", far)
    gate_first = spread({0: gate_weight.T}, "row", far)
    up_first = spread({0: up_weight.T}, "row", far)
    down_first = spread({0: down_weight}, "row", far)
    q_blocks = spread(q_first, "row", near)
    kv_blocks = spread(kv_first, "row", near)

    gains = lax.all_gather(jnp.stack([attn_gain, mlp_gain]), ("row", "col"), axis=1, tiled=True)
    gains = gains.reshape(2, count, cols, piece)
    gains = by_xor(gains, row, 1).swapaxes(1, 2)[..., None]
    gain_one, gain_two = gains[0], gains[1]

    cosine, sine = rope_parts(position_ids)
    other_seg = swapped(segment_ids, "row", 1)
    seg = jnp.where(parity == 0, other_seg, segment_ids)

    source = spread_cols(source_own)
    source, q_blocks, kv_blocks, mix_first, gate_first, gain_one, cosine, sine, seg = together(
        source, q_blocks, kv_blocks, mix_first, gate_first, gain_one, cosine, sine, seg
    )
    grad_own = row_tokens(output_grad)
    grad_own, source = together(grad_own, source)
    grad_all = spread_cols(grad_own)
    norm_one, scale_one, sets = qkv_project(
        source, gain_one, cosine, sine, listed(q_blocks), listed(kv_blocks)
    )
    own_set = lax.dynamic_index_in_dim(sets, parity, 0, keepdims=False)
    other_set = swapped(lax.dynamic_index_in_dim(sets, 1 - parity, 0, keepdims=False), "row", 1)
    attn_mine, attn_send, lse = attend(own_core, own_set, other_set, seg)
    attn_other = swapped(attn_send, "row", 1)
    mix_blocks = spread(mix_first, "row", near)
    attn_mine, attn_other, mix_blocks, up_first = together(
        attn_mine, attn_other, mix_blocks, up_first
    )
    attn_part = mix_out(own_core, attn_mine, attn_other, listed(mix_blocks), cols)
    attn_part, grad_all = together(attn_part, grad_all)
    attn_sum = sum_cols(attn_part)
    gate_blocks = spread(gate_first, "row", near)
    up_blocks = spread(up_first, "row", near)
    down_blocks = spread(down_first, "row", near)
    attn_sum, gate_blocks, up_blocks, down_blocks = together(
        attn_sum, gate_blocks, up_blocks, down_blocks
    )
    residual_own = source_own.astype(F32) + attn_sum.astype(F32)

    parts = 2 if rows % 256 == 0 else 1
    size = rows // parts
    spans = [slice(i * size, (i + 1) * size) for i in range(parts)]
    residual_low = residual_own.astype(BF)
    residual = [spread_cols(residual_low[..., span]) for span in spans]
    before, shares = (), []
    gain_share_two = 0.0
    for i in range(parts):
        out = feed_forward(
            residual[i],
            grad_all,
            i,
            parts,
            gain_two,
            listed(gate_blocks),
            listed(up_blocks),
            listed(down_blocks),
            before,
        )
        before = out[:5]
        shares.append(out[5])
        gain_share_two = gain_share_two + out[6]
    norm_two, grad_rows, act, dgate, dup = before
    share_sums = [sum_cols(share) for share in shares]
    down_near = fold({k: dot(act, grad_rows[k], NT).astype(BF) for k in range(count)}, "row", near)
    dgate, dup, norm_two, down_near = together(dgate, dup, norm_two, down_near)
    gate_near = {k: dot(dgate, norm_two[k], NT).astype(BF) for k in range(count)}
    gate_near = fold(gate_near, "row", near)
    up_near = {k: dot(dup, norm_two[k], NT).astype(BF) for k in range(count)}
    up_near = fold(up_near, "row", near)
    cut = act.shape[0] // 2
    down_head = {k: v[:cut] for k, v in down_near.items()}
    down_tail = {k: v[cut:] for k, v in down_near.items()}
    head_moved = {k: swapped(down_head[k], "row", far_mask) for k in down_head if k & far_mask}
    *share_sums, gate_near, up_near, down_head, down_tail, head_moved = together(
        *share_sums, gate_near, up_near, down_head, down_tail, head_moved
    )
    down_head = fold_landed(down_head, head_moved, far_mask)
    down_head = fold(down_head, "row", far[::-1][1:])[0]
    down_tail = fold(down_tail, "row", far[::-1])[0]
    down_tail, up_near = together(down_tail, up_near)
    down_far = jnp.concatenate([down_head, down_tail])
    residual_grad_own = grad_own.astype(F32) + jnp.concatenate(share_sums, axis=2).astype(F32)
    gate_far = fold(gate_near, "row", far)[0]
    up_moved = {k: swapped(up_near[k], "row", far_mask) for k in up_near if k & far_mask}
    down_total = over_dp(down_far)

    mix_cols = spread_cols(residual_grad_own.astype(BF))
    ff_part = fan_out(listed(down_blocks), act, cols)
    mix_cols, ff_part, down_total = together(mix_cols, ff_part, down_total)
    gate_total = over_dp(gate_far)
    mix_rows, grad_mine, grad_send = mix_back(own_core, [mix_cols], listed(mix_blocks))
    ff_sum = sum_cols(ff_part)
    grad_other = swapped(grad_send, "row", 1)
    grad_mine, up_moved, up_near = together(grad_mine, up_moved, up_near)
    up_far = fold_landed(up_near, up_moved, far_mask)
    grad_other, gate_total, up_far = together(grad_other, gate_total, up_far)
    up_total = over_dp(fold(up_far, "row", far[::-1][1:])[0])
    back_mine, back_send = attend_back(
        own_core, own_set, other_set, attn_mine, attn_send, grad_mine, grad_other, lse, seg
    )
    back_other = swapped(back_send, "row", 1)
    back_other, up_total = together(back_other, up_total)
    dq, dkv, share, gain_share_one = qkv_back(
        own_core,
        source,
        gain_one,
        scale_one,
        cosine,
        sine,
        sets,
        back_mine,
        back_other,
        listed(q_blocks),
        listed(kv_blocks),
    )
    share, attn_mine, mix_rows = together(share, attn_mine, mix_rows)
    attn_low = jnp.concatenate(
        [
            jnp.where(parity == 0, attn_mine, attn_other),
            jnp.where(parity == 0, attn_other, attn_mine),
        ]
    )
    mix_near = {k: dot(attn_low, mix_rows[k], NT).astype(BF) for k in range(count)}
    mix_near = fold(mix_near, "row", near)
    share, ff_sum, mix_near = together(share, ff_sum, mix_near)
    input_sum = sum_cols(share)

    share, dq, dkv = together(share, dq, dkv)
    mix_total = over_dp(fold(mix_near, "row", far)[0])
    q_near = fold({k: dot(norm_one[k], dq, NT).astype(BF) for k in range(count)}, "row", near)
    kv_near = fold({k: dot(dkv, norm_one[k], NT).astype(BF) for k in range(count)}, "row", near)
    ff_sum, gain_share_one, q_near, kv_near = together(ff_sum, gain_share_one, q_near, kv_near)
    q_total = over_dp(fold(q_near, "row", far)[0])
    kv_total = over_dp(fold(kv_near, "row", far)[0])
    output_own = (residual_own + ff_sum.astype(F32)).astype(BF)
    layer_output = all_tokens(output_own)

    bits = near + far[::-1]
    gain_shares = jnp.stack([gain_share_one[..., 0], gain_share_two[..., 0]], axis=2)
    gain_shares = by_xor(gain_shares, lax.axis_index("col"), 0)
    gain_shares = {c: gain_shares[c] for c in range(cols)}
    gain_shares = fold(gain_shares, "col", near_bits(cols) + far_bits(cols), low=False)[0]
    gain_shares = fold({k: gain_shares[k] for k in range(count)}, "row", bits, low=False)[0]
    gain_totals = over_dp(gain_shares)
    input_sum, q_total, kv_total, mix_total, gain_totals, layer_output = together(
        input_sum, q_total, kv_total, mix_total, gain_totals, layer_output
    )

    input_grad = all_tokens((residual_grad_own + input_sum.astype(F32)).astype(BF)).astype(F32)
    kv_rows = kv_total.shape[0] // 2
    return (
        layer_output,
        input_grad,
        gain_totals[0],
        gain_totals[1],
        q_total,
        kv_total[:kv_rows].T,
        kv_total[kv_rows:].T,
        mix_total,
        gate_total.T,
        up_total.T,
        down_total,
    )


def solution(mesh):
    return jax.shard_map(
        body,
        mesh=mesh,
        in_specs=(
            P("dp", ("row", "col")),
            P(("row", "col")),
            P(("row", "col")),
            P("row", "col"),
            P("row", "col"),
            P("row", "col"),
            P("col", "row"),
            P("row", "col"),
            P("row", "col"),
            P("col", "row"),
            P("dp", ("row", "col")),
            P(("dp", "row")),
            P(("dp", "row")),
        ),
        out_specs=(
            P("dp", ("row", "col")),
            P("dp", ("row", "col")),
            P(("row", "col")),
            P(("row", "col")),
            P("row", "col"),
            P("row", "col"),
            P("row", "col"),
            P("col", "row"),
            P("row", "col"),
            P("row", "col"),
            P("col", "row"),
        ),
        check_vma=False,
    )
```

```python
import functools

import jax
import jax.numpy as jnp
from jax import lax
from jax.experimental import pallas as pl
from jax.experimental.pallas import tpu as pltpu
from jax.sharding import PartitionSpec as P

D = 2560
HEAD = 80
EPS = 1e-05
THETA = 10000.0
NEG = -1e30
LOG2E = 1.4426950408889634
LN2 = 0.6931471805599453
ROOT = HEAD ** (-0.5)
BF = jnp.bfloat16
F32 = jnp.float32
NN = (((1,), (0,)), ((), ()))
TN = (((0,), (0,)), ((), ()))
NT = (((1,), (1,)), ((), ()))


def dot(left, right, dims=NN):
    return lax.dot_general(left, right, dims, preferred_element_type=F32)


def together(*values):
    return lax.optimization_barrier(values)


def swapped(value, axis, mask):
    size = lax.axis_size(axis)
    return lax.ppermute(value, axis, [(i, i ^ mask) for i in range(size)])


def spread(blocks, axis, bits):
    blocks = dict(blocks)
    for bit in bits:
        for k in list(blocks):
            blocks[k | bit] = swapped(blocks[k], axis, bit)
    return blocks


def fold(blocks, axis, bits, low=True):
    held = dict(blocks)
    for bit in bits:
        for k in [k for k in held if k & bit]:
            other = swapped(held.pop(k), axis, bit)
            total = held[k ^ bit].astype(F32) + other.astype(F32)
            held[k ^ bit] = total.astype(BF) if low else total
    return held


def far_bits(size):
    return [1 << i for i in range(1, size.bit_length() - 1)]


def near_bits(size):
    return [1] if size > 1 else []


def exchange_blocks(blocks, axis):
    return [blocks[0]] + [swapped(blocks[k], axis, k) for k in range(1, len(blocks))]


def by_xor(value, index, axis):
    parts = [
        lax.dynamic_index_in_dim(value, index ^ k, axis, keepdims=True)
        for k in range(value.shape[axis])
    ]
    return jnp.concatenate(parts, axis=axis)


def params(mib=58):
    return pltpu.CompilerParams(vmem_limit_bytes=mib * 1024 * 1024)


def takes(micros):
    return pl.CostEstimate(flops=int(micros * 0.1e9), transcendentals=0, bytes_accessed=0)


def shape(dims, dtype):
    return jax.ShapeDtypeStruct(dims, dtype)


SMALL = pl.BlockSpec(memory_space=pltpu.SMEM)
RAW = pl.BlockSpec(memory_space=pl.ANY)


def resident(dims, buffers=None):
    zeros = (0,) * len(dims)
    mode = {} if buffers is None else {"pipeline_mode": pl.Buffered(buffers)}
    return pl.BlockSpec(dims, lambda *_: zeros, **mode)


def normalise(x_ref, gain_ref, out_ref, scale_ref):
    cols, count, piece, _ = x_ref.shape
    total = None
    for c in range(cols):
        for k in range(count):
            value = x_ref[c, k].astype(F32)
            part = jnp.sum(value * value, axis=0, keepdims=True)
            total = part if total is None else total + part
    scale = lax.rsqrt(total / D + EPS)
    scale_ref[...] = scale
    for c in range(cols):
        for k in range(count):
            value = x_ref[c, k].astype(F32) * scale * gain_ref[c, k]
            out_ref[k, c * piece : (c + 1) * piece, :] = value.astype(BF)


def turn(value, cosine, sine):
    half = value.shape[0] // 2
    first, second = value[:half], value[half:]
    return jnp.concatenate([first * cosine - second * sine, second * cosine + first * sine])


def qkv_kernel(count, shared, x_ref, gain_ref, cos_ref, sin_ref, *refs):
    q_w, kv_w = refs[:count], refs[count : 2 * count]
    norm_ref, scale_ref, sets_ref = refs[2 * count :]
    normalise(x_ref, gain_ref, norm_ref, scale_ref)
    query = keyval = None
    for k in range(count):
        normed = norm_ref[k]
        part = dot(q_w[k][...], normed, TN)
        query = part if query is None else query + part
        part = dot(kv_w[k][...], normed)
        keyval = part if keyval is None else keyval + part
    cosine, sine = cos_ref[...], sin_ref[...]
    half = query.shape[0] // 2
    kv_half = keyval.shape[0] // 2
    for h in range(2):
        for at in range(0, half, HEAD):
            value = turn(query[h * half + at : h * half + at + HEAD], cosine, sine)
            sets_ref[h, at : at + HEAD, :] = (value * (ROOT * LOG2E)).astype(BF)
        at = 0 if shared else h * HEAD
        key = turn(keyval[at : at + HEAD], cosine, sine)
        sets_ref[h, half : half + HEAD, :] = key.astype(BF)
        sets_ref[h, half + HEAD : half + 2 * HEAD, :] = keyval[
            kv_half + at : kv_half + at + HEAD
        ].astype(BF)


def qkv_project(x, gain, cosine, sine, q_w, kv_w):
    cols, count, piece, tokens = x.shape
    half = q_w[0].shape[1] // 2
    shared = kv_w[0].shape[0] == 2 * HEAD
    return pl.pallas_call(
        functools.partial(qkv_kernel, count, shared),
        out_shape=(
            shape((count, cols * piece, tokens), BF),
            shape((1, tokens), F32),
            shape((2, half + 2 * HEAD, tokens), BF),
        ),
        compiler_params=params(),
        name="qkv_project",
        cost_estimate=takes(12),
    )(x, gain, cosine, sine, *q_w, *kv_w)


def pieces_of(half, at, tile, tokens):
    if half == 1:
        return [(0, 0, tokens, False), (1, 0, at + tile, True)]
    head = [(0, 0, at, False)] if at else []
    return head + [(0, at, at + tile, True)]


def seen_of(half, at, begin, end, tile, seg_row, seg_col):
    rows = lax.broadcasted_iota(jnp.int32, (end - begin, tile), 0) + begin
    cols = lax.broadcasted_iota(jnp.int32, (end - begin, tile), 1) + at
    seen = rows <= cols
    if half == 1:
        seen = seen & (seg_col[begin:end] == seg_row[:, at : at + tile])
    return seen


def place(parity, own_ref, other_ref, sets):
    sets[parity] = own_ref[...]
    sets[1 - parity] = other_ref[...]


def attend_kernel(
    tile, parity_ref, own_ref, other_ref, seg_row, seg_col, mine_ref, send_ref, lse_ref, sets, rows
):
    tokens = own_ref.shape[-1]
    heads = pl.num_programs(0)
    head = pl.program_id(0)
    parity = parity_ref[0]
    half_rows = own_ref.shape[0] - 2 * HEAD

    @pl.when(head == 0)
    def _():
        place(parity, own_ref, other_ref, sets)
        for half in range(2):
            keys = sets[half, half_rows : half_rows + HEAD, :]
            rows[half] = keys.astype(F32).T.astype(BF)

    at_head = pl.ds(pl.multiple_of(head * HEAD, 16), HEAD)
    for half in range(2):
        for at in range(0, tokens, tile):
            span = slice(at, at + tile)
            query = sets[half, at_head, span]
            pieces = pieces_of(half, at, tile, tokens)
            scores = []
            for which, begin, end, masked in pieces:
                part = dot(rows[which, begin:end, :], query)
                if masked:
                    part = jnp.where(
                        seen_of(half, at, begin, end, tile, seg_row, seg_col), part, NEG
                    )
                scores.append(part)
            peak = functools.reduce(
                jnp.maximum, [jnp.max(s, axis=0, keepdims=True) for s in scores]
            )
            total = out = None
            for (which, begin, end, _), part in zip(pieces, scores):
                weights = jnp.exp2(part - peak)
                mass = jnp.sum(weights, axis=0, keepdims=True)
                value = dot(sets[which, half_rows + HEAD :, begin:end], weights.astype(BF))
                total = mass if total is None else total + mass
                out = value if out is None else out + value
            out = (out / total).astype(BF)
            lse_ref[half, 0, :, span] = peak + jnp.log2(total)

            @pl.when(parity == half)
            def _():
                mine_ref[at_head, span] = out

            @pl.when(parity != half)
            def _():
                send_ref[at_head, span] = out


def attend(parity, own, other, seg):
    depth, tokens = own.shape
    half_rows = depth - 2 * HEAD
    heads = half_rows // HEAD
    tile = min(256, tokens)
    out = resident((half_rows, tokens))
    return pl.pallas_call(
        functools.partial(attend_kernel, tile),
        out_shape=(
            shape((half_rows, tokens), BF),
            shape((half_rows, tokens), BF),
            shape((2, heads, 1, tokens), F32),
        ),
        grid=(heads,),
        in_specs=[
            SMALL,
            resident((depth, tokens)),
            resident((depth, tokens)),
            resident((1, tokens)),
            resident((tokens, 1)),
        ],
        out_specs=(out, out, pl.BlockSpec((2, 1, 1, tokens), lambda h: (0, h, 0, 0))),
        scratch_shapes=[
            pltpu.VMEM((2, depth, tokens), BF),
            pltpu.VMEM((2, tokens, HEAD), BF),
        ],
        compiler_params=params(),
        name="attend",
        cost_estimate=takes(27),
    )(parity, own, other, seg[None, :], seg[:, None])


def attend_back_kernel(
    tile,
    parity_ref,
    own_ref,
    other_ref,
    own_out,
    other_out,
    own_grad,
    other_grad,
    lse_ref,
    seg_row,
    seg_col,
    mine_ref,
    send_ref,
    sets,
    outs,
    grads,
    rows,
    key_acc,
    value_acc,
):
    tokens = own_ref.shape[-1]
    heads = pl.num_programs(0)
    head = pl.program_id(0)
    parity = parity_ref[0]
    half_rows = own_ref.shape[0] - 2 * HEAD

    @pl.when(head == 0)
    def _():
        place(parity, own_ref, other_ref, sets)
        place(parity, own_out, other_out, outs)
        place(parity, own_grad, other_grad, grads)
        for half in range(2):
            for i in range(2):
                at = half_rows + i * HEAD
                rows[i, half] = sets[half, at : at + HEAD, :].astype(F32).T.astype(BF)
        key_acc[...] = jnp.zeros_like(key_acc)
        value_acc[...] = jnp.zeros_like(value_acc)

    at_head = pl.ds(pl.multiple_of(head * HEAD, 16), HEAD)
    for half in range(2):
        for at in range(0, tokens, tile):
            span = slice(at, at + tile)
            query = sets[half, at_head, span]
            grad = grads[half, at_head, span]
            lse = lse_ref[half, 0, :, span]
            delta = jnp.sum(
                grad.astype(F32) * outs[half, at_head, span].astype(F32), axis=0, keepdims=True
            )
            total = None
            for which, begin, end, masked in pieces_of(half, at, tile, tokens):
                part = dot(rows[0, which, begin:end, :], query)
                if masked:
                    part = jnp.where(
                        seen_of(half, at, begin, end, tile, seg_row, seg_col), part, NEG
                    )
                weights = jnp.exp2(part - lse)
                dprod = dot(rows[1, which, begin:end, :], grad)
                dscore = (weights * (dprod - delta)).astype(BF)
                value_acc[which, :, begin:end] += dot(grad, weights.astype(BF), NT)
                key_acc[which, :, begin:end] += dot(query, dscore, NT)
                more = dot(sets[which, half_rows : half_rows + HEAD, begin:end], dscore)
                total = more if total is None else total + more
            total = (total * ROOT).astype(BF)

            @pl.when(parity == half)
            def _():
                mine_ref[at_head, span] = total

            @pl.when(parity != half)
            def _():
                send_ref[at_head, span] = total

    @pl.when(head == heads - 1)
    def _():
        for ref, which in ((mine_ref, parity), (send_ref, 1 - parity)):
            ref[half_rows : half_rows + HEAD, :] = (key_acc[which] * LN2).astype(BF)
            ref[half_rows + HEAD :, :] = value_acc[which].astype(BF)


def attend_back(parity, own, other, own_out, other_out, own_grad, other_grad, lse, seg):
    depth, tokens = own.shape
    half_rows = depth - 2 * HEAD
    heads = half_rows // HEAD
    tile = min(256, tokens)
    full, part = resident((depth, tokens)), resident((half_rows, tokens))
    return pl.pallas_call(
        functools.partial(attend_back_kernel, tile),
        out_shape=(shape((depth, tokens), BF), shape((depth, tokens), BF)),
        grid=(heads,),
        in_specs=[
            SMALL,
            full,
            full,
            part,
            part,
            part,
            part,
            pl.BlockSpec((2, 1, 1, tokens), lambda h: (0, h, 0, 0)),
            resident((1, tokens)),
            resident((tokens, 1)),
        ],
        out_specs=(full, full),
        scratch_shapes=[
            pltpu.VMEM((2, depth, tokens), BF),
            pltpu.VMEM((2, half_rows, tokens), BF),
            pltpu.VMEM((2, half_rows, tokens), BF),
            pltpu.VMEM((2, 2, tokens, HEAD), BF),
            pltpu.VMEM((2, HEAD, tokens), F32),
            pltpu.VMEM((2, HEAD, tokens), F32),
        ],
        compiler_params=params(),
        name="attend_back",
        cost_estimate=takes(37),
    )(
        parity,
        own,
        other,
        own_out,
        other_out,
        own_grad,
        other_grad,
        lse,
        seg[None, :],
        seg[:, None],
    )


def halves_at(parity, half_rows):
    mine = pl.ds(pl.multiple_of(parity * half_rows, 16), half_rows)
    other = pl.ds(pl.multiple_of((1 - parity) * half_rows, 16), half_rows)
    return mine, other


def mix_out_kernel(count, parity_ref, own_ref, other_ref, *refs):
    weights, out_ref = refs[:count], refs[count]
    cols, _, piece, _ = out_ref.shape
    mine, other = halves_at(parity_ref[0], own_ref.shape[0])
    for k in range(count):
        part = dot(weights[k][mine, :], own_ref[...], TN)
        part = part + dot(weights[k][other, :], other_ref[...], TN)
        for c in range(cols):
            out_ref[c, k] = part[c * piece : (c + 1) * piece].astype(BF)


def mix_out(parity, own, other, weights, cols):
    count = len(weights)
    piece = weights[0].shape[1] // cols
    vmem = pl.BlockSpec(memory_space=pltpu.VMEM)
    return pl.pallas_call(
        functools.partial(mix_out_kernel, count),
        out_shape=shape((cols, count, piece, own.shape[1]), BF),
        in_specs=[SMALL] + [vmem] * (2 + count),
        compiler_params=params(),
        name="mix_out",
        cost_estimate=takes(10),
    )(parity, own, other, *weights)


def mix_back_kernel(count, parts, parity_ref, *refs):
    x_refs, weights = refs[:parts], refs[parts : parts + count]
    rows_ref, own_ref, other_ref = refs[parts + count :]
    for i, x_ref in enumerate(x_refs):
        cols, _, piece, tokens = x_ref.shape
        for c in range(cols):
            for k in range(count):
                rows_ref[k, c * piece : (c + 1) * piece, i * tokens : (i + 1) * tokens] = x_ref[
                    c, k
                ]
    mine, other = halves_at(parity_ref[0], own_ref.shape[0])
    for at, out_ref in ((other, other_ref), (mine, own_ref)):
        total = None
        for k in range(count):
            part = dot(weights[k][at, :], rows_ref[k])
            total = part if total is None else total + part
        out_ref[...] = total.astype(BF)


def mix_back(parity, x_parts, weights):
    parts = len(x_parts)
    cols, count, piece, tokens = x_parts[0].shape
    tokens = tokens * parts
    half_rows = weights[0].shape[0] // 2
    vmem = pl.BlockSpec(memory_space=pltpu.VMEM)
    return pl.pallas_call(
        functools.partial(mix_back_kernel, count, parts),
        out_shape=(
            shape((count, cols * piece, tokens), BF),
            shape((half_rows, tokens), BF),
            shape((half_rows, tokens), BF),
        ),
        in_specs=[SMALL] + [vmem] * (parts + count),
        compiler_params=params(),
        name="mix_back",
        cost_estimate=takes(9),
    )(parity, *x_parts, *weights)


def fan_kernel(count, x_ref, *refs):
    weights, out_ref = refs[:count], refs[count]
    cols, _, piece, _ = out_ref.shape
    for k in range(count):
        part = dot(weights[k][...], x_ref[...], TN)
        for c in range(cols):
            out_ref[c, k] = part[c * piece : (c + 1) * piece].astype(BF)


def fan_out(weights, x, cols):
    count = len(weights)
    piece = weights[0].shape[1] // cols
    return pl.pallas_call(
        functools.partial(fan_kernel, count),
        out_shape=shape((cols, count, piece, x.shape[1]), BF),
        compiler_params=params(),
        name="fan_out",
        cost_estimate=takes(17),
    )(x, *weights)


def norm_back(grads, k, x_ref, gain_ref, scale, coef, share_ref, gain_share_ref):
    cols, _, piece, _ = x_ref.shape
    for c in range(cols):
        grad = grads[c * piece : (c + 1) * piece]
        value = x_ref[c, k].astype(F32)
        gain_share_ref[c, k] = jnp.sum(grad * (value * scale), axis=1, keepdims=True)
        share_ref[c, k] = ((grad * gain_ref[c, k]) * scale - value * coef).astype(BF)


def ff_kernel(count, chained, x_ref, g_ref, gain_ref, *refs):
    gate_w, up_w, down_w = refs[:count], refs[count : 2 * count], refs[2 * count : 3 * count]
    refs = refs[3 * count + (5 if chained else 0) :]
    norm_ref, rows_ref, act_ref, dgate_ref, dup_ref, share_ref, gain_share_ref = refs[:7]
    scale_ref, inner_ref, back_ref = refs[7:]
    cols, _, piece, _ = x_ref.shape
    step = pl.program_id(0)

    @pl.when(step == 0)
    def _():
        normalise(x_ref, gain_ref, norm_ref, scale_ref)
        for c in range(cols):
            for k in range(count):
                rows_ref[k, c * piece : (c + 1) * piece, :] = g_ref[c, k]
        inner_ref[...] = jnp.zeros_like(inner_ref)
        back_ref[...] = jnp.zeros_like(back_ref)

    def summed(weights, ref):
        total = None
        for k in range(count):
            part = dot(weights[k][...], ref[k])
            total = part if total is None else total + part
        return total

    gate = summed(gate_w, norm_ref)
    up = summed(up_w, norm_ref)
    sigma = jax.nn.sigmoid(gate)
    silu = gate * sigma
    act_ref[...] = (silu * up).astype(BF)
    grad = summed(down_w, rows_ref)
    dup = grad * silu
    dgate = grad * up * (sigma + silu * (1.0 - sigma))
    inner_ref[...] += jnp.sum(dgate * gate + dup * up, axis=0, keepdims=True)
    dgate_ref[...] = dgate.astype(BF)
    dup_ref[...] = dup.astype(BF)
    for k in range(count):
        back_ref[k] += dot(gate_w[k][...], dgate_ref[...], TN) + dot(
            up_w[k][...], dup_ref[...], TN
        )

    @pl.when(step == pl.num_programs(0) - 1)
    def _():
        scale = scale_ref[...]
        coef = scale * scale * inner_ref[...] / D
        for k in range(count):
            norm_back(back_ref[k], k, x_ref, gain_ref, scale, coef, share_ref, gain_share_ref)


def feed_forward(x, g, part, parts, gain, gate_w, up_w, down_w, before):
    cols, count, piece, tokens = x.shape
    width, depth = gate_w[0].shape
    tile = 432 if width % 432 == 0 else width
    g_spec = pl.BlockSpec(x.shape, lambda n: (0, 0, 0, part), pipeline_mode=pl.Buffered(1))
    rows = (count, cols * piece, tokens)
    rows_spec = pl.BlockSpec(rows, lambda n: (0, 0, part), pipeline_mode=pl.Buffered(1))
    w_spec = pl.BlockSpec((tile, depth), lambda n: (n, 0))
    h_spec = pl.BlockSpec((tile, tokens), lambda n: (n, part))
    rows_all = shape((count, cols * piece, tokens * parts), BF)
    hidden = shape((width, tokens * parts), BF)
    first = 3 + 3 * count
    return pl.pallas_call(
        functools.partial(ff_kernel, count, bool(before)),
        out_shape=(
            rows_all,
            rows_all,
            hidden,
            hidden,
            hidden,
            shape(x.shape, BF),
            shape(gain.shape, F32),
        ),
        grid=(width // tile,),
        in_specs=[resident(x.shape, 1), g_spec, resident(gain.shape, 1)]
        + [w_spec] * (3 * count)
        + [RAW] * len(before),
        out_specs=(
            rows_spec,
            rows_spec,
            h_spec,
            h_spec,
            h_spec,
            resident(x.shape, 1),
            resident(gain.shape, 1),
        ),
        scratch_shapes=[
            pltpu.VMEM((1, tokens), F32),
            pltpu.VMEM((1, tokens), F32),
            pltpu.VMEM(rows, F32),
        ],
        input_output_aliases={first + i: i for i in range(len(before))},
        compiler_params=params(60),
        name="feed_forward",
        cost_estimate=takes(42),
    )(x, g, gain, *gate_w, *up_w, *down_w, *before)


def qkv_back_kernel(
    count,
    shared,
    parity_ref,
    x_ref,
    gain_ref,
    scale_ref,
    cos_ref,
    sin_ref,
    sets_ref,
    own_ref,
    other_ref,
    *refs,
):
    q_w, kv_w = refs[:count], refs[count : 2 * count]
    dq_ref, dkv_ref, share_ref, gain_share_ref = refs[2 * count :]
    parity = parity_ref[0]
    half_rows = own_ref.shape[0] - 2 * HEAD
    kv_half = dkv_ref.shape[0] // 2
    cosine, sine = cos_ref[...], -sin_ref[...]
    inner = None
    folded = None
    for grads, which in ((own_ref, parity), (other_ref, 1 - parity)):
        for at in range(0, half_rows + 2 * HEAD, HEAD):
            value = grads[at : at + HEAD, :].astype(F32)
            part = value * sets_ref[which, at : at + HEAD, :].astype(F32)
            part = jnp.sum(part, axis=0, keepdims=True)
            if at < half_rows:
                part = part * (1.0 / (ROOT * LOG2E))
                start = pl.multiple_of(which * half_rows + at, 16)
                dq_ref[pl.ds(start, HEAD), :] = turn(value, cosine, sine).astype(BF)
            else:
                is_key = at == half_rows
                raw = turn(value, cosine, sine) if is_key else value
                base = 0 if is_key else kv_half
                if not shared:
                    start = pl.multiple_of(base + which * HEAD, 16)
                    dkv_ref[pl.ds(start, HEAD), :] = raw.astype(BF)
                elif folded is None or at not in folded:
                    folded = {**(folded or {}), at: raw}
                else:
                    dkv_ref[base : base + HEAD, :] = (folded[at] + raw).astype(BF)
            inner = part if inner is None else inner + part
    scale = scale_ref[...]
    coef = scale * scale * inner / D
    for k in range(count):
        grads = dot(q_w[k][...], dq_ref[...]) + dot(kv_w[k][...], dkv_ref[...], TN)
        norm_back(grads, k, x_ref, gain_ref, scale, coef, share_ref, gain_share_ref)


def qkv_back(parity, x, gain, scale, cosine, sine, sets, own, other, q_w, kv_w):
    cols, count, piece, tokens = x.shape
    shared = kv_w[0].shape[0] == 2 * HEAD
    vmem = pl.BlockSpec(memory_space=pltpu.VMEM)
    return pl.pallas_call(
        functools.partial(qkv_back_kernel, count, shared),
        out_shape=(
            shape((q_w[0].shape[1], tokens), BF),
            shape((kv_w[0].shape[0], tokens), BF),
            shape(x.shape, BF),
            shape(gain.shape, F32),
        ),
        in_specs=[SMALL] + [vmem] * (8 + 2 * count),
        compiler_params=params(),
        name="qkv_back",
        cost_estimate=takes(17),
    )(parity, x, gain, scale, cosine, sine, sets, own, other, *q_w, *kv_w)


def rope_parts(positions):
    half = HEAD // 2
    freq = THETA ** (-jnp.arange(half, dtype=F32) * 2.0 / HEAD)
    angle = freq[:, None] * positions.astype(F32)[None, :]
    return (jnp.cos(angle), jnp.sin(angle))


def spread_cols(value):
    return lax.all_gather(value, "col", axis=0, tiled=False)


def sum_cols(value):
    return lax.psum_scatter(value, "col", scatter_dimension=0, tiled=False)


def over_dp(value):
    low = value.astype(BF)
    total = low.astype(F32)
    size = lax.axis_size("dp")
    for step in range(1, size):
        other = lax.ppermute(low, "dp", [(i, (i + step) % size) for i in range(size)])
        total = total + other.astype(F32)
    return total


def body(
    layer_input,
    attn_gain,
    mlp_gain,
    query_weight,
    key_weight,
    value_weight,
    mix_weight,
    gate_weight,
    up_weight,
    down_weight,
    output_grad,
    segment_ids,
    position_ids,
):
    rows = segment_ids.shape[0]
    count = lax.axis_size("row")
    cols = lax.axis_size("col")
    piece = layer_input.shape[1]
    row = lax.axis_index("row")
    parity = (row % 2).astype(jnp.int32)
    own_core = parity.reshape(1)
    q_half = query_weight.shape[1] // 2
    near, far = near_bits(count), far_bits(count)

    def row_tokens(value):
        turned = value.T
        outgoing = [
            lax.dynamic_slice(turned, (0, (row ^ k) * rows), (piece, rows)) for k in range(count)
        ]
        return jnp.stack(exchange_blocks(outgoing, "row"))

    def all_tokens(blocks):
        got = exchange_blocks([blocks[k] for k in range(count)], "row")
        result = jnp.zeros((piece, count * rows), blocks.dtype)
        for k in range(count):
            result = lax.dynamic_update_slice(result, got[k], (0, (row ^ k) * rows))
        return result.T

    def listed(blocks):
        return [blocks[k] for k in range(count)]

    source_own = row_tokens(layer_input)
    kv_weight = jnp.concatenate([key_weight.T, value_weight.T])
    q_first = spread({0: query_weight}, "row", far)
    kv_first = spread({0: kv_weight}, "row", far)
    mix_first = spread({0: mix_weight}, "row", far)
    gate_first = spread({0: gate_weight.T}, "row", far)
    up_first = spread({0: up_weight.T}, "row", far)
    down_first = spread({0: down_weight}, "row", far)
    q_blocks = spread(q_first, "row", near)
    kv_blocks = spread(kv_first, "row", near)

    gains = lax.all_gather(jnp.stack([attn_gain, mlp_gain]), ("row", "col"), axis=1, tiled=True)
    gains = gains.reshape(2, count, cols, piece)
    gains = by_xor(gains, row, 1).swapaxes(1, 2)[..., None]
    gain_one, gain_two = gains[0], gains[1]

    cosine, sine = rope_parts(position_ids)
    other_seg = swapped(segment_ids, "row", 1)
    seg = jnp.where(parity == 0, other_seg, segment_ids)

    source = spread_cols(source_own)
    source, q_blocks, kv_blocks, mix_first, gate_first, gain_one, cosine, sine, seg = together(
        source, q_blocks, kv_blocks, mix_first, gate_first, gain_one, cosine, sine, seg
    )
    grad_own = row_tokens(output_grad)
    grad_own, source = together(grad_own, source)
    grad_all = spread_cols(grad_own)
    norm_one, scale_one, sets = qkv_project(
        source, gain_one, cosine, sine, listed(q_blocks), listed(kv_blocks)
    )
    own_set = lax.dynamic_index_in_dim(sets, parity, 0, keepdims=False)
    other_set = swapped(lax.dynamic_index_in_dim(sets, 1 - parity, 0, keepdims=False), "row", 1)
    attn_mine, attn_send, lse = attend(own_core, own_set, other_set, seg)
    attn_other = swapped(attn_send, "row", 1)
    mix_blocks = spread(mix_first, "row", near)
    attn_mine, attn_other, mix_blocks, up_first = together(
        attn_mine, attn_other, mix_blocks, up_first
    )
    attn_part = mix_out(own_core, attn_mine, attn_other, listed(mix_blocks), cols)
    attn_part, grad_all = together(attn_part, grad_all)
    attn_sum = sum_cols(attn_part)
    gate_blocks = spread(gate_first, "row", near)
    up_blocks = spread(up_first, "row", near)
    down_blocks = spread(down_first, "row", near)
    attn_sum, gate_blocks, up_blocks, down_blocks = together(
        attn_sum, gate_blocks, up_blocks, down_blocks
    )
    residual_own = source_own.astype(F32) + attn_sum.astype(F32)

    parts = 2 if rows % 256 == 0 else 1
    size = rows // parts
    spans = [slice(i * size, (i + 1) * size) for i in range(parts)]
    residual_low = residual_own.astype(BF)
    residual = [spread_cols(residual_low[..., span]) for span in spans]
    before, shares = (), []
    gain_share_two = 0.0
    for i in range(parts):
        out = feed_forward(
            residual[i],
            grad_all,
            i,
            parts,
            gain_two,
            listed(gate_blocks),
            listed(up_blocks),
            listed(down_blocks),
            before,
        )
        before = out[:5]
        shares.append(out[5])
        gain_share_two = gain_share_two + out[6]
    norm_two, grad_rows, act, dgate, dup = before
    share_sums = [sum_cols(share) for share in shares]
    down_grads = {k: dot(act, grad_rows[k], NT).astype(BF) for k in range(count)}
    gate_grads = {k: dot(dgate, norm_two[k], NT).astype(BF) for k in range(count)}
    up_grads = {k: dot(dup, norm_two[k], NT).astype(BF) for k in range(count)}
    down_grads = fold(down_grads, "row", near)
    gate_grads = fold(gate_grads, "row", near)
    up_grads = fold(up_grads, "row", near)
    *share_sums, down_grads, gate_grads, up_grads = together(
        *share_sums, down_grads, gate_grads, up_grads
    )
    residual_grad_own = grad_own.astype(F32) + jnp.concatenate(share_sums, axis=2).astype(F32)
    down_total = fold(down_grads, "row", far)[0]
    gate_total = fold(gate_grads, "row", far)[0]

    mix_cols = spread_cols(residual_grad_own.astype(BF))
    ff_part = fan_out(listed(down_blocks), act, cols)
    down_total = over_dp(down_total)
    mix_cols, ff_part, down_total, gate_total, up_grads = together(
        mix_cols, ff_part, down_total, gate_total, up_grads
    )
    up_total = fold(up_grads, "row", far)[0]
    gate_total = over_dp(gate_total)
    mix_rows, grad_mine, grad_send = mix_back(own_core, [mix_cols], listed(mix_blocks))
    ff_sum = sum_cols(ff_part)
    grad_other = swapped(grad_send, "row", 1)
    back_mine, back_send = attend_back(
        own_core, own_set, other_set, attn_mine, attn_send, grad_mine, grad_other, lse, seg
    )
    back_other = swapped(back_send, "row", 1)
    back_other, up_total, gate_total, down_total = together(
        back_other, up_total, gate_total, down_total
    )
    cut = up_total.shape[0] * 5 // 9 // 16 * 16
    up_head, up_tail = over_dp(up_total[:cut]), over_dp(up_total[cut:])
    dq, dkv, share, gain_share_one = qkv_back(
        own_core,
        source,
        gain_one,
        scale_one,
        cosine,
        sine,
        sets,
        back_mine,
        back_other,
        listed(q_blocks),
        listed(kv_blocks),
    )
    share, attn_mine, mix_rows, up_head = together(share, attn_mine, mix_rows, up_head)
    attn_low = jnp.concatenate(
        [
            jnp.where(parity == 0, attn_mine, attn_other),
            jnp.where(parity == 0, attn_other, attn_mine),
        ]
    )
    mix_near = {k: dot(attn_low, mix_rows[k], NT).astype(BF) for k in range(count)}
    mix_near = fold(mix_near, "row", near)
    share, ff_sum, mix_near = together(share, ff_sum, mix_near)
    input_sum = sum_cols(share)

    share, dq, dkv = together(share, dq, dkv)
    mix_total = over_dp(fold(mix_near, "row", far)[0])
    q_near = fold({k: dot(norm_one[k], dq, NT).astype(BF) for k in range(count)}, "row", near)
    kv_near = fold({k: dot(dkv, norm_one[k], NT).astype(BF) for k in range(count)}, "row", near)
    ff_sum, gain_share_one, q_near, kv_near = together(ff_sum, gain_share_one, q_near, kv_near)
    q_total = over_dp(fold(q_near, "row", far)[0])
    kv_total = over_dp(fold(kv_near, "row", far)[0])
    output_own = (residual_own + ff_sum.astype(F32)).astype(BF)
    layer_output = all_tokens(output_own)

    bits = near + far[::-1]
    gain_shares = jnp.stack([gain_share_one[..., 0], gain_share_two[..., 0]], axis=2)
    gain_shares = by_xor(gain_shares, lax.axis_index("col"), 0)
    gain_shares = {c: gain_shares[c] for c in range(cols)}
    gain_shares = fold(gain_shares, "col", near_bits(cols) + far_bits(cols), low=False)[0]
    gain_shares = fold({k: gain_shares[k] for k in range(count)}, "row", bits, low=False)[0]
    gain_totals = over_dp(gain_shares)
    input_sum, q_total, kv_total, mix_total, gain_totals, layer_output, up_tail = together(
        input_sum, q_total, kv_total, mix_total, gain_totals, layer_output, up_tail
    )
    up_total = jnp.concatenate([up_head, up_tail])

    input_grad = all_tokens((residual_grad_own + input_sum.astype(F32)).astype(BF)).astype(F32)
    kv_rows = kv_total.shape[0] // 2
    return (
        layer_output,
        input_grad,
        gain_totals[0],
        gain_totals[1],
        q_total,
        kv_total[:kv_rows].T,
        kv_total[kv_rows:].T,
        mix_total,
        gate_total.T,
        up_total.T,
        down_total,
    )


def solution(mesh):
    return jax.shard_map(
        body,
        mesh=mesh,
        in_specs=(
            P("dp", ("row", "col")),
            P(("row", "col")),
            P(("row", "col")),
            P("row", "col"),
            P("row", "col"),
            P("row", "col"),
            P("col", "row"),
            P("row", "col"),
            P("row", "col"),
            P("col", "row"),
            P("dp", ("row", "col")),
            P(("dp", "row")),
            P(("dp", "row")),
        ),
        out_specs=(
            P("dp", ("row", "col")),
            P("dp", ("row", "col")),
            P(("row", "col")),
            P(("row", "col")),
            P("row", "col"),
            P("row", "col"),
            P("row", "col"),
            P("col", "row"),
            P("row", "col"),
            P("row", "col"),
            P("col", "row"),
        ),
        check_vma=False,
    )
```

```python
import functools

import jax
import jax.numpy as jnp
from jax import lax
from jax.experimental import pallas as pl
from jax.experimental.pallas import tpu as pltpu
from jax.sharding import PartitionSpec as P

D = 2560
HEAD = 80
EPS = 1e-05
THETA = 10000.0
NEG = -1e30
LOG2E = 1.4426950408889634
LN2 = 0.6931471805599453
ROOT = HEAD ** (-0.5)
BF = jnp.bfloat16
F32 = jnp.float32
NN = (((1,), (0,)), ((), ()))
TN = (((0,), (0,)), ((), ()))
NT = (((1,), (1,)), ((), ()))


def dot(left, right, dims=NN):
    return lax.dot_general(left, right, dims, preferred_element_type=F32)


def together(*values):
    return lax.optimization_barrier(values)


def swapped(value, axis, mask):
    size = lax.axis_size(axis)
    return lax.ppermute(value, axis, [(i, i ^ mask) for i in range(size)])


def spread(blocks, axis, bits):
    blocks = dict(blocks)
    for bit in bits:
        for k in list(blocks):
            blocks[k | bit] = swapped(blocks[k], axis, bit)
    return blocks


def fold(blocks, axis, bits, low=True):
    held = dict(blocks)
    for bit in bits:
        for k in [k for k in held if k & bit]:
            other = swapped(held.pop(k), axis, bit)
            total = held[k ^ bit].astype(F32) + other.astype(F32)
            held[k ^ bit] = total.astype(BF) if low else total
    return held


def far_bits(size):
    return [1 << i for i in range(1, size.bit_length() - 1)]


def near_bits(size):
    return [1] if size > 1 else []


def exchange_blocks(blocks, axis):
    return [blocks[0]] + [swapped(blocks[k], axis, k) for k in range(1, len(blocks))]


def by_xor(value, index, axis):
    parts = [
        lax.dynamic_index_in_dim(value, index ^ k, axis, keepdims=True)
        for k in range(value.shape[axis])
    ]
    return jnp.concatenate(parts, axis=axis)


def params(mib=58):
    return pltpu.CompilerParams(vmem_limit_bytes=mib * 1024 * 1024)


def takes(micros):
    return pl.CostEstimate(flops=int(micros * 0.1e9), transcendentals=0, bytes_accessed=0)


def shape(dims, dtype):
    return jax.ShapeDtypeStruct(dims, dtype)


SMALL = pl.BlockSpec(memory_space=pltpu.SMEM)
RAW = pl.BlockSpec(memory_space=pl.ANY)


def resident(dims, buffers=None):
    zeros = (0,) * len(dims)
    mode = {} if buffers is None else {"pipeline_mode": pl.Buffered(buffers)}
    return pl.BlockSpec(dims, lambda *_: zeros, **mode)


def normalise(x_ref, gain_ref, out_ref, scale_ref):
    cols, count, piece, _ = x_ref.shape
    total = None
    for c in range(cols):
        for k in range(count):
            value = x_ref[c, k].astype(F32)
            part = jnp.sum(value * value, axis=0, keepdims=True)
            total = part if total is None else total + part
    scale = lax.rsqrt(total / D + EPS)
    scale_ref[...] = scale
    for c in range(cols):
        for k in range(count):
            value = x_ref[c, k].astype(F32) * scale * gain_ref[c, k]
            out_ref[k, c * piece : (c + 1) * piece, :] = value.astype(BF)


def turn(value, cosine, sine):
    half = value.shape[0] // 2
    first, second = value[:half], value[half:]
    return jnp.concatenate([first * cosine - second * sine, second * cosine + first * sine])


def qkv_kernel(count, shared, x_ref, gain_ref, cos_ref, sin_ref, *refs):
    q_w, kv_w = refs[:count], refs[count : 2 * count]
    norm_ref, scale_ref, sets_ref = refs[2 * count :]
    normalise(x_ref, gain_ref, norm_ref, scale_ref)
    query = keyval = None
    for k in range(count):
        normed = norm_ref[k]
        part = dot(q_w[k][...], normed, TN)
        query = part if query is None else query + part
        part = dot(kv_w[k][...], normed)
        keyval = part if keyval is None else keyval + part
    cosine, sine = cos_ref[...], sin_ref[...]
    half = query.shape[0] // 2
    kv_half = keyval.shape[0] // 2
    for h in range(2):
        for at in range(0, half, HEAD):
            value = turn(query[h * half + at : h * half + at + HEAD], cosine, sine)
            sets_ref[h, at : at + HEAD, :] = (value * (ROOT * LOG2E)).astype(BF)
        at = 0 if shared else h * HEAD
        key = turn(keyval[at : at + HEAD], cosine, sine)
        sets_ref[h, half : half + HEAD, :] = key.astype(BF)
        sets_ref[h, half + HEAD : half + 2 * HEAD, :] = keyval[
            kv_half + at : kv_half + at + HEAD
        ].astype(BF)


def qkv_project(x, gain, cosine, sine, q_w, kv_w):
    cols, count, piece, tokens = x.shape
    half = q_w[0].shape[1] // 2
    shared = kv_w[0].shape[0] == 2 * HEAD
    return pl.pallas_call(
        functools.partial(qkv_kernel, count, shared),
        out_shape=(
            shape((count, cols * piece, tokens), BF),
            shape((1, tokens), F32),
            shape((2, half + 2 * HEAD, tokens), BF),
        ),
        compiler_params=params(),
        name="qkv_project",
        cost_estimate=takes(12),
    )(x, gain, cosine, sine, *q_w, *kv_w)


def pieces_of(half, at, tile, tokens):
    if half == 1:
        return [(0, 0, tokens, False), (1, 0, at + tile, True)]
    head = [(0, 0, at, False)] if at else []
    return head + [(0, at, at + tile, True)]


def seen_of(half, at, begin, end, tile, seg_row, seg_col):
    rows = lax.broadcasted_iota(jnp.int32, (end - begin, tile), 0) + begin
    cols = lax.broadcasted_iota(jnp.int32, (end - begin, tile), 1) + at
    seen = rows <= cols
    if half == 1:
        seen = seen & (seg_col[begin:end] == seg_row[:, at : at + tile])
    return seen


def place(parity, own_ref, other_ref, sets):
    sets[parity] = own_ref[...]
    sets[1 - parity] = other_ref[...]


def attend_kernel(
    tile, parity_ref, own_ref, other_ref, seg_row, seg_col, mine_ref, send_ref, lse_ref, sets, rows
):
    tokens = own_ref.shape[-1]
    heads = pl.num_programs(0)
    head = pl.program_id(0)
    parity = parity_ref[0]
    half_rows = own_ref.shape[0] - 2 * HEAD

    @pl.when(head == 0)
    def _():
        place(parity, own_ref, other_ref, sets)
        for half in range(2):
            keys = sets[half, half_rows : half_rows + HEAD, :]
            rows[half] = keys.astype(F32).T.astype(BF)

    at_head = pl.ds(pl.multiple_of(head * HEAD, 16), HEAD)
    for half in range(2):
        for at in range(0, tokens, tile):
            span = slice(at, at + tile)
            query = sets[half, at_head, span]
            pieces = pieces_of(half, at, tile, tokens)
            scores = []
            for which, begin, end, masked in pieces:
                part = dot(rows[which, begin:end, :], query)
                if masked:
                    part = jnp.where(
                        seen_of(half, at, begin, end, tile, seg_row, seg_col), part, NEG
                    )
                scores.append(part)
            peak = functools.reduce(
                jnp.maximum, [jnp.max(s, axis=0, keepdims=True) for s in scores]
            )
            total = out = None
            for (which, begin, end, _), part in zip(pieces, scores):
                weights = jnp.exp2(part - peak)
                mass = jnp.sum(weights, axis=0, keepdims=True)
                value = dot(sets[which, half_rows + HEAD :, begin:end], weights.astype(BF))
                total = mass if total is None else total + mass
                out = value if out is None else out + value
            out = (out / total).astype(BF)
            lse_ref[half, 0, :, span] = peak + jnp.log2(total)

            @pl.when(parity == half)
            def _():
                mine_ref[at_head, span] = out

            @pl.when(parity != half)
            def _():
                send_ref[at_head, span] = out


def attend(parity, own, other, seg):
    depth, tokens = own.shape
    half_rows = depth - 2 * HEAD
    heads = half_rows // HEAD
    tile = min(256, tokens)
    out = resident((half_rows, tokens))
    return pl.pallas_call(
        functools.partial(attend_kernel, tile),
        out_shape=(
            shape((half_rows, tokens), BF),
            shape((half_rows, tokens), BF),
            shape((2, heads, 1, tokens), F32),
        ),
        grid=(heads,),
        in_specs=[
            SMALL,
            resident((depth, tokens)),
            resident((depth, tokens)),
            resident((1, tokens)),
            resident((tokens, 1)),
        ],
        out_specs=(out, out, pl.BlockSpec((2, 1, 1, tokens), lambda h: (0, h, 0, 0))),
        scratch_shapes=[
            pltpu.VMEM((2, depth, tokens), BF),
            pltpu.VMEM((2, tokens, HEAD), BF),
        ],
        compiler_params=params(),
        name="attend",
        cost_estimate=takes(27),
    )(parity, own, other, seg[None, :], seg[:, None])


def attend_back_kernel(
    tile,
    parity_ref,
    own_ref,
    other_ref,
    own_out,
    other_out,
    own_grad,
    other_grad,
    lse_ref,
    seg_row,
    seg_col,
    mine_ref,
    send_ref,
    sets,
    outs,
    grads,
    rows,
    key_acc,
    value_acc,
):
    tokens = own_ref.shape[-1]
    heads = pl.num_programs(0)
    head = pl.program_id(0)
    parity = parity_ref[0]
    half_rows = own_ref.shape[0] - 2 * HEAD

    @pl.when(head == 0)
    def _():
        place(parity, own_ref, other_ref, sets)
        place(parity, own_out, other_out, outs)
        place(parity, own_grad, other_grad, grads)
        for half in range(2):
            for i in range(2):
                at = half_rows + i * HEAD
                rows[i, half] = sets[half, at : at + HEAD, :].astype(F32).T.astype(BF)
        key_acc[...] = jnp.zeros_like(key_acc)
        value_acc[...] = jnp.zeros_like(value_acc)

    at_head = pl.ds(pl.multiple_of(head * HEAD, 16), HEAD)
    for half in range(2):
        for at in range(0, tokens, tile):
            span = slice(at, at + tile)
            query = sets[half, at_head, span]
            grad = grads[half, at_head, span]
            lse = lse_ref[half, 0, :, span]
            delta = jnp.sum(
                grad.astype(F32) * outs[half, at_head, span].astype(F32), axis=0, keepdims=True
            )
            total = None
            for which, begin, end, masked in pieces_of(half, at, tile, tokens):
                part = dot(rows[0, which, begin:end, :], query)
                if masked:
                    part = jnp.where(
                        seen_of(half, at, begin, end, tile, seg_row, seg_col), part, NEG
                    )
                weights = jnp.exp2(part - lse)
                dprod = dot(rows[1, which, begin:end, :], grad)
                dscore = (weights * (dprod - delta)).astype(BF)
                value_acc[which, :, begin:end] += dot(grad, weights.astype(BF), NT)
                key_acc[which, :, begin:end] += dot(query, dscore, NT)
                more = dot(sets[which, half_rows : half_rows + HEAD, begin:end], dscore)
                total = more if total is None else total + more
            total = (total * ROOT).astype(BF)

            @pl.when(parity == half)
            def _():
                mine_ref[at_head, span] = total

            @pl.when(parity != half)
            def _():
                send_ref[at_head, span] = total

    @pl.when(head == heads - 1)
    def _():
        for ref, which in ((mine_ref, parity), (send_ref, 1 - parity)):
            ref[half_rows : half_rows + HEAD, :] = (key_acc[which] * LN2).astype(BF)
            ref[half_rows + HEAD :, :] = value_acc[which].astype(BF)


def attend_back(parity, own, other, own_out, other_out, own_grad, other_grad, lse, seg):
    depth, tokens = own.shape
    half_rows = depth - 2 * HEAD
    heads = half_rows // HEAD
    tile = min(256, tokens)
    full, part = resident((depth, tokens)), resident((half_rows, tokens))
    return pl.pallas_call(
        functools.partial(attend_back_kernel, tile),
        out_shape=(shape((depth, tokens), BF), shape((depth, tokens), BF)),
        grid=(heads,),
        in_specs=[
            SMALL,
            full,
            full,
            part,
            part,
            part,
            part,
            pl.BlockSpec((2, 1, 1, tokens), lambda h: (0, h, 0, 0)),
            resident((1, tokens)),
            resident((tokens, 1)),
        ],
        out_specs=(full, full),
        scratch_shapes=[
            pltpu.VMEM((2, depth, tokens), BF),
            pltpu.VMEM((2, half_rows, tokens), BF),
            pltpu.VMEM((2, half_rows, tokens), BF),
            pltpu.VMEM((2, 2, tokens, HEAD), BF),
            pltpu.VMEM((2, HEAD, tokens), F32),
            pltpu.VMEM((2, HEAD, tokens), F32),
        ],
        compiler_params=params(),
        name="attend_back",
        cost_estimate=takes(37),
    )(
        parity,
        own,
        other,
        own_out,
        other_out,
        own_grad,
        other_grad,
        lse,
        seg[None, :],
        seg[:, None],
    )


def halves_at(parity, half_rows):
    mine = pl.ds(pl.multiple_of(parity * half_rows, 16), half_rows)
    other = pl.ds(pl.multiple_of((1 - parity) * half_rows, 16), half_rows)
    return mine, other


def mix_out_kernel(count, parity_ref, own_ref, other_ref, *refs):
    weights, out_ref = refs[:count], refs[count]
    cols, _, piece, _ = out_ref.shape
    mine, other = halves_at(parity_ref[0], own_ref.shape[0])
    for k in range(count):
        part = dot(weights[k][mine, :], own_ref[...], TN)
        part = part + dot(weights[k][other, :], other_ref[...], TN)
        for c in range(cols):
            out_ref[c, k] = part[c * piece : (c + 1) * piece].astype(BF)


def mix_out(parity, own, other, weights, cols):
    count = len(weights)
    piece = weights[0].shape[1] // cols
    vmem = pl.BlockSpec(memory_space=pltpu.VMEM)
    return pl.pallas_call(
        functools.partial(mix_out_kernel, count),
        out_shape=shape((cols, count, piece, own.shape[1]), BF),
        in_specs=[SMALL] + [vmem] * (2 + count),
        compiler_params=params(),
        name="mix_out",
        cost_estimate=takes(10),
    )(parity, own, other, *weights)


def mix_back_kernel(count, parts, parity_ref, *refs):
    x_refs, weights = refs[:parts], refs[parts : parts + count]
    rows_ref, own_ref, other_ref = refs[parts + count :]
    for i, x_ref in enumerate(x_refs):
        cols, _, piece, tokens = x_ref.shape
        for c in range(cols):
            for k in range(count):
                rows_ref[k, c * piece : (c + 1) * piece, i * tokens : (i + 1) * tokens] = x_ref[
                    c, k
                ]
    mine, other = halves_at(parity_ref[0], own_ref.shape[0])
    for at, out_ref in ((other, other_ref), (mine, own_ref)):
        total = None
        for k in range(count):
            part = dot(weights[k][at, :], rows_ref[k])
            total = part if total is None else total + part
        out_ref[...] = total.astype(BF)


def mix_back(parity, x_parts, weights):
    parts = len(x_parts)
    cols, count, piece, tokens = x_parts[0].shape
    tokens = tokens * parts
    half_rows = weights[0].shape[0] // 2
    vmem = pl.BlockSpec(memory_space=pltpu.VMEM)
    return pl.pallas_call(
        functools.partial(mix_back_kernel, count, parts),
        out_shape=(
            shape((count, cols * piece, tokens), BF),
            shape((half_rows, tokens), BF),
            shape((half_rows, tokens), BF),
        ),
        in_specs=[SMALL] + [vmem] * (parts + count),
        compiler_params=params(),
        name="mix_back",
        cost_estimate=takes(9),
    )(parity, *x_parts, *weights)


def fan_kernel(count, x_ref, *refs):
    weights, out_ref = refs[:count], refs[count]
    cols, _, piece, _ = out_ref.shape
    for k in range(count):
        part = dot(weights[k][...], x_ref[...], TN)
        for c in range(cols):
            out_ref[c, k] = part[c * piece : (c + 1) * piece].astype(BF)


def fan_out(weights, x, cols):
    count = len(weights)
    piece = weights[0].shape[1] // cols
    return pl.pallas_call(
        functools.partial(fan_kernel, count),
        out_shape=shape((cols, count, piece, x.shape[1]), BF),
        compiler_params=params(),
        name="fan_out",
        cost_estimate=takes(17),
    )(x, *weights)


def norm_back(grads, k, x_ref, gain_ref, scale, coef, share_ref, gain_share_ref):
    cols, _, piece, _ = x_ref.shape
    for c in range(cols):
        grad = grads[c * piece : (c + 1) * piece]
        value = x_ref[c, k].astype(F32)
        gain_share_ref[c, k] = jnp.sum(grad * (value * scale), axis=1, keepdims=True)
        share_ref[c, k] = ((grad * gain_ref[c, k]) * scale - value * coef).astype(BF)


def ff_kernel(count, chained, x_ref, g_ref, gain_ref, *refs):
    gate_w, up_w, down_w = refs[:count], refs[count : 2 * count], refs[2 * count : 3 * count]
    refs = refs[3 * count + (5 if chained else 0) :]
    norm_ref, rows_ref, act_ref, dgate_ref, dup_ref, share_ref, gain_share_ref = refs[:7]
    scale_ref, inner_ref, back_ref = refs[7:]
    cols, _, piece, _ = x_ref.shape
    step = pl.program_id(0)

    @pl.when(step == 0)
    def _():
        normalise(x_ref, gain_ref, norm_ref, scale_ref)
        for c in range(cols):
            for k in range(count):
                rows_ref[k, c * piece : (c + 1) * piece, :] = g_ref[c, k]
        inner_ref[...] = jnp.zeros_like(inner_ref)
        back_ref[...] = jnp.zeros_like(back_ref)

    def summed(weights, ref):
        total = None
        for k in range(count):
            part = dot(weights[k][...], ref[k])
            total = part if total is None else total + part
        return total

    gate = summed(gate_w, norm_ref)
    up = summed(up_w, norm_ref)
    sigma = jax.nn.sigmoid(gate)
    silu = gate * sigma
    act_ref[...] = (silu * up).astype(BF)
    grad = summed(down_w, rows_ref)
    dup = grad * silu
    dgate = grad * up * (sigma + silu * (1.0 - sigma))
    inner_ref[...] += jnp.sum(dgate * gate + dup * up, axis=0, keepdims=True)
    dgate_ref[...] = dgate.astype(BF)
    dup_ref[...] = dup.astype(BF)
    for k in range(count):
        back_ref[k] += dot(gate_w[k][...], dgate_ref[...], TN) + dot(
            up_w[k][...], dup_ref[...], TN
        )

    @pl.when(step == pl.num_programs(0) - 1)
    def _():
        scale = scale_ref[...]
        coef = scale * scale * inner_ref[...] / D
        for k in range(count):
            norm_back(back_ref[k], k, x_ref, gain_ref, scale, coef, share_ref, gain_share_ref)


def feed_forward(x, g, part, parts, gain, gate_w, up_w, down_w, before):
    cols, count, piece, tokens = x.shape
    width, depth = gate_w[0].shape
    tile = 432 if width % 432 == 0 else width
    g_spec = pl.BlockSpec(x.shape, lambda n: (0, 0, 0, part), pipeline_mode=pl.Buffered(1))
    rows = (count, cols * piece, tokens)
    rows_spec = pl.BlockSpec(rows, lambda n: (0, 0, part), pipeline_mode=pl.Buffered(1))
    w_spec = pl.BlockSpec((tile, depth), lambda n: (n, 0))
    h_spec = pl.BlockSpec((tile, tokens), lambda n: (n, part))
    rows_all = shape((count, cols * piece, tokens * parts), BF)
    hidden = shape((width, tokens * parts), BF)
    first = 3 + 3 * count
    return pl.pallas_call(
        functools.partial(ff_kernel, count, bool(before)),
        out_shape=(
            rows_all,
            rows_all,
            hidden,
            hidden,
            hidden,
            shape(x.shape, BF),
            shape(gain.shape, F32),
        ),
        grid=(width // tile,),
        in_specs=[resident(x.shape, 1), g_spec, resident(gain.shape, 1)]
        + [w_spec] * (3 * count)
        + [RAW] * len(before),
        out_specs=(
            rows_spec,
            rows_spec,
            h_spec,
            h_spec,
            h_spec,
            resident(x.shape, 1),
            resident(gain.shape, 1),
        ),
        scratch_shapes=[
            pltpu.VMEM((1, tokens), F32),
            pltpu.VMEM((1, tokens), F32),
            pltpu.VMEM(rows, F32),
        ],
        input_output_aliases={first + i: i for i in range(len(before))},
        compiler_params=params(60),
        name="feed_forward",
        cost_estimate=takes(42),
    )(x, g, gain, *gate_w, *up_w, *down_w, *before)


def qkv_back_kernel(
    count,
    shared,
    parity_ref,
    x_ref,
    gain_ref,
    scale_ref,
    cos_ref,
    sin_ref,
    sets_ref,
    own_ref,
    other_ref,
    *refs,
):
    q_w, kv_w = refs[:count], refs[count : 2 * count]
    dq_ref, dkv_ref, share_ref, gain_share_ref = refs[2 * count :]
    parity = parity_ref[0]
    half_rows = own_ref.shape[0] - 2 * HEAD
    kv_half = dkv_ref.shape[0] // 2
    cosine, sine = cos_ref[...], -sin_ref[...]
    inner = None
    folded = None
    for grads, which in ((own_ref, parity), (other_ref, 1 - parity)):
        for at in range(0, half_rows + 2 * HEAD, HEAD):
            value = grads[at : at + HEAD, :].astype(F32)
            part = value * sets_ref[which, at : at + HEAD, :].astype(F32)
            part = jnp.sum(part, axis=0, keepdims=True)
            if at < half_rows:
                part = part * (1.0 / (ROOT * LOG2E))
                start = pl.multiple_of(which * half_rows + at, 16)
                dq_ref[pl.ds(start, HEAD), :] = turn(value, cosine, sine).astype(BF)
            else:
                is_key = at == half_rows
                raw = turn(value, cosine, sine) if is_key else value
                base = 0 if is_key else kv_half
                if not shared:
                    start = pl.multiple_of(base + which * HEAD, 16)
                    dkv_ref[pl.ds(start, HEAD), :] = raw.astype(BF)
                elif folded is None or at not in folded:
                    folded = {**(folded or {}), at: raw}
                else:
                    dkv_ref[base : base + HEAD, :] = (folded[at] + raw).astype(BF)
            inner = part if inner is None else inner + part
    scale = scale_ref[...]
    coef = scale * scale * inner / D
    for k in range(count):
        grads = dot(q_w[k][...], dq_ref[...]) + dot(kv_w[k][...], dkv_ref[...], TN)
        norm_back(grads, k, x_ref, gain_ref, scale, coef, share_ref, gain_share_ref)


def qkv_back(parity, x, gain, scale, cosine, sine, sets, own, other, q_w, kv_w):
    cols, count, piece, tokens = x.shape
    shared = kv_w[0].shape[0] == 2 * HEAD
    vmem = pl.BlockSpec(memory_space=pltpu.VMEM)
    return pl.pallas_call(
        functools.partial(qkv_back_kernel, count, shared),
        out_shape=(
            shape((q_w[0].shape[1], tokens), BF),
            shape((kv_w[0].shape[0], tokens), BF),
            shape(x.shape, BF),
            shape(gain.shape, F32),
        ),
        in_specs=[SMALL] + [vmem] * (8 + 2 * count),
        compiler_params=params(),
        name="qkv_back",
        cost_estimate=takes(17),
    )(parity, x, gain, scale, cosine, sine, sets, own, other, *q_w, *kv_w)


def rope_parts(positions):
    half = HEAD // 2
    freq = THETA ** (-jnp.arange(half, dtype=F32) * 2.0 / HEAD)
    angle = freq[:, None] * positions.astype(F32)[None, :]
    return (jnp.cos(angle), jnp.sin(angle))


def spread_cols(value):
    return lax.all_gather(value, "col", axis=0, tiled=False)


def sum_cols(value):
    return lax.psum_scatter(value, "col", scatter_dimension=0, tiled=False)


def sent_over_dp(value):
    low = value.astype(BF)
    size = lax.axis_size("dp")
    others = [
        lax.ppermute(low, "dp", [(i, (i + step) % size) for i in range(size)])
        for step in range(1, size)
    ]
    return [low] + others


def summed_up(parts):
    total = parts[0].astype(F32)
    for other in parts[1:]:
        total = total + other.astype(F32)
    return total


def over_dp(value):
    return summed_up(sent_over_dp(value))


def body(
    layer_input,
    attn_gain,
    mlp_gain,
    query_weight,
    key_weight,
    value_weight,
    mix_weight,
    gate_weight,
    up_weight,
    down_weight,
    output_grad,
    segment_ids,
    position_ids,
):
    rows = segment_ids.shape[0]
    count = lax.axis_size("row")
    cols = lax.axis_size("col")
    piece = layer_input.shape[1]
    row = lax.axis_index("row")
    parity = (row % 2).astype(jnp.int32)
    own_core = parity.reshape(1)
    q_half = query_weight.shape[1] // 2
    near, far = near_bits(count), far_bits(count)

    def row_tokens(value):
        turned = value.T
        outgoing = [
            lax.dynamic_slice(turned, (0, (row ^ k) * rows), (piece, rows)) for k in range(count)
        ]
        return jnp.stack(exchange_blocks(outgoing, "row"))

    def all_tokens(blocks):
        got = exchange_blocks([blocks[k] for k in range(count)], "row")
        result = jnp.zeros((piece, count * rows), blocks.dtype)
        for k in range(count):
            result = lax.dynamic_update_slice(result, got[k], (0, (row ^ k) * rows))
        return result.T

    def listed(blocks):
        return [blocks[k] for k in range(count)]

    source_own = row_tokens(layer_input)
    kv_weight = jnp.concatenate([key_weight.T, value_weight.T])
    q_first = spread({0: query_weight}, "row", far)
    kv_first = spread({0: kv_weight}, "row", far)
    mix_first = spread({0: mix_weight}, "row", far)
    gate_first = spread({0: gate_weight.T}, "row", far)
    up_first = spread({0: up_weight.T}, "row", far)
    down_first = spread({0: down_weight}, "row", far)
    q_blocks = spread(q_first, "row", near)
    kv_blocks = spread(kv_first, "row", near)

    gains = lax.all_gather(jnp.stack([attn_gain, mlp_gain]), ("row", "col"), axis=1, tiled=True)
    gains = gains.reshape(2, count, cols, piece)
    gains = by_xor(gains, row, 1).swapaxes(1, 2)[..., None]
    gain_one, gain_two = gains[0], gains[1]

    cosine, sine = rope_parts(position_ids)
    other_seg = swapped(segment_ids, "row", 1)
    seg = jnp.where(parity == 0, other_seg, segment_ids)

    source = spread_cols(source_own)
    source, q_blocks, kv_blocks, mix_first, gate_first, gain_one, cosine, sine, seg = together(
        source, q_blocks, kv_blocks, mix_first, gate_first, gain_one, cosine, sine, seg
    )
    grad_own = row_tokens(output_grad)
    grad_own, source = together(grad_own, source)
    grad_all = spread_cols(grad_own)
    norm_one, scale_one, sets = qkv_project(
        source, gain_one, cosine, sine, listed(q_blocks), listed(kv_blocks)
    )
    own_set = lax.dynamic_index_in_dim(sets, parity, 0, keepdims=False)
    other_set = swapped(lax.dynamic_index_in_dim(sets, 1 - parity, 0, keepdims=False), "row", 1)
    attn_mine, attn_send, lse = attend(own_core, own_set, other_set, seg)
    attn_other = swapped(attn_send, "row", 1)
    mix_blocks = spread(mix_first, "row", near)
    attn_mine, attn_other, mix_blocks, up_first = together(
        attn_mine, attn_other, mix_blocks, up_first
    )
    attn_part = mix_out(own_core, attn_mine, attn_other, listed(mix_blocks), cols)
    attn_part, grad_all = together(attn_part, grad_all)
    attn_sum = sum_cols(attn_part)
    gate_blocks = spread(gate_first, "row", near)
    up_blocks = spread(up_first, "row", near)
    down_blocks = spread(down_first, "row", near)
    attn_sum, gate_blocks, up_blocks, down_blocks = together(
        attn_sum, gate_blocks, up_blocks, down_blocks
    )
    residual_own = source_own.astype(F32) + attn_sum.astype(F32)

    parts = 2 if rows % 256 == 0 else 1
    size = rows // parts
    spans = [slice(i * size, (i + 1) * size) for i in range(parts)]
    residual_low = residual_own.astype(BF)
    residual = [spread_cols(residual_low[..., span]) for span in spans]
    before, shares = (), []
    gain_share_two = 0.0
    for i in range(parts):
        out = feed_forward(
            residual[i],
            grad_all,
            i,
            parts,
            gain_two,
            listed(gate_blocks),
            listed(up_blocks),
            listed(down_blocks),
            before,
        )
        before = out[:5]
        shares.append(out[5])
        gain_share_two = gain_share_two + out[6]
    norm_two, grad_rows, act, dgate, dup = before
    share_sums = [sum_cols(share) for share in shares]
    down_grads = {k: dot(act, grad_rows[k], NT).astype(BF) for k in range(count)}
    gate_grads = {k: dot(dgate, norm_two[k], NT).astype(BF) for k in range(count)}
    up_grads = {k: dot(dup, norm_two[k], NT).astype(BF) for k in range(count)}
    down_grads = fold(down_grads, "row", near)
    gate_grads = fold(gate_grads, "row", near)
    up_grads = fold(up_grads, "row", near)
    *share_sums, down_grads, gate_grads, up_grads = together(
        *share_sums, down_grads, gate_grads, up_grads
    )
    residual_grad_own = grad_own.astype(F32) + jnp.concatenate(share_sums, axis=2).astype(F32)
    down_total = fold(down_grads, "row", far)[0]
    gate_total = fold(gate_grads, "row", far)[0]

    mix_cols = spread_cols(residual_grad_own.astype(BF))
    ff_part = fan_out(listed(down_blocks), act, cols)
    down_total = over_dp(down_total)
    mix_cols, ff_part, down_total, gate_total, up_grads = together(
        mix_cols, ff_part, down_total, gate_total, up_grads
    )
    up_total = fold(up_grads, "row", far)[0]
    gate_total = over_dp(gate_total)
    mix_rows, grad_mine, grad_send = mix_back(own_core, [mix_cols], listed(mix_blocks))
    ff_sum = sum_cols(ff_part)
    grad_other = swapped(grad_send, "row", 1)
    back_mine, back_send = attend_back(
        own_core, own_set, other_set, attn_mine, attn_send, grad_mine, grad_other, lse, seg
    )
    back_other = swapped(back_send, "row", 1)
    back_other, up_total, gate_total, down_total = together(
        back_other, up_total, gate_total, down_total
    )
    cut = up_total.shape[0] * 5 // 9 // 16 * 16
    up_head, up_tail = over_dp(up_total[:cut]), sent_over_dp(up_total[cut:])
    dq, dkv, share, gain_share_one = qkv_back(
        own_core,
        source,
        gain_one,
        scale_one,
        cosine,
        sine,
        sets,
        back_mine,
        back_other,
        listed(q_blocks),
        listed(kv_blocks),
    )
    share, attn_mine, mix_rows = together(share, attn_mine, mix_rows)
    attn_low = jnp.concatenate(
        [
            jnp.where(parity == 0, attn_mine, attn_other),
            jnp.where(parity == 0, attn_other, attn_mine),
        ]
    )
    mix_odd = {k: dot(attn_low, mix_rows[k], NT).astype(BF) for k in range(1, count, 2)}
    share, ff_sum, mix_odd, up_head = together(share, ff_sum, mix_odd, up_head)
    input_sum = sum_cols(share)

    gain_shares = jnp.stack([gain_share_one[..., 0], gain_share_two[..., 0]], axis=2)
    bits = near + far[::-1]
    gain_shares = fold({k: gain_shares[:, k] for k in range(count)}, "row", bits, low=False)[0]
    share, dq, dkv, attn_low, mix_rows = together(share, dq, dkv, attn_low, mix_rows)
    mix_even = {k: dot(attn_low, mix_rows[k], NT).astype(BF) for k in range(0, count, 2)}
    mix_near = fold({**mix_even, **mix_odd}, "row", near)
    q_near = fold({k: dot(norm_one[k], dq, NT).astype(BF) for k in range(count)}, "row", near)
    kv_near = fold({k: dot(dkv, norm_one[k], NT).astype(BF) for k in range(count)}, "row", near)
    mix_total = over_dp(fold(mix_near, "row", far)[0])
    ff_sum, gain_shares, q_near, kv_near, up_tail = together(
        ff_sum, gain_shares, q_near, kv_near, up_tail
    )
    q_far = fold(q_near, "row", far)[0]
    kv_far = fold(kv_near, "row", far)[0]
    q_total, kv_total = over_dp(q_far), over_dp(kv_far)
    output_own = (residual_own + ff_sum.astype(F32)).astype(BF)
    layer_output = all_tokens(output_own)

    gain_shares = by_xor(gain_shares, lax.axis_index("col"), 0)
    gain_shares = {c: gain_shares[c] for c in range(cols)}
    gain_shares = fold(gain_shares, "col", near_bits(cols) + far_bits(cols), low=False)[0]
    gain_totals = over_dp(gain_shares)
    up_total = jnp.concatenate([up_head, summed_up(up_tail)])
    input_sum, q_total, kv_total, mix_total, gain_totals, layer_output, up_total = together(
        input_sum, q_total, kv_total, mix_total, gain_totals, layer_output, up_total
    )

    input_grad = all_tokens((residual_grad_own + input_sum.astype(F32)).astype(BF)).astype(F32)
    kv_rows = kv_total.shape[0] // 2
    return (
        layer_output,
        input_grad,
        gain_totals[0],
        gain_totals[1],
        q_total,
        kv_total[:kv_rows].T,
        kv_total[kv_rows:].T,
        mix_total,
        gate_total.T,
        up_total.T,
        down_total,
    )


def solution(mesh):
    return jax.shard_map(
        body,
        mesh=mesh,
        in_specs=(
            P("dp", ("row", "col")),
            P(("row", "col")),
            P(("row", "col")),
            P("row", "col"),
            P("row", "col"),
            P("row", "col"),
            P("col", "row"),
            P("row", "col"),
            P("row", "col"),
            P("col", "row"),
            P("dp", ("row", "col")),
            P(("dp", "row")),
            P(("dp", "row")),
        ),
        out_specs=(
            P("dp", ("row", "col")),
            P("dp", ("row", "col")),
            P(("row", "col")),
            P(("row", "col")),
            P("row", "col"),
            P("row", "col"),
            P("row", "col"),
            P("col", "row"),
            P("row", "col"),
            P("row", "col"),
            P("col", "row"),
        ),
        check_vma=False,
    )
```

```python
import functools

import jax
import jax.numpy as jnp
from jax import lax
from jax.experimental import pallas as pl
from jax.experimental.pallas import tpu as pltpu
from jax.sharding import PartitionSpec as P

D = 2560
HEAD = 80
EPS = 1e-05
THETA = 10000.0
NEG = -1e30
LOG2E = 1.4426950408889634
LN2 = 0.6931471805599453
ROOT = HEAD ** (-0.5)
BF = jnp.bfloat16
F32 = jnp.float32
NN = (((1,), (0,)), ((), ()))
TN = (((0,), (0,)), ((), ()))
NT = (((1,), (1,)), ((), ()))


def dot(left, right, dims=NN):
    return lax.dot_general(left, right, dims, preferred_element_type=F32)


def together(*values):
    return lax.optimization_barrier(values)


def swapped(value, axis, mask):
    size = lax.axis_size(axis)
    return lax.ppermute(value, axis, [(i, i ^ mask) for i in range(size)])


def spread(blocks, axis, bits):
    blocks = dict(blocks)
    for bit in bits:
        for k in list(blocks):
            blocks[k | bit] = swapped(blocks[k], axis, bit)
    return blocks


def fold(blocks, axis, bits, low=True):
    held = dict(blocks)
    for bit in bits:
        for k in [k for k in held if k & bit]:
            other = swapped(held.pop(k), axis, bit)
            total = held[k ^ bit].astype(F32) + other.astype(F32)
            held[k ^ bit] = total.astype(BF) if low else total
    return held


def fold_landed(held, moved, bit):
    return {
        k ^ bit: (held[k ^ bit].astype(F32) + other.astype(F32)).astype(BF)
        for k, other in moved.items()
    }


def far_bits(size):
    return [1 << i for i in range(1, size.bit_length() - 1)]


def near_bits(size):
    return [1] if size > 1 else []


def exchange_blocks(blocks, axis):
    return [blocks[0]] + [swapped(blocks[k], axis, k) for k in range(1, len(blocks))]


def by_xor(value, index, axis):
    parts = [
        lax.dynamic_index_in_dim(value, index ^ k, axis, keepdims=True)
        for k in range(value.shape[axis])
    ]
    return jnp.concatenate(parts, axis=axis)


def params(mib=58):
    return pltpu.CompilerParams(vmem_limit_bytes=mib * 1024 * 1024)


def takes(micros):
    return pl.CostEstimate(flops=int(micros * 0.1e9), transcendentals=0, bytes_accessed=0)


def shape(dims, dtype):
    return jax.ShapeDtypeStruct(dims, dtype)


SMALL = pl.BlockSpec(memory_space=pltpu.SMEM)
RAW = pl.BlockSpec(memory_space=pl.ANY)


def resident(dims, buffers=None):
    zeros = (0,) * len(dims)
    mode = {} if buffers is None else {"pipeline_mode": pl.Buffered(buffers)}
    return pl.BlockSpec(dims, lambda *_: zeros, **mode)


def normalise(x_ref, gain_ref, out_ref, scale_ref):
    cols, count, piece, _ = x_ref.shape
    total = None
    for c in range(cols):
        for k in range(count):
            value = x_ref[c, k].astype(F32)
            part = jnp.sum(value * value, axis=0, keepdims=True)
            total = part if total is None else total + part
    scale = lax.rsqrt(total / D + EPS)
    scale_ref[...] = scale
    for c in range(cols):
        for k in range(count):
            value = x_ref[c, k].astype(F32) * scale * gain_ref[c, k]
            out_ref[k, c * piece : (c + 1) * piece, :] = value.astype(BF)


def turn(value, cosine, sine):
    half = value.shape[0] // 2
    first, second = value[:half], value[half:]
    return jnp.concatenate([first * cosine - second * sine, second * cosine + first * sine])


def qkv_kernel(count, shared, x_ref, gain_ref, cos_ref, sin_ref, *refs):
    q_w, kv_w = refs[:count], refs[count : 2 * count]
    norm_ref, scale_ref, sets_ref = refs[2 * count :]
    normalise(x_ref, gain_ref, norm_ref, scale_ref)
    query = keyval = None
    for k in range(count):
        normed = norm_ref[k]
        part = dot(q_w[k][...], normed, TN)
        query = part if query is None else query + part
        part = dot(kv_w[k][...], normed)
        keyval = part if keyval is None else keyval + part
    cosine, sine = cos_ref[...], sin_ref[...]
    half = query.shape[0] // 2
    kv_half = keyval.shape[0] // 2
    for h in range(2):
        for at in range(0, half, HEAD):
            value = turn(query[h * half + at : h * half + at + HEAD], cosine, sine)
            sets_ref[h, at : at + HEAD, :] = (value * (ROOT * LOG2E)).astype(BF)
        at = 0 if shared else h * HEAD
        key = turn(keyval[at : at + HEAD], cosine, sine)
        sets_ref[h, half : half + HEAD, :] = key.astype(BF)
        sets_ref[h, half + HEAD : half + 2 * HEAD, :] = keyval[
            kv_half + at : kv_half + at + HEAD
        ].astype(BF)


def qkv_project(x, gain, cosine, sine, q_w, kv_w):
    cols, count, piece, tokens = x.shape
    half = q_w[0].shape[1] // 2
    shared = kv_w[0].shape[0] == 2 * HEAD
    return pl.pallas_call(
        functools.partial(qkv_kernel, count, shared),
        out_shape=(
            shape((count, cols * piece, tokens), BF),
            shape((1, tokens), F32),
            shape((2, half + 2 * HEAD, tokens), BF),
        ),
        compiler_params=params(),
        name="qkv_project",
        cost_estimate=takes(12),
    )(x, gain, cosine, sine, *q_w, *kv_w)


def pieces_of(half, at, tile, tokens):
    if half == 1:
        return [(0, 0, tokens, False), (1, 0, at + tile, True)]
    head = [(0, 0, at, False)] if at else []
    return head + [(0, at, at + tile, True)]


def seen_of(half, at, begin, end, tile, seg_row, seg_col):
    rows = lax.broadcasted_iota(jnp.int32, (end - begin, tile), 0) + begin
    cols = lax.broadcasted_iota(jnp.int32, (end - begin, tile), 1) + at
    seen = rows <= cols
    if half == 1:
        seen = seen & (seg_col[begin:end] == seg_row[:, at : at + tile])
    return seen


def place(parity, own_ref, other_ref, sets):
    sets[parity] = own_ref[...]
    sets[1 - parity] = other_ref[...]


def attend_kernel(
    tile, parity_ref, own_ref, other_ref, seg_row, seg_col, mine_ref, send_ref, lse_ref, sets, rows
):
    tokens = own_ref.shape[-1]
    heads = pl.num_programs(0)
    head = pl.program_id(0)
    parity = parity_ref[0]
    half_rows = own_ref.shape[0] - 2 * HEAD

    @pl.when(head == 0)
    def _():
        place(parity, own_ref, other_ref, sets)
        for half in range(2):
            keys = sets[half, half_rows : half_rows + HEAD, :]
            rows[half] = keys.astype(F32).T.astype(BF)

    at_head = pl.ds(pl.multiple_of(head * HEAD, 16), HEAD)
    for half in range(2):
        for at in range(0, tokens, tile):
            span = slice(at, at + tile)
            query = sets[half, at_head, span]
            pieces = pieces_of(half, at, tile, tokens)
            scores = []
            for which, begin, end, masked in pieces:
                part = dot(rows[which, begin:end, :], query)
                if masked:
                    part = jnp.where(
                        seen_of(half, at, begin, end, tile, seg_row, seg_col), part, NEG
                    )
                scores.append(part)
            peak = functools.reduce(
                jnp.maximum, [jnp.max(s, axis=0, keepdims=True) for s in scores]
            )
            total = out = None
            for (which, begin, end, _), part in zip(pieces, scores):
                weights = jnp.exp2(part - peak)
                mass = jnp.sum(weights, axis=0, keepdims=True)
                value = dot(sets[which, half_rows + HEAD :, begin:end], weights.astype(BF))
                total = mass if total is None else total + mass
                out = value if out is None else out + value
            out = (out / total).astype(BF)
            lse_ref[half, 0, :, span] = peak + jnp.log2(total)

            @pl.when(parity == half)
            def _():
                mine_ref[at_head, span] = out

            @pl.when(parity != half)
            def _():
                send_ref[at_head, span] = out


def attend(parity, own, other, seg):
    depth, tokens = own.shape
    half_rows = depth - 2 * HEAD
    heads = half_rows // HEAD
    tile = min(256, tokens)
    out = resident((half_rows, tokens))
    return pl.pallas_call(
        functools.partial(attend_kernel, tile),
        out_shape=(
            shape((half_rows, tokens), BF),
            shape((half_rows, tokens), BF),
            shape((2, heads, 1, tokens), F32),
        ),
        grid=(heads,),
        in_specs=[
            SMALL,
            resident((depth, tokens)),
            resident((depth, tokens)),
            resident((1, tokens)),
            resident((tokens, 1)),
        ],
        out_specs=(out, out, pl.BlockSpec((2, 1, 1, tokens), lambda h: (0, h, 0, 0))),
        scratch_shapes=[
            pltpu.VMEM((2, depth, tokens), BF),
            pltpu.VMEM((2, tokens, HEAD), BF),
        ],
        compiler_params=params(),
        name="attend",
        cost_estimate=takes(27),
    )(parity, own, other, seg[None, :], seg[:, None])


def attend_back_kernel(
    tile,
    parity_ref,
    own_ref,
    other_ref,
    own_out,
    other_out,
    own_grad,
    other_grad,
    lse_ref,
    seg_row,
    seg_col,
    mine_ref,
    send_ref,
    sets,
    outs,
    grads,
    rows,
    key_acc,
    value_acc,
):
    tokens = own_ref.shape[-1]
    heads = pl.num_programs(0)
    head = pl.program_id(0)
    parity = parity_ref[0]
    half_rows = own_ref.shape[0] - 2 * HEAD

    @pl.when(head == 0)
    def _():
        place(parity, own_ref, other_ref, sets)
        place(parity, own_out, other_out, outs)
        place(parity, own_grad, other_grad, grads)
        for half in range(2):
            for i in range(2):
                at = half_rows + i * HEAD
                rows[i, half] = sets[half, at : at + HEAD, :].astype(F32).T.astype(BF)
        key_acc[...] = jnp.zeros_like(key_acc)
        value_acc[...] = jnp.zeros_like(value_acc)

    at_head = pl.ds(pl.multiple_of(head * HEAD, 16), HEAD)
    for half in range(2):
        for at in range(0, tokens, tile):
            span = slice(at, at + tile)
            query = sets[half, at_head, span]
            grad = grads[half, at_head, span]
            lse = lse_ref[half, 0, :, span]
            delta = jnp.sum(
                grad.astype(F32) * outs[half, at_head, span].astype(F32), axis=0, keepdims=True
            )
            total = None
            for which, begin, end, masked in pieces_of(half, at, tile, tokens):
                part = dot(rows[0, which, begin:end, :], query)
                if masked:
                    part = jnp.where(
                        seen_of(half, at, begin, end, tile, seg_row, seg_col), part, NEG
                    )
                weights = jnp.exp2(part - lse)
                dprod = dot(rows[1, which, begin:end, :], grad)
                dscore = (weights * (dprod - delta)).astype(BF)
                value_acc[which, :, begin:end] += dot(grad, weights.astype(BF), NT)
                key_acc[which, :, begin:end] += dot(query, dscore, NT)
                more = dot(sets[which, half_rows : half_rows + HEAD, begin:end], dscore)
                total = more if total is None else total + more
            total = (total * ROOT).astype(BF)

            @pl.when(parity == half)
            def _():
                mine_ref[at_head, span] = total

            @pl.when(parity != half)
            def _():
                send_ref[at_head, span] = total

    @pl.when(head == heads - 1)
    def _():
        for ref, which in ((mine_ref, parity), (send_ref, 1 - parity)):
            ref[half_rows : half_rows + HEAD, :] = (key_acc[which] * LN2).astype(BF)
            ref[half_rows + HEAD :, :] = value_acc[which].astype(BF)


def attend_back(parity, own, other, own_out, other_out, own_grad, other_grad, lse, seg):
    depth, tokens = own.shape
    half_rows = depth - 2 * HEAD
    heads = half_rows // HEAD
    tile = min(256, tokens)
    full, part = resident((depth, tokens)), resident((half_rows, tokens))
    return pl.pallas_call(
        functools.partial(attend_back_kernel, tile),
        out_shape=(shape((depth, tokens), BF), shape((depth, tokens), BF)),
        grid=(heads,),
        in_specs=[
            SMALL,
            full,
            full,
            part,
            part,
            part,
            part,
            pl.BlockSpec((2, 1, 1, tokens), lambda h: (0, h, 0, 0)),
            resident((1, tokens)),
            resident((tokens, 1)),
        ],
        out_specs=(full, full),
        scratch_shapes=[
            pltpu.VMEM((2, depth, tokens), BF),
            pltpu.VMEM((2, half_rows, tokens), BF),
            pltpu.VMEM((2, half_rows, tokens), BF),
            pltpu.VMEM((2, 2, tokens, HEAD), BF),
            pltpu.VMEM((2, HEAD, tokens), F32),
            pltpu.VMEM((2, HEAD, tokens), F32),
        ],
        compiler_params=params(),
        name="attend_back",
        cost_estimate=takes(37),
    )(
        parity,
        own,
        other,
        own_out,
        other_out,
        own_grad,
        other_grad,
        lse,
        seg[None, :],
        seg[:, None],
    )


def halves_at(parity, half_rows):
    mine = pl.ds(pl.multiple_of(parity * half_rows, 16), half_rows)
    other = pl.ds(pl.multiple_of((1 - parity) * half_rows, 16), half_rows)
    return mine, other


def mix_out_kernel(count, parity_ref, own_ref, other_ref, *refs):
    weights, out_ref = refs[:count], refs[count]
    cols, _, piece, _ = out_ref.shape
    mine, other = halves_at(parity_ref[0], own_ref.shape[0])
    for k in range(count):
        part = dot(weights[k][mine, :], own_ref[...], TN)
        part = part + dot(weights[k][other, :], other_ref[...], TN)
        for c in range(cols):
            out_ref[c, k] = part[c * piece : (c + 1) * piece].astype(BF)


def mix_out(parity, own, other, weights, cols):
    count = len(weights)
    piece = weights[0].shape[1] // cols
    vmem = pl.BlockSpec(memory_space=pltpu.VMEM)
    return pl.pallas_call(
        functools.partial(mix_out_kernel, count),
        out_shape=shape((cols, count, piece, own.shape[1]), BF),
        in_specs=[SMALL] + [vmem] * (2 + count),
        compiler_params=params(),
        name="mix_out",
        cost_estimate=takes(10),
    )(parity, own, other, *weights)


def mix_back_kernel(count, parts, parity_ref, *refs):
    x_refs, weights = refs[:parts], refs[parts : parts + count]
    rows_ref, own_ref, other_ref = refs[parts + count :]
    for i, x_ref in enumerate(x_refs):
        cols, _, piece, tokens = x_ref.shape
        for c in range(cols):
            for k in range(count):
                rows_ref[k, c * piece : (c + 1) * piece, i * tokens : (i + 1) * tokens] = x_ref[
                    c, k
                ]
    mine, other = halves_at(parity_ref[0], own_ref.shape[0])
    for at, out_ref in ((other, other_ref), (mine, own_ref)):
        total = None
        for k in range(count):
            part = dot(weights[k][at, :], rows_ref[k])
            total = part if total is None else total + part
        out_ref[...] = total.astype(BF)


def mix_back(parity, x_parts, weights):
    parts = len(x_parts)
    cols, count, piece, tokens = x_parts[0].shape
    tokens = tokens * parts
    half_rows = weights[0].shape[0] // 2
    vmem = pl.BlockSpec(memory_space=pltpu.VMEM)
    return pl.pallas_call(
        functools.partial(mix_back_kernel, count, parts),
        out_shape=(
            shape((count, cols * piece, tokens), BF),
            shape((half_rows, tokens), BF),
            shape((half_rows, tokens), BF),
        ),
        in_specs=[SMALL] + [vmem] * (parts + count),
        compiler_params=params(),
        name="mix_back",
        cost_estimate=takes(9),
    )(parity, *x_parts, *weights)


def fan_kernel(count, x_ref, *refs):
    weights, out_ref = refs[:count], refs[count]
    cols, _, piece, _ = out_ref.shape
    for k in range(count):
        part = dot(weights[k][...], x_ref[...], TN)
        for c in range(cols):
            out_ref[c, k] = part[c * piece : (c + 1) * piece].astype(BF)


def fan_out(weights, x, cols):
    count = len(weights)
    piece = weights[0].shape[1] // cols
    return pl.pallas_call(
        functools.partial(fan_kernel, count),
        out_shape=shape((cols, count, piece, x.shape[1]), BF),
        compiler_params=params(),
        name="fan_out",
        cost_estimate=takes(17),
    )(x, *weights)


def norm_back(grads, k, x_ref, gain_ref, scale, coef, share_ref, gain_share_ref):
    cols, _, piece, _ = x_ref.shape
    for c in range(cols):
        grad = grads[c * piece : (c + 1) * piece]
        value = x_ref[c, k].astype(F32)
        gain_share_ref[c, k] = jnp.sum(grad * (value * scale), axis=1, keepdims=True)
        share_ref[c, k] = ((grad * gain_ref[c, k]) * scale - value * coef).astype(BF)


def ff_kernel(count, chained, x_ref, g_ref, gain_ref, *refs):
    gate_w, up_w, down_w = refs[:count], refs[count : 2 * count], refs[2 * count : 3 * count]
    refs = refs[3 * count + (5 if chained else 0) :]
    norm_ref, rows_ref, act_ref, dgate_ref, dup_ref, share_ref, gain_share_ref = refs[:7]
    scale_ref, inner_ref, back_ref = refs[7:]
    cols, _, piece, _ = x_ref.shape
    step = pl.program_id(0)

    @pl.when(step == 0)
    def _():
        normalise(x_ref, gain_ref, norm_ref, scale_ref)
        for c in range(cols):
            for k in range(count):
                rows_ref[k, c * piece : (c + 1) * piece, :] = g_ref[c, k]
        inner_ref[...] = jnp.zeros_like(inner_ref)
        back_ref[...] = jnp.zeros_like(back_ref)

    def summed(weights, ref):
        total = None
        for k in range(count):
            part = dot(weights[k][...], ref[k])
            total = part if total is None else total + part
        return total

    gate = summed(gate_w, norm_ref)
    up = summed(up_w, norm_ref)
    sigma = jax.nn.sigmoid(gate)
    silu = gate * sigma
    act_ref[...] = (silu * up).astype(BF)
    grad = summed(down_w, rows_ref)
    dup = grad * silu
    dgate = grad * up * (sigma + silu * (1.0 - sigma))
    inner_ref[...] += jnp.sum(dgate * gate + dup * up, axis=0, keepdims=True)
    dgate_ref[...] = dgate.astype(BF)
    dup_ref[...] = dup.astype(BF)
    for k in range(count):
        back_ref[k] += dot(gate_w[k][...], dgate_ref[...], TN) + dot(
            up_w[k][...], dup_ref[...], TN
        )

    @pl.when(step == pl.num_programs(0) - 1)
    def _():
        scale = scale_ref[...]
        coef = scale * scale * inner_ref[...] / D
        for k in range(count):
            norm_back(back_ref[k], k, x_ref, gain_ref, scale, coef, share_ref, gain_share_ref)


def feed_forward(x, g, part, parts, gain, gate_w, up_w, down_w, before):
    cols, count, piece, tokens = x.shape
    width, depth = gate_w[0].shape
    tile = 432 if width % 432 == 0 else width
    g_spec = pl.BlockSpec(x.shape, lambda n: (0, 0, 0, part), pipeline_mode=pl.Buffered(1))
    rows = (count, cols * piece, tokens)
    rows_spec = pl.BlockSpec(rows, lambda n: (0, 0, part), pipeline_mode=pl.Buffered(1))
    w_spec = pl.BlockSpec((tile, depth), lambda n: (n, 0))
    h_spec = pl.BlockSpec((tile, tokens), lambda n: (n, part))
    rows_all = shape((count, cols * piece, tokens * parts), BF)
    hidden = shape((width, tokens * parts), BF)
    first = 3 + 3 * count
    return pl.pallas_call(
        functools.partial(ff_kernel, count, bool(before)),
        out_shape=(
            rows_all,
            rows_all,
            hidden,
            hidden,
            hidden,
            shape(x.shape, BF),
            shape(gain.shape, F32),
        ),
        grid=(width // tile,),
        in_specs=[resident(x.shape, 1), g_spec, resident(gain.shape, 1)]
        + [w_spec] * (3 * count)
        + [RAW] * len(before),
        out_specs=(
            rows_spec,
            rows_spec,
            h_spec,
            h_spec,
            h_spec,
            resident(x.shape, 1),
            resident(gain.shape, 1),
        ),
        scratch_shapes=[
            pltpu.VMEM((1, tokens), F32),
            pltpu.VMEM((1, tokens), F32),
            pltpu.VMEM(rows, F32),
        ],
        input_output_aliases={first + i: i for i in range(len(before))},
        compiler_params=params(60),
        name="feed_forward",
        cost_estimate=takes(42),
    )(x, g, gain, *gate_w, *up_w, *down_w, *before)


def qkv_back_kernel(
    count,
    shared,
    parity_ref,
    x_ref,
    gain_ref,
    scale_ref,
    cos_ref,
    sin_ref,
    sets_ref,
    own_ref,
    other_ref,
    *refs,
):
    q_w, kv_w = refs[:count], refs[count : 2 * count]
    dq_ref, dkv_ref, share_ref, gain_share_ref = refs[2 * count :]
    parity = parity_ref[0]
    half_rows = own_ref.shape[0] - 2 * HEAD
    kv_half = dkv_ref.shape[0] // 2
    cosine, sine = cos_ref[...], -sin_ref[...]
    inner = None
    folded = None
    for grads, which in ((own_ref, parity), (other_ref, 1 - parity)):
        for at in range(0, half_rows + 2 * HEAD, HEAD):
            value = grads[at : at + HEAD, :].astype(F32)
            part = value * sets_ref[which, at : at + HEAD, :].astype(F32)
            part = jnp.sum(part, axis=0, keepdims=True)
            if at < half_rows:
                part = part * (1.0 / (ROOT * LOG2E))
                start = pl.multiple_of(which * half_rows + at, 16)
                dq_ref[pl.ds(start, HEAD), :] = turn(value, cosine, sine).astype(BF)
            else:
                is_key = at == half_rows
                raw = turn(value, cosine, sine) if is_key else value
                base = 0 if is_key else kv_half
                if not shared:
                    start = pl.multiple_of(base + which * HEAD, 16)
                    dkv_ref[pl.ds(start, HEAD), :] = raw.astype(BF)
                elif folded is None or at not in folded:
                    folded = {**(folded or {}), at: raw}
                else:
                    dkv_ref[base : base + HEAD, :] = (folded[at] + raw).astype(BF)
            inner = part if inner is None else inner + part
    scale = scale_ref[...]
    coef = scale * scale * inner / D
    for k in range(count):
        grads = dot(q_w[k][...], dq_ref[...]) + dot(kv_w[k][...], dkv_ref[...], TN)
        norm_back(grads, k, x_ref, gain_ref, scale, coef, share_ref, gain_share_ref)


def qkv_back(parity, x, gain, scale, cosine, sine, sets, own, other, q_w, kv_w):
    cols, count, piece, tokens = x.shape
    shared = kv_w[0].shape[0] == 2 * HEAD
    vmem = pl.BlockSpec(memory_space=pltpu.VMEM)
    return pl.pallas_call(
        functools.partial(qkv_back_kernel, count, shared),
        out_shape=(
            shape((q_w[0].shape[1], tokens), BF),
            shape((kv_w[0].shape[0], tokens), BF),
            shape(x.shape, BF),
            shape(gain.shape, F32),
        ),
        in_specs=[SMALL] + [vmem] * (8 + 2 * count),
        compiler_params=params(),
        name="qkv_back",
        cost_estimate=takes(17),
    )(parity, x, gain, scale, cosine, sine, sets, own, other, *q_w, *kv_w)


def rope_parts(positions):
    half = HEAD // 2
    freq = THETA ** (-jnp.arange(half, dtype=F32) * 2.0 / HEAD)
    angle = freq[:, None] * positions.astype(F32)[None, :]
    return (jnp.cos(angle), jnp.sin(angle))


def spread_cols(value):
    return lax.all_gather(value, "col", axis=0, tiled=False)


def sum_cols(value):
    return lax.psum_scatter(value, "col", scatter_dimension=0, tiled=False)


def sent_over_dp(value):
    low = value.astype(BF)
    size = lax.axis_size("dp")
    others = [
        lax.ppermute(low, "dp", [(i, (i + step) % size) for i in range(size)])
        for step in range(1, size)
    ]
    return [low] + others


def summed_up(parts):
    total = parts[0].astype(F32)
    for other in parts[1:]:
        total = total + other.astype(F32)
    return total


def over_dp(value):
    return summed_up(sent_over_dp(value))


def body(
    layer_input,
    attn_gain,
    mlp_gain,
    query_weight,
    key_weight,
    value_weight,
    mix_weight,
    gate_weight,
    up_weight,
    down_weight,
    output_grad,
    segment_ids,
    position_ids,
):
    rows = segment_ids.shape[0]
    count = lax.axis_size("row")
    cols = lax.axis_size("col")
    piece = layer_input.shape[1]
    row = lax.axis_index("row")
    parity = (row % 2).astype(jnp.int32)
    own_core = parity.reshape(1)
    q_half = query_weight.shape[1] // 2
    near, far = near_bits(count), far_bits(count)
    far_mask = far[-1]

    def row_tokens(value):
        turned = value.T
        outgoing = [
            lax.dynamic_slice(turned, (0, (row ^ k) * rows), (piece, rows)) for k in range(count)
        ]
        return jnp.stack(exchange_blocks(outgoing, "row"))

    def all_tokens(blocks):
        got = exchange_blocks([blocks[k] for k in range(count)], "row")
        result = jnp.zeros((piece, count * rows), blocks.dtype)
        for k in range(count):
            result = lax.dynamic_update_slice(result, got[k], (0, (row ^ k) * rows))
        return result.T

    def listed(blocks):
        return [blocks[k] for k in range(count)]

    source_own = row_tokens(layer_input)
    kv_weight = jnp.concatenate([key_weight.T, value_weight.T])
    q_first = spread({0: query_weight}, "row", far)
    kv_first = spread({0: kv_weight}, "row", far)
    mix_first = spread({0: mix_weight}, "row", far)
    gate_first = spread({0: gate_weight.T}, "row", far)
    up_first = spread({0: up_weight.T}, "row", far)
    down_first = spread({0: down_weight}, "row", far)
    q_blocks = spread(q_first, "row", near)
    kv_blocks = spread(kv_first, "row", near)

    gains = lax.all_gather(jnp.stack([attn_gain, mlp_gain]), ("row", "col"), axis=1, tiled=True)
    gains = gains.reshape(2, count, cols, piece)
    gains = by_xor(gains, row, 1).swapaxes(1, 2)[..., None]
    gain_one, gain_two = gains[0], gains[1]

    cosine, sine = rope_parts(position_ids)
    other_seg = swapped(segment_ids, "row", 1)
    seg = jnp.where(parity == 0, other_seg, segment_ids)

    source = spread_cols(source_own)
    source, q_blocks, kv_blocks, mix_first, gate_first, gain_one, cosine, sine, seg = together(
        source, q_blocks, kv_blocks, mix_first, gate_first, gain_one, cosine, sine, seg
    )
    grad_own = row_tokens(output_grad)
    grad_own, source = together(grad_own, source)
    grad_all = spread_cols(grad_own)
    norm_one, scale_one, sets = qkv_project(
        source, gain_one, cosine, sine, listed(q_blocks), listed(kv_blocks)
    )
    own_set = lax.dynamic_index_in_dim(sets, parity, 0, keepdims=False)
    other_set = swapped(lax.dynamic_index_in_dim(sets, 1 - parity, 0, keepdims=False), "row", 1)
    attn_mine, attn_send, lse = attend(own_core, own_set, other_set, seg)
    attn_other = swapped(attn_send, "row", 1)
    mix_blocks = spread(mix_first, "row", near)
    attn_mine, attn_other, mix_blocks, up_first = together(
        attn_mine, attn_other, mix_blocks, up_first
    )
    attn_part = mix_out(own_core, attn_mine, attn_other, listed(mix_blocks), cols)
    attn_part, grad_all = together(attn_part, grad_all)
    attn_sum = sum_cols(attn_part)
    gate_blocks = spread(gate_first, "row", near)
    up_blocks = spread(up_first, "row", near)
    down_blocks = spread(down_first, "row", near)
    attn_sum, gate_blocks, up_blocks, down_blocks = together(
        attn_sum, gate_blocks, up_blocks, down_blocks
    )
    residual_own = source_own.astype(F32) + attn_sum.astype(F32)

    parts = 2 if rows % 256 == 0 else 1
    size = rows // parts
    spans = [slice(i * size, (i + 1) * size) for i in range(parts)]
    residual_low = residual_own.astype(BF)
    residual = [spread_cols(residual_low[..., span]) for span in spans]
    before, shares = (), []
    gain_share_two = 0.0
    for i in range(parts):
        out = feed_forward(
            residual[i],
            grad_all,
            i,
            parts,
            gain_two,
            listed(gate_blocks),
            listed(up_blocks),
            listed(down_blocks),
            before,
        )
        before = out[:5]
        shares.append(out[5])
        gain_share_two = gain_share_two + out[6]
    norm_two, grad_rows, act, dgate, dup = before
    share_sums = [sum_cols(share) for share in shares]
    down_grads = {k: dot(act, grad_rows[k], NT).astype(BF) for k in range(count)}
    gate_grads = {k: dot(dgate, norm_two[k], NT).astype(BF) for k in range(count)}
    up_grads = {k: dot(dup, norm_two[k], NT).astype(BF) for k in range(count)}
    down_grads = fold(down_grads, "row", near)
    gate_grads = fold(gate_grads, "row", near)
    up_grads = fold(up_grads, "row", near)
    *share_sums, down_grads, gate_grads, up_grads = together(
        *share_sums, down_grads, gate_grads, up_grads
    )
    residual_grad_own = grad_own.astype(F32) + jnp.concatenate(share_sums, axis=2).astype(F32)
    down_total = fold(down_grads, "row", far)[0]
    gate_total = fold(gate_grads, "row", far)[0]

    mix_cols = spread_cols(residual_grad_own.astype(BF))
    ff_part = fan_out(listed(down_blocks), act, cols)
    down_total = over_dp(down_total)
    mix_cols, ff_part, down_total, gate_total, up_grads = together(
        mix_cols, ff_part, down_total, gate_total, up_grads
    )
    up_total = fold(up_grads, "row", far)[0]
    gate_total = over_dp(gate_total)
    mix_rows, grad_mine, grad_send = mix_back(own_core, [mix_cols], listed(mix_blocks))
    ff_sum = sum_cols(ff_part)
    grad_other = swapped(grad_send, "row", 1)
    back_mine, back_send = attend_back(
        own_core, own_set, other_set, attn_mine, attn_send, grad_mine, grad_other, lse, seg
    )
    back_other = swapped(back_send, "row", 1)
    back_other, up_total, gate_total, down_total = together(
        back_other, up_total, gate_total, down_total
    )
    cut = up_total.shape[0] * 5 // 9 // 16 * 16
    up_head, up_tail = over_dp(up_total[:cut]), sent_over_dp(up_total[cut:])
    dq, dkv, share, gain_share_one = qkv_back(
        own_core,
        source,
        gain_one,
        scale_one,
        cosine,
        sine,
        sets,
        back_mine,
        back_other,
        listed(q_blocks),
        listed(kv_blocks),
    )
    share, attn_mine, mix_rows = together(share, attn_mine, mix_rows)
    attn_low = jnp.concatenate(
        [
            jnp.where(parity == 0, attn_mine, attn_other),
            jnp.where(parity == 0, attn_other, attn_mine),
        ]
    )
    mix_odd = {k: dot(attn_low, mix_rows[k], NT).astype(BF) for k in range(1, count, 2)}
    gain_shares = jnp.stack([gain_share_one[..., 0], gain_share_two[..., 0]], axis=2)
    share, ff_sum, mix_odd, up_head, gain_shares = together(
        share, ff_sum, mix_odd, up_head, gain_shares
    )
    input_sum = sum_cols(share)

    bits = near + far[::-1]
    gain_shares = fold({k: gain_shares[:, k] for k in range(count)}, "row", bits, low=False)[0]
    share, dq, dkv, attn_low, mix_rows = together(share, dq, dkv, attn_low, mix_rows)
    mix_even = {k: dot(attn_low, mix_rows[k], NT).astype(BF) for k in range(0, count, 2)}
    mix_near = fold({**mix_even, **mix_odd}, "row", near)
    dq, dkv, mix_near = together(dq, dkv, mix_near)
    mix_moved = {k: swapped(mix_near[k], "row", far_mask) for k in mix_near if k & far_mask}
    q_near = fold({k: dot(norm_one[k], dq, NT).astype(BF) for k in range(count)}, "row", near)
    kv_near = fold({k: dot(dkv, norm_one[k], NT).astype(BF) for k in range(count)}, "row", near)
    ff_sum, gain_shares, q_near, kv_near, up_tail, mix_near, mix_moved = together(
        ff_sum, gain_shares, q_near, kv_near, up_tail, mix_near, mix_moved
    )
    mix_far = fold_landed(mix_near, mix_moved, far_mask)
    mix_total = over_dp(fold(mix_far, "row", far[::-1][1:])[0])
    q_far = fold(q_near, "row", far)[0]
    kv_far = fold(kv_near, "row", far)[0]
    q_total, kv_total = over_dp(q_far), over_dp(kv_far)
    output_own = (residual_own + ff_sum.astype(F32)).astype(BF)
    layer_output = all_tokens(output_own)

    gain_shares = by_xor(gain_shares, lax.axis_index("col"), 0)
    gain_shares = {c: gain_shares[c] for c in range(cols)}
    gain_shares = fold(gain_shares, "col", near_bits(cols) + far_bits(cols), low=False)[0]
    gain_totals = over_dp(gain_shares)
    up_total = jnp.concatenate([up_head, summed_up(up_tail)])
    input_sum, q_total, kv_total, mix_total, gain_totals, layer_output, up_total = together(
        input_sum, q_total, kv_total, mix_total, gain_totals, layer_output, up_total
    )

    input_grad = all_tokens((residual_grad_own + input_sum.astype(F32)).astype(BF)).astype(F32)
    kv_rows = kv_total.shape[0] // 2
    return (
        layer_output,
        input_grad,
        gain_totals[0],
        gain_totals[1],
        q_total,
        kv_total[:kv_rows].T,
        kv_total[kv_rows:].T,
        mix_total,
        gate_total.T,
        up_total.T,
        down_total,
    )


def solution(mesh):
    return jax.shard_map(
        body,
        mesh=mesh,
        in_specs=(
            P("dp", ("row", "col")),
            P(("row", "col")),
            P(("row", "col")),
            P("row", "col"),
            P("row", "col"),
            P("row", "col"),
            P("col", "row"),
            P("row", "col"),
            P("row", "col"),
            P("col", "row"),
            P("dp", ("row", "col")),
            P(("dp", "row")),
            P(("dp", "row")),
        ),
        out_specs=(
            P("dp", ("row", "col")),
            P("dp", ("row", "col")),
            P(("row", "col")),
            P(("row", "col")),
            P("row", "col"),
            P("row", "col"),
            P("row", "col"),
            P("col", "row"),
            P("row", "col"),
            P("row", "col"),
            P("col", "row"),
        ),
        check_vma=False,
    )
```

```python
import functools

import jax
import jax.numpy as jnp
from jax import lax
from jax.experimental import pallas as pl
from jax.experimental.pallas import tpu as pltpu
from jax.sharding import PartitionSpec as P

D = 2560
HEAD = 80
EPS = 1e-05
THETA = 10000.0
NEG = -1e30
LOG2E = 1.4426950408889634
LN2 = 0.6931471805599453
ROOT = HEAD ** (-0.5)
BF = jnp.bfloat16
F32 = jnp.float32
NN = (((1,), (0,)), ((), ()))
TN = (((0,), (0,)), ((), ()))
NT = (((1,), (1,)), ((), ()))


def dot(left, right, dims=NN):
    return lax.dot_general(left, right, dims, preferred_element_type=F32)


def together(*values):
    return lax.optimization_barrier(values)


def swapped(value, axis, mask):
    size = lax.axis_size(axis)
    return lax.ppermute(value, axis, [(i, i ^ mask) for i in range(size)])


def spread(blocks, axis, bits):
    blocks = dict(blocks)
    for bit in bits:
        for k in list(blocks):
            blocks[k | bit] = swapped(blocks[k], axis, bit)
    return blocks


def fold(blocks, axis, bits, low=True):
    held = dict(blocks)
    for bit in bits:
        for k in [k for k in held if k & bit]:
            other = swapped(held.pop(k), axis, bit)
            total = held[k ^ bit].astype(F32) + other.astype(F32)
            held[k ^ bit] = total.astype(BF) if low else total
    return held


def fold_landed(held, moved, bit):
    return {
        k ^ bit: (held[k ^ bit].astype(F32) + other.astype(F32)).astype(BF)
        for k, other in moved.items()
    }


def far_bits(size):
    return [1 << i for i in range(1, size.bit_length() - 1)]


def near_bits(size):
    return [1] if size > 1 else []


def exchange_blocks(blocks, axis):
    return [blocks[0]] + [swapped(blocks[k], axis, k) for k in range(1, len(blocks))]


def by_xor(value, index, axis):
    parts = [
        lax.dynamic_index_in_dim(value, index ^ k, axis, keepdims=True)
        for k in range(value.shape[axis])
    ]
    return jnp.concatenate(parts, axis=axis)


def params(mib=58):
    return pltpu.CompilerParams(vmem_limit_bytes=mib * 1024 * 1024)


def takes(micros):
    return pl.CostEstimate(flops=int(micros * 0.1e9), transcendentals=0, bytes_accessed=0)


def shape(dims, dtype):
    return jax.ShapeDtypeStruct(dims, dtype)


SMALL = pl.BlockSpec(memory_space=pltpu.SMEM)
RAW = pl.BlockSpec(memory_space=pl.ANY)


def resident(dims, buffers=None):
    zeros = (0,) * len(dims)
    mode = {} if buffers is None else {"pipeline_mode": pl.Buffered(buffers)}
    return pl.BlockSpec(dims, lambda *_: zeros, **mode)


def normalise(x_ref, gain_ref, out_ref, scale_ref):
    cols, count, piece, _ = x_ref.shape
    total = None
    for c in range(cols):
        for k in range(count):
            value = x_ref[c, k].astype(F32)
            part = jnp.sum(value * value, axis=0, keepdims=True)
            total = part if total is None else total + part
    scale = lax.rsqrt(total / D + EPS)
    scale_ref[...] = scale
    for c in range(cols):
        for k in range(count):
            value = x_ref[c, k].astype(F32) * scale * gain_ref[c, k]
            out_ref[k, c * piece : (c + 1) * piece, :] = value.astype(BF)


def turn(value, cosine, sine):
    half = value.shape[0] // 2
    first, second = value[:half], value[half:]
    return jnp.concatenate([first * cosine - second * sine, second * cosine + first * sine])


def qkv_kernel(count, shared, x_ref, gain_ref, cos_ref, sin_ref, *refs):
    q_w, kv_w = refs[:count], refs[count : 2 * count]
    norm_ref, scale_ref, sets_ref = refs[2 * count :]
    normalise(x_ref, gain_ref, norm_ref, scale_ref)
    query = keyval = None
    for k in range(count):
        normed = norm_ref[k]
        part = dot(q_w[k][...], normed, TN)
        query = part if query is None else query + part
        part = dot(kv_w[k][...], normed)
        keyval = part if keyval is None else keyval + part
    cosine, sine = cos_ref[...], sin_ref[...]
    half = query.shape[0] // 2
    kv_half = keyval.shape[0] // 2
    for h in range(2):
        for at in range(0, half, HEAD):
            value = turn(query[h * half + at : h * half + at + HEAD], cosine, sine)
            sets_ref[h, at : at + HEAD, :] = (value * (ROOT * LOG2E)).astype(BF)
        at = 0 if shared else h * HEAD
        key = turn(keyval[at : at + HEAD], cosine, sine)
        sets_ref[h, half : half + HEAD, :] = key.astype(BF)
        sets_ref[h, half + HEAD : half + 2 * HEAD, :] = keyval[
            kv_half + at : kv_half + at + HEAD
        ].astype(BF)


def qkv_project(x, gain, cosine, sine, q_w, kv_w):
    cols, count, piece, tokens = x.shape
    half = q_w[0].shape[1] // 2
    shared = kv_w[0].shape[0] == 2 * HEAD
    return pl.pallas_call(
        functools.partial(qkv_kernel, count, shared),
        out_shape=(
            shape((count, cols * piece, tokens), BF),
            shape((1, tokens), F32),
            shape((2, half + 2 * HEAD, tokens), BF),
        ),
        compiler_params=params(),
        name="qkv_project",
        cost_estimate=takes(12),
    )(x, gain, cosine, sine, *q_w, *kv_w)


def pieces_of(half, at, tile, tokens):
    if half == 1:
        return [(0, 0, tokens, False), (1, 0, at + tile, True)]
    head = [(0, 0, at, False)] if at else []
    return head + [(0, at, at + tile, True)]


def seen_of(half, at, begin, end, tile, seg_row, seg_col):
    rows = lax.broadcasted_iota(jnp.int32, (end - begin, tile), 0) + begin
    cols = lax.broadcasted_iota(jnp.int32, (end - begin, tile), 1) + at
    seen = rows <= cols
    if half == 1:
        seen = seen & (seg_col[begin:end] == seg_row[:, at : at + tile])
    return seen


def place(parity, own_ref, other_ref, sets):
    sets[parity] = own_ref[...]
    sets[1 - parity] = other_ref[...]


def attend_kernel(
    tile, parity_ref, own_ref, other_ref, seg_row, seg_col, mine_ref, send_ref, lse_ref, sets, rows
):
    tokens = own_ref.shape[-1]
    heads = pl.num_programs(0)
    head = pl.program_id(0)
    parity = parity_ref[0]
    half_rows = own_ref.shape[0] - 2 * HEAD

    @pl.when(head == 0)
    def _():
        place(parity, own_ref, other_ref, sets)
        for half in range(2):
            keys = sets[half, half_rows : half_rows + HEAD, :]
            rows[half] = keys.astype(F32).T.astype(BF)

    at_head = pl.ds(pl.multiple_of(head * HEAD, 16), HEAD)
    for half in range(2):
        for at in range(0, tokens, tile):
            span = slice(at, at + tile)
            query = sets[half, at_head, span]
            pieces = pieces_of(half, at, tile, tokens)
            scores = []
            for which, begin, end, masked in pieces:
                part = dot(rows[which, begin:end, :], query)
                if masked:
                    part = jnp.where(
                        seen_of(half, at, begin, end, tile, seg_row, seg_col), part, NEG
                    )
                scores.append(part)
            peak = functools.reduce(
                jnp.maximum, [jnp.max(s, axis=0, keepdims=True) for s in scores]
            )
            total = out = None
            for (which, begin, end, _), part in zip(pieces, scores):
                weights = jnp.exp2(part - peak)
                mass = jnp.sum(weights, axis=0, keepdims=True)
                value = dot(sets[which, half_rows + HEAD :, begin:end], weights.astype(BF))
                total = mass if total is None else total + mass
                out = value if out is None else out + value
            out = (out / total).astype(BF)
            lse_ref[half, 0, :, span] = peak + jnp.log2(total)

            @pl.when(parity == half)
            def _():
                mine_ref[at_head, span] = out

            @pl.when(parity != half)
            def _():
                send_ref[at_head, span] = out


def attend(parity, own, other, seg):
    depth, tokens = own.shape
    half_rows = depth - 2 * HEAD
    heads = half_rows // HEAD
    tile = min(256, tokens)
    out = resident((half_rows, tokens))
    return pl.pallas_call(
        functools.partial(attend_kernel, tile),
        out_shape=(
            shape((half_rows, tokens), BF),
            shape((half_rows, tokens), BF),
            shape((2, heads, 1, tokens), F32),
        ),
        grid=(heads,),
        in_specs=[
            SMALL,
            resident((depth, tokens)),
            resident((depth, tokens)),
            resident((1, tokens)),
            resident((tokens, 1)),
        ],
        out_specs=(out, out, pl.BlockSpec((2, 1, 1, tokens), lambda h: (0, h, 0, 0))),
        scratch_shapes=[
            pltpu.VMEM((2, depth, tokens), BF),
            pltpu.VMEM((2, tokens, HEAD), BF),
        ],
        compiler_params=params(),
        name="attend",
        cost_estimate=takes(27),
    )(parity, own, other, seg[None, :], seg[:, None])


def attend_back_kernel(
    tile,
    parity_ref,
    own_ref,
    other_ref,
    own_out,
    other_out,
    own_grad,
    other_grad,
    lse_ref,
    seg_row,
    seg_col,
    mine_ref,
    send_ref,
    sets,
    outs,
    grads,
    rows,
    key_acc,
    value_acc,
):
    tokens = own_ref.shape[-1]
    heads = pl.num_programs(0)
    head = pl.program_id(0)
    parity = parity_ref[0]
    half_rows = own_ref.shape[0] - 2 * HEAD

    @pl.when(head == 0)
    def _():
        place(parity, own_ref, other_ref, sets)
        place(parity, own_out, other_out, outs)
        place(parity, own_grad, other_grad, grads)
        for half in range(2):
            for i in range(2):
                at = half_rows + i * HEAD
                rows[i, half] = sets[half, at : at + HEAD, :].astype(F32).T.astype(BF)
        key_acc[...] = jnp.zeros_like(key_acc)
        value_acc[...] = jnp.zeros_like(value_acc)

    at_head = pl.ds(pl.multiple_of(head * HEAD, 16), HEAD)
    for half in range(2):
        for at in range(0, tokens, tile):
            span = slice(at, at + tile)
            query = sets[half, at_head, span]
            grad = grads[half, at_head, span]
            lse = lse_ref[half, 0, :, span]
            delta = jnp.sum(
                grad.astype(F32) * outs[half, at_head, span].astype(F32), axis=0, keepdims=True
            )
            total = None
            for which, begin, end, masked in pieces_of(half, at, tile, tokens):
                part = dot(rows[0, which, begin:end, :], query)
                if masked:
                    part = jnp.where(
                        seen_of(half, at, begin, end, tile, seg_row, seg_col), part, NEG
                    )
                weights = jnp.exp2(part - lse)
                dprod = dot(rows[1, which, begin:end, :], grad)
                dscore = (weights * (dprod - delta)).astype(BF)
                value_acc[which, :, begin:end] += dot(grad, weights.astype(BF), NT)
                key_acc[which, :, begin:end] += dot(query, dscore, NT)
                more = dot(sets[which, half_rows : half_rows + HEAD, begin:end], dscore)
                total = more if total is None else total + more
            total = (total * ROOT).astype(BF)

            @pl.when(parity == half)
            def _():
                mine_ref[at_head, span] = total

            @pl.when(parity != half)
            def _():
                send_ref[at_head, span] = total

    @pl.when(head == heads - 1)
    def _():
        for ref, which in ((mine_ref, parity), (send_ref, 1 - parity)):
            ref[half_rows : half_rows + HEAD, :] = (key_acc[which] * LN2).astype(BF)
            ref[half_rows + HEAD :, :] = value_acc[which].astype(BF)


def attend_back(parity, own, other, own_out, other_out, own_grad, other_grad, lse, seg):
    depth, tokens = own.shape
    half_rows = depth - 2 * HEAD
    heads = half_rows // HEAD
    tile = min(256, tokens)
    full, part = resident((depth, tokens)), resident((half_rows, tokens))
    return pl.pallas_call(
        functools.partial(attend_back_kernel, tile),
        out_shape=(shape((depth, tokens), BF), shape((depth, tokens), BF)),
        grid=(heads,),
        in_specs=[
            SMALL,
            full,
            full,
            part,
            part,
            part,
            part,
            pl.BlockSpec((2, 1, 1, tokens), lambda h: (0, h, 0, 0)),
            resident((1, tokens)),
            resident((tokens, 1)),
        ],
        out_specs=(full, full),
        scratch_shapes=[
            pltpu.VMEM((2, depth, tokens), BF),
            pltpu.VMEM((2, half_rows, tokens), BF),
            pltpu.VMEM((2, half_rows, tokens), BF),
            pltpu.VMEM((2, 2, tokens, HEAD), BF),
            pltpu.VMEM((2, HEAD, tokens), F32),
            pltpu.VMEM((2, HEAD, tokens), F32),
        ],
        compiler_params=params(),
        name="attend_back",
        cost_estimate=takes(37),
    )(
        parity,
        own,
        other,
        own_out,
        other_out,
        own_grad,
        other_grad,
        lse,
        seg[None, :],
        seg[:, None],
    )


def halves_at(parity, half_rows):
    mine = pl.ds(pl.multiple_of(parity * half_rows, 16), half_rows)
    other = pl.ds(pl.multiple_of((1 - parity) * half_rows, 16), half_rows)
    return mine, other


def mix_out_kernel(count, parity_ref, own_ref, other_ref, *refs):
    weights, out_ref = refs[:count], refs[count]
    cols, _, piece, _ = out_ref.shape
    mine, other = halves_at(parity_ref[0], own_ref.shape[0])
    for k in range(count):
        part = dot(weights[k][mine, :], own_ref[...], TN)
        part = part + dot(weights[k][other, :], other_ref[...], TN)
        for c in range(cols):
            out_ref[c, k] = part[c * piece : (c + 1) * piece].astype(BF)


def mix_out(parity, own, other, weights, cols):
    count = len(weights)
    piece = weights[0].shape[1] // cols
    vmem = pl.BlockSpec(memory_space=pltpu.VMEM)
    return pl.pallas_call(
        functools.partial(mix_out_kernel, count),
        out_shape=shape((cols, count, piece, own.shape[1]), BF),
        in_specs=[SMALL] + [vmem] * (2 + count),
        compiler_params=params(),
        name="mix_out",
        cost_estimate=takes(10),
    )(parity, own, other, *weights)


def mix_back_kernel(count, parts, parity_ref, *refs):
    x_refs, weights = refs[:parts], refs[parts : parts + count]
    rows_ref, own_ref, other_ref = refs[parts + count :]
    for i, x_ref in enumerate(x_refs):
        cols, _, piece, tokens = x_ref.shape
        for c in range(cols):
            for k in range(count):
                rows_ref[k, c * piece : (c + 1) * piece, i * tokens : (i + 1) * tokens] = x_ref[
                    c, k
                ]
    mine, other = halves_at(parity_ref[0], own_ref.shape[0])
    for at, out_ref in ((other, other_ref), (mine, own_ref)):
        total = None
        for k in range(count):
            part = dot(weights[k][at, :], rows_ref[k])
            total = part if total is None else total + part
        out_ref[...] = total.astype(BF)


def mix_back(parity, x_parts, weights):
    parts = len(x_parts)
    cols, count, piece, tokens = x_parts[0].shape
    tokens = tokens * parts
    half_rows = weights[0].shape[0] // 2
    vmem = pl.BlockSpec(memory_space=pltpu.VMEM)
    return pl.pallas_call(
        functools.partial(mix_back_kernel, count, parts),
        out_shape=(
            shape((count, cols * piece, tokens), BF),
            shape((half_rows, tokens), BF),
            shape((half_rows, tokens), BF),
        ),
        in_specs=[SMALL] + [vmem] * (parts + count),
        compiler_params=params(),
        name="mix_back",
        cost_estimate=takes(9),
    )(parity, *x_parts, *weights)


def fan_kernel(count, x_ref, *refs):
    weights, out_ref = refs[:count], refs[count]
    cols, _, piece, _ = out_ref.shape
    for k in range(count):
        part = dot(weights[k][...], x_ref[...], TN)
        for c in range(cols):
            out_ref[c, k] = part[c * piece : (c + 1) * piece].astype(BF)


def fan_out(weights, x, cols):
    count = len(weights)
    piece = weights[0].shape[1] // cols
    return pl.pallas_call(
        functools.partial(fan_kernel, count),
        out_shape=shape((cols, count, piece, x.shape[1]), BF),
        compiler_params=params(),
        name="fan_out",
        cost_estimate=takes(17),
    )(x, *weights)


def norm_back(grads, k, x_ref, gain_ref, scale, coef, share_ref, gain_share_ref):
    cols, _, piece, _ = x_ref.shape
    for c in range(cols):
        grad = grads[c * piece : (c + 1) * piece]
        value = x_ref[c, k].astype(F32)
        gain_share_ref[c, k] = jnp.sum(grad * (value * scale), axis=1, keepdims=True)
        share_ref[c, k] = ((grad * gain_ref[c, k]) * scale - value * coef).astype(BF)


def ff_kernel(count, chained, x_ref, g_ref, gain_ref, *refs):
    gate_w, up_w, down_w = refs[:count], refs[count : 2 * count], refs[2 * count : 3 * count]
    refs = refs[3 * count + (5 if chained else 0) :]
    norm_ref, rows_ref, act_ref, dgate_ref, dup_ref, share_ref, gain_share_ref = refs[:7]
    scale_ref, inner_ref, back_ref = refs[7:]
    cols, _, piece, _ = x_ref.shape
    step = pl.program_id(0)

    @pl.when(step == 0)
    def _():
        normalise(x_ref, gain_ref, norm_ref, scale_ref)
        for c in range(cols):
            for k in range(count):
                rows_ref[k, c * piece : (c + 1) * piece, :] = g_ref[c, k]
        inner_ref[...] = jnp.zeros_like(inner_ref)
        back_ref[...] = jnp.zeros_like(back_ref)

    def summed(weights, ref):
        total = None
        for k in range(count):
            part = dot(weights[k][...], ref[k])
            total = part if total is None else total + part
        return total

    gate = summed(gate_w, norm_ref)
    up = summed(up_w, norm_ref)
    sigma = jax.nn.sigmoid(gate)
    silu = gate * sigma
    act_ref[...] = (silu * up).astype(BF)
    grad = summed(down_w, rows_ref)
    dup = grad * silu
    dgate = grad * up * (sigma + silu * (1.0 - sigma))
    inner_ref[...] += jnp.sum(dgate * gate + dup * up, axis=0, keepdims=True)
    dgate_ref[...] = dgate.astype(BF)
    dup_ref[...] = dup.astype(BF)
    for k in range(count):
        back_ref[k] += dot(gate_w[k][...], dgate_ref[...], TN) + dot(
            up_w[k][...], dup_ref[...], TN
        )

    @pl.when(step == pl.num_programs(0) - 1)
    def _():
        scale = scale_ref[...]
        coef = scale * scale * inner_ref[...] / D
        for k in range(count):
            norm_back(back_ref[k], k, x_ref, gain_ref, scale, coef, share_ref, gain_share_ref)


def feed_forward(x, g, part, parts, gain, gate_w, up_w, down_w, before):
    cols, count, piece, tokens = x.shape
    width, depth = gate_w[0].shape
    tile = 432 if width % 432 == 0 else width
    g_spec = pl.BlockSpec(x.shape, lambda n: (0, 0, 0, part), pipeline_mode=pl.Buffered(1))
    rows = (count, cols * piece, tokens)
    rows_spec = pl.BlockSpec(rows, lambda n: (0, 0, part), pipeline_mode=pl.Buffered(1))
    w_spec = pl.BlockSpec((tile, depth), lambda n: (n, 0))
    h_spec = pl.BlockSpec((tile, tokens), lambda n: (n, part))
    rows_all = shape((count, cols * piece, tokens * parts), BF)
    hidden = shape((width, tokens * parts), BF)
    first = 3 + 3 * count
    return pl.pallas_call(
        functools.partial(ff_kernel, count, bool(before)),
        out_shape=(
            rows_all,
            rows_all,
            hidden,
            hidden,
            hidden,
            shape(x.shape, BF),
            shape(gain.shape, F32),
        ),
        grid=(width // tile,),
        in_specs=[resident(x.shape, 1), g_spec, resident(gain.shape, 1)]
        + [w_spec] * (3 * count)
        + [RAW] * len(before),
        out_specs=(
            rows_spec,
            rows_spec,
            h_spec,
            h_spec,
            h_spec,
            resident(x.shape, 1),
            resident(gain.shape, 1),
        ),
        scratch_shapes=[
            pltpu.VMEM((1, tokens), F32),
            pltpu.VMEM((1, tokens), F32),
            pltpu.VMEM(rows, F32),
        ],
        input_output_aliases={first + i: i for i in range(len(before))},
        compiler_params=params(60),
        name="feed_forward",
        cost_estimate=takes(42),
    )(x, g, gain, *gate_w, *up_w, *down_w, *before)


def qkv_back_kernel(
    count,
    shared,
    parity_ref,
    x_ref,
    gain_ref,
    scale_ref,
    cos_ref,
    sin_ref,
    sets_ref,
    own_ref,
    other_ref,
    *refs,
):
    q_w, kv_w = refs[:count], refs[count : 2 * count]
    dq_ref, dkv_ref, share_ref, gain_share_ref = refs[2 * count :]
    parity = parity_ref[0]
    half_rows = own_ref.shape[0] - 2 * HEAD
    kv_half = dkv_ref.shape[0] // 2
    cosine, sine = cos_ref[...], -sin_ref[...]
    inner = None
    folded = None
    for grads, which in ((own_ref, parity), (other_ref, 1 - parity)):
        for at in range(0, half_rows + 2 * HEAD, HEAD):
            value = grads[at : at + HEAD, :].astype(F32)
            part = value * sets_ref[which, at : at + HEAD, :].astype(F32)
            part = jnp.sum(part, axis=0, keepdims=True)
            if at < half_rows:
                part = part * (1.0 / (ROOT * LOG2E))
                start = pl.multiple_of(which * half_rows + at, 16)
                dq_ref[pl.ds(start, HEAD), :] = turn(value, cosine, sine).astype(BF)
            else:
                is_key = at == half_rows
                raw = turn(value, cosine, sine) if is_key else value
                base = 0 if is_key else kv_half
                if not shared:
                    start = pl.multiple_of(base + which * HEAD, 16)
                    dkv_ref[pl.ds(start, HEAD), :] = raw.astype(BF)
                elif folded is None or at not in folded:
                    folded = {**(folded or {}), at: raw}
                else:
                    dkv_ref[base : base + HEAD, :] = (folded[at] + raw).astype(BF)
            inner = part if inner is None else inner + part
    scale = scale_ref[...]
    coef = scale * scale * inner / D
    for k in range(count):
        grads = dot(q_w[k][...], dq_ref[...]) + dot(kv_w[k][...], dkv_ref[...], TN)
        norm_back(grads, k, x_ref, gain_ref, scale, coef, share_ref, gain_share_ref)


def qkv_back(parity, x, gain, scale, cosine, sine, sets, own, other, q_w, kv_w):
    cols, count, piece, tokens = x.shape
    shared = kv_w[0].shape[0] == 2 * HEAD
    vmem = pl.BlockSpec(memory_space=pltpu.VMEM)
    return pl.pallas_call(
        functools.partial(qkv_back_kernel, count, shared),
        out_shape=(
            shape((q_w[0].shape[1], tokens), BF),
            shape((kv_w[0].shape[0], tokens), BF),
            shape(x.shape, BF),
            shape(gain.shape, F32),
        ),
        in_specs=[SMALL] + [vmem] * (8 + 2 * count),
        compiler_params=params(),
        name="qkv_back",
        cost_estimate=takes(17),
    )(parity, x, gain, scale, cosine, sine, sets, own, other, *q_w, *kv_w)


def rope_parts(positions):
    half = HEAD // 2
    freq = THETA ** (-jnp.arange(half, dtype=F32) * 2.0 / HEAD)
    angle = freq[:, None] * positions.astype(F32)[None, :]
    return (jnp.cos(angle), jnp.sin(angle))


def spread_cols(value):
    return lax.all_gather(value, "col", axis=0, tiled=False)


def sum_cols(value):
    return lax.psum_scatter(value, "col", scatter_dimension=0, tiled=False)


def sent_over_dp(value):
    low = value.astype(BF)
    size = lax.axis_size("dp")
    others = [
        lax.ppermute(low, "dp", [(i, (i + step) % size) for i in range(size)])
        for step in range(1, size)
    ]
    return [low] + others


def summed_up(parts):
    total = parts[0].astype(F32)
    for other in parts[1:]:
        total = total + other.astype(F32)
    return total


def over_dp(value):
    return summed_up(sent_over_dp(value))


def body(
    layer_input,
    attn_gain,
    mlp_gain,
    query_weight,
    key_weight,
    value_weight,
    mix_weight,
    gate_weight,
    up_weight,
    down_weight,
    output_grad,
    segment_ids,
    position_ids,
):
    rows = segment_ids.shape[0]
    count = lax.axis_size("row")
    cols = lax.axis_size("col")
    piece = layer_input.shape[1]
    row = lax.axis_index("row")
    parity = (row % 2).astype(jnp.int32)
    own_core = parity.reshape(1)
    q_half = query_weight.shape[1] // 2
    near, far = near_bits(count), far_bits(count)
    far_mask = far[-1]

    def row_tokens(value):
        turned = value.T
        outgoing = [
            lax.dynamic_slice(turned, (0, (row ^ k) * rows), (piece, rows)) for k in range(count)
        ]
        return jnp.stack(exchange_blocks(outgoing, "row"))

    def all_tokens(blocks):
        got = exchange_blocks([blocks[k] for k in range(count)], "row")
        result = jnp.zeros((piece, count * rows), blocks.dtype)
        for k in range(count):
            result = lax.dynamic_update_slice(result, got[k], (0, (row ^ k) * rows))
        return result.T

    def listed(blocks):
        return [blocks[k] for k in range(count)]

    source_own = row_tokens(layer_input)
    source_own, output_grad = together(source_own, output_grad)
    grad_own = row_tokens(output_grad)
    kv_weight = jnp.concatenate([key_weight.T, value_weight.T])
    grad_own, query_weight, kv_weight = together(grad_own, query_weight, kv_weight)
    q_first = spread({0: query_weight}, "row", far)
    kv_first = spread({0: kv_weight}, "row", far)
    q_first, kv_first, mix_weight, gate_weight, attn_gain = together(
        q_first, kv_first, mix_weight, gate_weight, attn_gain
    )
    mix_first = spread({0: mix_weight}, "row", far)
    mix_first, up_weight = together(mix_first, up_weight)
    gate_first = spread({0: gate_weight.T}, "row", far)
    up_first = spread({0: up_weight.T}, "row", far)
    down_first = spread({0: down_weight}, "row", far)
    q_blocks = spread(q_first, "row", near)
    kv_blocks = spread(kv_first, "row", near)

    gains = lax.all_gather(jnp.stack([attn_gain, mlp_gain]), ("row", "col"), axis=1, tiled=True)
    gains = gains.reshape(2, count, cols, piece)
    gains = by_xor(gains, row, 1).swapaxes(1, 2)[..., None]
    gain_one, gain_two = gains[0], gains[1]

    cosine, sine = rope_parts(position_ids)
    other_seg = swapped(segment_ids, "row", 1)
    seg = jnp.where(parity == 0, other_seg, segment_ids)

    source = spread_cols(source_own)
    source, q_blocks, kv_blocks, gate_first, gain_one, cosine, sine, seg = together(
        source, q_blocks, kv_blocks, gate_first, gain_one, cosine, sine, seg
    )
    grad_own, source = together(grad_own, source)
    grad_all = spread_cols(grad_own)
    norm_one, scale_one, sets = qkv_project(
        source, gain_one, cosine, sine, listed(q_blocks), listed(kv_blocks)
    )
    own_set = lax.dynamic_index_in_dim(sets, parity, 0, keepdims=False)
    other_set = swapped(lax.dynamic_index_in_dim(sets, 1 - parity, 0, keepdims=False), "row", 1)
    attn_mine, attn_send, lse = attend(own_core, own_set, other_set, seg)
    attn_other = swapped(attn_send, "row", 1)
    mix_blocks = spread(mix_first, "row", near)
    attn_mine, attn_other, mix_blocks, up_first = together(
        attn_mine, attn_other, mix_blocks, up_first
    )
    attn_part = mix_out(own_core, attn_mine, attn_other, listed(mix_blocks), cols)
    attn_part, grad_all = together(attn_part, grad_all)
    attn_sum = sum_cols(attn_part)
    gate_blocks = spread(gate_first, "row", near)
    up_blocks = spread(up_first, "row", near)
    down_blocks = spread(down_first, "row", near)
    attn_sum, gate_blocks, up_blocks, down_blocks = together(
        attn_sum, gate_blocks, up_blocks, down_blocks
    )
    residual_own = source_own.astype(F32) + attn_sum.astype(F32)

    parts = 2 if rows % 256 == 0 else 1
    size = rows // parts
    spans = [slice(i * size, (i + 1) * size) for i in range(parts)]
    residual_low = residual_own.astype(BF)
    residual = [spread_cols(residual_low[..., span]) for span in spans]
    before, shares = (), []
    gain_share_two = 0.0
    for i in range(parts):
        out = feed_forward(
            residual[i],
            grad_all,
            i,
            parts,
            gain_two,
            listed(gate_blocks),
            listed(up_blocks),
            listed(down_blocks),
            before,
        )
        before = out[:5]
        shares.append(out[5])
        gain_share_two = gain_share_two + out[6]
    norm_two, grad_rows, act, dgate, dup = before
    share_sums = [sum_cols(share) for share in shares]
    down_grads = {k: dot(act, grad_rows[k], NT).astype(BF) for k in range(count)}
    gate_grads = {k: dot(dgate, norm_two[k], NT).astype(BF) for k in range(count)}
    up_grads = {k: dot(dup, norm_two[k], NT).astype(BF) for k in range(count)}
    down_grads = fold(down_grads, "row", near)
    gate_grads = fold(gate_grads, "row", near)
    up_grads = fold(up_grads, "row", near)
    *share_sums, down_grads, gate_grads, up_grads = together(
        *share_sums, down_grads, gate_grads, up_grads
    )
    residual_grad_own = grad_own.astype(F32) + jnp.concatenate(share_sums, axis=2).astype(F32)
    down_total = fold(down_grads, "row", far)[0]
    gate_total = fold(gate_grads, "row", far)[0]

    mix_cols = spread_cols(residual_grad_own.astype(BF))
    ff_part = fan_out(listed(down_blocks), act, cols)
    down_total = over_dp(down_total)
    mix_cols, ff_part, down_total, gate_total, up_grads = together(
        mix_cols, ff_part, down_total, gate_total, up_grads
    )
    up_total = fold(up_grads, "row", far)[0]
    gate_total = over_dp(gate_total)
    mix_rows, grad_mine, grad_send = mix_back(own_core, [mix_cols], listed(mix_blocks))
    ff_sum = sum_cols(ff_part)
    grad_other = swapped(grad_send, "row", 1)
    back_mine, back_send = attend_back(
        own_core, own_set, other_set, attn_mine, attn_send, grad_mine, grad_other, lse, seg
    )
    back_other = swapped(back_send, "row", 1)
    back_other, up_total, gate_total, down_total = together(
        back_other, up_total, gate_total, down_total
    )
    cut = up_total.shape[0] * 5 // 9 // 16 * 16
    up_head, up_tail = over_dp(up_total[:cut]), sent_over_dp(up_total[cut:])
    dq, dkv, share, gain_share_one = qkv_back(
        own_core,
        source,
        gain_one,
        scale_one,
        cosine,
        sine,
        sets,
        back_mine,
        back_other,
        listed(q_blocks),
        listed(kv_blocks),
    )
    share, attn_mine, mix_rows = together(share, attn_mine, mix_rows)
    attn_low = jnp.concatenate(
        [
            jnp.where(parity == 0, attn_mine, attn_other),
            jnp.where(parity == 0, attn_other, attn_mine),
        ]
    )
    mix_odd = {k: dot(attn_low, mix_rows[k], NT).astype(BF) for k in range(1, count, 2)}
    gain_shares = jnp.stack([gain_share_one[..., 0], gain_share_two[..., 0]], axis=2)
    share, ff_sum, mix_odd, up_head, gain_shares = together(
        share, ff_sum, mix_odd, up_head, gain_shares
    )
    input_sum = sum_cols(share)

    bits = near + far[::-1]
    gain_shares = fold({k: gain_shares[:, k] for k in range(count)}, "row", bits, low=False)[0]
    share, dq, dkv, attn_low, mix_rows = together(share, dq, dkv, attn_low, mix_rows)
    mix_even = {k: dot(attn_low, mix_rows[k], NT).astype(BF) for k in range(0, count, 2)}
    mix_near = fold({**mix_even, **mix_odd}, "row", near)
    dq, dkv, mix_near = together(dq, dkv, mix_near)
    mix_moved = {k: swapped(mix_near[k], "row", far_mask) for k in mix_near if k & far_mask}
    q_near = fold({k: dot(norm_one[k], dq, NT).astype(BF) for k in range(count)}, "row", near)
    kv_near = fold({k: dot(dkv, norm_one[k], NT).astype(BF) for k in range(count)}, "row", near)
    ff_sum, gain_shares, q_near, kv_near, up_tail, mix_near, mix_moved = together(
        ff_sum, gain_shares, q_near, kv_near, up_tail, mix_near, mix_moved
    )
    mix_far = fold_landed(mix_near, mix_moved, far_mask)
    mix_total = over_dp(fold(mix_far, "row", far[::-1][1:])[0])
    q_far = fold(q_near, "row", far)[0]
    kv_far = fold(kv_near, "row", far)[0]
    q_total, kv_total = over_dp(q_far), over_dp(kv_far)
    output_own = (residual_own + ff_sum.astype(F32)).astype(BF)
    layer_output = all_tokens(output_own)

    gain_shares = by_xor(gain_shares, lax.axis_index("col"), 0)
    gain_shares = {c: gain_shares[c] for c in range(cols)}
    gain_shares = fold(gain_shares, "col", near_bits(cols) + far_bits(cols), low=False)[0]
    gain_totals = over_dp(gain_shares)
    up_total = jnp.concatenate([up_head, summed_up(up_tail)])
    input_sum, q_total, kv_total, mix_total, gain_totals, layer_output, up_total = together(
        input_sum, q_total, kv_total, mix_total, gain_totals, layer_output, up_total
    )

    input_grad = all_tokens((residual_grad_own + input_sum.astype(F32)).astype(BF)).astype(F32)
    kv_rows = kv_total.shape[0] // 2
    return (
        layer_output,
        input_grad,
        gain_totals[0],
        gain_totals[1],
        q_total,
        kv_total[:kv_rows].T,
        kv_total[kv_rows:].T,
        mix_total,
        gate_total.T,
        up_total.T,
        down_total,
    )


def solution(mesh):
    return jax.shard_map(
        body,
        mesh=mesh,
        in_specs=(
            P("dp", ("row", "col")),
            P(("row", "col")),
            P(("row", "col")),
            P("row", "col"),
            P("row", "col"),
            P("row", "col"),
            P("col", "row"),
            P("row", "col"),
            P("row", "col"),
            P("col", "row"),
            P("dp", ("row", "col")),
            P(("dp", "row")),
            P(("dp", "row")),
        ),
        out_specs=(
            P("dp", ("row", "col")),
            P("dp", ("row", "col")),
            P(("row", "col")),
            P(("row", "col")),
            P("row", "col"),
            P("row", "col"),
            P("row", "col"),
            P("col", "row"),
            P("row", "col"),
            P("row", "col"),
            P("col", "row"),
        ),
        check_vma=False,
    )
```

```python
import functools

import jax
import jax.numpy as jnp
from jax import lax
from jax.experimental import pallas as pl
from jax.experimental.pallas import tpu as pltpu
from jax.sharding import PartitionSpec as P

D = 2560
HEAD = 80
EPS = 1e-05
THETA = 10000.0
NEG = -1e30
LOG2E = 1.4426950408889634
LN2 = 0.6931471805599453
ROOT = HEAD ** (-0.5)
BF = jnp.bfloat16
F32 = jnp.float32
NN = (((1,), (0,)), ((), ()))
TN = (((0,), (0,)), ((), ()))
NT = (((1,), (1,)), ((), ()))


def dot(left, right, dims=NN):
    return lax.dot_general(left, right, dims, preferred_element_type=F32)


def together(*values):
    return lax.optimization_barrier(values)


def swapped(value, axis, mask):
    size = lax.axis_size(axis)
    return lax.ppermute(value, axis, [(i, i ^ mask) for i in range(size)])


def spread(blocks, axis, bits):
    blocks = dict(blocks)
    for bit in bits:
        for k in list(blocks):
            blocks[k | bit] = swapped(blocks[k], axis, bit)
    return blocks


def fold(blocks, axis, bits, low=True):
    held = dict(blocks)
    for bit in bits:
        for k in [k for k in held if k & bit]:
            other = swapped(held.pop(k), axis, bit)
            total = held[k ^ bit].astype(F32) + other.astype(F32)
            held[k ^ bit] = total.astype(BF) if low else total
    return held


def fold_landed(held, moved, bit):
    return {
        k ^ bit: (held[k ^ bit].astype(F32) + other.astype(F32)).astype(BF)
        for k, other in moved.items()
    }


def far_bits(size):
    return [1 << i for i in range(1, size.bit_length() - 1)]


def near_bits(size):
    return [1] if size > 1 else []


def exchange_blocks(blocks, axis):
    return [blocks[0]] + [swapped(blocks[k], axis, k) for k in range(1, len(blocks))]


def by_xor(value, index, axis):
    parts = [
        lax.dynamic_index_in_dim(value, index ^ k, axis, keepdims=True)
        for k in range(value.shape[axis])
    ]
    return jnp.concatenate(parts, axis=axis)


def params(mib=58):
    return pltpu.CompilerParams(vmem_limit_bytes=mib * 1024 * 1024)


def takes(micros):
    return pl.CostEstimate(flops=int(micros * 0.1e9), transcendentals=0, bytes_accessed=0)


def shape(dims, dtype):
    return jax.ShapeDtypeStruct(dims, dtype)


SMALL = pl.BlockSpec(memory_space=pltpu.SMEM)
RAW = pl.BlockSpec(memory_space=pl.ANY)


def resident(dims, buffers=None):
    zeros = (0,) * len(dims)
    mode = {} if buffers is None else {"pipeline_mode": pl.Buffered(buffers)}
    return pl.BlockSpec(dims, lambda *_: zeros, **mode)


def normalise(x_ref, gain_ref, out_ref, scale_ref):
    cols, count, piece, _ = x_ref.shape
    total = None
    for c in range(cols):
        for k in range(count):
            value = x_ref[c, k].astype(F32)
            part = jnp.sum(value * value, axis=0, keepdims=True)
            total = part if total is None else total + part
    scale = lax.rsqrt(total / D + EPS)
    scale_ref[...] = scale
    for c in range(cols):
        for k in range(count):
            value = x_ref[c, k].astype(F32) * scale * gain_ref[c, k]
            out_ref[k, c * piece : (c + 1) * piece, :] = value.astype(BF)


def turn(value, cosine, sine):
    half = value.shape[0] // 2
    first, second = value[:half], value[half:]
    return jnp.concatenate([first * cosine - second * sine, second * cosine + first * sine])


def qkv_kernel(count, shared, x_ref, gain_ref, cos_ref, sin_ref, *refs):
    q_w, kv_w = refs[:count], refs[count : 2 * count]
    norm_ref, scale_ref, sets_ref = refs[2 * count :]
    normalise(x_ref, gain_ref, norm_ref, scale_ref)
    query = keyval = None
    for k in range(count):
        normed = norm_ref[k]
        part = dot(q_w[k][...], normed, TN)
        query = part if query is None else query + part
        part = dot(kv_w[k][...], normed)
        keyval = part if keyval is None else keyval + part
    cosine, sine = cos_ref[...], sin_ref[...]
    half = query.shape[0] // 2
    kv_half = keyval.shape[0] // 2
    for h in range(2):
        for at in range(0, half, HEAD):
            value = turn(query[h * half + at : h * half + at + HEAD], cosine, sine)
            sets_ref[h, at : at + HEAD, :] = (value * (ROOT * LOG2E)).astype(BF)
        at = 0 if shared else h * HEAD
        key = turn(keyval[at : at + HEAD], cosine, sine)
        sets_ref[h, half : half + HEAD, :] = key.astype(BF)
        sets_ref[h, half + HEAD : half + 2 * HEAD, :] = keyval[
            kv_half + at : kv_half + at + HEAD
        ].astype(BF)


def qkv_project(x, gain, cosine, sine, q_w, kv_w):
    cols, count, piece, tokens = x.shape
    half = q_w[0].shape[1] // 2
    shared = kv_w[0].shape[0] == 2 * HEAD
    return pl.pallas_call(
        functools.partial(qkv_kernel, count, shared),
        out_shape=(
            shape((count, cols * piece, tokens), BF),
            shape((1, tokens), F32),
            shape((2, half + 2 * HEAD, tokens), BF),
        ),
        compiler_params=params(),
        name="qkv_project",
        cost_estimate=takes(12),
    )(x, gain, cosine, sine, *q_w, *kv_w)


def pieces_of(half, at, tile, tokens):
    if half == 1:
        return [(0, 0, tokens, False), (1, 0, at + tile, True)]
    head = [(0, 0, at, False)] if at else []
    return head + [(0, at, at + tile, True)]


def seen_of(half, at, begin, end, tile, seg_row, seg_col):
    rows = lax.broadcasted_iota(jnp.int32, (end - begin, tile), 0) + begin
    cols = lax.broadcasted_iota(jnp.int32, (end - begin, tile), 1) + at
    seen = rows <= cols
    if half == 1:
        seen = seen & (seg_col[begin:end] == seg_row[:, at : at + tile])
    return seen


def place(parity, own_ref, other_ref, sets):
    sets[parity] = own_ref[...]
    sets[1 - parity] = other_ref[...]


def attend_kernel(
    tile, parity_ref, own_ref, other_ref, seg_row, seg_col, mine_ref, send_ref, lse_ref, sets, rows
):
    tokens = own_ref.shape[-1]
    heads = pl.num_programs(0)
    head = pl.program_id(0)
    parity = parity_ref[0]
    half_rows = own_ref.shape[0] - 2 * HEAD

    @pl.when(head == 0)
    def _():
        place(parity, own_ref, other_ref, sets)
        for half in range(2):
            keys = sets[half, half_rows : half_rows + HEAD, :]
            rows[half] = keys.astype(F32).T.astype(BF)

    at_head = pl.ds(pl.multiple_of(head * HEAD, 16), HEAD)
    for half in range(2):
        for at in range(0, tokens, tile):
            span = slice(at, at + tile)
            query = sets[half, at_head, span]
            pieces = pieces_of(half, at, tile, tokens)
            scores = []
            for which, begin, end, masked in pieces:
                part = dot(rows[which, begin:end, :], query)
                if masked:
                    part = jnp.where(
                        seen_of(half, at, begin, end, tile, seg_row, seg_col), part, NEG
                    )
                scores.append(part)
            peak = functools.reduce(
                jnp.maximum, [jnp.max(s, axis=0, keepdims=True) for s in scores]
            )
            total = out = None
            for (which, begin, end, _), part in zip(pieces, scores):
                weights = jnp.exp2(part - peak)
                mass = jnp.sum(weights, axis=0, keepdims=True)
                value = dot(sets[which, half_rows + HEAD :, begin:end], weights.astype(BF))
                total = mass if total is None else total + mass
                out = value if out is None else out + value
            out = (out / total).astype(BF)
            lse_ref[half, 0, :, span] = peak + jnp.log2(total)

            @pl.when(parity == half)
            def _():
                mine_ref[at_head, span] = out

            @pl.when(parity != half)
            def _():
                send_ref[at_head, span] = out


def attend(parity, own, other, seg):
    depth, tokens = own.shape
    half_rows = depth - 2 * HEAD
    heads = half_rows // HEAD
    tile = min(256, tokens)
    out = resident((half_rows, tokens))
    return pl.pallas_call(
        functools.partial(attend_kernel, tile),
        out_shape=(
            shape((half_rows, tokens), BF),
            shape((half_rows, tokens), BF),
            shape((2, heads, 1, tokens), F32),
        ),
        grid=(heads,),
        in_specs=[
            SMALL,
            resident((depth, tokens)),
            resident((depth, tokens)),
            resident((1, tokens)),
            resident((tokens, 1)),
        ],
        out_specs=(out, out, pl.BlockSpec((2, 1, 1, tokens), lambda h: (0, h, 0, 0))),
        scratch_shapes=[
            pltpu.VMEM((2, depth, tokens), BF),
            pltpu.VMEM((2, tokens, HEAD), BF),
        ],
        compiler_params=params(),
        name="attend",
        cost_estimate=takes(27),
    )(parity, own, other, seg[None, :], seg[:, None])


def attend_back_kernel(
    tile,
    parity_ref,
    own_ref,
    other_ref,
    own_out,
    other_out,
    own_grad,
    other_grad,
    lse_ref,
    seg_row,
    seg_col,
    mine_ref,
    send_ref,
    sets,
    outs,
    grads,
    rows,
    key_acc,
    value_acc,
):
    tokens = own_ref.shape[-1]
    heads = pl.num_programs(0)
    head = pl.program_id(0)
    parity = parity_ref[0]
    half_rows = own_ref.shape[0] - 2 * HEAD

    @pl.when(head == 0)
    def _():
        place(parity, own_ref, other_ref, sets)
        place(parity, own_out, other_out, outs)
        place(parity, own_grad, other_grad, grads)
        for half in range(2):
            for i in range(2):
                at = half_rows + i * HEAD
                rows[i, half] = sets[half, at : at + HEAD, :].astype(F32).T.astype(BF)
        key_acc[...] = jnp.zeros_like(key_acc)
        value_acc[...] = jnp.zeros_like(value_acc)

    at_head = pl.ds(pl.multiple_of(head * HEAD, 16), HEAD)
    for half in range(2):
        for at in range(0, tokens, tile):
            span = slice(at, at + tile)
            query = sets[half, at_head, span]
            grad = grads[half, at_head, span]
            lse = lse_ref[half, 0, :, span]
            delta = jnp.sum(
                grad.astype(F32) * outs[half, at_head, span].astype(F32), axis=0, keepdims=True
            )
            total = None
            for which, begin, end, masked in pieces_of(half, at, tile, tokens):
                part = dot(rows[0, which, begin:end, :], query)
                if masked:
                    part = jnp.where(
                        seen_of(half, at, begin, end, tile, seg_row, seg_col), part, NEG
                    )
                weights = jnp.exp2(part - lse)
                dprod = dot(rows[1, which, begin:end, :], grad)
                dscore = (weights * (dprod - delta)).astype(BF)
                value_acc[which, :, begin:end] += dot(grad, weights.astype(BF), NT)
                key_acc[which, :, begin:end] += dot(query, dscore, NT)
                more = dot(sets[which, half_rows : half_rows + HEAD, begin:end], dscore)
                total = more if total is None else total + more
            total = (total * ROOT).astype(BF)

            @pl.when(parity == half)
            def _():
                mine_ref[at_head, span] = total

            @pl.when(parity != half)
            def _():
                send_ref[at_head, span] = total

    @pl.when(head == heads - 1)
    def _():
        for ref, which in ((mine_ref, parity), (send_ref, 1 - parity)):
            ref[half_rows : half_rows + HEAD, :] = (key_acc[which] * LN2).astype(BF)
            ref[half_rows + HEAD :, :] = value_acc[which].astype(BF)


def attend_back(parity, own, other, own_out, other_out, own_grad, other_grad, lse, seg):
    depth, tokens = own.shape
    half_rows = depth - 2 * HEAD
    heads = half_rows // HEAD
    tile = min(256, tokens)
    full, part = resident((depth, tokens)), resident((half_rows, tokens))
    return pl.pallas_call(
        functools.partial(attend_back_kernel, tile),
        out_shape=(shape((depth, tokens), BF), shape((depth, tokens), BF)),
        grid=(heads,),
        in_specs=[
            SMALL,
            full,
            full,
            part,
            part,
            part,
            part,
            pl.BlockSpec((2, 1, 1, tokens), lambda h: (0, h, 0, 0)),
            resident((1, tokens)),
            resident((tokens, 1)),
        ],
        out_specs=(full, full),
        scratch_shapes=[
            pltpu.VMEM((2, depth, tokens), BF),
            pltpu.VMEM((2, half_rows, tokens), BF),
            pltpu.VMEM((2, half_rows, tokens), BF),
            pltpu.VMEM((2, 2, tokens, HEAD), BF),
            pltpu.VMEM((2, HEAD, tokens), F32),
            pltpu.VMEM((2, HEAD, tokens), F32),
        ],
        compiler_params=params(),
        name="attend_back",
        cost_estimate=takes(37),
    )(
        parity,
        own,
        other,
        own_out,
        other_out,
        own_grad,
        other_grad,
        lse,
        seg[None, :],
        seg[:, None],
    )


def halves_at(parity, half_rows):
    mine = pl.ds(pl.multiple_of(parity * half_rows, 16), half_rows)
    other = pl.ds(pl.multiple_of((1 - parity) * half_rows, 16), half_rows)
    return mine, other


def mix_out_kernel(count, parity_ref, own_ref, other_ref, *refs):
    weights, out_ref = refs[:count], refs[count]
    cols, _, piece, _ = out_ref.shape
    mine, other = halves_at(parity_ref[0], own_ref.shape[0])
    for k in range(count):
        part = dot(weights[k][mine, :], own_ref[...], TN)
        part = part + dot(weights[k][other, :], other_ref[...], TN)
        for c in range(cols):
            out_ref[c, k] = part[c * piece : (c + 1) * piece].astype(BF)


def mix_out(parity, own, other, weights, cols):
    count = len(weights)
    piece = weights[0].shape[1] // cols
    vmem = pl.BlockSpec(memory_space=pltpu.VMEM)
    return pl.pallas_call(
        functools.partial(mix_out_kernel, count),
        out_shape=shape((cols, count, piece, own.shape[1]), BF),
        in_specs=[SMALL] + [vmem] * (2 + count),
        compiler_params=params(),
        name="mix_out",
        cost_estimate=takes(10),
    )(parity, own, other, *weights)


def mix_back_kernel(count, parts, parity_ref, *refs):
    x_refs, weights = refs[:parts], refs[parts : parts + count]
    rows_ref, own_ref, other_ref = refs[parts + count :]
    for i, x_ref in enumerate(x_refs):
        cols, _, piece, tokens = x_ref.shape
        for c in range(cols):
            for k in range(count):
                rows_ref[k, c * piece : (c + 1) * piece, i * tokens : (i + 1) * tokens] = x_ref[
                    c, k
                ]
    mine, other = halves_at(parity_ref[0], own_ref.shape[0])
    for at, out_ref in ((other, other_ref), (mine, own_ref)):
        total = None
        for k in range(count):
            part = dot(weights[k][at, :], rows_ref[k])
            total = part if total is None else total + part
        out_ref[...] = total.astype(BF)


def mix_back(parity, x_parts, weights):
    parts = len(x_parts)
    cols, count, piece, tokens = x_parts[0].shape
    tokens = tokens * parts
    half_rows = weights[0].shape[0] // 2
    vmem = pl.BlockSpec(memory_space=pltpu.VMEM)
    return pl.pallas_call(
        functools.partial(mix_back_kernel, count, parts),
        out_shape=(
            shape((count, cols * piece, tokens), BF),
            shape((half_rows, tokens), BF),
            shape((half_rows, tokens), BF),
        ),
        in_specs=[SMALL] + [vmem] * (parts + count),
        compiler_params=params(),
        name="mix_back",
        cost_estimate=takes(9),
    )(parity, *x_parts, *weights)


def fan_kernel(count, x_ref, *refs):
    weights, out_ref = refs[:count], refs[count]
    cols, _, piece, _ = out_ref.shape
    for k in range(count):
        part = dot(weights[k][...], x_ref[...], TN)
        for c in range(cols):
            out_ref[c, k] = part[c * piece : (c + 1) * piece].astype(BF)


def fan_out(weights, x, cols):
    count = len(weights)
    piece = weights[0].shape[1] // cols
    return pl.pallas_call(
        functools.partial(fan_kernel, count),
        out_shape=shape((cols, count, piece, x.shape[1]), BF),
        compiler_params=params(),
        name="fan_out",
        cost_estimate=takes(17),
    )(x, *weights)


def norm_back(grads, k, x_ref, gain_ref, scale, coef, share_ref, gain_share_ref):
    cols, _, piece, _ = x_ref.shape
    for c in range(cols):
        grad = grads[c * piece : (c + 1) * piece]
        value = x_ref[c, k].astype(F32)
        gain_share_ref[c, k] = jnp.sum(grad * (value * scale), axis=1, keepdims=True)
        share_ref[c, k] = ((grad * gain_ref[c, k]) * scale - value * coef).astype(BF)


def ff_kernel(count, chained, x_ref, g_ref, gain_ref, *refs):
    gate_w, up_w, down_w = refs[:count], refs[count : 2 * count], refs[2 * count : 3 * count]
    refs = refs[3 * count + (5 if chained else 0) :]
    norm_ref, rows_ref, act_ref, dgate_ref, dup_ref, share_ref, gain_share_ref = refs[:7]
    scale_ref, inner_ref, back_ref = refs[7:]
    cols, _, piece, _ = x_ref.shape
    step = pl.program_id(0)

    @pl.when(step == 0)
    def _():
        normalise(x_ref, gain_ref, norm_ref, scale_ref)
        for c in range(cols):
            for k in range(count):
                rows_ref[k, c * piece : (c + 1) * piece, :] = g_ref[c, k]
        inner_ref[...] = jnp.zeros_like(inner_ref)
        back_ref[...] = jnp.zeros_like(back_ref)

    def summed(weights, ref):
        total = None
        for k in range(count):
            part = dot(weights[k][...], ref[k])
            total = part if total is None else total + part
        return total

    gate = summed(gate_w, norm_ref)
    up = summed(up_w, norm_ref)
    sigma = jax.nn.sigmoid(gate)
    silu = gate * sigma
    act_ref[...] = (silu * up).astype(BF)
    grad = summed(down_w, rows_ref)
    dup = grad * silu
    dgate = grad * up * (sigma + silu * (1.0 - sigma))
    inner_ref[...] += jnp.sum(dgate * gate + dup * up, axis=0, keepdims=True)
    dgate_ref[...] = dgate.astype(BF)
    dup_ref[...] = dup.astype(BF)
    for k in range(count):
        back_ref[k] += dot(gate_w[k][...], dgate_ref[...], TN) + dot(
            up_w[k][...], dup_ref[...], TN
        )

    @pl.when(step == pl.num_programs(0) - 1)
    def _():
        scale = scale_ref[...]
        coef = scale * scale * inner_ref[...] / D
        for k in range(count):
            norm_back(back_ref[k], k, x_ref, gain_ref, scale, coef, share_ref, gain_share_ref)


def feed_forward(x, g, part, parts, gain, gate_w, up_w, down_w, before):
    cols, count, piece, tokens = x.shape
    width, depth = gate_w[0].shape
    tile = 432 if width % 432 == 0 else width
    g_spec = pl.BlockSpec(x.shape, lambda n: (0, 0, 0, part), pipeline_mode=pl.Buffered(1))
    rows = (count, cols * piece, tokens)
    rows_spec = pl.BlockSpec(rows, lambda n: (0, 0, part), pipeline_mode=pl.Buffered(1))
    w_spec = pl.BlockSpec((tile, depth), lambda n: (n, 0))
    h_spec = pl.BlockSpec((tile, tokens), lambda n: (n, part))
    rows_all = shape((count, cols * piece, tokens * parts), BF)
    hidden = shape((width, tokens * parts), BF)
    first = 3 + 3 * count
    return pl.pallas_call(
        functools.partial(ff_kernel, count, bool(before)),
        out_shape=(
            rows_all,
            rows_all,
            hidden,
            hidden,
            hidden,
            shape(x.shape, BF),
            shape(gain.shape, F32),
        ),
        grid=(width // tile,),
        in_specs=[resident(x.shape, 1), g_spec, resident(gain.shape, 1)]
        + [w_spec] * (3 * count)
        + [RAW] * len(before),
        out_specs=(
            rows_spec,
            rows_spec,
            h_spec,
            h_spec,
            h_spec,
            resident(x.shape, 1),
            resident(gain.shape, 1),
        ),
        scratch_shapes=[
            pltpu.VMEM((1, tokens), F32),
            pltpu.VMEM((1, tokens), F32),
            pltpu.VMEM(rows, F32),
        ],
        input_output_aliases={first + i: i for i in range(len(before))},
        compiler_params=params(60),
        name="feed_forward",
        cost_estimate=takes(42),
    )(x, g, gain, *gate_w, *up_w, *down_w, *before)


def qkv_back_kernel(
    count,
    shared,
    parity_ref,
    x_ref,
    gain_ref,
    scale_ref,
    cos_ref,
    sin_ref,
    sets_ref,
    own_ref,
    other_ref,
    *refs,
):
    q_w, kv_w = refs[:count], refs[count : 2 * count]
    dq_ref, dkv_ref, share_ref, gain_share_ref = refs[2 * count :]
    parity = parity_ref[0]
    half_rows = own_ref.shape[0] - 2 * HEAD
    kv_half = dkv_ref.shape[0] // 2
    cosine, sine = cos_ref[...], -sin_ref[...]
    inner = None
    folded = None
    for grads, which in ((own_ref, parity), (other_ref, 1 - parity)):
        for at in range(0, half_rows + 2 * HEAD, HEAD):
            value = grads[at : at + HEAD, :].astype(F32)
            part = value * sets_ref[which, at : at + HEAD, :].astype(F32)
            part = jnp.sum(part, axis=0, keepdims=True)
            if at < half_rows:
                part = part * (1.0 / (ROOT * LOG2E))
                start = pl.multiple_of(which * half_rows + at, 16)
                dq_ref[pl.ds(start, HEAD), :] = turn(value, cosine, sine).astype(BF)
            else:
                is_key = at == half_rows
                raw = turn(value, cosine, sine) if is_key else value
                base = 0 if is_key else kv_half
                if not shared:
                    start = pl.multiple_of(base + which * HEAD, 16)
                    dkv_ref[pl.ds(start, HEAD), :] = raw.astype(BF)
                elif folded is None or at not in folded:
                    folded = {**(folded or {}), at: raw}
                else:
                    dkv_ref[base : base + HEAD, :] = (folded[at] + raw).astype(BF)
            inner = part if inner is None else inner + part
    scale = scale_ref[...]
    coef = scale * scale * inner / D
    for k in range(count):
        grads = dot(q_w[k][...], dq_ref[...]) + dot(kv_w[k][...], dkv_ref[...], TN)
        norm_back(grads, k, x_ref, gain_ref, scale, coef, share_ref, gain_share_ref)


def qkv_back(parity, x, gain, scale, cosine, sine, sets, own, other, q_w, kv_w):
    cols, count, piece, tokens = x.shape
    shared = kv_w[0].shape[0] == 2 * HEAD
    vmem = pl.BlockSpec(memory_space=pltpu.VMEM)
    return pl.pallas_call(
        functools.partial(qkv_back_kernel, count, shared),
        out_shape=(
            shape((q_w[0].shape[1], tokens), BF),
            shape((kv_w[0].shape[0], tokens), BF),
            shape(x.shape, BF),
            shape(gain.shape, F32),
        ),
        in_specs=[SMALL] + [vmem] * (8 + 2 * count),
        compiler_params=params(),
        name="qkv_back",
        cost_estimate=takes(17),
    )(parity, x, gain, scale, cosine, sine, sets, own, other, *q_w, *kv_w)


def rope_parts(positions):
    half = HEAD // 2
    freq = THETA ** (-jnp.arange(half, dtype=F32) * 2.0 / HEAD)
    angle = freq[:, None] * positions.astype(F32)[None, :]
    return (jnp.cos(angle), jnp.sin(angle))


def spread_cols(value):
    return lax.all_gather(value, "col", axis=0, tiled=False)


def sum_cols(value):
    return lax.psum_scatter(value, "col", scatter_dimension=0, tiled=False)


def sent_over_dp(value):
    low = value.astype(BF)
    size = lax.axis_size("dp")
    others = [
        lax.ppermute(low, "dp", [(i, (i + step) % size) for i in range(size)])
        for step in range(1, size)
    ]
    return [low] + others


def summed_up(parts):
    total = parts[0].astype(F32)
    for other in parts[1:]:
        total = total + other.astype(F32)
    return total


def over_dp(value):
    return summed_up(sent_over_dp(value))


def body(
    layer_input,
    attn_gain,
    mlp_gain,
    query_weight,
    key_weight,
    value_weight,
    mix_weight,
    gate_weight,
    up_weight,
    down_weight,
    output_grad,
    segment_ids,
    position_ids,
):
    rows = segment_ids.shape[0]
    count = lax.axis_size("row")
    cols = lax.axis_size("col")
    piece = layer_input.shape[1]
    row = lax.axis_index("row")
    parity = (row % 2).astype(jnp.int32)
    own_core = parity.reshape(1)
    q_half = query_weight.shape[1] // 2
    near, far = near_bits(count), far_bits(count)
    far_mask = far[-1]

    def row_tokens(value):
        turned = value.T
        outgoing = [
            lax.dynamic_slice(turned, (0, (row ^ k) * rows), (piece, rows)) for k in range(count)
        ]
        return jnp.stack(exchange_blocks(outgoing, "row"))

    def all_tokens(blocks):
        got = exchange_blocks([blocks[k] for k in range(count)], "row")
        result = jnp.zeros((piece, count * rows), blocks.dtype)
        for k in range(count):
            result = lax.dynamic_update_slice(result, got[k], (0, (row ^ k) * rows))
        return result.T

    def listed(blocks):
        return [blocks[k] for k in range(count)]

    source_own = row_tokens(layer_input)
    source_own, output_grad = together(source_own, output_grad)
    grad_own = row_tokens(output_grad)
    kv_weight = jnp.concatenate([key_weight.T, value_weight.T])
    grad_own, query_weight, kv_weight = together(grad_own, query_weight, kv_weight)
    q_first = spread({0: query_weight}, "row", far)
    kv_first = spread({0: kv_weight}, "row", far)
    q_first, kv_first, mix_weight, gate_weight, attn_gain = together(
        q_first, kv_first, mix_weight, gate_weight, attn_gain
    )
    mix_first = spread({0: mix_weight}, "row", far)
    mix_first, up_weight = together(mix_first, up_weight)
    gate_first = spread({0: gate_weight.T}, "row", far)
    up_first = spread({0: up_weight.T}, "row", far)
    down_first = spread({0: down_weight}, "row", far)
    q_blocks = spread(q_first, "row", near)
    kv_blocks = spread(kv_first, "row", near)

    gains = lax.all_gather(jnp.stack([attn_gain, mlp_gain]), ("row", "col"), axis=1, tiled=True)
    gains = gains.reshape(2, count, cols, piece)
    gains = by_xor(gains, row, 1).swapaxes(1, 2)[..., None]
    gain_one, gain_two = gains[0], gains[1]

    cosine, sine = rope_parts(position_ids)
    other_seg = swapped(segment_ids, "row", 1)
    seg = jnp.where(parity == 0, other_seg, segment_ids)

    source = spread_cols(source_own)
    source, q_blocks, kv_blocks, gate_first, gain_one, cosine, sine, seg = together(
        source, q_blocks, kv_blocks, gate_first, gain_one, cosine, sine, seg
    )
    grad_own, source = together(grad_own, source)
    grad_all = spread_cols(grad_own)
    norm_one, scale_one, sets = qkv_project(
        source, gain_one, cosine, sine, listed(q_blocks), listed(kv_blocks)
    )
    own_set = lax.dynamic_index_in_dim(sets, parity, 0, keepdims=False)
    other_set = swapped(lax.dynamic_index_in_dim(sets, 1 - parity, 0, keepdims=False), "row", 1)
    attn_mine, attn_send, lse = attend(own_core, own_set, other_set, seg)
    attn_other = swapped(attn_send, "row", 1)
    mix_blocks = spread(mix_first, "row", near)
    attn_mine, attn_other, mix_blocks, up_first = together(
        attn_mine, attn_other, mix_blocks, up_first
    )
    attn_part = mix_out(own_core, attn_mine, attn_other, listed(mix_blocks), cols)
    attn_part, grad_all = together(attn_part, grad_all)
    attn_sum = sum_cols(attn_part)
    gate_blocks = spread(gate_first, "row", near)
    up_blocks = spread(up_first, "row", near)
    down_blocks = spread(down_first, "row", near)
    attn_sum, gate_blocks, up_blocks, down_blocks = together(
        attn_sum, gate_blocks, up_blocks, down_blocks
    )
    residual_own = source_own.astype(F32) + attn_sum.astype(F32)

    parts = 2 if rows % 256 == 0 else 1
    size = rows // parts
    spans = [slice(i * size, (i + 1) * size) for i in range(parts)]
    residual_low = residual_own.astype(BF)
    residual = [spread_cols(residual_low[..., span]) for span in spans]
    before, shares = (), []
    gain_share_two = 0.0
    for i in range(parts):
        out = feed_forward(
            residual[i],
            grad_all,
            i,
            parts,
            gain_two,
            listed(gate_blocks),
            listed(up_blocks),
            listed(down_blocks),
            before,
        )
        before = out[:5]
        shares.append(out[5])
        gain_share_two = gain_share_two + out[6]
    norm_two, grad_rows, act, dgate, dup = before
    if parts == 2 and cols == 4:
        blocks = [
            lax.dynamic_index_in_dim(shares[0], lax.axis_index("col") ^ m, 0, keepdims=False)
            for m in range(cols)
        ]
        moved = exchange_blocks(blocks, "col")
        norm_two, grad_rows, act, dgate, dup, moved = together(
            norm_two, grad_rows, act, dgate, dup, moved
        )
        share_sums = [summed_up(moved), sum_cols(shares[1])]
    else:
        share_sums = [sum_cols(share) for share in shares]
    share_sums = [total.astype(F32) for total in share_sums]
    down_grads = {k: dot(act, grad_rows[k], NT).astype(BF) for k in range(count)}
    gate_grads = {k: dot(dgate, norm_two[k], NT).astype(BF) for k in range(count)}
    down_grads = fold(down_grads, "row", near)
    gate_grads = fold(gate_grads, "row", near)
    *share_sums, down_grads, gate_grads, dup, norm_two = together(
        *share_sums, down_grads, gate_grads, dup, norm_two
    )
    up_grads = {k: dot(dup, norm_two[k], NT).astype(BF) for k in range(count)}
    up_grads = fold(up_grads, "row", near)
    residual_grad_own = grad_own.astype(F32) + jnp.concatenate(share_sums, axis=2)
    down_total = fold(down_grads, "row", far)[0]
    gate_total = fold(gate_grads, "row", far)[0]

    mix_cols = spread_cols(residual_grad_own.astype(BF))
    ff_part = fan_out(listed(down_blocks), act, cols)
    down_total = over_dp(down_total)
    mix_cols, ff_part, down_total, gate_total, up_grads = together(
        mix_cols, ff_part, down_total, gate_total, up_grads
    )
    up_total = fold(up_grads, "row", far)[0]
    gate_total = over_dp(gate_total)
    mix_rows, grad_mine, grad_send = mix_back(own_core, [mix_cols], listed(mix_blocks))
    ff_sum = sum_cols(ff_part)
    grad_other = swapped(grad_send, "row", 1)
    back_mine, back_send = attend_back(
        own_core, own_set, other_set, attn_mine, attn_send, grad_mine, grad_other, lse, seg
    )
    back_other = swapped(back_send, "row", 1)
    back_other, up_total, gate_total, down_total = together(
        back_other, up_total, gate_total, down_total
    )
    cut = up_total.shape[0] * 5 // 9 // 16 * 16
    up_head, up_tail = over_dp(up_total[:cut]), sent_over_dp(up_total[cut:])
    dq, dkv, share, gain_share_one = qkv_back(
        own_core,
        source,
        gain_one,
        scale_one,
        cosine,
        sine,
        sets,
        back_mine,
        back_other,
        listed(q_blocks),
        listed(kv_blocks),
    )
    share, attn_mine, mix_rows = together(share, attn_mine, mix_rows)
    attn_low = jnp.concatenate(
        [
            jnp.where(parity == 0, attn_mine, attn_other),
            jnp.where(parity == 0, attn_other, attn_mine),
        ]
    )
    mix_odd = {k: dot(attn_low, mix_rows[k], NT).astype(BF) for k in range(1, count, 2)}
    gain_shares = jnp.stack([gain_share_one[..., 0], gain_share_two[..., 0]], axis=2)
    share, ff_sum, mix_odd, up_head, gain_shares = together(
        share, ff_sum, mix_odd, up_head, gain_shares
    )
    input_sum = sum_cols(share)

    bits = near + far[::-1]
    gain_shares = fold({k: gain_shares[:, k] for k in range(count)}, "row", bits, low=False)[0]
    share, dq, dkv, attn_low, mix_rows = together(share, dq, dkv, attn_low, mix_rows)
    mix_even = {k: dot(attn_low, mix_rows[k], NT).astype(BF) for k in range(0, count, 2)}
    mix_near = fold({**mix_even, **mix_odd}, "row", near)
    dq, dkv, mix_near = together(dq, dkv, mix_near)
    mix_moved = {k: swapped(mix_near[k], "row", far_mask) for k in mix_near if k & far_mask}
    q_near = fold({k: dot(norm_one[k], dq, NT).astype(BF) for k in range(count)}, "row", near)
    kv_near = fold({k: dot(dkv, norm_one[k], NT).astype(BF) for k in range(count)}, "row", near)
    ff_sum, gain_shares, q_near, kv_near, up_tail, mix_near, mix_moved = together(
        ff_sum, gain_shares, q_near, kv_near, up_tail, mix_near, mix_moved
    )
    mix_far = fold_landed(mix_near, mix_moved, far_mask)
    mix_total = over_dp(fold(mix_far, "row", far[::-1][1:])[0])
    q_far = fold(q_near, "row", far)[0]
    kv_far = fold(kv_near, "row", far)[0]
    q_total, kv_total = over_dp(q_far), over_dp(kv_far)
    output_own = (residual_own + ff_sum.astype(F32)).astype(BF)
    layer_output = all_tokens(output_own)

    gain_shares = by_xor(gain_shares, lax.axis_index("col"), 0)
    gain_shares = {c: gain_shares[c] for c in range(cols)}
    gain_shares = fold(gain_shares, "col", near_bits(cols) + far_bits(cols), low=False)[0]
    gain_totals = over_dp(gain_shares)
    up_total = jnp.concatenate([up_head, summed_up(up_tail)])
    input_sum, q_total, kv_total, mix_total, gain_totals, layer_output, up_total = together(
        input_sum, q_total, kv_total, mix_total, gain_totals, layer_output, up_total
    )

    input_grad = all_tokens((residual_grad_own + input_sum.astype(F32)).astype(BF)).astype(F32)
    kv_rows = kv_total.shape[0] // 2
    return (
        layer_output,
        input_grad,
        gain_totals[0],
        gain_totals[1],
        q_total,
        kv_total[:kv_rows].T,
        kv_total[kv_rows:].T,
        mix_total,
        gate_total.T,
        up_total.T,
        down_total,
    )


def solution(mesh):
    return jax.shard_map(
        body,
        mesh=mesh,
        in_specs=(
            P("dp", ("row", "col")),
            P(("row", "col")),
            P(("row", "col")),
            P("row", "col"),
            P("row", "col"),
            P("row", "col"),
            P("col", "row"),
            P("row", "col"),
            P("row", "col"),
            P("col", "row"),
            P("dp", ("row", "col")),
            P(("dp", "row")),
            P(("dp", "row")),
        ),
        out_specs=(
            P("dp", ("row", "col")),
            P("dp", ("row", "col")),
            P(("row", "col")),
            P(("row", "col")),
            P("row", "col"),
            P("row", "col"),
            P("row", "col"),
            P("col", "row"),
            P("row", "col"),
            P("row", "col"),
            P("col", "row"),
        ),
        check_vma=False,
    )
```

```python
import functools

import jax
import jax.numpy as jnp
from jax import lax
from jax.experimental import pallas as pl
from jax.experimental.pallas import tpu as pltpu
from jax.sharding import PartitionSpec as P

D = 2560
HEAD = 80
EPS = 1e-05
THETA = 10000.0
NEG = -1e30
LOG2E = 1.4426950408889634
LN2 = 0.6931471805599453
ROOT = HEAD ** (-0.5)
BF = jnp.bfloat16
F32 = jnp.float32
NN = (((1,), (0,)), ((), ()))
TN = (((0,), (0,)), ((), ()))
NT = (((1,), (1,)), ((), ()))


def dot(left, right, dims=NN):
    return lax.dot_general(left, right, dims, preferred_element_type=F32)


def together(*values):
    return lax.optimization_barrier(values)


def swapped(value, axis, mask):
    size = lax.axis_size(axis)
    return lax.ppermute(value, axis, [(i, i ^ mask) for i in range(size)])


def spread(blocks, axis, bits):
    blocks = dict(blocks)
    for bit in bits:
        for k in list(blocks):
            blocks[k | bit] = swapped(blocks[k], axis, bit)
    return blocks


def fold(blocks, axis, bits, low=True):
    held = dict(blocks)
    for bit in bits:
        for k in [k for k in held if k & bit]:
            other = swapped(held.pop(k), axis, bit)
            total = held[k ^ bit].astype(F32) + other.astype(F32)
            held[k ^ bit] = total.astype(BF) if low else total
    return held


def fold_landed(held, moved, bit):
    return {
        k ^ bit: (held[k ^ bit].astype(F32) + other.astype(F32)).astype(BF)
        for k, other in moved.items()
    }


def far_bits(size):
    return [1 << i for i in range(1, size.bit_length() - 1)]


def near_bits(size):
    return [1] if size > 1 else []


def exchange_blocks(blocks, axis):
    return [blocks[0]] + [swapped(blocks[k], axis, k) for k in range(1, len(blocks))]


def by_xor(value, index, axis):
    parts = [
        lax.dynamic_index_in_dim(value, index ^ k, axis, keepdims=True)
        for k in range(value.shape[axis])
    ]
    return jnp.concatenate(parts, axis=axis)


def params(mib=58):
    return pltpu.CompilerParams(vmem_limit_bytes=mib * 1024 * 1024)


def takes(micros):
    return pl.CostEstimate(flops=int(micros * 0.1e9), transcendentals=0, bytes_accessed=0)


def shape(dims, dtype):
    return jax.ShapeDtypeStruct(dims, dtype)


SMALL = pl.BlockSpec(memory_space=pltpu.SMEM)
RAW = pl.BlockSpec(memory_space=pl.ANY)


def resident(dims, buffers=None):
    zeros = (0,) * len(dims)
    mode = {} if buffers is None else {"pipeline_mode": pl.Buffered(buffers)}
    return pl.BlockSpec(dims, lambda *_: zeros, **mode)


def normalise(x_ref, gain_ref, out_ref, scale_ref):
    cols, count, piece, _ = x_ref.shape
    total = None
    for c in range(cols):
        for k in range(count):
            value = x_ref[c, k].astype(F32)
            part = jnp.sum(value * value, axis=0, keepdims=True)
            total = part if total is None else total + part
    scale = lax.rsqrt(total / D + EPS)
    scale_ref[...] = scale
    for c in range(cols):
        for k in range(count):
            value = x_ref[c, k].astype(F32) * scale * gain_ref[c, k]
            out_ref[k, c * piece : (c + 1) * piece, :] = value.astype(BF)


def turn(value, cosine, sine):
    half = value.shape[0] // 2
    first, second = value[:half], value[half:]
    return jnp.concatenate([first * cosine - second * sine, second * cosine + first * sine])


def qkv_kernel(count, shared, x_ref, gain_ref, cos_ref, sin_ref, *refs):
    q_w, kv_w = refs[:count], refs[count : 2 * count]
    norm_ref, scale_ref, sets_ref = refs[2 * count :]
    normalise(x_ref, gain_ref, norm_ref, scale_ref)
    query = keyval = None
    for k in range(count):
        normed = norm_ref[k]
        part = dot(q_w[k][...], normed, TN)
        query = part if query is None else query + part
        part = dot(kv_w[k][...], normed)
        keyval = part if keyval is None else keyval + part
    cosine, sine = cos_ref[...], sin_ref[...]
    half = query.shape[0] // 2
    kv_half = keyval.shape[0] // 2
    for h in range(2):
        for at in range(0, half, HEAD):
            value = turn(query[h * half + at : h * half + at + HEAD], cosine, sine)
            sets_ref[h, at : at + HEAD, :] = (value * (ROOT * LOG2E)).astype(BF)
        at = 0 if shared else h * HEAD
        key = turn(keyval[at : at + HEAD], cosine, sine)
        sets_ref[h, half : half + HEAD, :] = key.astype(BF)
        sets_ref[h, half + HEAD : half + 2 * HEAD, :] = keyval[
            kv_half + at : kv_half + at + HEAD
        ].astype(BF)


def qkv_project(x, gain, cosine, sine, q_w, kv_w):
    cols, count, piece, tokens = x.shape
    half = q_w[0].shape[1] // 2
    shared = kv_w[0].shape[0] == 2 * HEAD
    return pl.pallas_call(
        functools.partial(qkv_kernel, count, shared),
        out_shape=(
            shape((count, cols * piece, tokens), BF),
            shape((1, tokens), F32),
            shape((2, half + 2 * HEAD, tokens), BF),
        ),
        compiler_params=params(),
        name="qkv_project",
        cost_estimate=takes(12),
    )(x, gain, cosine, sine, *q_w, *kv_w)


def pieces_of(half, at, tile, tokens):
    if half == 1:
        return [(0, 0, tokens, False), (1, 0, at + tile, True)]
    head = [(0, 0, at, False)] if at else []
    return head + [(0, at, at + tile, True)]


def seen_of(half, at, begin, end, tile, seg_row, seg_col):
    rows = lax.broadcasted_iota(jnp.int32, (end - begin, tile), 0) + begin
    cols = lax.broadcasted_iota(jnp.int32, (end - begin, tile), 1) + at
    seen = rows <= cols
    if half == 1:
        seen = seen & (seg_col[begin:end] == seg_row[:, at : at + tile])
    return seen


def place(parity, own_ref, other_ref, sets):
    sets[parity] = own_ref[...]
    sets[1 - parity] = other_ref[...]


def attend_kernel(
    tile, parity_ref, own_ref, other_ref, seg_row, seg_col, mine_ref, send_ref, lse_ref, sets, rows
):
    tokens = own_ref.shape[-1]
    heads = pl.num_programs(0)
    head = pl.program_id(0)
    parity = parity_ref[0]
    half_rows = own_ref.shape[0] - 2 * HEAD

    @pl.when(head == 0)
    def _():
        place(parity, own_ref, other_ref, sets)
        for half in range(2):
            keys = sets[half, half_rows : half_rows + HEAD, :]
            rows[half] = keys.astype(F32).T.astype(BF)

    at_head = pl.ds(pl.multiple_of(head * HEAD, 16), HEAD)
    for half in range(2):
        for at in range(0, tokens, tile):
            span = slice(at, at + tile)
            query = sets[half, at_head, span]
            pieces = pieces_of(half, at, tile, tokens)
            scores = []
            for which, begin, end, masked in pieces:
                part = dot(rows[which, begin:end, :], query)
                if masked:
                    part = jnp.where(
                        seen_of(half, at, begin, end, tile, seg_row, seg_col), part, NEG
                    )
                scores.append(part)
            peak = functools.reduce(
                jnp.maximum, [jnp.max(s, axis=0, keepdims=True) for s in scores]
            )
            total = out = None
            for (which, begin, end, _), part in zip(pieces, scores):
                weights = jnp.exp2(part - peak)
                mass = jnp.sum(weights, axis=0, keepdims=True)
                value = dot(sets[which, half_rows + HEAD :, begin:end], weights.astype(BF))
                total = mass if total is None else total + mass
                out = value if out is None else out + value
            out = (out / total).astype(BF)
            lse_ref[half, 0, :, span] = peak + jnp.log2(total)

            @pl.when(parity == half)
            def _():
                mine_ref[at_head, span] = out

            @pl.when(parity != half)
            def _():
                send_ref[at_head, span] = out


def attend(parity, own, other, seg):
    depth, tokens = own.shape
    half_rows = depth - 2 * HEAD
    heads = half_rows // HEAD
    tile = min(256, tokens)
    out = resident((half_rows, tokens))
    return pl.pallas_call(
        functools.partial(attend_kernel, tile),
        out_shape=(
            shape((half_rows, tokens), BF),
            shape((half_rows, tokens), BF),
            shape((2, heads, 1, tokens), F32),
        ),
        grid=(heads,),
        in_specs=[
            SMALL,
            resident((depth, tokens)),
            resident((depth, tokens)),
            resident((1, tokens)),
            resident((tokens, 1)),
        ],
        out_specs=(out, out, pl.BlockSpec((2, 1, 1, tokens), lambda h: (0, h, 0, 0))),
        scratch_shapes=[
            pltpu.VMEM((2, depth, tokens), BF),
            pltpu.VMEM((2, tokens, HEAD), BF),
        ],
        compiler_params=params(),
        name="attend",
        cost_estimate=takes(27),
    )(parity, own, other, seg[None, :], seg[:, None])


def attend_back_kernel(
    tile,
    parity_ref,
    own_ref,
    other_ref,
    own_out,
    other_out,
    own_grad,
    other_grad,
    lse_ref,
    seg_row,
    seg_col,
    mine_ref,
    send_ref,
    sets,
    outs,
    grads,
    rows,
    key_acc,
    value_acc,
):
    tokens = own_ref.shape[-1]
    heads = pl.num_programs(0)
    head = pl.program_id(0)
    parity = parity_ref[0]
    half_rows = own_ref.shape[0] - 2 * HEAD

    @pl.when(head == 0)
    def _():
        place(parity, own_ref, other_ref, sets)
        place(parity, own_out, other_out, outs)
        place(parity, own_grad, other_grad, grads)
        for half in range(2):
            for i in range(2):
                at = half_rows + i * HEAD
                rows[i, half] = sets[half, at : at + HEAD, :].astype(F32).T.astype(BF)
        key_acc[...] = jnp.zeros_like(key_acc)
        value_acc[...] = jnp.zeros_like(value_acc)

    at_head = pl.ds(pl.multiple_of(head * HEAD, 16), HEAD)
    for half in range(2):
        for at in range(0, tokens, tile):
            span = slice(at, at + tile)
            query = sets[half, at_head, span]
            grad = grads[half, at_head, span]
            lse = lse_ref[half, 0, :, span]
            delta = jnp.sum(
                grad.astype(F32) * outs[half, at_head, span].astype(F32), axis=0, keepdims=True
            )
            total = None
            for which, begin, end, masked in pieces_of(half, at, tile, tokens):
                part = dot(rows[0, which, begin:end, :], query)
                if masked:
                    part = jnp.where(
                        seen_of(half, at, begin, end, tile, seg_row, seg_col), part, NEG
                    )
                weights = jnp.exp2(part - lse)
                dprod = dot(rows[1, which, begin:end, :], grad)
                dscore = (weights * (dprod - delta)).astype(BF)
                value_acc[which, :, begin:end] += dot(grad, weights.astype(BF), NT)
                key_acc[which, :, begin:end] += dot(query, dscore, NT)
                more = dot(sets[which, half_rows : half_rows + HEAD, begin:end], dscore)
                total = more if total is None else total + more
            total = (total * ROOT).astype(BF)

            @pl.when(parity == half)
            def _():
                mine_ref[at_head, span] = total

            @pl.when(parity != half)
            def _():
                send_ref[at_head, span] = total

    @pl.when(head == heads - 1)
    def _():
        for ref, which in ((mine_ref, parity), (send_ref, 1 - parity)):
            ref[half_rows : half_rows + HEAD, :] = (key_acc[which] * LN2).astype(BF)
            ref[half_rows + HEAD :, :] = value_acc[which].astype(BF)


def attend_back(parity, own, other, own_out, other_out, own_grad, other_grad, lse, seg):
    depth, tokens = own.shape
    half_rows = depth - 2 * HEAD
    heads = half_rows // HEAD
    tile = min(256, tokens)
    full, part = resident((depth, tokens)), resident((half_rows, tokens))
    return pl.pallas_call(
        functools.partial(attend_back_kernel, tile),
        out_shape=(shape((depth, tokens), BF), shape((depth, tokens), BF)),
        grid=(heads,),
        in_specs=[
            SMALL,
            full,
            full,
            part,
            part,
            part,
            part,
            pl.BlockSpec((2, 1, 1, tokens), lambda h: (0, h, 0, 0)),
            resident((1, tokens)),
            resident((tokens, 1)),
        ],
        out_specs=(full, full),
        scratch_shapes=[
            pltpu.VMEM((2, depth, tokens), BF),
            pltpu.VMEM((2, half_rows, tokens), BF),
            pltpu.VMEM((2, half_rows, tokens), BF),
            pltpu.VMEM((2, 2, tokens, HEAD), BF),
            pltpu.VMEM((2, HEAD, tokens), F32),
            pltpu.VMEM((2, HEAD, tokens), F32),
        ],
        compiler_params=params(),
        name="attend_back",
        cost_estimate=takes(37),
    )(
        parity,
        own,
        other,
        own_out,
        other_out,
        own_grad,
        other_grad,
        lse,
        seg[None, :],
        seg[:, None],
    )


def halves_at(parity, half_rows):
    mine = pl.ds(pl.multiple_of(parity * half_rows, 16), half_rows)
    other = pl.ds(pl.multiple_of((1 - parity) * half_rows, 16), half_rows)
    return mine, other


def mix_out_kernel(count, parity_ref, own_ref, other_ref, *refs):
    weights, out_ref = refs[:count], refs[count]
    cols, _, piece, _ = out_ref.shape
    mine, other = halves_at(parity_ref[0], own_ref.shape[0])
    for k in range(count):
        part = dot(weights[k][mine, :], own_ref[...], TN)
        part = part + dot(weights[k][other, :], other_ref[...], TN)
        for c in range(cols):
            out_ref[c, k] = part[c * piece : (c + 1) * piece].astype(BF)


def mix_out(parity, own, other, weights, cols):
    count = len(weights)
    piece = weights[0].shape[1] // cols
    vmem = pl.BlockSpec(memory_space=pltpu.VMEM)
    return pl.pallas_call(
        functools.partial(mix_out_kernel, count),
        out_shape=shape((cols, count, piece, own.shape[1]), BF),
        in_specs=[SMALL] + [vmem] * (2 + count),
        compiler_params=params(),
        name="mix_out",
        cost_estimate=takes(10),
    )(parity, own, other, *weights)


def mix_back_kernel(count, parts, parity_ref, *refs):
    x_refs, weights = refs[:parts], refs[parts : parts + count]
    rows_ref, own_ref, other_ref = refs[parts + count :]
    for i, x_ref in enumerate(x_refs):
        cols, _, piece, tokens = x_ref.shape
        for c in range(cols):
            for k in range(count):
                rows_ref[k, c * piece : (c + 1) * piece, i * tokens : (i + 1) * tokens] = x_ref[
                    c, k
                ]
    mine, other = halves_at(parity_ref[0], own_ref.shape[0])
    for at, out_ref in ((other, other_ref), (mine, own_ref)):
        total = None
        for k in range(count):
            part = dot(weights[k][at, :], rows_ref[k])
            total = part if total is None else total + part
        out_ref[...] = total.astype(BF)


def mix_back(parity, x_parts, weights):
    parts = len(x_parts)
    cols, count, piece, tokens = x_parts[0].shape
    tokens = tokens * parts
    half_rows = weights[0].shape[0] // 2
    vmem = pl.BlockSpec(memory_space=pltpu.VMEM)
    return pl.pallas_call(
        functools.partial(mix_back_kernel, count, parts),
        out_shape=(
            shape((count, cols * piece, tokens), BF),
            shape((half_rows, tokens), BF),
            shape((half_rows, tokens), BF),
        ),
        in_specs=[SMALL] + [vmem] * (parts + count),
        compiler_params=params(),
        name="mix_back",
        cost_estimate=takes(9),
    )(parity, *x_parts, *weights)


def fan_kernel(count, x_ref, *refs):
    weights, out_ref = refs[:count], refs[count]
    cols, _, piece, _ = out_ref.shape
    for k in range(count):
        part = dot(weights[k][...], x_ref[...], TN)
        for c in range(cols):
            out_ref[c, k] = part[c * piece : (c + 1) * piece].astype(BF)


def fan_out(weights, x, cols):
    count = len(weights)
    piece = weights[0].shape[1] // cols
    return pl.pallas_call(
        functools.partial(fan_kernel, count),
        out_shape=shape((cols, count, piece, x.shape[1]), BF),
        compiler_params=params(),
        name="fan_out",
        cost_estimate=takes(17),
    )(x, *weights)


def norm_back(grads, k, x_ref, gain_ref, scale, coef, share_ref, gain_share_ref):
    cols, _, piece, _ = x_ref.shape
    for c in range(cols):
        grad = grads[c * piece : (c + 1) * piece]
        value = x_ref[c, k].astype(F32)
        gain_share_ref[c, k] = jnp.sum(grad * (value * scale), axis=1, keepdims=True)
        share_ref[c, k] = ((grad * gain_ref[c, k]) * scale - value * coef).astype(BF)


def ff_kernel(count, chained, x_ref, g_ref, gain_ref, *refs):
    gate_w, up_w, down_w = refs[:count], refs[count : 2 * count], refs[2 * count : 3 * count]
    refs = refs[3 * count + (5 if chained else 0) :]
    norm_ref, rows_ref, act_ref, dgate_ref, dup_ref, share_ref, gain_share_ref = refs[:7]
    scale_ref, inner_ref, back_ref = refs[7:]
    cols, _, piece, _ = x_ref.shape
    step = pl.program_id(0)

    @pl.when(step == 0)
    def _():
        normalise(x_ref, gain_ref, norm_ref, scale_ref)
        for c in range(cols):
            for k in range(count):
                rows_ref[k, c * piece : (c + 1) * piece, :] = g_ref[c, k]
        inner_ref[...] = jnp.zeros_like(inner_ref)
        back_ref[...] = jnp.zeros_like(back_ref)

    def summed(weights, ref):
        total = None
        for k in range(count):
            part = dot(weights[k][...], ref[k])
            total = part if total is None else total + part
        return total

    gate = summed(gate_w, norm_ref)
    up = summed(up_w, norm_ref)
    sigma = jax.nn.sigmoid(gate)
    silu = gate * sigma
    act_ref[...] = (silu * up).astype(BF)
    grad = summed(down_w, rows_ref)
    dup = grad * silu
    dgate = grad * up * (sigma + silu * (1.0 - sigma))
    inner_ref[...] += jnp.sum(dgate * gate + dup * up, axis=0, keepdims=True)
    dgate_ref[...] = dgate.astype(BF)
    dup_ref[...] = dup.astype(BF)
    for k in range(count):
        back_ref[k] += dot(gate_w[k][...], dgate_ref[...], TN) + dot(
            up_w[k][...], dup_ref[...], TN
        )

    @pl.when(step == pl.num_programs(0) - 1)
    def _():
        scale = scale_ref[...]
        coef = scale * scale * inner_ref[...] / D
        for k in range(count):
            norm_back(back_ref[k], k, x_ref, gain_ref, scale, coef, share_ref, gain_share_ref)


def feed_forward(x, g, part, parts, gain, gate_w, up_w, down_w, before):
    cols, count, piece, tokens = x.shape
    width, depth = gate_w[0].shape
    tile = 432 if width % 432 == 0 else width
    g_spec = pl.BlockSpec(x.shape, lambda n: (0, 0, 0, part), pipeline_mode=pl.Buffered(1))
    rows = (count, cols * piece, tokens)
    rows_spec = pl.BlockSpec(rows, lambda n: (0, 0, part), pipeline_mode=pl.Buffered(1))
    w_spec = pl.BlockSpec((tile, depth), lambda n: (n, 0))
    h_spec = pl.BlockSpec((tile, tokens), lambda n: (n, part))
    rows_all = shape((count, cols * piece, tokens * parts), BF)
    hidden = shape((width, tokens * parts), BF)
    first = 3 + 3 * count
    return pl.pallas_call(
        functools.partial(ff_kernel, count, bool(before)),
        out_shape=(
            rows_all,
            rows_all,
            hidden,
            hidden,
            hidden,
            shape(x.shape, BF),
            shape(gain.shape, F32),
        ),
        grid=(width // tile,),
        in_specs=[resident(x.shape, 1), g_spec, resident(gain.shape, 1)]
        + [w_spec] * (3 * count)
        + [RAW] * len(before),
        out_specs=(
            rows_spec,
            rows_spec,
            h_spec,
            h_spec,
            h_spec,
            resident(x.shape, 1),
            resident(gain.shape, 1),
        ),
        scratch_shapes=[
            pltpu.VMEM((1, tokens), F32),
            pltpu.VMEM((1, tokens), F32),
            pltpu.VMEM(rows, F32),
        ],
        input_output_aliases={first + i: i for i in range(len(before))},
        compiler_params=params(60),
        name="feed_forward",
        cost_estimate=takes(42),
    )(x, g, gain, *gate_w, *up_w, *down_w, *before)


def qkv_back_kernel(
    count,
    shared,
    parity_ref,
    x_ref,
    gain_ref,
    scale_ref,
    cos_ref,
    sin_ref,
    sets_ref,
    own_ref,
    other_ref,
    *refs,
):
    q_w, kv_w = refs[:count], refs[count : 2 * count]
    dq_ref, dkv_ref, share_ref, gain_share_ref = refs[2 * count :]
    parity = parity_ref[0]
    half_rows = own_ref.shape[0] - 2 * HEAD
    kv_half = dkv_ref.shape[0] // 2
    cosine, sine = cos_ref[...], -sin_ref[...]
    inner = None
    folded = None
    for grads, which in ((own_ref, parity), (other_ref, 1 - parity)):
        for at in range(0, half_rows + 2 * HEAD, HEAD):
            value = grads[at : at + HEAD, :].astype(F32)
            part = value * sets_ref[which, at : at + HEAD, :].astype(F32)
            part = jnp.sum(part, axis=0, keepdims=True)
            if at < half_rows:
                part = part * (1.0 / (ROOT * LOG2E))
                start = pl.multiple_of(which * half_rows + at, 16)
                dq_ref[pl.ds(start, HEAD), :] = turn(value, cosine, sine).astype(BF)
            else:
                is_key = at == half_rows
                raw = turn(value, cosine, sine) if is_key else value
                base = 0 if is_key else kv_half
                if not shared:
                    start = pl.multiple_of(base + which * HEAD, 16)
                    dkv_ref[pl.ds(start, HEAD), :] = raw.astype(BF)
                elif folded is None or at not in folded:
                    folded = {**(folded or {}), at: raw}
                else:
                    dkv_ref[base : base + HEAD, :] = (folded[at] + raw).astype(BF)
            inner = part if inner is None else inner + part
    scale = scale_ref[...]
    coef = scale * scale * inner / D
    for k in range(count):
        grads = dot(q_w[k][...], dq_ref[...]) + dot(kv_w[k][...], dkv_ref[...], TN)
        norm_back(grads, k, x_ref, gain_ref, scale, coef, share_ref, gain_share_ref)


def qkv_back(parity, x, gain, scale, cosine, sine, sets, own, other, q_w, kv_w):
    cols, count, piece, tokens = x.shape
    shared = kv_w[0].shape[0] == 2 * HEAD
    vmem = pl.BlockSpec(memory_space=pltpu.VMEM)
    return pl.pallas_call(
        functools.partial(qkv_back_kernel, count, shared),
        out_shape=(
            shape((q_w[0].shape[1], tokens), BF),
            shape((kv_w[0].shape[0], tokens), BF),
            shape(x.shape, BF),
            shape(gain.shape, F32),
        ),
        in_specs=[SMALL] + [vmem] * (8 + 2 * count),
        compiler_params=params(),
        name="qkv_back",
        cost_estimate=takes(17),
    )(parity, x, gain, scale, cosine, sine, sets, own, other, *q_w, *kv_w)


def rope_parts(positions):
    half = HEAD // 2
    freq = THETA ** (-jnp.arange(half, dtype=F32) * 2.0 / HEAD)
    angle = freq[:, None] * positions.astype(F32)[None, :]
    return (jnp.cos(angle), jnp.sin(angle))


def spread_cols(value):
    return lax.all_gather(value, "col", axis=0, tiled=False)


def sum_cols(value):
    return lax.psum_scatter(value, "col", scatter_dimension=0, tiled=False)


def sent_over_dp(value):
    low = value.astype(BF)
    size = lax.axis_size("dp")
    others = [
        lax.ppermute(low, "dp", [(i, (i + step) % size) for i in range(size)])
        for step in range(1, size)
    ]
    return [low] + others


def summed_up(parts):
    total = parts[0].astype(F32)
    for other in parts[1:]:
        total = total + other.astype(F32)
    return total


def over_dp(value):
    return summed_up(sent_over_dp(value))


def body(
    layer_input,
    attn_gain,
    mlp_gain,
    query_weight,
    key_weight,
    value_weight,
    mix_weight,
    gate_weight,
    up_weight,
    down_weight,
    output_grad,
    segment_ids,
    position_ids,
):
    rows = segment_ids.shape[0]
    count = lax.axis_size("row")
    cols = lax.axis_size("col")
    piece = layer_input.shape[1]
    row = lax.axis_index("row")
    parity = (row % 2).astype(jnp.int32)
    own_core = parity.reshape(1)
    q_half = query_weight.shape[1] // 2
    near, far = near_bits(count), far_bits(count)
    far_mask = far[-1]

    def row_tokens(value):
        turned = value.T
        outgoing = [
            lax.dynamic_slice(turned, (0, (row ^ k) * rows), (piece, rows)) for k in range(count)
        ]
        return jnp.stack(exchange_blocks(outgoing, "row"))

    def all_tokens(blocks):
        got = exchange_blocks([blocks[k] for k in range(count)], "row")
        result = jnp.zeros((piece, count * rows), blocks.dtype)
        for k in range(count):
            result = lax.dynamic_update_slice(result, got[k], (0, (row ^ k) * rows))
        return result.T

    def listed(blocks):
        return [blocks[k] for k in range(count)]

    source_own = row_tokens(layer_input)
    source_own, output_grad = together(source_own, output_grad)
    grad_own = row_tokens(output_grad)
    kv_weight = jnp.concatenate([key_weight.T, value_weight.T])
    grad_own, query_weight, kv_weight = together(grad_own, query_weight, kv_weight)
    q_first = spread({0: query_weight}, "row", far)
    kv_first = spread({0: kv_weight}, "row", far)
    q_first, kv_first, mix_weight, gate_weight, attn_gain = together(
        q_first, kv_first, mix_weight, gate_weight, attn_gain
    )
    mix_first = spread({0: mix_weight}, "row", far)
    mix_first, up_weight = together(mix_first, up_weight)
    gate_first = spread({0: gate_weight.T}, "row", far)
    up_first = spread({0: up_weight.T}, "row", far)
    down_first = spread({0: down_weight}, "row", far)
    q_blocks = spread(q_first, "row", near)
    kv_blocks = spread(kv_first, "row", near)

    gains = lax.all_gather(jnp.stack([attn_gain, mlp_gain]), ("row", "col"), axis=1, tiled=True)
    gains = gains.reshape(2, count, cols, piece)
    gains = by_xor(gains, row, 1).swapaxes(1, 2)[..., None]
    gain_one, gain_two = gains[0], gains[1]

    cosine, sine = rope_parts(position_ids)
    other_seg = swapped(segment_ids, "row", 1)
    seg = jnp.where(parity == 0, other_seg, segment_ids)

    source = spread_cols(source_own)
    source, q_blocks, kv_blocks, gate_first, gain_one, cosine, sine, seg = together(
        source, q_blocks, kv_blocks, gate_first, gain_one, cosine, sine, seg
    )
    grad_own, source = together(grad_own, source)
    grad_all = spread_cols(grad_own)
    norm_one, scale_one, sets = qkv_project(
        source, gain_one, cosine, sine, listed(q_blocks), listed(kv_blocks)
    )
    own_set = lax.dynamic_index_in_dim(sets, parity, 0, keepdims=False)
    other_set = swapped(lax.dynamic_index_in_dim(sets, 1 - parity, 0, keepdims=False), "row", 1)
    attn_mine, attn_send, lse = attend(own_core, own_set, other_set, seg)
    attn_other = swapped(attn_send, "row", 1)
    mix_blocks = spread(mix_first, "row", near)
    attn_mine, attn_other, mix_blocks, up_first = together(
        attn_mine, attn_other, mix_blocks, up_first
    )
    attn_part = mix_out(own_core, attn_mine, attn_other, listed(mix_blocks), cols)
    attn_part, grad_all = together(attn_part, grad_all)
    attn_sum = sum_cols(attn_part)
    gate_blocks = spread(gate_first, "row", near)
    up_blocks = spread(up_first, "row", near)
    down_blocks = spread(down_first, "row", near)
    attn_sum, gate_blocks, up_blocks, down_blocks = together(
        attn_sum, gate_blocks, up_blocks, down_blocks
    )
    residual_own = source_own.astype(F32) + attn_sum.astype(F32)

    parts = 2 if rows % 256 == 0 else 1
    size = rows // parts
    spans = [slice(i * size, (i + 1) * size) for i in range(parts)]
    residual_low = residual_own.astype(BF)
    residual = [spread_cols(residual_low[..., span]) for span in spans]
    before, shares = (), []
    gain_share_two = 0.0
    for i in range(parts):
        out = feed_forward(
            residual[i],
            grad_all,
            i,
            parts,
            gain_two,
            listed(gate_blocks),
            listed(up_blocks),
            listed(down_blocks),
            before,
        )
        before = out[:5]
        shares.append(out[5])
        gain_share_two = gain_share_two + out[6]
    norm_two, grad_rows, act, dgate, dup = before
    share_sums = [sum_cols(share) for share in shares]
    down_grads = {k: dot(act, grad_rows[k], NT).astype(BF) for k in range(count)}
    down_grads = fold(down_grads, "row", near)
    dgate, dup, norm_two, down_grads = together(dgate, dup, norm_two, down_grads)
    gate_grads = {k: dot(dgate, norm_two[k], NT).astype(BF) for k in range(count)}
    up_grads = {k: dot(dup, norm_two[k], NT).astype(BF) for k in range(count)}
    gate_grads = fold(gate_grads, "row", near)
    up_grads = fold(up_grads, "row", near)
    *share_sums, down_grads, gate_grads, up_grads = together(
        *share_sums, down_grads, gate_grads, up_grads
    )
    residual_grad_own = grad_own.astype(F32) + jnp.concatenate(share_sums, axis=2).astype(F32)
    down_total = fold(down_grads, "row", far)[0]
    gate_total = fold(gate_grads, "row", far)[0]

    mix_cols = spread_cols(residual_grad_own.astype(BF))
    ff_part = fan_out(listed(down_blocks), act, cols)
    down_total = over_dp(down_total)
    mix_cols, ff_part, down_total, gate_total, up_grads = together(
        mix_cols, ff_part, down_total, gate_total, up_grads
    )
    up_total = fold(up_grads, "row", far)[0]
    gate_total = over_dp(gate_total)
    mix_rows, grad_mine, grad_send = mix_back(own_core, [mix_cols], listed(mix_blocks))
    ff_sum = sum_cols(ff_part)
    grad_other = swapped(grad_send, "row", 1)
    back_mine, back_send = attend_back(
        own_core, own_set, other_set, attn_mine, attn_send, grad_mine, grad_other, lse, seg
    )
    back_other = swapped(back_send, "row", 1)
    back_other, up_total, gate_total, down_total = together(
        back_other, up_total, gate_total, down_total
    )
    cut = up_total.shape[0] * 5 // 9 // 16 * 16
    up_head, up_tail = over_dp(up_total[:cut]), sent_over_dp(up_total[cut:])
    dq, dkv, share, gain_share_one = qkv_back(
        own_core,
        source,
        gain_one,
        scale_one,
        cosine,
        sine,
        sets,
        back_mine,
        back_other,
        listed(q_blocks),
        listed(kv_blocks),
    )
    share, attn_mine, mix_rows = together(share, attn_mine, mix_rows)
    attn_low = jnp.concatenate(
        [
            jnp.where(parity == 0, attn_mine, attn_other),
            jnp.where(parity == 0, attn_other, attn_mine),
        ]
    )
    mix_odd = {k: dot(attn_low, mix_rows[k], NT).astype(BF) for k in range(1, count, 2)}
    gain_shares = jnp.stack([gain_share_one[..., 0], gain_share_two[..., 0]], axis=2)
    share, ff_sum, mix_odd, up_head, gain_shares = together(
        share, ff_sum, mix_odd, up_head, gain_shares
    )
    input_sum = sum_cols(share)

    bits = near + far[::-1]
    gain_shares = fold({k: gain_shares[:, k] for k in range(count)}, "row", bits, low=False)[0]
    share, dq, dkv, attn_low, mix_rows = together(share, dq, dkv, attn_low, mix_rows)
    mix_even = {k: dot(attn_low, mix_rows[k], NT).astype(BF) for k in range(0, count, 2)}
    mix_near = fold({**mix_even, **mix_odd}, "row", near)
    dq, dkv, mix_near = together(dq, dkv, mix_near)
    mix_moved = {k: swapped(mix_near[k], "row", far_mask) for k in mix_near if k & far_mask}
    q_near = fold({k: dot(norm_one[k], dq, NT).astype(BF) for k in range(count)}, "row", near)
    kv_near = fold({k: dot(dkv, norm_one[k], NT).astype(BF) for k in range(count)}, "row", near)
    ff_sum, gain_shares, q_near, kv_near, up_tail, mix_near, mix_moved = together(
        ff_sum, gain_shares, q_near, kv_near, up_tail, mix_near, mix_moved
    )
    mix_far = fold_landed(mix_near, mix_moved, far_mask)
    mix_total = over_dp(fold(mix_far, "row", far[::-1][1:])[0])
    q_far = fold(q_near, "row", far)[0]
    kv_far = fold(kv_near, "row", far)[0]
    q_total, kv_total = over_dp(q_far), over_dp(kv_far)
    output_own = (residual_own + ff_sum.astype(F32)).astype(BF)
    layer_output = all_tokens(output_own)

    gain_shares = by_xor(gain_shares, lax.axis_index("col"), 0)
    gain_shares = {c: gain_shares[c] for c in range(cols)}
    gain_shares = fold(gain_shares, "col", near_bits(cols) + far_bits(cols), low=False)[0]
    gain_totals = over_dp(gain_shares)
    up_total = jnp.concatenate([up_head, summed_up(up_tail)])
    input_sum, q_total, kv_total, mix_total, gain_totals, layer_output, up_total = together(
        input_sum, q_total, kv_total, mix_total, gain_totals, layer_output, up_total
    )

    input_grad = all_tokens((residual_grad_own + input_sum.astype(F32)).astype(BF)).astype(F32)
    kv_rows = kv_total.shape[0] // 2
    return (
        layer_output,
        input_grad,
        gain_totals[0],
        gain_totals[1],
        q_total,
        kv_total[:kv_rows].T,
        kv_total[kv_rows:].T,
        mix_total,
        gate_total.T,
        up_total.T,
        down_total,
    )


def solution(mesh):
    return jax.shard_map(
        body,
        mesh=mesh,
        in_specs=(
            P("dp", ("row", "col")),
            P(("row", "col")),
            P(("row", "col")),
            P("row", "col"),
            P("row", "col"),
            P("row", "col"),
            P("col", "row"),
            P("row", "col"),
            P("row", "col"),
            P("col", "row"),
            P("dp", ("row", "col")),
            P(("dp", "row")),
            P(("dp", "row")),
        ),
        out_specs=(
            P("dp", ("row", "col")),
            P("dp", ("row", "col")),
            P(("row", "col")),
            P(("row", "col")),
            P("row", "col"),
            P("row", "col"),
            P("row", "col"),
            P("col", "row"),
            P("row", "col"),
            P("row", "col"),
            P("col", "row"),
        ),
        check_vma=False,
    )
```

```python
import functools

import jax
import jax.numpy as jnp
from jax import lax
from jax.experimental import pallas as pl
from jax.experimental.pallas import tpu as pltpu
from jax.sharding import PartitionSpec as P

D = 2560
HEAD = 80
EPS = 1e-05
THETA = 10000.0
NEG = -1e30
LOG2E = 1.4426950408889634
LN2 = 0.6931471805599453
ROOT = HEAD ** (-0.5)
BF = jnp.bfloat16
F32 = jnp.float32
NN = (((1,), (0,)), ((), ()))
TN = (((0,), (0,)), ((), ()))
NT = (((1,), (1,)), ((), ()))


def dot(left, right, dims=NN):
    return lax.dot_general(left, right, dims, preferred_element_type=F32)


def together(*values):
    return lax.optimization_barrier(values)


def swapped(value, axis, mask):
    size = lax.axis_size(axis)
    return lax.ppermute(value, axis, [(i, i ^ mask) for i in range(size)])


def spread(blocks, axis, bits):
    blocks = dict(blocks)
    for bit in bits:
        for k in list(blocks):
            blocks[k | bit] = swapped(blocks[k], axis, bit)
    return blocks


def fold(blocks, axis, bits, low=True):
    held = dict(blocks)
    for bit in bits:
        for k in [k for k in held if k & bit]:
            other = swapped(held.pop(k), axis, bit)
            total = held[k ^ bit].astype(F32) + other.astype(F32)
            held[k ^ bit] = total.astype(BF) if low else total
    return held


def fold_landed(held, moved, bit):
    return {
        k ^ bit: (held[k ^ bit].astype(F32) + other.astype(F32)).astype(BF)
        for k, other in moved.items()
    }


def far_bits(size):
    return [1 << i for i in range(1, size.bit_length() - 1)]


def near_bits(size):
    return [1] if size > 1 else []


def exchange_blocks(blocks, axis):
    return [blocks[0]] + [swapped(blocks[k], axis, k) for k in range(1, len(blocks))]


def by_xor(value, index, axis):
    parts = [
        lax.dynamic_index_in_dim(value, index ^ k, axis, keepdims=True)
        for k in range(value.shape[axis])
    ]
    return jnp.concatenate(parts, axis=axis)


def params(mib=58):
    return pltpu.CompilerParams(vmem_limit_bytes=mib * 1024 * 1024)


def takes(micros):
    return pl.CostEstimate(flops=int(micros * 0.1e9), transcendentals=0, bytes_accessed=0)


def shape(dims, dtype):
    return jax.ShapeDtypeStruct(dims, dtype)


SMALL = pl.BlockSpec(memory_space=pltpu.SMEM)
RAW = pl.BlockSpec(memory_space=pl.ANY)


def resident(dims, buffers=None):
    zeros = (0,) * len(dims)
    mode = {} if buffers is None else {"pipeline_mode": pl.Buffered(buffers)}
    return pl.BlockSpec(dims, lambda *_: zeros, **mode)


def normalise(x_ref, gain_ref, out_ref, scale_ref):
    cols, count, piece, _ = x_ref.shape
    total = None
    for c in range(cols):
        for k in range(count):
            value = x_ref[c, k].astype(F32)
            part = jnp.sum(value * value, axis=0, keepdims=True)
            total = part if total is None else total + part
    scale = lax.rsqrt(total / D + EPS)
    scale_ref[...] = scale
    for c in range(cols):
        for k in range(count):
            value = x_ref[c, k].astype(F32) * scale * gain_ref[c, k]
            out_ref[k, c * piece : (c + 1) * piece, :] = value.astype(BF)


def turn(value, cosine, sine):
    half = value.shape[0] // 2
    first, second = value[:half], value[half:]
    return jnp.concatenate([first * cosine - second * sine, second * cosine + first * sine])


def qkv_kernel(count, shared, x_ref, gain_ref, cos_ref, sin_ref, *refs):
    q_w, kv_w = refs[:count], refs[count : 2 * count]
    norm_ref, scale_ref, sets_ref = refs[2 * count :]
    normalise(x_ref, gain_ref, norm_ref, scale_ref)
    query = keyval = None
    for k in range(count):
        normed = norm_ref[k]
        part = dot(q_w[k][...], normed, TN)
        query = part if query is None else query + part
        part = dot(kv_w[k][...], normed)
        keyval = part if keyval is None else keyval + part
    cosine, sine = cos_ref[...], sin_ref[...]
    half = query.shape[0] // 2
    kv_half = keyval.shape[0] // 2
    for h in range(2):
        for at in range(0, half, HEAD):
            value = turn(query[h * half + at : h * half + at + HEAD], cosine, sine)
            sets_ref[h, at : at + HEAD, :] = (value * (ROOT * LOG2E)).astype(BF)
        at = 0 if shared else h * HEAD
        key = turn(keyval[at : at + HEAD], cosine, sine)
        sets_ref[h, half : half + HEAD, :] = key.astype(BF)
        sets_ref[h, half + HEAD : half + 2 * HEAD, :] = keyval[
            kv_half + at : kv_half + at + HEAD
        ].astype(BF)


def qkv_project(x, gain, cosine, sine, q_w, kv_w):
    cols, count, piece, tokens = x.shape
    half = q_w[0].shape[1] // 2
    shared = kv_w[0].shape[0] == 2 * HEAD
    return pl.pallas_call(
        functools.partial(qkv_kernel, count, shared),
        out_shape=(
            shape((count, cols * piece, tokens), BF),
            shape((1, tokens), F32),
            shape((2, half + 2 * HEAD, tokens), BF),
        ),
        compiler_params=params(),
        name="qkv_project",
        cost_estimate=takes(12),
    )(x, gain, cosine, sine, *q_w, *kv_w)


def pieces_of(half, at, tile, tokens):
    if half == 1:
        return [(0, 0, tokens, False), (1, 0, at + tile, True)]
    head = [(0, 0, at, False)] if at else []
    return head + [(0, at, at + tile, True)]


def seen_of(half, at, begin, end, tile, seg_row, seg_col):
    rows = lax.broadcasted_iota(jnp.int32, (end - begin, tile), 0) + begin
    cols = lax.broadcasted_iota(jnp.int32, (end - begin, tile), 1) + at
    seen = rows <= cols
    if half == 1:
        seen = seen & (seg_col[begin:end] == seg_row[:, at : at + tile])
    return seen


def place(parity, own_ref, other_ref, sets):
    sets[parity] = own_ref[...]
    sets[1 - parity] = other_ref[...]


def attend_kernel(
    tile, parity_ref, own_ref, other_ref, seg_row, seg_col, mine_ref, send_ref, lse_ref, sets, rows
):
    tokens = own_ref.shape[-1]
    heads = pl.num_programs(0)
    head = pl.program_id(0)
    parity = parity_ref[0]
    half_rows = own_ref.shape[0] - 2 * HEAD

    @pl.when(head == 0)
    def _():
        place(parity, own_ref, other_ref, sets)
        for half in range(2):
            keys = sets[half, half_rows : half_rows + HEAD, :]
            rows[half] = keys.astype(F32).T.astype(BF)

    at_head = pl.ds(pl.multiple_of(head * HEAD, 16), HEAD)
    for half in range(2):
        for at in range(0, tokens, tile):
            span = slice(at, at + tile)
            query = sets[half, at_head, span]
            pieces = pieces_of(half, at, tile, tokens)
            scores = []
            for which, begin, end, masked in pieces:
                part = dot(rows[which, begin:end, :], query)
                if masked:
                    part = jnp.where(
                        seen_of(half, at, begin, end, tile, seg_row, seg_col), part, NEG
                    )
                scores.append(part)
            peak = functools.reduce(
                jnp.maximum, [jnp.max(s, axis=0, keepdims=True) for s in scores]
            )
            total = out = None
            for (which, begin, end, _), part in zip(pieces, scores):
                weights = jnp.exp2(part - peak)
                mass = jnp.sum(weights, axis=0, keepdims=True)
                value = dot(sets[which, half_rows + HEAD :, begin:end], weights.astype(BF))
                total = mass if total is None else total + mass
                out = value if out is None else out + value
            out = (out / total).astype(BF)
            lse_ref[half, 0, :, span] = peak + jnp.log2(total)

            @pl.when(parity == half)
            def _():
                mine_ref[at_head, span] = out

            @pl.when(parity != half)
            def _():
                send_ref[at_head, span] = out


def attend(parity, own, other, seg):
    depth, tokens = own.shape
    half_rows = depth - 2 * HEAD
    heads = half_rows // HEAD
    tile = min(256, tokens)
    out = resident((half_rows, tokens))
    return pl.pallas_call(
        functools.partial(attend_kernel, tile),
        out_shape=(
            shape((half_rows, tokens), BF),
            shape((half_rows, tokens), BF),
            shape((2, heads, 1, tokens), F32),
        ),
        grid=(heads,),
        in_specs=[
            SMALL,
            resident((depth, tokens)),
            resident((depth, tokens)),
            resident((1, tokens)),
            resident((tokens, 1)),
        ],
        out_specs=(out, out, pl.BlockSpec((2, 1, 1, tokens), lambda h: (0, h, 0, 0))),
        scratch_shapes=[
            pltpu.VMEM((2, depth, tokens), BF),
            pltpu.VMEM((2, tokens, HEAD), BF),
        ],
        compiler_params=params(),
        name="attend",
        cost_estimate=takes(27),
    )(parity, own, other, seg[None, :], seg[:, None])


def attend_back_kernel(
    tile,
    parity_ref,
    own_ref,
    other_ref,
    own_out,
    other_out,
    own_grad,
    other_grad,
    lse_ref,
    seg_row,
    seg_col,
    mine_ref,
    send_ref,
    sets,
    outs,
    grads,
    rows,
    key_acc,
    value_acc,
):
    tokens = own_ref.shape[-1]
    heads = pl.num_programs(0)
    head = pl.program_id(0)
    parity = parity_ref[0]
    half_rows = own_ref.shape[0] - 2 * HEAD

    @pl.when(head == 0)
    def _():
        place(parity, own_ref, other_ref, sets)
        place(parity, own_out, other_out, outs)
        place(parity, own_grad, other_grad, grads)
        for half in range(2):
            for i in range(2):
                at = half_rows + i * HEAD
                rows[i, half] = sets[half, at : at + HEAD, :].astype(F32).T.astype(BF)
        key_acc[...] = jnp.zeros_like(key_acc)
        value_acc[...] = jnp.zeros_like(value_acc)

    at_head = pl.ds(pl.multiple_of(head * HEAD, 16), HEAD)
    for half in range(2):
        for at in range(0, tokens, tile):
            span = slice(at, at + tile)
            query = sets[half, at_head, span]
            grad = grads[half, at_head, span]
            lse = lse_ref[half, 0, :, span]
            delta = jnp.sum(
                grad.astype(F32) * outs[half, at_head, span].astype(F32), axis=0, keepdims=True
            )
            total = None
            for which, begin, end, masked in pieces_of(half, at, tile, tokens):
                part = dot(rows[0, which, begin:end, :], query)
                if masked:
                    part = jnp.where(
                        seen_of(half, at, begin, end, tile, seg_row, seg_col), part, NEG
                    )
                weights = jnp.exp2(part - lse)
                dprod = dot(rows[1, which, begin:end, :], grad)
                dscore = (weights * (dprod - delta)).astype(BF)
                value_acc[which, :, begin:end] += dot(grad, weights.astype(BF), NT)
                key_acc[which, :, begin:end] += dot(query, dscore, NT)
                more = dot(sets[which, half_rows : half_rows + HEAD, begin:end], dscore)
                total = more if total is None else total + more
            total = (total * ROOT).astype(BF)

            @pl.when(parity == half)
            def _():
                mine_ref[at_head, span] = total

            @pl.when(parity != half)
            def _():
                send_ref[at_head, span] = total

    @pl.when(head == heads - 1)
    def _():
        for ref, which in ((mine_ref, parity), (send_ref, 1 - parity)):
            ref[half_rows : half_rows + HEAD, :] = (key_acc[which] * LN2).astype(BF)
            ref[half_rows + HEAD :, :] = value_acc[which].astype(BF)


def attend_back(parity, own, other, own_out, other_out, own_grad, other_grad, lse, seg):
    depth, tokens = own.shape
    half_rows = depth - 2 * HEAD
    heads = half_rows // HEAD
    tile = min(256, tokens)
    full, part = resident((depth, tokens)), resident((half_rows, tokens))
    return pl.pallas_call(
        functools.partial(attend_back_kernel, tile),
        out_shape=(shape((depth, tokens), BF), shape((depth, tokens), BF)),
        grid=(heads,),
        in_specs=[
            SMALL,
            full,
            full,
            part,
            part,
            part,
            part,
            pl.BlockSpec((2, 1, 1, tokens), lambda h: (0, h, 0, 0)),
            resident((1, tokens)),
            resident((tokens, 1)),
        ],
        out_specs=(full, full),
        scratch_shapes=[
            pltpu.VMEM((2, depth, tokens), BF),
            pltpu.VMEM((2, half_rows, tokens), BF),
            pltpu.VMEM((2, half_rows, tokens), BF),
            pltpu.VMEM((2, 2, tokens, HEAD), BF),
            pltpu.VMEM((2, HEAD, tokens), F32),
            pltpu.VMEM((2, HEAD, tokens), F32),
        ],
        compiler_params=params(),
        name="attend_back",
        cost_estimate=takes(37),
    )(
        parity,
        own,
        other,
        own_out,
        other_out,
        own_grad,
        other_grad,
        lse,
        seg[None, :],
        seg[:, None],
    )


def halves_at(parity, half_rows):
    mine = pl.ds(pl.multiple_of(parity * half_rows, 16), half_rows)
    other = pl.ds(pl.multiple_of((1 - parity) * half_rows, 16), half_rows)
    return mine, other


def mix_out_kernel(count, parity_ref, own_ref, other_ref, *refs):
    weights, out_ref = refs[:count], refs[count]
    cols, _, piece, _ = out_ref.shape
    mine, other = halves_at(parity_ref[0], own_ref.shape[0])
    for k in range(count):
        part = dot(weights[k][mine, :], own_ref[...], TN)
        part = part + dot(weights[k][other, :], other_ref[...], TN)
        for c in range(cols):
            out_ref[c, k] = part[c * piece : (c + 1) * piece].astype(BF)


def mix_out(parity, own, other, weights, cols):
    count = len(weights)
    piece = weights[0].shape[1] // cols
    vmem = pl.BlockSpec(memory_space=pltpu.VMEM)
    return pl.pallas_call(
        functools.partial(mix_out_kernel, count),
        out_shape=shape((cols, count, piece, own.shape[1]), BF),
        in_specs=[SMALL] + [vmem] * (2 + count),
        compiler_params=params(),
        name="mix_out",
        cost_estimate=takes(10),
    )(parity, own, other, *weights)


def mix_back_kernel(count, parts, parity_ref, *refs):
    x_refs, weights = refs[:parts], refs[parts : parts + count]
    rows_ref, own_ref, other_ref = refs[parts + count :]
    for i, x_ref in enumerate(x_refs):
        cols, _, piece, tokens = x_ref.shape
        for c in range(cols):
            for k in range(count):
                rows_ref[k, c * piece : (c + 1) * piece, i * tokens : (i + 1) * tokens] = x_ref[
                    c, k
                ]
    mine, other = halves_at(parity_ref[0], own_ref.shape[0])
    for at, out_ref in ((other, other_ref), (mine, own_ref)):
        total = None
        for k in range(count):
            part = dot(weights[k][at, :], rows_ref[k])
            total = part if total is None else total + part
        out_ref[...] = total.astype(BF)


def mix_back(parity, x_parts, weights):
    parts = len(x_parts)
    cols, count, piece, tokens = x_parts[0].shape
    tokens = tokens * parts
    half_rows = weights[0].shape[0] // 2
    vmem = pl.BlockSpec(memory_space=pltpu.VMEM)
    return pl.pallas_call(
        functools.partial(mix_back_kernel, count, parts),
        out_shape=(
            shape((count, cols * piece, tokens), BF),
            shape((half_rows, tokens), BF),
            shape((half_rows, tokens), BF),
        ),
        in_specs=[SMALL] + [vmem] * (parts + count),
        compiler_params=params(),
        name="mix_back",
        cost_estimate=takes(9),
    )(parity, *x_parts, *weights)


def fan_kernel(count, x_ref, *refs):
    weights, out_ref = refs[:count], refs[count]
    cols, _, piece, _ = out_ref.shape
    for k in range(count):
        part = dot(weights[k][...], x_ref[...], TN)
        for c in range(cols):
            out_ref[c, k] = part[c * piece : (c + 1) * piece].astype(BF)


def fan_out(weights, x, cols):
    count = len(weights)
    piece = weights[0].shape[1] // cols
    return pl.pallas_call(
        functools.partial(fan_kernel, count),
        out_shape=shape((cols, count, piece, x.shape[1]), BF),
        compiler_params=params(),
        name="fan_out",
        cost_estimate=takes(17),
    )(x, *weights)


def norm_back(grads, k, x_ref, gain_ref, scale, coef, share_ref, gain_share_ref):
    cols, _, piece, _ = x_ref.shape
    for c in range(cols):
        grad = grads[c * piece : (c + 1) * piece]
        value = x_ref[c, k].astype(F32)
        gain_share_ref[c, k] = jnp.sum(grad * (value * scale), axis=1, keepdims=True)
        share_ref[c, k] = ((grad * gain_ref[c, k]) * scale - value * coef).astype(BF)


def ff_kernel(count, chained, x_ref, g_ref, gain_ref, *refs):
    gate_w, up_w, down_w = refs[:count], refs[count : 2 * count], refs[2 * count : 3 * count]
    refs = refs[3 * count + (5 if chained else 0) :]
    norm_ref, rows_ref, act_ref, dgate_ref, dup_ref, share_ref, gain_share_ref = refs[:7]
    scale_ref, inner_ref, back_ref = refs[7:]
    cols, _, piece, _ = x_ref.shape
    step = pl.program_id(0)

    @pl.when(step == 0)
    def _():
        normalise(x_ref, gain_ref, norm_ref, scale_ref)
        for c in range(cols):
            for k in range(count):
                rows_ref[k, c * piece : (c + 1) * piece, :] = g_ref[c, k]
        inner_ref[...] = jnp.zeros_like(inner_ref)
        back_ref[...] = jnp.zeros_like(back_ref)

    def summed(weights, ref):
        total = None
        for k in range(count):
            part = dot(weights[k][...], ref[k])
            total = part if total is None else total + part
        return total

    gate = summed(gate_w, norm_ref)
    up = summed(up_w, norm_ref)
    sigma = jax.nn.sigmoid(gate)
    silu = gate * sigma
    act_ref[...] = (silu * up).astype(BF)
    grad = summed(down_w, rows_ref)
    dup = grad * silu
    dgate = grad * up * (sigma + silu * (1.0 - sigma))
    inner_ref[...] += jnp.sum(dgate * gate + dup * up, axis=0, keepdims=True)
    dgate_ref[...] = dgate.astype(BF)
    dup_ref[...] = dup.astype(BF)
    for k in range(count):
        back_ref[k] += dot(gate_w[k][...], dgate_ref[...], TN) + dot(
            up_w[k][...], dup_ref[...], TN
        )

    @pl.when(step == pl.num_programs(0) - 1)
    def _():
        scale = scale_ref[...]
        coef = scale * scale * inner_ref[...] / D
        for k in range(count):
            norm_back(back_ref[k], k, x_ref, gain_ref, scale, coef, share_ref, gain_share_ref)


def feed_forward(x, g, part, parts, gain, gate_w, up_w, down_w, before):
    cols, count, piece, tokens = x.shape
    width, depth = gate_w[0].shape
    tile = 432 if width % 432 == 0 else width
    g_spec = pl.BlockSpec(x.shape, lambda n: (0, 0, 0, part), pipeline_mode=pl.Buffered(1))
    rows = (count, cols * piece, tokens)
    rows_spec = pl.BlockSpec(rows, lambda n: (0, 0, part), pipeline_mode=pl.Buffered(1))
    w_spec = pl.BlockSpec((tile, depth), lambda n: (n, 0))
    h_spec = pl.BlockSpec((tile, tokens), lambda n: (n, part))
    rows_all = shape((count, cols * piece, tokens * parts), BF)
    hidden = shape((width, tokens * parts), BF)
    first = 3 + 3 * count
    return pl.pallas_call(
        functools.partial(ff_kernel, count, bool(before)),
        out_shape=(
            rows_all,
            rows_all,
            hidden,
            hidden,
            hidden,
            shape(x.shape, BF),
            shape(gain.shape, F32),
        ),
        grid=(width // tile,),
        in_specs=[resident(x.shape, 1), g_spec, resident(gain.shape, 1)]
        + [w_spec] * (3 * count)
        + [RAW] * len(before),
        out_specs=(
            rows_spec,
            rows_spec,
            h_spec,
            h_spec,
            h_spec,
            resident(x.shape, 1),
            resident(gain.shape, 1),
        ),
        scratch_shapes=[
            pltpu.VMEM((1, tokens), F32),
            pltpu.VMEM((1, tokens), F32),
            pltpu.VMEM(rows, F32),
        ],
        input_output_aliases={first + i: i for i in range(len(before))},
        compiler_params=params(60),
        name="feed_forward",
        cost_estimate=takes(42),
    )(x, g, gain, *gate_w, *up_w, *down_w, *before)


def qkv_back_kernel(
    count,
    shared,
    parity_ref,
    x_ref,
    gain_ref,
    scale_ref,
    cos_ref,
    sin_ref,
    sets_ref,
    own_ref,
    other_ref,
    *refs,
):
    q_w, kv_w = refs[:count], refs[count : 2 * count]
    dq_ref, dkv_ref, share_ref, gain_share_ref = refs[2 * count :]
    parity = parity_ref[0]
    half_rows = own_ref.shape[0] - 2 * HEAD
    kv_half = dkv_ref.shape[0] // 2
    cosine, sine = cos_ref[...], -sin_ref[...]
    inner = None
    folded = None
    for grads, which in ((own_ref, parity), (other_ref, 1 - parity)):
        for at in range(0, half_rows + 2 * HEAD, HEAD):
            value = grads[at : at + HEAD, :].astype(F32)
            part = value * sets_ref[which, at : at + HEAD, :].astype(F32)
            part = jnp.sum(part, axis=0, keepdims=True)
            if at < half_rows:
                part = part * (1.0 / (ROOT * LOG2E))
                start = pl.multiple_of(which * half_rows + at, 16)
                dq_ref[pl.ds(start, HEAD), :] = turn(value, cosine, sine).astype(BF)
            else:
                is_key = at == half_rows
                raw = turn(value, cosine, sine) if is_key else value
                base = 0 if is_key else kv_half
                if not shared:
                    start = pl.multiple_of(base + which * HEAD, 16)
                    dkv_ref[pl.ds(start, HEAD), :] = raw.astype(BF)
                elif folded is None or at not in folded:
                    folded = {**(folded or {}), at: raw}
                else:
                    dkv_ref[base : base + HEAD, :] = (folded[at] + raw).astype(BF)
            inner = part if inner is None else inner + part
    scale = scale_ref[...]
    coef = scale * scale * inner / D
    for k in range(count):
        grads = dot(q_w[k][...], dq_ref[...]) + dot(kv_w[k][...], dkv_ref[...], TN)
        norm_back(grads, k, x_ref, gain_ref, scale, coef, share_ref, gain_share_ref)


def qkv_back(parity, x, gain, scale, cosine, sine, sets, own, other, q_w, kv_w):
    cols, count, piece, tokens = x.shape
    shared = kv_w[0].shape[0] == 2 * HEAD
    vmem = pl.BlockSpec(memory_space=pltpu.VMEM)
    return pl.pallas_call(
        functools.partial(qkv_back_kernel, count, shared),
        out_shape=(
            shape((q_w[0].shape[1], tokens), BF),
            shape((kv_w[0].shape[0], tokens), BF),
            shape(x.shape, BF),
            shape(gain.shape, F32),
        ),
        in_specs=[SMALL] + [vmem] * (8 + 2 * count),
        compiler_params=params(),
        name="qkv_back",
        cost_estimate=takes(17),
    )(parity, x, gain, scale, cosine, sine, sets, own, other, *q_w, *kv_w)


def rope_parts(positions):
    half = HEAD // 2
    freq = THETA ** (-jnp.arange(half, dtype=F32) * 2.0 / HEAD)
    angle = freq[:, None] * positions.astype(F32)[None, :]
    return (jnp.cos(angle), jnp.sin(angle))


def spread_cols(value):
    return lax.all_gather(value, "col", axis=0, tiled=False)


def sum_cols(value):
    return lax.psum_scatter(value, "col", scatter_dimension=0, tiled=False)


def sent_over_dp(value):
    low = value.astype(BF)
    size = lax.axis_size("dp")
    others = [
        lax.ppermute(low, "dp", [(i, (i + step) % size) for i in range(size)])
        for step in range(1, size)
    ]
    return [low] + others


def summed_up(parts):
    total = parts[0].astype(F32)
    for other in parts[1:]:
        total = total + other.astype(F32)
    return total


def over_dp(value):
    return summed_up(sent_over_dp(value))


def body(
    layer_input,
    attn_gain,
    mlp_gain,
    query_weight,
    key_weight,
    value_weight,
    mix_weight,
    gate_weight,
    up_weight,
    down_weight,
    output_grad,
    segment_ids,
    position_ids,
):
    rows = segment_ids.shape[0]
    count = lax.axis_size("row")
    cols = lax.axis_size("col")
    piece = layer_input.shape[1]
    row = lax.axis_index("row")
    parity = (row % 2).astype(jnp.int32)
    own_core = parity.reshape(1)
    q_half = query_weight.shape[1] // 2
    near, far = near_bits(count), far_bits(count)
    far_mask = far[-1]

    def row_tokens(value):
        turned = value.T
        outgoing = [
            lax.dynamic_slice(turned, (0, (row ^ k) * rows), (piece, rows)) for k in range(count)
        ]
        return jnp.stack(exchange_blocks(outgoing, "row"))

    def all_tokens(blocks):
        got = exchange_blocks([blocks[k] for k in range(count)], "row")
        result = jnp.zeros((piece, count * rows), blocks.dtype)
        for k in range(count):
            result = lax.dynamic_update_slice(result, got[k], (0, (row ^ k) * rows))
        return result.T

    def listed(blocks):
        return [blocks[k] for k in range(count)]

    source_own = row_tokens(layer_input)
    source_own, output_grad = together(source_own, output_grad)
    grad_own = row_tokens(output_grad)
    kv_weight = jnp.concatenate([key_weight.T, value_weight.T])
    grad_own, query_weight, kv_weight = together(grad_own, query_weight, kv_weight)
    q_first = spread({0: query_weight}, "row", far)
    kv_first = spread({0: kv_weight}, "row", far)
    q_first, kv_first, mix_weight, gate_weight, attn_gain = together(
        q_first, kv_first, mix_weight, gate_weight, attn_gain
    )
    mix_first = spread({0: mix_weight}, "row", far)
    mix_first, up_weight = together(mix_first, up_weight)
    gate_first = spread({0: gate_weight.T}, "row", far)
    up_first = spread({0: up_weight.T}, "row", far)
    down_first = spread({0: down_weight}, "row", far)
    q_blocks = spread(q_first, "row", near)
    kv_blocks = spread(kv_first, "row", near)

    gains = lax.all_gather(jnp.stack([attn_gain, mlp_gain]), ("row", "col"), axis=1, tiled=True)
    gains = gains.reshape(2, count, cols, piece)
    gains = by_xor(gains, row, 1).swapaxes(1, 2)[..., None]
    gain_one, gain_two = gains[0], gains[1]

    cosine, sine = rope_parts(position_ids)
    other_seg = swapped(segment_ids, "row", 1)
    seg = jnp.where(parity == 0, other_seg, segment_ids)

    source = spread_cols(source_own)
    source, q_blocks, kv_blocks, gate_first, gain_one, cosine, sine, seg = together(
        source, q_blocks, kv_blocks, gate_first, gain_one, cosine, sine, seg
    )
    grad_own, source = together(grad_own, source)
    grad_all = spread_cols(grad_own)
    norm_one, scale_one, sets = qkv_project(
        source, gain_one, cosine, sine, listed(q_blocks), listed(kv_blocks)
    )
    own_set = lax.dynamic_index_in_dim(sets, parity, 0, keepdims=False)
    other_set = swapped(lax.dynamic_index_in_dim(sets, 1 - parity, 0, keepdims=False), "row", 1)
    attn_mine, attn_send, lse = attend(own_core, own_set, other_set, seg)
    attn_other = swapped(attn_send, "row", 1)
    mix_blocks = spread(mix_first, "row", near)
    attn_mine, attn_other, mix_blocks, up_first = together(
        attn_mine, attn_other, mix_blocks, up_first
    )
    attn_part = mix_out(own_core, attn_mine, attn_other, listed(mix_blocks), cols)
    attn_part, grad_all = together(attn_part, grad_all)
    attn_sum = sum_cols(attn_part)
    gate_blocks = spread(gate_first, "row", near)
    up_blocks = spread(up_first, "row", near)
    down_blocks = spread(down_first, "row", near)
    attn_sum, gate_blocks, up_blocks, down_blocks = together(
        attn_sum, gate_blocks, up_blocks, down_blocks
    )
    residual_own = source_own.astype(F32) + attn_sum.astype(F32)

    parts = 2 if rows % 256 == 0 else 1
    size = rows // parts
    spans = [slice(i * size, (i + 1) * size) for i in range(parts)]
    residual_low = residual_own.astype(BF)
    residual = [spread_cols(residual_low[..., span]) for span in spans]
    before, shares = (), []
    gain_share_two = 0.0
    for i in range(parts):
        out = feed_forward(
            residual[i],
            grad_all,
            i,
            parts,
            gain_two,
            listed(gate_blocks),
            listed(up_blocks),
            listed(down_blocks),
            before,
        )
        before = out[:5]
        shares.append(out[5])
        gain_share_two = gain_share_two + out[6]
    norm_two, grad_rows, act, dgate, dup = before
    share_sums = [sum_cols(share) for share in shares]
    down_grads = {k: dot(act, grad_rows[k], NT).astype(BF) for k in range(count)}
    down_grads = fold(down_grads, "row", near)
    dgate, dup, norm_two, down_grads = together(dgate, dup, norm_two, down_grads)
    gate_grads = {k: dot(dgate, norm_two[k], NT).astype(BF) for k in range(count)}
    up_grads = {k: dot(dup, norm_two[k], NT).astype(BF) for k in range(count)}
    gate_grads = fold(gate_grads, "row", near)
    up_grads = fold(up_grads, "row", near)
    cut = down_grads[0].shape[0] // 32 * 16
    head = {k: v[:cut] for k, v in down_grads.items()}
    tail = {k: v[cut:] for k, v in down_grads.items()}
    head_moved = {k: swapped(head[k], "row", far_mask) for k in head if k & far_mask}
    *share_sums, head, tail, head_moved, gate_grads, up_grads = together(
        *share_sums, head, tail, head_moved, gate_grads, up_grads
    )
    residual_grad_own = grad_own.astype(F32) + jnp.concatenate(share_sums, axis=2).astype(F32)
    head = fold(fold_landed(head, head_moved, far_mask), "row", far[::-1][1:])[0]
    tail = fold(tail, "row", far[::-1])[0]
    tail, gate_grads = together(tail, gate_grads)
    down_parts = sent_over_dp(jnp.concatenate([head, tail]))
    gate_total = fold(gate_grads, "row", far)[0]

    mix_cols = spread_cols(residual_grad_own.astype(BF))
    ff_part = fan_out(listed(down_blocks), act, cols)
    mix_cols, ff_part, down_parts, gate_total, up_grads = together(
        mix_cols, ff_part, down_parts, gate_total, up_grads
    )
    up_total = fold(up_grads, "row", far)[0]
    gate_parts = sent_over_dp(gate_total)
    mix_rows, grad_mine, grad_send = mix_back(own_core, [mix_cols], listed(mix_blocks))
    ff_sum = sum_cols(ff_part)
    grad_other = swapped(grad_send, "row", 1)
    back_mine, back_send = attend_back(
        own_core, own_set, other_set, attn_mine, attn_send, grad_mine, grad_other, lse, seg
    )
    back_other = swapped(back_send, "row", 1)
    back_other, up_total, gate_parts = together(back_other, up_total, gate_parts)
    cut = up_total.shape[0] * 5 // 9 // 16 * 16
    up_head, up_tail = over_dp(up_total[:cut]), sent_over_dp(up_total[cut:])
    dq, dkv, share, gain_share_one = qkv_back(
        own_core,
        source,
        gain_one,
        scale_one,
        cosine,
        sine,
        sets,
        back_mine,
        back_other,
        listed(q_blocks),
        listed(kv_blocks),
    )
    share, attn_mine, mix_rows = together(share, attn_mine, mix_rows)
    attn_low = jnp.concatenate(
        [
            jnp.where(parity == 0, attn_mine, attn_other),
            jnp.where(parity == 0, attn_other, attn_mine),
        ]
    )
    mix_odd = {k: dot(attn_low, mix_rows[k], NT).astype(BF) for k in range(1, count, 2)}
    gain_shares = jnp.stack([gain_share_one[..., 0], gain_share_two[..., 0]], axis=2)
    share, ff_sum, mix_odd, up_head, gain_shares = together(
        share, ff_sum, mix_odd, up_head, gain_shares
    )
    input_sum = sum_cols(share)

    bits = near + far[::-1]
    gain_shares = fold({k: gain_shares[:, k] for k in range(count)}, "row", bits, low=False)[0]
    share, dq, dkv, attn_low, mix_rows = together(share, dq, dkv, attn_low, mix_rows)
    mix_even = {k: dot(attn_low, mix_rows[k], NT).astype(BF) for k in range(0, count, 2)}
    mix_near = fold({**mix_even, **mix_odd}, "row", near)
    dq, dkv, mix_near = together(dq, dkv, mix_near)
    mix_moved = {k: swapped(mix_near[k], "row", far_mask) for k in mix_near if k & far_mask}
    q_near = fold({k: dot(norm_one[k], dq, NT).astype(BF) for k in range(count)}, "row", near)
    kv_near = fold({k: dot(dkv, norm_one[k], NT).astype(BF) for k in range(count)}, "row", near)
    ff_sum, gain_shares, q_near, kv_near, up_tail, mix_near, mix_moved = together(
        ff_sum, gain_shares, q_near, kv_near, up_tail, mix_near, mix_moved
    )
    q_near, gate_parts, down_parts = together(q_near, gate_parts, down_parts)
    gate_total, down_total = summed_up(gate_parts), summed_up(down_parts)
    mix_far = fold_landed(mix_near, mix_moved, far_mask)
    mix_total = over_dp(fold(mix_far, "row", far[::-1][1:])[0])
    q_far = fold(q_near, "row", far)[0]
    q_far, kv_near = together(q_far, kv_near)
    kv_far = fold(kv_near, "row", far)[0]
    q_total, kv_total = over_dp(q_far), over_dp(kv_far)
    output_own = (residual_own + ff_sum.astype(F32)).astype(BF)
    layer_output = all_tokens(output_own)

    gain_shares = by_xor(gain_shares, lax.axis_index("col"), 0)
    gain_shares = {c: gain_shares[c] for c in range(cols)}
    gain_shares = fold(gain_shares, "col", near_bits(cols) + far_bits(cols), low=False)[0]
    gain_totals = over_dp(gain_shares)
    up_total = jnp.concatenate([up_head, summed_up(up_tail)])
    input_sum, q_total, kv_total, mix_total, gain_totals, layer_output, up_total = together(
        input_sum, q_total, kv_total, mix_total, gain_totals, layer_output, up_total
    )

    input_grad = all_tokens((residual_grad_own + input_sum.astype(F32)).astype(BF)).astype(F32)
    kv_rows = kv_total.shape[0] // 2
    return (
        layer_output,
        input_grad,
        gain_totals[0],
        gain_totals[1],
        q_total,
        kv_total[:kv_rows].T,
        kv_total[kv_rows:].T,
        mix_total,
        gate_total.T,
        up_total.T,
        down_total,
    )


def solution(mesh):
    return jax.shard_map(
        body,
        mesh=mesh,
        in_specs=(
            P("dp", ("row", "col")),
            P(("row", "col")),
            P(("row", "col")),
            P("row", "col"),
            P("row", "col"),
            P("row", "col"),
            P("col", "row"),
            P("row", "col"),
            P("row", "col"),
            P("col", "row"),
            P("dp", ("row", "col")),
            P(("dp", "row")),
            P(("dp", "row")),
        ),
        out_specs=(
            P("dp", ("row", "col")),
            P("dp", ("row", "col")),
            P(("row", "col")),
            P(("row", "col")),
            P("row", "col"),
            P("row", "col"),
            P("row", "col"),
            P("col", "row"),
            P("row", "col"),
            P("row", "col"),
            P("col", "row"),
        ),
        check_vma=False,
    )
```

```python
import functools

import jax
import jax.numpy as jnp
from jax import lax
from jax.experimental import pallas as pl
from jax.experimental.pallas import tpu as pltpu
from jax.sharding import PartitionSpec as P

D = 2560
HEAD = 80
EPS = 1e-05
THETA = 10000.0
NEG = -1e30
LOG2E = 1.4426950408889634
LN2 = 0.6931471805599453
ROOT = HEAD ** (-0.5)
BF = jnp.bfloat16
F32 = jnp.float32
NN = (((1,), (0,)), ((), ()))
TN = (((0,), (0,)), ((), ()))
NT = (((1,), (1,)), ((), ()))


def dot(left, right, dims=NN):
    return lax.dot_general(left, right, dims, preferred_element_type=F32)


def together(*values):
    return lax.optimization_barrier(values)


def swapped(value, axis, mask):
    size = lax.axis_size(axis)
    return lax.ppermute(value, axis, [(i, i ^ mask) for i in range(size)])


def spread(blocks, axis, bits):
    blocks = dict(blocks)
    for bit in bits:
        for k in list(blocks):
            blocks[k | bit] = swapped(blocks[k], axis, bit)
    return blocks


def fold(blocks, axis, bits, low=True):
    held = dict(blocks)
    for bit in bits:
        for k in [k for k in held if k & bit]:
            other = swapped(held.pop(k), axis, bit)
            total = held[k ^ bit].astype(F32) + other.astype(F32)
            held[k ^ bit] = total.astype(BF) if low else total
    return held


def fold_landed(held, moved, bit):
    return {
        k ^ bit: (held[k ^ bit].astype(F32) + other.astype(F32)).astype(BF)
        for k, other in moved.items()
    }


def far_bits(size):
    return [1 << i for i in range(1, size.bit_length() - 1)]


def near_bits(size):
    return [1] if size > 1 else []


def exchange_blocks(blocks, axis):
    return [blocks[0]] + [swapped(blocks[k], axis, k) for k in range(1, len(blocks))]


def by_xor(value, index, axis):
    parts = [
        lax.dynamic_index_in_dim(value, index ^ k, axis, keepdims=True)
        for k in range(value.shape[axis])
    ]
    return jnp.concatenate(parts, axis=axis)


def params(mib=58):
    return pltpu.CompilerParams(vmem_limit_bytes=mib * 1024 * 1024)


def takes(micros):
    return pl.CostEstimate(flops=int(micros * 0.1e9), transcendentals=0, bytes_accessed=0)


def shape(dims, dtype):
    return jax.ShapeDtypeStruct(dims, dtype)


SMALL = pl.BlockSpec(memory_space=pltpu.SMEM)
RAW = pl.BlockSpec(memory_space=pl.ANY)


def resident(dims, buffers=None):
    zeros = (0,) * len(dims)
    mode = {} if buffers is None else {"pipeline_mode": pl.Buffered(buffers)}
    return pl.BlockSpec(dims, lambda *_: zeros, **mode)


def normalise(x_ref, gain_ref, out_ref, scale_ref):
    cols, count, piece, _ = x_ref.shape
    total = None
    for c in range(cols):
        for k in range(count):
            value = x_ref[c, k].astype(F32)
            part = jnp.sum(value * value, axis=0, keepdims=True)
            total = part if total is None else total + part
    scale = lax.rsqrt(total / D + EPS)
    scale_ref[...] = scale
    for c in range(cols):
        for k in range(count):
            value = x_ref[c, k].astype(F32) * scale * gain_ref[c, k]
            out_ref[k, c * piece : (c + 1) * piece, :] = value.astype(BF)


def turn(value, cosine, sine):
    half = value.shape[0] // 2
    first, second = value[:half], value[half:]
    return jnp.concatenate([first * cosine - second * sine, second * cosine + first * sine])


def qkv_kernel(count, shared, x_ref, gain_ref, cos_ref, sin_ref, *refs):
    q_w, kv_w = refs[:count], refs[count : 2 * count]
    norm_ref, scale_ref, sets_ref = refs[2 * count :]
    normalise(x_ref, gain_ref, norm_ref, scale_ref)
    query = keyval = None
    for k in range(count):
        normed = norm_ref[k]
        part = dot(q_w[k][...], normed, TN)
        query = part if query is None else query + part
        part = dot(kv_w[k][...], normed)
        keyval = part if keyval is None else keyval + part
    cosine, sine = cos_ref[...], sin_ref[...]
    half = query.shape[0] // 2
    kv_half = keyval.shape[0] // 2
    for h in range(2):
        for at in range(0, half, HEAD):
            value = turn(query[h * half + at : h * half + at + HEAD], cosine, sine)
            sets_ref[h, at : at + HEAD, :] = (value * (ROOT * LOG2E)).astype(BF)
        at = 0 if shared else h * HEAD
        key = turn(keyval[at : at + HEAD], cosine, sine)
        sets_ref[h, half : half + HEAD, :] = key.astype(BF)
        sets_ref[h, half + HEAD : half + 2 * HEAD, :] = keyval[
            kv_half + at : kv_half + at + HEAD
        ].astype(BF)


def qkv_project(x, gain, cosine, sine, q_w, kv_w):
    cols, count, piece, tokens = x.shape
    half = q_w[0].shape[1] // 2
    shared = kv_w[0].shape[0] == 2 * HEAD
    return pl.pallas_call(
        functools.partial(qkv_kernel, count, shared),
        out_shape=(
            shape((count, cols * piece, tokens), BF),
            shape((1, tokens), F32),
            shape((2, half + 2 * HEAD, tokens), BF),
        ),
        compiler_params=params(),
        name="qkv_project",
        cost_estimate=takes(12),
    )(x, gain, cosine, sine, *q_w, *kv_w)


def pieces_of(half, at, tile, tokens):
    if half == 1:
        return [(0, 0, tokens, False), (1, 0, at + tile, True)]
    head = [(0, 0, at, False)] if at else []
    return head + [(0, at, at + tile, True)]


def seen_of(half, at, begin, end, tile, seg_row, seg_col):
    rows = lax.broadcasted_iota(jnp.int32, (end - begin, tile), 0) + begin
    cols = lax.broadcasted_iota(jnp.int32, (end - begin, tile), 1) + at
    seen = rows <= cols
    if half == 1:
        seen = seen & (seg_col[begin:end] == seg_row[:, at : at + tile])
    return seen


def place(parity, own_ref, other_ref, sets):
    sets[parity] = own_ref[...]
    sets[1 - parity] = other_ref[...]


def attend_kernel(
    tile, parity_ref, own_ref, other_ref, seg_row, seg_col, mine_ref, send_ref, lse_ref, sets, rows
):
    tokens = own_ref.shape[-1]
    heads = pl.num_programs(0)
    head = pl.program_id(0)
    parity = parity_ref[0]
    half_rows = own_ref.shape[0] - 2 * HEAD

    @pl.when(head == 0)
    def _():
        place(parity, own_ref, other_ref, sets)
        for half in range(2):
            keys = sets[half, half_rows : half_rows + HEAD, :]
            rows[half] = keys.astype(F32).T.astype(BF)

    at_head = pl.ds(pl.multiple_of(head * HEAD, 16), HEAD)
    for half in range(2):
        for at in range(0, tokens, tile):
            span = slice(at, at + tile)
            query = sets[half, at_head, span]
            pieces = pieces_of(half, at, tile, tokens)
            scores = []
            for which, begin, end, masked in pieces:
                part = dot(rows[which, begin:end, :], query)
                if masked:
                    part = jnp.where(
                        seen_of(half, at, begin, end, tile, seg_row, seg_col), part, NEG
                    )
                scores.append(part)
            peak = functools.reduce(
                jnp.maximum, [jnp.max(s, axis=0, keepdims=True) for s in scores]
            )
            total = out = None
            for (which, begin, end, _), part in zip(pieces, scores):
                weights = jnp.exp2(part - peak)
                mass = jnp.sum(weights, axis=0, keepdims=True)
                value = dot(sets[which, half_rows + HEAD :, begin:end], weights.astype(BF))
                total = mass if total is None else total + mass
                out = value if out is None else out + value
            out = (out / total).astype(BF)
            lse_ref[half, 0, :, span] = peak + jnp.log2(total)

            @pl.when(parity == half)
            def _():
                mine_ref[at_head, span] = out

            @pl.when(parity != half)
            def _():
                send_ref[at_head, span] = out


def attend(parity, own, other, seg):
    depth, tokens = own.shape
    half_rows = depth - 2 * HEAD
    heads = half_rows // HEAD
    tile = min(256, tokens)
    out = resident((half_rows, tokens))
    return pl.pallas_call(
        functools.partial(attend_kernel, tile),
        out_shape=(
            shape((half_rows, tokens), BF),
            shape((half_rows, tokens), BF),
            shape((2, heads, 1, tokens), F32),
        ),
        grid=(heads,),
        in_specs=[
            SMALL,
            resident((depth, tokens)),
            resident((depth, tokens)),
            resident((1, tokens)),
            resident((tokens, 1)),
        ],
        out_specs=(out, out, pl.BlockSpec((2, 1, 1, tokens), lambda h: (0, h, 0, 0))),
        scratch_shapes=[
            pltpu.VMEM((2, depth, tokens), BF),
            pltpu.VMEM((2, tokens, HEAD), BF),
        ],
        compiler_params=params(),
        name="attend",
        cost_estimate=takes(27),
    )(parity, own, other, seg[None, :], seg[:, None])


def attend_back_kernel(
    tile,
    parity_ref,
    own_ref,
    other_ref,
    own_out,
    other_out,
    own_grad,
    other_grad,
    lse_ref,
    seg_row,
    seg_col,
    mine_ref,
    send_ref,
    sets,
    outs,
    grads,
    rows,
    key_acc,
    value_acc,
):
    tokens = own_ref.shape[-1]
    heads = pl.num_programs(0)
    head = pl.program_id(0)
    parity = parity_ref[0]
    half_rows = own_ref.shape[0] - 2 * HEAD

    @pl.when(head == 0)
    def _():
        place(parity, own_ref, other_ref, sets)
        place(parity, own_out, other_out, outs)
        place(parity, own_grad, other_grad, grads)
        for half in range(2):
            for i in range(2):
                at = half_rows + i * HEAD
                rows[i, half] = sets[half, at : at + HEAD, :].astype(F32).T.astype(BF)
        key_acc[...] = jnp.zeros_like(key_acc)
        value_acc[...] = jnp.zeros_like(value_acc)

    at_head = pl.ds(pl.multiple_of(head * HEAD, 16), HEAD)
    for half in range(2):
        for at in range(0, tokens, tile):
            span = slice(at, at + tile)
            query = sets[half, at_head, span]
            grad = grads[half, at_head, span]
            lse = lse_ref[half, 0, :, span]
            delta = jnp.sum(
                grad.astype(F32) * outs[half, at_head, span].astype(F32), axis=0, keepdims=True
            )
            total = None
            for which, begin, end, masked in pieces_of(half, at, tile, tokens):
                part = dot(rows[0, which, begin:end, :], query)
                if masked:
                    part = jnp.where(
                        seen_of(half, at, begin, end, tile, seg_row, seg_col), part, NEG
                    )
                weights = jnp.exp2(part - lse)
                dprod = dot(rows[1, which, begin:end, :], grad)
                dscore = (weights * (dprod - delta)).astype(BF)
                value_acc[which, :, begin:end] += dot(grad, weights.astype(BF), NT)
                key_acc[which, :, begin:end] += dot(query, dscore, NT)
                more = dot(sets[which, half_rows : half_rows + HEAD, begin:end], dscore)
                total = more if total is None else total + more
            total = (total * ROOT).astype(BF)

            @pl.when(parity == half)
            def _():
                mine_ref[at_head, span] = total

            @pl.when(parity != half)
            def _():
                send_ref[at_head, span] = total

    @pl.when(head == heads - 1)
    def _():
        for ref, which in ((mine_ref, parity), (send_ref, 1 - parity)):
            ref[half_rows : half_rows + HEAD, :] = (key_acc[which] * LN2).astype(BF)
            ref[half_rows + HEAD :, :] = value_acc[which].astype(BF)


def attend_back(parity, own, other, own_out, other_out, own_grad, other_grad, lse, seg):
    depth, tokens = own.shape
    half_rows = depth - 2 * HEAD
    heads = half_rows // HEAD
    tile = min(256, tokens)
    full, part = resident((depth, tokens)), resident((half_rows, tokens))
    return pl.pallas_call(
        functools.partial(attend_back_kernel, tile),
        out_shape=(shape((depth, tokens), BF), shape((depth, tokens), BF)),
        grid=(heads,),
        in_specs=[
            SMALL,
            full,
            full,
            part,
            part,
            part,
            part,
            pl.BlockSpec((2, 1, 1, tokens), lambda h: (0, h, 0, 0)),
            resident((1, tokens)),
            resident((tokens, 1)),
        ],
        out_specs=(full, full),
        scratch_shapes=[
            pltpu.VMEM((2, depth, tokens), BF),
            pltpu.VMEM((2, half_rows, tokens), BF),
            pltpu.VMEM((2, half_rows, tokens), BF),
            pltpu.VMEM((2, 2, tokens, HEAD), BF),
            pltpu.VMEM((2, HEAD, tokens), F32),
            pltpu.VMEM((2, HEAD, tokens), F32),
        ],
        compiler_params=params(),
        name="attend_back",
        cost_estimate=takes(37),
    )(
        parity,
        own,
        other,
        own_out,
        other_out,
        own_grad,
        other_grad,
        lse,
        seg[None, :],
        seg[:, None],
    )


def halves_at(parity, half_rows):
    mine = pl.ds(pl.multiple_of(parity * half_rows, 16), half_rows)
    other = pl.ds(pl.multiple_of((1 - parity) * half_rows, 16), half_rows)
    return mine, other


def mix_out_kernel(count, parity_ref, own_ref, other_ref, *refs):
    weights, out_ref = refs[:count], refs[count]
    cols, _, piece, _ = out_ref.shape
    mine, other = halves_at(parity_ref[0], own_ref.shape[0])
    for k in range(count):
        part = dot(weights[k][mine, :], own_ref[...], TN)
        part = part + dot(weights[k][other, :], other_ref[...], TN)
        for c in range(cols):
            out_ref[c, k] = part[c * piece : (c + 1) * piece].astype(BF)


def mix_out(parity, own, other, weights, cols):
    count = len(weights)
    piece = weights[0].shape[1] // cols
    vmem = pl.BlockSpec(memory_space=pltpu.VMEM)
    return pl.pallas_call(
        functools.partial(mix_out_kernel, count),
        out_shape=shape((cols, count, piece, own.shape[1]), BF),
        in_specs=[SMALL] + [vmem] * (2 + count),
        compiler_params=params(),
        name="mix_out",
        cost_estimate=takes(10),
    )(parity, own, other, *weights)


def mix_back_kernel(count, parts, parity_ref, *refs):
    x_refs, weights = refs[:parts], refs[parts : parts + count]
    rows_ref, own_ref, other_ref = refs[parts + count :]
    for i, x_ref in enumerate(x_refs):
        cols, _, piece, tokens = x_ref.shape
        for c in range(cols):
            for k in range(count):
                rows_ref[k, c * piece : (c + 1) * piece, i * tokens : (i + 1) * tokens] = x_ref[
                    c, k
                ]
    mine, other = halves_at(parity_ref[0], own_ref.shape[0])
    for at, out_ref in ((other, other_ref), (mine, own_ref)):
        total = None
        for k in range(count):
            part = dot(weights[k][at, :], rows_ref[k])
            total = part if total is None else total + part
        out_ref[...] = total.astype(BF)


def mix_back(parity, x_parts, weights):
    parts = len(x_parts)
    cols, count, piece, tokens = x_parts[0].shape
    tokens = tokens * parts
    half_rows = weights[0].shape[0] // 2
    vmem = pl.BlockSpec(memory_space=pltpu.VMEM)
    return pl.pallas_call(
        functools.partial(mix_back_kernel, count, parts),
        out_shape=(
            shape((count, cols * piece, tokens), BF),
            shape((half_rows, tokens), BF),
            shape((half_rows, tokens), BF),
        ),
        in_specs=[SMALL] + [vmem] * (parts + count),
        compiler_params=params(),
        name="mix_back",
        cost_estimate=takes(9),
    )(parity, *x_parts, *weights)


def fan_kernel(count, x_ref, *refs):
    weights, out_ref = refs[:count], refs[count]
    cols, _, piece, _ = out_ref.shape
    for k in range(count):
        part = dot(weights[k][...], x_ref[...], TN)
        for c in range(cols):
            out_ref[c, k] = part[c * piece : (c + 1) * piece].astype(BF)


def fan_out(weights, x, cols):
    count = len(weights)
    piece = weights[0].shape[1] // cols
    return pl.pallas_call(
        functools.partial(fan_kernel, count),
        out_shape=shape((cols, count, piece, x.shape[1]), BF),
        compiler_params=params(),
        name="fan_out",
        cost_estimate=takes(17),
    )(x, *weights)


def norm_back(grads, k, x_ref, gain_ref, scale, coef, share_ref, gain_share_ref):
    cols, _, piece, _ = x_ref.shape
    for c in range(cols):
        grad = grads[c * piece : (c + 1) * piece]
        value = x_ref[c, k].astype(F32)
        gain_share_ref[c, k] = jnp.sum(grad * (value * scale), axis=1, keepdims=True)
        share_ref[c, k] = ((grad * gain_ref[c, k]) * scale - value * coef).astype(BF)


def ff_kernel(count, chained, x_ref, g_ref, gain_ref, *refs):
    gate_w, up_w, down_w = refs[:count], refs[count : 2 * count], refs[2 * count : 3 * count]
    refs = refs[3 * count + (5 if chained else 0) :]
    norm_ref, rows_ref, act_ref, dgate_ref, dup_ref, share_ref, gain_share_ref = refs[:7]
    scale_ref, inner_ref, back_ref = refs[7:]
    cols, _, piece, _ = x_ref.shape
    step = pl.program_id(0)

    @pl.when(step == 0)
    def _():
        normalise(x_ref, gain_ref, norm_ref, scale_ref)
        for c in range(cols):
            for k in range(count):
                rows_ref[k, c * piece : (c + 1) * piece, :] = g_ref[c, k]
        inner_ref[...] = jnp.zeros_like(inner_ref)
        back_ref[...] = jnp.zeros_like(back_ref)

    def summed(weights, ref):
        total = None
        for k in range(count):
            part = dot(weights[k][...], ref[k])
            total = part if total is None else total + part
        return total

    gate = summed(gate_w, norm_ref)
    up = summed(up_w, norm_ref)
    sigma = jax.nn.sigmoid(gate)
    silu = gate * sigma
    act_ref[...] = (silu * up).astype(BF)
    grad = summed(down_w, rows_ref)
    dup = grad * silu
    dgate = grad * up * (sigma + silu * (1.0 - sigma))
    inner_ref[...] += jnp.sum(dgate * gate + dup * up, axis=0, keepdims=True)
    dgate_ref[...] = dgate.astype(BF)
    dup_ref[...] = dup.astype(BF)
    for k in range(count):
        back_ref[k] += dot(gate_w[k][...], dgate_ref[...], TN) + dot(
            up_w[k][...], dup_ref[...], TN
        )

    @pl.when(step == pl.num_programs(0) - 1)
    def _():
        scale = scale_ref[...]
        coef = scale * scale * inner_ref[...] / D
        for k in range(count):
            norm_back(back_ref[k], k, x_ref, gain_ref, scale, coef, share_ref, gain_share_ref)


def feed_forward(x, g, part, parts, gain, gate_w, up_w, down_w, before):
    cols, count, piece, tokens = x.shape
    width, depth = gate_w[0].shape
    tile = 432 if width % 432 == 0 else width
    g_spec = pl.BlockSpec(x.shape, lambda n: (0, 0, 0, part), pipeline_mode=pl.Buffered(1))
    rows = (count, cols * piece, tokens)
    rows_spec = pl.BlockSpec(rows, lambda n: (0, 0, part), pipeline_mode=pl.Buffered(1))
    w_spec = pl.BlockSpec((tile, depth), lambda n: (n, 0))
    h_spec = pl.BlockSpec((tile, tokens), lambda n: (n, part))
    rows_all = shape((count, cols * piece, tokens * parts), BF)
    hidden = shape((width, tokens * parts), BF)
    first = 3 + 3 * count
    return pl.pallas_call(
        functools.partial(ff_kernel, count, bool(before)),
        out_shape=(
            rows_all,
            rows_all,
            hidden,
            hidden,
            hidden,
            shape(x.shape, BF),
            shape(gain.shape, F32),
        ),
        grid=(width // tile,),
        in_specs=[resident(x.shape, 1), g_spec, resident(gain.shape, 1)]
        + [w_spec] * (3 * count)
        + [RAW] * len(before),
        out_specs=(
            rows_spec,
            rows_spec,
            h_spec,
            h_spec,
            h_spec,
            resident(x.shape, 1),
            resident(gain.shape, 1),
        ),
        scratch_shapes=[
            pltpu.VMEM((1, tokens), F32),
            pltpu.VMEM((1, tokens), F32),
            pltpu.VMEM(rows, F32),
        ],
        input_output_aliases={first + i: i for i in range(len(before))},
        compiler_params=params(60),
        name="feed_forward",
        cost_estimate=takes(42),
    )(x, g, gain, *gate_w, *up_w, *down_w, *before)


def qkv_back_kernel(
    count,
    shared,
    parity_ref,
    x_ref,
    gain_ref,
    scale_ref,
    cos_ref,
    sin_ref,
    sets_ref,
    own_ref,
    other_ref,
    *refs,
):
    q_w, kv_w = refs[:count], refs[count : 2 * count]
    dq_ref, dkv_ref, share_ref, gain_share_ref = refs[2 * count :]
    parity = parity_ref[0]
    half_rows = own_ref.shape[0] - 2 * HEAD
    kv_half = dkv_ref.shape[0] // 2
    cosine, sine = cos_ref[...], -sin_ref[...]
    inner = None
    folded = None
    for grads, which in ((own_ref, parity), (other_ref, 1 - parity)):
        for at in range(0, half_rows + 2 * HEAD, HEAD):
            value = grads[at : at + HEAD, :].astype(F32)
            part = value * sets_ref[which, at : at + HEAD, :].astype(F32)
            part = jnp.sum(part, axis=0, keepdims=True)
            if at < half_rows:
                part = part * (1.0 / (ROOT * LOG2E))
                start = pl.multiple_of(which * half_rows + at, 16)
                dq_ref[pl.ds(start, HEAD), :] = turn(value, cosine, sine).astype(BF)
            else:
                is_key = at == half_rows
                raw = turn(value, cosine, sine) if is_key else value
                base = 0 if is_key else kv_half
                if not shared:
                    start = pl.multiple_of(base + which * HEAD, 16)
                    dkv_ref[pl.ds(start, HEAD), :] = raw.astype(BF)
                elif folded is None or at not in folded:
                    folded = {**(folded or {}), at: raw}
                else:
                    dkv_ref[base : base + HEAD, :] = (folded[at] + raw).astype(BF)
            inner = part if inner is None else inner + part
    scale = scale_ref[...]
    coef = scale * scale * inner / D
    for k in range(count):
        grads = dot(q_w[k][...], dq_ref[...]) + dot(kv_w[k][...], dkv_ref[...], TN)
        norm_back(grads, k, x_ref, gain_ref, scale, coef, share_ref, gain_share_ref)


def qkv_back(parity, x, gain, scale, cosine, sine, sets, own, other, q_w, kv_w):
    cols, count, piece, tokens = x.shape
    shared = kv_w[0].shape[0] == 2 * HEAD
    vmem = pl.BlockSpec(memory_space=pltpu.VMEM)
    return pl.pallas_call(
        functools.partial(qkv_back_kernel, count, shared),
        out_shape=(
            shape((q_w[0].shape[1], tokens), BF),
            shape((kv_w[0].shape[0], tokens), BF),
            shape(x.shape, BF),
            shape(gain.shape, F32),
        ),
        in_specs=[SMALL] + [vmem] * (8 + 2 * count),
        compiler_params=params(),
        name="qkv_back",
        cost_estimate=takes(17),
    )(parity, x, gain, scale, cosine, sine, sets, own, other, *q_w, *kv_w)


def rope_parts(positions):
    half = HEAD // 2
    freq = THETA ** (-jnp.arange(half, dtype=F32) * 2.0 / HEAD)
    angle = freq[:, None] * positions.astype(F32)[None, :]
    return (jnp.cos(angle), jnp.sin(angle))


def spread_cols(value):
    return lax.all_gather(value, "col", axis=0, tiled=False)


def sum_cols(value):
    return lax.psum_scatter(value, "col", scatter_dimension=0, tiled=False)


def sent_over_dp(value):
    low = value.astype(BF)
    size = lax.axis_size("dp")
    others = [
        lax.ppermute(low, "dp", [(i, (i + step) % size) for i in range(size)])
        for step in range(1, size)
    ]
    return [low] + others


def summed_up(parts):
    total = parts[0].astype(F32)
    for other in parts[1:]:
        total = total + other.astype(F32)
    return total


def over_dp(value):
    return summed_up(sent_over_dp(value))


def body(
    layer_input,
    attn_gain,
    mlp_gain,
    query_weight,
    key_weight,
    value_weight,
    mix_weight,
    gate_weight,
    up_weight,
    down_weight,
    output_grad,
    segment_ids,
    position_ids,
):
    rows = segment_ids.shape[0]
    count = lax.axis_size("row")
    cols = lax.axis_size("col")
    piece = layer_input.shape[1]
    row = lax.axis_index("row")
    parity = (row % 2).astype(jnp.int32)
    own_core = parity.reshape(1)
    q_half = query_weight.shape[1] // 2
    near, far = near_bits(count), far_bits(count)
    far_mask = far[-1]

    def row_tokens(value):
        turned = value.T
        outgoing = [
            lax.dynamic_slice(turned, (0, (row ^ k) * rows), (piece, rows)) for k in range(count)
        ]
        return jnp.stack(exchange_blocks(outgoing, "row"))

    def all_tokens(blocks):
        got = exchange_blocks([blocks[k] for k in range(count)], "row")
        result = jnp.zeros((piece, count * rows), BF)
        for k in range(count):
            result = lax.dynamic_update_slice(result, got[k], (0, (row ^ k) * rows))
        return result.T

    def listed(blocks):
        return [blocks[k] for k in range(count)]

    source_own = row_tokens(layer_input)
    source_own, output_grad = together(source_own, output_grad)
    grad_own = row_tokens(output_grad)
    kv_weight = jnp.concatenate([key_weight.T, value_weight.T])
    grad_own, query_weight, kv_weight = together(grad_own, query_weight, kv_weight)
    q_first = spread({0: query_weight}, "row", far)
    kv_first = spread({0: kv_weight}, "row", far)
    q_first, kv_first, mix_weight, gate_weight, attn_gain = together(
        q_first, kv_first, mix_weight, gate_weight, attn_gain
    )
    mix_first = spread({0: mix_weight}, "row", far)
    mix_first, up_weight = together(mix_first, up_weight)
    gate_first = spread({0: gate_weight.T}, "row", far)
    up_first = spread({0: up_weight.T}, "row", far)
    down_first = spread({0: down_weight}, "row", far)
    q_blocks = spread(q_first, "row", near)
    kv_blocks = spread(kv_first, "row", near)

    gains = lax.all_gather(jnp.stack([attn_gain, mlp_gain]), ("row", "col"), axis=1, tiled=True)
    gains = gains.reshape(2, count, cols, piece)
    gains = by_xor(gains, row, 1).swapaxes(1, 2)[..., None]
    gain_one, gain_two = gains[0], gains[1]

    cosine, sine = rope_parts(position_ids)
    other_seg = swapped(segment_ids, "row", 1)
    seg = jnp.where(parity == 0, other_seg, segment_ids)

    source = spread_cols(source_own)
    source, q_blocks, kv_blocks, gate_first, gain_one, cosine, sine, seg = together(
        source, q_blocks, kv_blocks, gate_first, gain_one, cosine, sine, seg
    )
    grad_own, source = together(grad_own, source)
    grad_all = spread_cols(grad_own)
    norm_one, scale_one, sets = qkv_project(
        source, gain_one, cosine, sine, listed(q_blocks), listed(kv_blocks)
    )
    own_set = lax.dynamic_index_in_dim(sets, parity, 0, keepdims=False)
    other_set = swapped(lax.dynamic_index_in_dim(sets, 1 - parity, 0, keepdims=False), "row", 1)
    attn_mine, attn_send, lse = attend(own_core, own_set, other_set, seg)
    attn_other = swapped(attn_send, "row", 1)
    mix_blocks = spread(mix_first, "row", near)
    attn_mine, attn_other, mix_blocks, up_first = together(
        attn_mine, attn_other, mix_blocks, up_first
    )
    attn_part = mix_out(own_core, attn_mine, attn_other, listed(mix_blocks), cols)
    attn_part, grad_all = together(attn_part, grad_all)
    attn_sum = sum_cols(attn_part)
    gate_blocks = spread(gate_first, "row", near)
    up_blocks = spread(up_first, "row", near)
    down_blocks = spread(down_first, "row", near)
    attn_sum, gate_blocks, up_blocks, down_blocks = together(
        attn_sum, gate_blocks, up_blocks, down_blocks
    )
    residual_own = source_own.astype(F32) + attn_sum.astype(F32)

    parts = 2 if rows % 256 == 0 else 1
    size = rows // parts
    spans = [slice(i * size, (i + 1) * size) for i in range(parts)]
    residual_low = residual_own.astype(BF)
    residual = [spread_cols(residual_low[..., span]) for span in spans]
    before, shares = (), []
    gain_share_two = 0.0
    for i in range(parts):
        out = feed_forward(
            residual[i],
            grad_all,
            i,
            parts,
            gain_two,
            listed(gate_blocks),
            listed(up_blocks),
            listed(down_blocks),
            before,
        )
        before = out[:5]
        shares.append(out[5])
        gain_share_two = gain_share_two + out[6]
    norm_two, grad_rows, act, dgate, dup = before
    share_sums = [sum_cols(share) for share in shares]
    down_grads = {k: dot(act, grad_rows[k], NT).astype(BF) for k in range(count)}
    down_grads = fold(down_grads, "row", near)
    dgate, dup, norm_two, down_grads = together(dgate, dup, norm_two, down_grads)
    gate_grads = {k: dot(dgate, norm_two[k], NT).astype(BF) for k in range(count)}
    up_grads = {k: dot(dup, norm_two[k], NT).astype(BF) for k in range(count)}
    gate_grads = fold(gate_grads, "row", near)
    up_grads = fold(up_grads, "row", near)
    cut = down_grads[0].shape[0] // 32 * 16
    head = {k: v[:cut] for k, v in down_grads.items()}
    tail = {k: v[cut:] for k, v in down_grads.items()}
    head_moved = {k: swapped(head[k], "row", far_mask) for k in head if k & far_mask}
    *share_sums, head, tail, head_moved, gate_grads, up_grads = together(
        *share_sums, head, tail, head_moved, gate_grads, up_grads
    )
    residual_grad_own = grad_own.astype(F32) + jnp.concatenate(share_sums, axis=2).astype(F32)
    head = fold(fold_landed(head, head_moved, far_mask), "row", far[::-1][1:])[0]
    tail = fold(tail, "row", far[::-1])[0]
    tail, gate_grads = together(tail, gate_grads)
    down_parts = sent_over_dp(jnp.concatenate([head, tail]))
    gate_total = fold(gate_grads, "row", far)[0]

    mix_cols = spread_cols(residual_grad_own.astype(BF))
    ff_part = fan_out(listed(down_blocks), act, cols)
    mix_cols, ff_part, down_parts, gate_total, up_grads = together(
        mix_cols, ff_part, down_parts, gate_total, up_grads
    )
    up_total = fold(up_grads, "row", far)[0]
    gate_parts = sent_over_dp(gate_total)
    mix_rows, grad_mine, grad_send = mix_back(own_core, [mix_cols], listed(mix_blocks))
    ff_sum = sum_cols(ff_part)
    grad_other = swapped(grad_send, "row", 1)
    back_mine, back_send = attend_back(
        own_core, own_set, other_set, attn_mine, attn_send, grad_mine, grad_other, lse, seg
    )
    back_other = swapped(back_send, "row", 1)
    back_other, up_total, gate_parts = together(back_other, up_total, gate_parts)
    cut = up_total.shape[0] * 5 // 9 // 16 * 16
    up_head, up_tail = over_dp(up_total[:cut]), up_total[cut:]
    dq, dkv, share, gain_share_one = qkv_back(
        own_core,
        source,
        gain_one,
        scale_one,
        cosine,
        sine,
        sets,
        back_mine,
        back_other,
        listed(q_blocks),
        listed(kv_blocks),
    )
    share, attn_mine, mix_rows = together(share, attn_mine, mix_rows)
    attn_low = jnp.concatenate(
        [
            jnp.where(parity == 0, attn_mine, attn_other),
            jnp.where(parity == 0, attn_other, attn_mine),
        ]
    )
    mix_odd = {k: dot(attn_low, mix_rows[k], NT).astype(BF) for k in range(1, count, 2)}
    gain_shares = jnp.stack([gain_share_one[..., 0], gain_share_two[..., 0]], axis=2)
    share, ff_sum, mix_odd, up_head, gain_shares = together(
        share, ff_sum, mix_odd, up_head, gain_shares
    )
    input_sum = sum_cols(share)

    bits = near + far[::-1]
    gain_shares = fold({k: gain_shares[:, k] for k in range(count)}, "row", bits, low=False)[0]
    share, dq, dkv, attn_low, mix_rows = together(share, dq, dkv, attn_low, mix_rows)
    mix_even = {k: dot(attn_low, mix_rows[k], NT).astype(BF) for k in range(0, count, 2)}
    mix_near = fold({**mix_even, **mix_odd}, "row", near)
    mix_even, up_tail = together(mix_even, up_tail)
    up_tail = sent_over_dp(up_tail)
    dq, dkv, mix_near = together(dq, dkv, mix_near)
    mix_moved = {k: swapped(mix_near[k], "row", far_mask) for k in mix_near if k & far_mask}
    q_near = fold({k: dot(norm_one[k], dq, NT).astype(BF) for k in range(count)}, "row", near)
    kv_near = fold({k: dot(dkv, norm_one[k], NT).astype(BF) for k in range(count)}, "row", near)
    ff_sum, gain_shares, q_near, kv_near, up_tail, mix_near, mix_moved = together(
        ff_sum, gain_shares, q_near, kv_near, up_tail, mix_near, mix_moved
    )
    q_near, gate_parts, down_parts = together(q_near, gate_parts, down_parts)
    gate_total, down_total = summed_up(gate_parts), summed_up(down_parts)
    mix_far = fold_landed(mix_near, mix_moved, far_mask)
    mix_total = over_dp(fold(mix_far, "row", far[::-1][1:])[0])
    q_far = fold(q_near, "row", far)[0]
    q_far, kv_near = together(q_far, kv_near)
    kv_far = fold(kv_near, "row", far)[0]
    q_total, kv_total = over_dp(q_far), over_dp(kv_far)
    output_own = (residual_own + ff_sum.astype(F32)).astype(BF)
    layer_output = all_tokens(output_own)

    gain_shares = by_xor(gain_shares, lax.axis_index("col"), 0)
    gain_shares = {c: gain_shares[c] for c in range(cols)}
    gain_shares = fold(gain_shares, "col", near_bits(cols) + far_bits(cols), low=False)[0]
    gain_totals = over_dp(gain_shares)
    up_total = jnp.concatenate([up_head, summed_up(up_tail)])
    input_sum, q_total, kv_total, mix_total, gain_totals, layer_output, up_total = together(
        input_sum, q_total, kv_total, mix_total, gain_totals, layer_output, up_total
    )

    input_blocks = [
        (residual_grad_own[k] + input_sum[k].astype(F32)).astype(BF) for k in range(count)
    ]
    input_grad = all_tokens(input_blocks).astype(F32)
    kv_rows = kv_total.shape[0] // 2
    return (
        layer_output,
        input_grad,
        gain_totals[0],
        gain_totals[1],
        q_total,
        kv_total[:kv_rows].T,
        kv_total[kv_rows:].T,
        mix_total,
        gate_total.T,
        up_total.T,
        down_total,
    )


def solution(mesh):
    return jax.shard_map(
        body,
        mesh=mesh,
        in_specs=(
            P("dp", ("row", "col")),
            P(("row", "col")),
            P(("row", "col")),
            P("row", "col"),
            P("row", "col"),
            P("row", "col"),
            P("col", "row"),
            P("row", "col"),
            P("row", "col"),
            P("col", "row"),
            P("dp", ("row", "col")),
            P(("dp", "row")),
            P(("dp", "row")),
        ),
        out_specs=(
            P("dp", ("row", "col")),
            P("dp", ("row", "col")),
            P(("row", "col")),
            P(("row", "col")),
            P("row", "col"),
            P("row", "col"),
            P("row", "col"),
            P("col", "row"),
            P("row", "col"),
            P("row", "col"),
            P("col", "row"),
        ),
        check_vma=False,
    )
```

```python
import functools

import jax
import jax.numpy as jnp
from jax import lax
from jax.experimental import pallas as pl
from jax.experimental.pallas import tpu as pltpu
from jax.sharding import PartitionSpec as P

D = 2560
HEAD = 80
EPS = 1e-05
THETA = 10000.0
NEG = -1e30
LOG2E = 1.4426950408889634
LN2 = 0.6931471805599453
ROOT = HEAD ** (-0.5)
BF = jnp.bfloat16
F32 = jnp.float32
NN = (((1,), (0,)), ((), ()))
TN = (((0,), (0,)), ((), ()))
NT = (((1,), (1,)), ((), ()))


def dot(left, right, dims=NN):
    return lax.dot_general(left, right, dims, preferred_element_type=F32)


def together(*values):
    return lax.optimization_barrier(values)


def swapped(value, axis, mask):
    size = lax.axis_size(axis)
    return lax.ppermute(value, axis, [(i, i ^ mask) for i in range(size)])


def spread(blocks, axis, bits):
    blocks = dict(blocks)
    for bit in bits:
        for k in list(blocks):
            blocks[k | bit] = swapped(blocks[k], axis, bit)
    return blocks


def fold(blocks, axis, bits, low=True):
    held = dict(blocks)
    for bit in bits:
        for k in [k for k in held if k & bit]:
            other = swapped(held.pop(k), axis, bit)
            total = held[k ^ bit].astype(F32) + other.astype(F32)
            held[k ^ bit] = total.astype(BF) if low else total
    return held


def fold_landed(held, moved, bit):
    return {
        k ^ bit: (held[k ^ bit].astype(F32) + other.astype(F32)).astype(BF)
        for k, other in moved.items()
    }


def far_bits(size):
    return [1 << i for i in range(1, size.bit_length() - 1)]


def near_bits(size):
    return [1] if size > 1 else []


def exchange_blocks(blocks, axis):
    return [blocks[0]] + [swapped(blocks[k], axis, k) for k in range(1, len(blocks))]


def by_xor(value, index, axis):
    parts = [
        lax.dynamic_index_in_dim(value, index ^ k, axis, keepdims=True)
        for k in range(value.shape[axis])
    ]
    return jnp.concatenate(parts, axis=axis)


def params(mib=58):
    return pltpu.CompilerParams(vmem_limit_bytes=mib * 1024 * 1024)


def takes(micros):
    return pl.CostEstimate(flops=int(micros * 0.1e9), transcendentals=0, bytes_accessed=0)


def shape(dims, dtype):
    return jax.ShapeDtypeStruct(dims, dtype)


SMALL = pl.BlockSpec(memory_space=pltpu.SMEM)
RAW = pl.BlockSpec(memory_space=pl.ANY)


def resident(dims, buffers=None):
    zeros = (0,) * len(dims)
    mode = {} if buffers is None else {"pipeline_mode": pl.Buffered(buffers)}
    return pl.BlockSpec(dims, lambda *_: zeros, **mode)


def normalise(x_ref, gain_ref, out_ref, scale_ref):
    cols, count, piece, _ = x_ref.shape
    total = None
    for c in range(cols):
        for k in range(count):
            value = x_ref[c, k].astype(F32)
            part = jnp.sum(value * value, axis=0, keepdims=True)
            total = part if total is None else total + part
    scale = lax.rsqrt(total / D + EPS)
    scale_ref[...] = scale
    for c in range(cols):
        for k in range(count):
            value = x_ref[c, k].astype(F32) * scale * gain_ref[c, k]
            out_ref[k, c * piece : (c + 1) * piece, :] = value.astype(BF)


def turn(value, cosine, sine):
    half = value.shape[0] // 2
    first, second = value[:half], value[half:]
    return jnp.concatenate([first * cosine - second * sine, second * cosine + first * sine])


def qkv_kernel(count, shared, x_ref, gain_ref, cos_ref, sin_ref, *refs):
    q_w, kv_w = refs[:count], refs[count : 2 * count]
    norm_ref, scale_ref, sets_ref = refs[2 * count :]
    normalise(x_ref, gain_ref, norm_ref, scale_ref)
    query = keyval = None
    for k in range(count):
        normed = norm_ref[k]
        part = dot(q_w[k][...], normed, TN)
        query = part if query is None else query + part
        part = dot(kv_w[k][...], normed)
        keyval = part if keyval is None else keyval + part
    cosine, sine = cos_ref[...], sin_ref[...]
    half = query.shape[0] // 2
    kv_half = keyval.shape[0] // 2
    for h in range(2):
        for at in range(0, half, HEAD):
            value = turn(query[h * half + at : h * half + at + HEAD], cosine, sine)
            sets_ref[h, at : at + HEAD, :] = (value * (ROOT * LOG2E)).astype(BF)
        at = 0 if shared else h * HEAD
        key = turn(keyval[at : at + HEAD], cosine, sine)
        sets_ref[h, half : half + HEAD, :] = key.astype(BF)
        sets_ref[h, half + HEAD : half + 2 * HEAD, :] = keyval[
            kv_half + at : kv_half + at + HEAD
        ].astype(BF)


def qkv_project(x, gain, cosine, sine, q_w, kv_w):
    cols, count, piece, tokens = x.shape
    half = q_w[0].shape[1] // 2
    shared = kv_w[0].shape[0] == 2 * HEAD
    return pl.pallas_call(
        functools.partial(qkv_kernel, count, shared),
        out_shape=(
            shape((count, cols * piece, tokens), BF),
            shape((1, tokens), F32),
            shape((2, half + 2 * HEAD, tokens), BF),
        ),
        compiler_params=params(),
        name="qkv_project",
        cost_estimate=takes(12),
    )(x, gain, cosine, sine, *q_w, *kv_w)


def pieces_of(half, at, tile, tokens):
    if half == 1:
        return [(0, 0, tokens, False), (1, 0, at + tile, True)]
    head = [(0, 0, at, False)] if at else []
    return head + [(0, at, at + tile, True)]


def seen_of(half, at, begin, end, tile, seg_row, seg_col):
    rows = lax.broadcasted_iota(jnp.int32, (end - begin, tile), 0) + begin
    cols = lax.broadcasted_iota(jnp.int32, (end - begin, tile), 1) + at
    seen = rows <= cols
    if half == 1:
        seen = seen & (seg_col[begin:end] == seg_row[:, at : at + tile])
    return seen


def place(parity, own_ref, other_ref, sets):
    sets[parity] = own_ref[...]
    sets[1 - parity] = other_ref[...]


def attend_kernel(
    tile, parity_ref, own_ref, other_ref, seg_row, seg_col, mine_ref, send_ref, lse_ref, sets, rows
):
    tokens = own_ref.shape[-1]
    heads = pl.num_programs(0)
    head = pl.program_id(0)
    parity = parity_ref[0]
    half_rows = own_ref.shape[0] - 2 * HEAD

    @pl.when(head == 0)
    def _():
        place(parity, own_ref, other_ref, sets)
        for half in range(2):
            keys = sets[half, half_rows : half_rows + HEAD, :]
            rows[half] = keys.astype(F32).T.astype(BF)

    at_head = pl.ds(pl.multiple_of(head * HEAD, 16), HEAD)
    for half in range(2):
        for at in range(0, tokens, tile):
            span = slice(at, at + tile)
            query = sets[half, at_head, span]
            pieces = pieces_of(half, at, tile, tokens)
            scores = []
            for which, begin, end, masked in pieces:
                part = dot(rows[which, begin:end, :], query)
                if masked:
                    part = jnp.where(
                        seen_of(half, at, begin, end, tile, seg_row, seg_col), part, NEG
                    )
                scores.append(part)
            peak = functools.reduce(
                jnp.maximum, [jnp.max(s, axis=0, keepdims=True) for s in scores]
            )
            total = out = None
            for (which, begin, end, _), part in zip(pieces, scores):
                weights = jnp.exp2(part - peak)
                mass = jnp.sum(weights, axis=0, keepdims=True)
                value = dot(sets[which, half_rows + HEAD :, begin:end], weights.astype(BF))
                total = mass if total is None else total + mass
                out = value if out is None else out + value
            out = (out / total).astype(BF)
            lse_ref[half, 0, :, span] = peak + jnp.log2(total)

            @pl.when(parity == half)
            def _():
                mine_ref[at_head, span] = out

            @pl.when(parity != half)
            def _():
                send_ref[at_head, span] = out


def attend(parity, own, other, seg):
    depth, tokens = own.shape
    half_rows = depth - 2 * HEAD
    heads = half_rows // HEAD
    tile = min(256, tokens)
    out = resident((half_rows, tokens))
    return pl.pallas_call(
        functools.partial(attend_kernel, tile),
        out_shape=(
            shape((half_rows, tokens), BF),
            shape((half_rows, tokens), BF),
            shape((2, heads, 1, tokens), F32),
        ),
        grid=(heads,),
        in_specs=[
            SMALL,
            resident((depth, tokens)),
            resident((depth, tokens)),
            resident((1, tokens)),
            resident((tokens, 1)),
        ],
        out_specs=(out, out, pl.BlockSpec((2, 1, 1, tokens), lambda h: (0, h, 0, 0))),
        scratch_shapes=[
            pltpu.VMEM((2, depth, tokens), BF),
            pltpu.VMEM((2, tokens, HEAD), BF),
        ],
        compiler_params=params(),
        name="attend",
        cost_estimate=takes(27),
    )(parity, own, other, seg[None, :], seg[:, None])


def attend_back_kernel(
    tile,
    parity_ref,
    own_ref,
    other_ref,
    own_out,
    other_out,
    own_grad,
    other_grad,
    lse_ref,
    seg_row,
    seg_col,
    mine_ref,
    send_ref,
    sets,
    outs,
    grads,
    rows,
    key_acc,
    value_acc,
):
    tokens = own_ref.shape[-1]
    heads = pl.num_programs(0)
    head = pl.program_id(0)
    parity = parity_ref[0]
    half_rows = own_ref.shape[0] - 2 * HEAD

    @pl.when(head == 0)
    def _():
        place(parity, own_ref, other_ref, sets)
        place(parity, own_out, other_out, outs)
        place(parity, own_grad, other_grad, grads)
        for half in range(2):
            for i in range(2):
                at = half_rows + i * HEAD
                rows[i, half] = sets[half, at : at + HEAD, :].astype(F32).T.astype(BF)
        key_acc[...] = jnp.zeros_like(key_acc)
        value_acc[...] = jnp.zeros_like(value_acc)

    at_head = pl.ds(pl.multiple_of(head * HEAD, 16), HEAD)
    for half in range(2):
        for at in range(0, tokens, tile):
            span = slice(at, at + tile)
            query = sets[half, at_head, span]
            grad = grads[half, at_head, span]
            lse = lse_ref[half, 0, :, span]
            delta = jnp.sum(
                grad.astype(F32) * outs[half, at_head, span].astype(F32), axis=0, keepdims=True
            )
            total = None
            for which, begin, end, masked in pieces_of(half, at, tile, tokens):
                part = dot(rows[0, which, begin:end, :], query)
                if masked:
                    part = jnp.where(
                        seen_of(half, at, begin, end, tile, seg_row, seg_col), part, NEG
                    )
                weights = jnp.exp2(part - lse)
                dprod = dot(rows[1, which, begin:end, :], grad)
                dscore = (weights * (dprod - delta)).astype(BF)
                value_acc[which, :, begin:end] += dot(grad, weights.astype(BF), NT)
                key_acc[which, :, begin:end] += dot(query, dscore, NT)
                more = dot(sets[which, half_rows : half_rows + HEAD, begin:end], dscore)
                total = more if total is None else total + more
            total = (total * ROOT).astype(BF)

            @pl.when(parity == half)
            def _():
                mine_ref[at_head, span] = total

            @pl.when(parity != half)
            def _():
                send_ref[at_head, span] = total

    @pl.when(head == heads - 1)
    def _():
        for ref, which in ((mine_ref, parity), (send_ref, 1 - parity)):
            ref[half_rows : half_rows + HEAD, :] = (key_acc[which] * LN2).astype(BF)
            ref[half_rows + HEAD :, :] = value_acc[which].astype(BF)


def attend_back(parity, own, other, own_out, other_out, own_grad, other_grad, lse, seg):
    depth, tokens = own.shape
    half_rows = depth - 2 * HEAD
    heads = half_rows // HEAD
    tile = min(256, tokens)
    full, part = resident((depth, tokens)), resident((half_rows, tokens))
    return pl.pallas_call(
        functools.partial(attend_back_kernel, tile),
        out_shape=(shape((depth, tokens), BF), shape((depth, tokens), BF)),
        grid=(heads,),
        in_specs=[
            SMALL,
            full,
            full,
            part,
            part,
            part,
            part,
            pl.BlockSpec((2, 1, 1, tokens), lambda h: (0, h, 0, 0)),
            resident((1, tokens)),
            resident((tokens, 1)),
        ],
        out_specs=(full, full),
        scratch_shapes=[
            pltpu.VMEM((2, depth, tokens), BF),
            pltpu.VMEM((2, half_rows, tokens), BF),
            pltpu.VMEM((2, half_rows, tokens), BF),
            pltpu.VMEM((2, 2, tokens, HEAD), BF),
            pltpu.VMEM((2, HEAD, tokens), F32),
            pltpu.VMEM((2, HEAD, tokens), F32),
        ],
        compiler_params=params(),
        name="attend_back",
        cost_estimate=takes(37),
    )(
        parity,
        own,
        other,
        own_out,
        other_out,
        own_grad,
        other_grad,
        lse,
        seg[None, :],
        seg[:, None],
    )


def halves_at(parity, half_rows):
    mine = pl.ds(pl.multiple_of(parity * half_rows, 16), half_rows)
    other = pl.ds(pl.multiple_of((1 - parity) * half_rows, 16), half_rows)
    return mine, other


def mix_out_kernel(count, parity_ref, own_ref, other_ref, *refs):
    weights, out_ref = refs[:count], refs[count]
    cols, _, piece, _ = out_ref.shape
    mine, other = halves_at(parity_ref[0], own_ref.shape[0])
    for k in range(count):
        part = dot(weights[k][mine, :], own_ref[...], TN)
        part = part + dot(weights[k][other, :], other_ref[...], TN)
        for c in range(cols):
            out_ref[c, k] = part[c * piece : (c + 1) * piece].astype(BF)


def mix_out(parity, own, other, weights, cols):
    count = len(weights)
    piece = weights[0].shape[1] // cols
    vmem = pl.BlockSpec(memory_space=pltpu.VMEM)
    return pl.pallas_call(
        functools.partial(mix_out_kernel, count),
        out_shape=shape((cols, count, piece, own.shape[1]), BF),
        in_specs=[SMALL] + [vmem] * (2 + count),
        compiler_params=params(),
        name="mix_out",
        cost_estimate=takes(10),
    )(parity, own, other, *weights)


def mix_back_kernel(count, parts, parity_ref, *refs):
    x_refs, weights = refs[:parts], refs[parts : parts + count]
    rows_ref, own_ref, other_ref = refs[parts + count :]
    for i, x_ref in enumerate(x_refs):
        cols, _, piece, tokens = x_ref.shape
        for c in range(cols):
            for k in range(count):
                rows_ref[k, c * piece : (c + 1) * piece, i * tokens : (i + 1) * tokens] = x_ref[
                    c, k
                ]
    mine, other = halves_at(parity_ref[0], own_ref.shape[0])
    for at, out_ref in ((other, other_ref), (mine, own_ref)):
        total = None
        for k in range(count):
            part = dot(weights[k][at, :], rows_ref[k])
            total = part if total is None else total + part
        out_ref[...] = total.astype(BF)


def mix_back(parity, x_parts, weights):
    parts = len(x_parts)
    cols, count, piece, tokens = x_parts[0].shape
    tokens = tokens * parts
    half_rows = weights[0].shape[0] // 2
    vmem = pl.BlockSpec(memory_space=pltpu.VMEM)
    return pl.pallas_call(
        functools.partial(mix_back_kernel, count, parts),
        out_shape=(
            shape((count, cols * piece, tokens), BF),
            shape((half_rows, tokens), BF),
            shape((half_rows, tokens), BF),
        ),
        in_specs=[SMALL] + [vmem] * (parts + count),
        compiler_params=params(),
        name="mix_back",
        cost_estimate=takes(9),
    )(parity, *x_parts, *weights)


def fan_kernel(count, x_ref, *refs):
    weights, out_ref = refs[:count], refs[count]
    cols, _, piece, _ = out_ref.shape
    for k in range(count):
        part = dot(weights[k][...], x_ref[...], TN)
        for c in range(cols):
            out_ref[c, k] = part[c * piece : (c + 1) * piece].astype(BF)


def fan_out(weights, x, cols):
    count = len(weights)
    piece = weights[0].shape[1] // cols
    return pl.pallas_call(
        functools.partial(fan_kernel, count),
        out_shape=shape((cols, count, piece, x.shape[1]), BF),
        compiler_params=params(),
        name="fan_out",
        cost_estimate=takes(17),
    )(x, *weights)


def norm_back(grads, k, x_ref, gain_ref, scale, coef, share_ref, gain_share_ref):
    cols, _, piece, _ = x_ref.shape
    for c in range(cols):
        grad = grads[c * piece : (c + 1) * piece]
        value = x_ref[c, k].astype(F32)
        gain_share_ref[c, k] = jnp.sum(grad * (value * scale), axis=1, keepdims=True)
        share_ref[c, k] = ((grad * gain_ref[c, k]) * scale - value * coef).astype(BF)


def ff_kernel(count, chained, x_ref, g_ref, gain_ref, *refs):
    gate_w, up_w, down_w = refs[:count], refs[count : 2 * count], refs[2 * count : 3 * count]
    refs = refs[3 * count + (5 if chained else 0) :]
    norm_ref, rows_ref, act_ref, dgate_ref, dup_ref, share_ref, gain_share_ref = refs[:7]
    scale_ref, inner_ref, back_ref = refs[7:]
    cols, _, piece, _ = x_ref.shape
    step = pl.program_id(0)

    @pl.when(step == 0)
    def _():
        normalise(x_ref, gain_ref, norm_ref, scale_ref)
        for c in range(cols):
            for k in range(count):
                rows_ref[k, c * piece : (c + 1) * piece, :] = g_ref[c, k]
        inner_ref[...] = jnp.zeros_like(inner_ref)
        back_ref[...] = jnp.zeros_like(back_ref)

    def summed(weights, ref):
        total = None
        for k in range(count):
            part = dot(weights[k][...], ref[k])
            total = part if total is None else total + part
        return total

    gate = summed(gate_w, norm_ref)
    up = summed(up_w, norm_ref)
    sigma = jax.nn.sigmoid(gate)
    silu = gate * sigma
    act_ref[...] = (silu * up).astype(BF)
    grad = summed(down_w, rows_ref)
    dup = grad * silu
    dgate = grad * up * (sigma + silu * (1.0 - sigma))
    inner_ref[...] += jnp.sum(dgate * gate + dup * up, axis=0, keepdims=True)
    dgate_ref[...] = dgate.astype(BF)
    dup_ref[...] = dup.astype(BF)
    for k in range(count):
        back_ref[k] += dot(gate_w[k][...], dgate_ref[...], TN) + dot(
            up_w[k][...], dup_ref[...], TN
        )

    @pl.when(step == pl.num_programs(0) - 1)
    def _():
        scale = scale_ref[...]
        coef = scale * scale * inner_ref[...] / D
        for k in range(count):
            norm_back(back_ref[k], k, x_ref, gain_ref, scale, coef, share_ref, gain_share_ref)


def feed_forward(x, g, part, parts, gain, gate_w, up_w, down_w, before):
    cols, count, piece, tokens = x.shape
    width, depth = gate_w[0].shape
    tile = 432 if width % 432 == 0 else width
    g_spec = pl.BlockSpec(x.shape, lambda n: (0, 0, 0, part), pipeline_mode=pl.Buffered(1))
    rows = (count, cols * piece, tokens)
    rows_spec = pl.BlockSpec(rows, lambda n: (0, 0, part), pipeline_mode=pl.Buffered(1))
    w_spec = pl.BlockSpec((tile, depth), lambda n: (n, 0))
    h_spec = pl.BlockSpec((tile, tokens), lambda n: (n, part))
    rows_all = shape((count, cols * piece, tokens * parts), BF)
    hidden = shape((width, tokens * parts), BF)
    first = 3 + 3 * count
    return pl.pallas_call(
        functools.partial(ff_kernel, count, bool(before)),
        out_shape=(
            rows_all,
            rows_all,
            hidden,
            hidden,
            hidden,
            shape(x.shape, BF),
            shape(gain.shape, F32),
        ),
        grid=(width // tile,),
        in_specs=[resident(x.shape, 1), g_spec, resident(gain.shape, 1)]
        + [w_spec] * (3 * count)
        + [RAW] * len(before),
        out_specs=(
            rows_spec,
            rows_spec,
            h_spec,
            h_spec,
            h_spec,
            resident(x.shape, 1),
            resident(gain.shape, 1),
        ),
        scratch_shapes=[
            pltpu.VMEM((1, tokens), F32),
            pltpu.VMEM((1, tokens), F32),
            pltpu.VMEM(rows, F32),
        ],
        input_output_aliases={first + i: i for i in range(len(before))},
        compiler_params=params(60),
        name="feed_forward",
        cost_estimate=takes(42),
    )(x, g, gain, *gate_w, *up_w, *down_w, *before)


def qkv_back_kernel(
    count,
    shared,
    parity_ref,
    x_ref,
    gain_ref,
    scale_ref,
    cos_ref,
    sin_ref,
    sets_ref,
    own_ref,
    other_ref,
    *refs,
):
    q_w, kv_w = refs[:count], refs[count : 2 * count]
    dq_ref, dkv_ref, share_ref, gain_share_ref = refs[2 * count :]
    parity = parity_ref[0]
    half_rows = own_ref.shape[0] - 2 * HEAD
    kv_half = dkv_ref.shape[0] // 2
    cosine, sine = cos_ref[...], -sin_ref[...]
    inner = None
    folded = None
    for grads, which in ((own_ref, parity), (other_ref, 1 - parity)):
        for at in range(0, half_rows + 2 * HEAD, HEAD):
            value = grads[at : at + HEAD, :].astype(F32)
            part = value * sets_ref[which, at : at + HEAD, :].astype(F32)
            part = jnp.sum(part, axis=0, keepdims=True)
            if at < half_rows:
                part = part * (1.0 / (ROOT * LOG2E))
                start = pl.multiple_of(which * half_rows + at, 16)
                dq_ref[pl.ds(start, HEAD), :] = turn(value, cosine, sine).astype(BF)
            else:
                is_key = at == half_rows
                raw = turn(value, cosine, sine) if is_key else value
                base = 0 if is_key else kv_half
                if not shared:
                    start = pl.multiple_of(base + which * HEAD, 16)
                    dkv_ref[pl.ds(start, HEAD), :] = raw.astype(BF)
                elif folded is None or at not in folded:
                    folded = {**(folded or {}), at: raw}
                else:
                    dkv_ref[base : base + HEAD, :] = (folded[at] + raw).astype(BF)
            inner = part if inner is None else inner + part
    scale = scale_ref[...]
    coef = scale * scale * inner / D
    for k in range(count):
        grads = dot(q_w[k][...], dq_ref[...]) + dot(kv_w[k][...], dkv_ref[...], TN)
        norm_back(grads, k, x_ref, gain_ref, scale, coef, share_ref, gain_share_ref)


def qkv_back(parity, x, gain, scale, cosine, sine, sets, own, other, q_w, kv_w):
    cols, count, piece, tokens = x.shape
    shared = kv_w[0].shape[0] == 2 * HEAD
    vmem = pl.BlockSpec(memory_space=pltpu.VMEM)
    return pl.pallas_call(
        functools.partial(qkv_back_kernel, count, shared),
        out_shape=(
            shape((q_w[0].shape[1], tokens), BF),
            shape((kv_w[0].shape[0], tokens), BF),
            shape(x.shape, BF),
            shape(gain.shape, F32),
        ),
        in_specs=[SMALL] + [vmem] * (8 + 2 * count),
        compiler_params=params(),
        name="qkv_back",
        cost_estimate=takes(17),
    )(parity, x, gain, scale, cosine, sine, sets, own, other, *q_w, *kv_w)


def rope_parts(positions):
    half = HEAD // 2
    freq = THETA ** (-jnp.arange(half, dtype=F32) * 2.0 / HEAD)
    angle = freq[:, None] * positions.astype(F32)[None, :]
    return (jnp.cos(angle), jnp.sin(angle))


def spread_cols(value):
    return lax.all_gather(value, "col", axis=0, tiled=False)


def sum_cols(value):
    return lax.psum_scatter(value, "col", scatter_dimension=0, tiled=False)


def sent_over_dp(value):
    low = value.astype(BF)
    size = lax.axis_size("dp")
    others = [
        lax.ppermute(low, "dp", [(i, (i + step) % size) for i in range(size)])
        for step in range(1, size)
    ]
    return [low] + others


def summed_up(parts):
    total = parts[0].astype(F32)
    for other in parts[1:]:
        total = total + other.astype(F32)
    return total


def over_dp(value):
    return summed_up(sent_over_dp(value))


def body(
    layer_input,
    attn_gain,
    mlp_gain,
    query_weight,
    key_weight,
    value_weight,
    mix_weight,
    gate_weight,
    up_weight,
    down_weight,
    output_grad,
    segment_ids,
    position_ids,
):
    rows = segment_ids.shape[0]
    count = lax.axis_size("row")
    cols = lax.axis_size("col")
    piece = layer_input.shape[1]
    row = lax.axis_index("row")
    parity = (row % 2).astype(jnp.int32)
    own_core = parity.reshape(1)
    q_half = query_weight.shape[1] // 2
    near, far = near_bits(count), far_bits(count)
    far_mask = far[-1]

    def row_tokens(value):
        turned = value.T
        outgoing = [
            lax.dynamic_slice(turned, (0, (row ^ k) * rows), (piece, rows)) for k in range(count)
        ]
        return jnp.stack(exchange_blocks(outgoing, "row"))

    def all_tokens(blocks, dtype=BF):
        got = exchange_blocks([blocks[k] for k in range(count)], "row")
        result = jnp.zeros((piece, count * rows), dtype)
        for k in range(count):
            result = lax.dynamic_update_slice(
                result, got[k].astype(dtype), (0, (row ^ k) * rows)
            )
        return result.T

    def listed(blocks):
        return [blocks[k] for k in range(count)]

    source_own = row_tokens(layer_input)
    source_own, output_grad = together(source_own, output_grad)
    grad_own = row_tokens(output_grad)
    kv_weight = jnp.concatenate([key_weight.T, value_weight.T])
    grad_own, query_weight, kv_weight = together(grad_own, query_weight, kv_weight)
    q_first = spread({0: query_weight}, "row", far)
    kv_first = spread({0: kv_weight}, "row", far)
    q_first, kv_first, mix_weight, gate_weight, attn_gain = together(
        q_first, kv_first, mix_weight, gate_weight, attn_gain
    )
    mix_first = spread({0: mix_weight}, "row", far)
    mix_first, up_weight = together(mix_first, up_weight)
    gate_first = spread({0: gate_weight.T}, "row", far)
    up_first = spread({0: up_weight.T}, "row", far)
    down_first = spread({0: down_weight}, "row", far)
    q_blocks = spread(q_first, "row", near)
    kv_blocks = spread(kv_first, "row", near)

    gains = lax.all_gather(jnp.stack([attn_gain, mlp_gain]), ("row", "col"), axis=1, tiled=True)
    gains = gains.reshape(2, count, cols, piece)
    gains = by_xor(gains, row, 1).swapaxes(1, 2)[..., None]
    gain_one, gain_two = gains[0], gains[1]

    cosine, sine = rope_parts(position_ids)
    other_seg = swapped(segment_ids, "row", 1)
    seg = jnp.where(parity == 0, other_seg, segment_ids)

    source = spread_cols(source_own)
    source, q_blocks, kv_blocks, gate_first, gain_one, cosine, sine, seg = together(
        source, q_blocks, kv_blocks, gate_first, gain_one, cosine, sine, seg
    )
    grad_own, source = together(grad_own, source)
    grad_all = spread_cols(grad_own)
    norm_one, scale_one, sets = qkv_project(
        source, gain_one, cosine, sine, listed(q_blocks), listed(kv_blocks)
    )
    own_set = lax.dynamic_index_in_dim(sets, parity, 0, keepdims=False)
    other_set = swapped(lax.dynamic_index_in_dim(sets, 1 - parity, 0, keepdims=False), "row", 1)
    attn_mine, attn_send, lse = attend(own_core, own_set, other_set, seg)
    attn_other = swapped(attn_send, "row", 1)
    mix_blocks = spread(mix_first, "row", near)
    attn_mine, attn_other, mix_blocks, up_first = together(
        attn_mine, attn_other, mix_blocks, up_first
    )
    attn_part = mix_out(own_core, attn_mine, attn_other, listed(mix_blocks), cols)
    attn_part, grad_all = together(attn_part, grad_all)
    attn_sum = sum_cols(attn_part)
    gate_blocks = spread(gate_first, "row", near)
    up_blocks = spread(up_first, "row", near)
    down_blocks = spread(down_first, "row", near)
    attn_sum, gate_blocks, up_blocks, down_blocks = together(
        attn_sum, gate_blocks, up_blocks, down_blocks
    )
    residual_own = source_own.astype(F32) + attn_sum.astype(F32)

    parts = 2 if rows % 256 == 0 else 1
    size = rows // parts
    spans = [slice(i * size, (i + 1) * size) for i in range(parts)]
    lows = []
    for span in spans:
        low = source_own[..., span].astype(F32) + attn_sum[..., span].astype(F32)
        lows.append(low.astype(BF))
        attn_sum, *lows = together(attn_sum, *lows)
    residual = [spread_cols(low) for low in lows]
    before, shares = (), []
    gain_share_two = 0.0
    for i in range(parts):
        out = feed_forward(
            residual[i],
            grad_all,
            i,
            parts,
            gain_two,
            listed(gate_blocks),
            listed(up_blocks),
            listed(down_blocks),
            before,
        )
        before = out[:5]
        shares.append(out[5])
        gain_share_two = gain_share_two + out[6]
    norm_two, grad_rows, act, dgate, dup = before
    share_sums = [sum_cols(share) for share in shares]
    down_grads = {k: dot(act, grad_rows[k], NT).astype(BF) for k in range(count)}
    down_grads = fold(down_grads, "row", near)
    dgate, dup, norm_two, down_grads = together(dgate, dup, norm_two, down_grads)
    gate_grads = {k: dot(dgate, norm_two[k], NT).astype(BF) for k in range(count)}
    up_grads = {k: dot(dup, norm_two[k], NT).astype(BF) for k in range(count)}
    gate_grads = fold(gate_grads, "row", near)
    up_grads = fold(up_grads, "row", near)
    cut = down_grads[0].shape[0] // 32 * 16
    head = {k: v[:cut] for k, v in down_grads.items()}
    tail = {k: v[cut:] for k, v in down_grads.items()}
    head_moved = {k: swapped(head[k], "row", far_mask) for k in head if k & far_mask}
    *share_sums, head, tail, head_moved, gate_grads, up_grads = together(
        *share_sums, head, tail, head_moved, gate_grads, up_grads
    )
    residual_grad_own = grad_own.astype(F32) + jnp.concatenate(share_sums, axis=2).astype(F32)
    head = fold(fold_landed(head, head_moved, far_mask), "row", far[::-1][1:])[0]
    tail = fold(tail, "row", far[::-1])[0]
    tail, gate_grads = together(tail, gate_grads)
    down_parts = sent_over_dp(jnp.concatenate([head, tail]))
    gate_total = fold(gate_grads, "row", far)[0]

    mix_cols = spread_cols(residual_grad_own.astype(BF))
    ff_part = fan_out(listed(down_blocks), act, cols)
    mix_cols, ff_part, down_parts, gate_total, up_grads = together(
        mix_cols, ff_part, down_parts, gate_total, up_grads
    )
    up_total = fold(up_grads, "row", far)[0]
    gate_parts = sent_over_dp(gate_total)
    mix_rows, grad_mine, grad_send = mix_back(own_core, [mix_cols], listed(mix_blocks))
    ff_sum = sum_cols(ff_part)
    grad_other = swapped(grad_send, "row", 1)
    back_mine, back_send = attend_back(
        own_core, own_set, other_set, attn_mine, attn_send, grad_mine, grad_other, lse, seg
    )
    back_other = swapped(back_send, "row", 1)
    back_other, up_total, gate_parts = together(back_other, up_total, gate_parts)
    cut = up_total.shape[0] * 5 // 9 // 16 * 16
    up_head, up_tail = over_dp(up_total[:cut]), sent_over_dp(up_total[cut:])
    dq, dkv, share, gain_share_one = qkv_back(
        own_core,
        source,
        gain_one,
        scale_one,
        cosine,
        sine,
        sets,
        back_mine,
        back_other,
        listed(q_blocks),
        listed(kv_blocks),
    )
    share, attn_mine, mix_rows = together(share, attn_mine, mix_rows)
    attn_low = jnp.concatenate(
        [
            jnp.where(parity == 0, attn_mine, attn_other),
            jnp.where(parity == 0, attn_other, attn_mine),
        ]
    )
    mix_odd = {k: dot(attn_low, mix_rows[k], NT).astype(BF) for k in range(1, count, 2)}
    gain_shares = jnp.stack([gain_share_one[..., 0], gain_share_two[..., 0]], axis=2)
    share, ff_sum, mix_odd, up_head, gain_shares = together(
        share, ff_sum, mix_odd, up_head, gain_shares
    )
    input_sum = sum_cols(share)

    bits = near + far[::-1]
    gain_shares = fold({k: gain_shares[:, k] for k in range(count)}, "row", bits, low=False)[0]
    share, dq, dkv, attn_low, mix_rows = together(share, dq, dkv, attn_low, mix_rows)
    mix_even = {k: dot(attn_low, mix_rows[k], NT).astype(BF) for k in range(0, count, 2)}
    mix_near = fold({**mix_even, **mix_odd}, "row", near)
    dq, dkv, mix_near = together(dq, dkv, mix_near)
    mix_moved = {k: swapped(mix_near[k], "row", far_mask) for k in mix_near if k & far_mask}
    q_near = fold({k: dot(norm_one[k], dq, NT).astype(BF) for k in range(count)}, "row", near)
    kv_near = fold({k: dot(dkv, norm_one[k], NT).astype(BF) for k in range(count)}, "row", near)
    ff_sum, gain_shares, q_near, kv_near, up_tail, mix_near, mix_moved = together(
        ff_sum, gain_shares, q_near, kv_near, up_tail, mix_near, mix_moved
    )
    q_near, gate_parts, down_parts = together(q_near, gate_parts, down_parts)
    gate_total, down_total = summed_up(gate_parts), summed_up(down_parts)
    mix_far = fold_landed(mix_near, mix_moved, far_mask)
    mix_total = over_dp(fold(mix_far, "row", far[::-1][1:])[0])
    q_far = fold(q_near, "row", far)[0]
    q_far, kv_near = together(q_far, kv_near)
    kv_far = fold(kv_near, "row", far)[0]
    q_total, kv_total = over_dp(q_far), over_dp(kv_far)
    output_own = (residual_own + ff_sum.astype(F32)).astype(BF)
    layer_output = all_tokens(output_own)

    gain_shares = by_xor(gain_shares, lax.axis_index("col"), 0)
    gain_shares = {c: gain_shares[c] for c in range(cols)}
    gain_shares = fold(gain_shares, "col", near_bits(cols) + far_bits(cols), low=False)[0]
    gain_totals = over_dp(gain_shares)
    up_total = jnp.concatenate([up_head, summed_up(up_tail)])
    input_sum, q_total, kv_total, mix_total, gain_totals, layer_output, up_total = together(
        input_sum, q_total, kv_total, mix_total, gain_totals, layer_output, up_total
    )

    input_low = (residual_grad_own + input_sum.astype(F32)).astype(BF)
    input_grad = all_tokens(input_low, F32)
    kv_rows = kv_total.shape[0] // 2
    return (
        layer_output,
        input_grad,
        gain_totals[0],
        gain_totals[1],
        q_total,
        kv_total[:kv_rows].T,
        kv_total[kv_rows:].T,
        mix_total,
        gate_total.T,
        up_total.T,
        down_total,
    )


def solution(mesh):
    return jax.shard_map(
        body,
        mesh=mesh,
        in_specs=(
            P("dp", ("row", "col")),
            P(("row", "col")),
            P(("row", "col")),
            P("row", "col"),
            P("row", "col"),
            P("row", "col"),
            P("col", "row"),
            P("row", "col"),
            P("row", "col"),
            P("col", "row"),
            P("dp", ("row", "col")),
            P(("dp", "row")),
            P(("dp", "row")),
        ),
        out_specs=(
            P("dp", ("row", "col")),
            P("dp", ("row", "col")),
            P(("row", "col")),
            P(("row", "col")),
            P("row", "col"),
            P("row", "col"),
            P("row", "col"),
            P("col", "row"),
            P("row", "col"),
            P("row", "col"),
            P("col", "row"),
        ),
        check_vma=False,
    )
```
